128 devices in a mesh: tile: 16 (over z, y), band: 8 (over x, core).
Axes of the slice: x: 4, y: 4, z: 4, core: 2. Of those that a mesh axis runs over, the one named last changes fastest.
Arguments:
- points: float32 [32768, 3, 128], P(('tile', 'band')), may hold values from -6 to 6
- normals: float32 [32768, 3, 128], P(('tile', 'band')), may hold values from -4 to 4
- poses: float32 [6, 1024], P(None, ('tile', 'band')), may hold values from -4 to 4
- directions: float32 [2, 6, 1024], P(None, None, ('tile', 'band')), may hold values from -6 to 6
- local_pairs: int32 [2, 32768], P(None, ('tile', 'band')), may hold values from 0 to 255
- local_maps: int32 [32768, 128], P(('tile', 'band')), may hold values from 0 to 127
- remote_src: int32 [128, 1024], P(('tile', 'band')), may hold values from 0 to 255
- remote_maps: int32 [128, 1024, 128], P(('tile', 'band')), may hold values from 0 to 127
- remote_dst: int32 [128, 1024], P(('tile', 'band')), may hold values from 0 to 255
- counts: int32 [128, 128], P(('tile', 'band')), may hold values from 4 to 8, as said below
Outputs:
- gradient: float32 [6, 1024], P(None, ('tile', 'band'))
- hess_products: float32 [2, 6, 1024], P(None, None, ('tile', 'band'))
The draws below stay inside these ranges and needn't reach their ends.
Inputs may be any that keep to these rules, and one draw needn't show every extreme that they name: `counts`: in every row some device pair uses all 8 slots.
All inputs are finite; a program needn't handle non-finite values.
Results may differ from the reference program's by a relative error of at most 0.0003.
Values sent between devices are 32-bit elements; how exact they have to be, the bound alone decides.
A program may use at most 64 MiB of HBM per device.

```python
import jax
import jax.numpy as jnp
from jax import lax

F_DEV = 8
BF = 32
PB = 128
NLOC = 256
CAP = 8
NBL = 256
FRAGS = 1024
BLOCKS = 32768
N_TILE = 16
N_BAND = 8


def draw_counts(key, part):
    devices = N_TILE * N_BAND
    key_base, key_full = jax.random.split(key)
    counts_base = jax.random.randint(key_base, (devices, devices), CAP // 2, CAP + 1)
    full_peer = jax.random.randint(key_full, (devices,), 0, devices)
    return jnp.where(jnp.arange(devices)[None, :] == full_peer[:, None], CAP, counts_base).astype(jnp.int32)


def plant(values, stream_key, smallest, largest):
    extent = values.shape
    place = [jax.random.randint(jax.random.fold_in(stream_key, axis), (), 0, extent[axis]) for axis in range(len(extent))]
    values = values.at[tuple(place)].set(smallest)
    longest = extent.index(max(extent))
    place[longest] = (place[longest] + 1) % extent[longest]
    return values.at[tuple(place)].set(largest)


def levels(rng, shape, cuts, smallest, largest):
    gain = 1.0
    for dim, blocks in cuts:
        heights = jax.random.uniform(jax.random.fold_in(jax.random.fold_in(rng, 6), dim), (blocks,), jnp.float32, smallest / len(cuts), largest / len(cuts))
        gain = gain * jnp.repeat(jnp.exp(heights), shape[dim] // blocks).reshape((-1,) + (1,) * (len(shape) - 1 - dim))
    return gain


def scatter_about(stream_key, extent, scale, limit, pieces=(), held_as=jnp.bfloat16):
    entries = jax.random.normal(stream_key, extent, jnp.float32) * scale
    if len(pieces) > 0:
        entries = levels(stream_key, extent, pieces, -0.22, 0.18) * entries
    return jnp.clip(entries, min=-limit, max=limit).astype(held_as)


def setup_inputs(seed: int = 0) -> dict:
    streams_of = jax.random.split(jax.random.key(seed), 11)
    return {
        "points": scatter_about(streams_of[0], (BLOCKS, 3, PB), 1.0, 6.0, ((0, 128),), jnp.float32),
        "normals": scatter_about(streams_of[1], (BLOCKS, 3, PB), 0.6, 4.0, ((0, 128),), jnp.float32),
        "poses": scatter_about(streams_of[2], (6, FRAGS), 0.6, 4.0, ((1, 128),), jnp.float32),
        "directions": scatter_about(streams_of[3], (2, 6, FRAGS), 1.0, 6.0, ((2, 128),), jnp.float32),
        "local_pairs": plant(jax.random.randint(streams_of[4], (2, NLOC * N_TILE * N_BAND), 0, NBL), jax.random.fold_in(streams_of[4], 1), 0, NBL - 1).astype(jnp.int32),
        "local_maps": plant(jax.random.randint(streams_of[5], (NLOC * N_TILE * N_BAND, PB), 0, PB), jax.random.fold_in(streams_of[5], 1), 0, PB - 1).astype(jnp.int32),
        "remote_src": plant(jax.random.randint(streams_of[6], (N_TILE * N_BAND, N_TILE * N_BAND * CAP), 0, NBL), jax.random.fold_in(streams_of[6], 1), 0, NBL - 1).astype(jnp.int32),
        "remote_maps": plant(jax.random.randint(streams_of[7], (N_TILE * N_BAND, N_TILE * N_BAND * CAP, PB), 0, PB), jax.random.fold_in(streams_of[7], 1), 0, PB - 1).astype(jnp.int32),
        "remote_dst": plant(jax.random.randint(streams_of[8], (N_TILE * N_BAND, N_TILE * N_BAND * CAP), 0, NBL), jax.random.fold_in(streams_of[8], 1), 0, NBL - 1).astype(jnp.int32),
        "counts": draw_counts(jax.random.fold_in(streams_of[10], 71), 0),
    }


def rotations(poses):
    half_angle = poses[0:3] * 0.5
    inverse = 1.0 / jnp.sqrt(1.0 + half_angle[0] * half_angle[0] + half_angle[1] * half_angle[1] + half_angle[2] * half_angle[2])
    quat_w = inverse
    quat_x = half_angle[0] * inverse
    quat_y = half_angle[1] * inverse
    quat_z = half_angle[2] * inverse
    rotation = [[1.0 - 2.0 * (quat_y * quat_y + quat_z * quat_z), 2.0 * (quat_x * quat_y - quat_w * quat_z), 2.0 * (quat_x * quat_z + quat_w * quat_y)], [2.0 * (quat_x * quat_y + quat_w * quat_z), 1.0 - 2.0 * (quat_x * quat_x + quat_z * quat_z), 2.0 * (quat_y * quat_z - quat_w * quat_x)], [2.0 * (quat_x * quat_z - quat_w * quat_y), 2.0 * (quat_y * quat_z + quat_w * quat_x), 1.0 - 2.0 * (quat_x * quat_x + quat_y * quat_y)]]
    return (rotation, poses[3:6])

def to_world(points, normals, poses, per_pose):
    rotation, translation = rotations(poses)

    def spread(values):
        return jnp.repeat(values, per_pose)[:, None]
    world_rows = []
    normal_rows = []
    for i in range(3):
        coeffs = [spread(rotation[i][j]) for j in range(3)]
        world_rows.append(coeffs[0] * points[:, 0] + coeffs[1] * points[:, 1] + coeffs[2] * points[:, 2] + spread(translation[i]))
        normal_rows.append(coeffs[0] * normals[:, 0] + coeffs[1] * normals[:, 1] + coeffs[2] * normals[:, 2])
    return (jnp.stack(world_rows, axis=1), jnp.stack(normal_rows, axis=1))

def cross_rows(left, right):
    return [left[:, 1] * right[:, 2] - left[:, 2] * right[:, 1], left[:, 2] * right[:, 0] - left[:, 0] * right[:, 2], left[:, 0] * right[:, 1] - left[:, 1] * right[:, 0]]

def pick_points(world_pts, normal_pts, point_maps):
    index = jnp.broadcast_to(point_maps[:, None, :], world_pts.shape)
    return (jnp.take_along_axis(world_pts, index, axis=2), jnp.take_along_axis(normal_pts, index, axis=2))

def pair_terms(world_a, world_b, normal_b, dirs_a, dirs_b, valid_mask, blocks_frag):
    count = world_a.shape[2]
    offset = world_a - world_b
    residual = (normal_b[:, 0] * offset[:, 0] + normal_b[:, 1] * offset[:, 1] + normal_b[:, 2] * offset[:, 2]) * valid_mask[:, None]
    normal_list = [normal_b[:, 0], normal_b[:, 1], normal_b[:, 2]]
    jac_a = jnp.stack(cross_rows(world_a, normal_b) + normal_list, axis=1)
    jac_b = -jnp.stack(cross_rows(world_b, normal_b) + normal_list, axis=1)
    grad_scale = 1.0 / count
    hess_scale = 1.0 / (count * blocks_frag)
    parts_a = [lax.optimization_barrier(jnp.sum(residual[:, None] * jac_a, axis=2)) * grad_scale]
    parts_b = [lax.optimization_barrier(jnp.sum(residual[:, None] * jac_b, axis=2)) * grad_scale]
    for v in range(2):
        along_dir = (lax.optimization_barrier(jnp.sum(jac_a * dirs_a[:, 6 * v:6 * v + 6, None], axis=1)) + lax.optimization_barrier(jnp.sum(jac_b * dirs_b[:, 6 * v:6 * v + 6, None], axis=1))) * valid_mask[:, None]
        parts_a.append(lax.optimization_barrier(jnp.sum(along_dir[:, None] * jac_a, axis=2)) * hess_scale)
        parts_b.append(lax.optimization_barrier(jnp.sum(along_dir[:, None] * jac_b, axis=2)) * hess_scale)
    return (jnp.concatenate(parts_a, axis=1), jnp.concatenate(parts_b, axis=1))

def reference(points, normals, poses, directions, local_pairs, local_maps, remote_src, remote_maps, remote_dst, counts):
    devices = N_TILE * N_BAND
    blocks_dev = F_DEV * BF
    frag_total = F_DEV * devices
    world_pts, normal_pts = to_world(points, normals, poses, BF)
    frag_dirs = directions.reshape(12, frag_total).T
    slot_iota = jnp.arange(CAP, dtype=jnp.int32)
    peer_iota = jnp.arange(devices, dtype=jnp.int32)
    local_ones = jnp.ones((NLOC,), jnp.float32)

    def step(totals, device):
        block_base = device * blocks_dev
        local_idx = lax.dynamic_slice_in_dim(local_pairs, device * NLOC, NLOC, 1)
        point_maps = lax.dynamic_slice_in_dim(local_maps, device * NLOC, NLOC, 0)
        source = block_base + local_idx[0]
        target = block_base + local_idx[1]
        world_b, normal_b = pick_points(world_pts[target], normal_pts[target], point_maps)
        terms_a, terms_b = pair_terms(world_pts[source], world_b, normal_b, frag_dirs[source // BF], frag_dirs[target // BF], local_ones, BF)
        totals = totals.at[source // BF].add(terms_a).at[target // BF].add(terms_b)
        source = block_base + lax.dynamic_index_in_dim(remote_src, device, 0, keepdims=False)
        point_maps = lax.dynamic_index_in_dim(remote_maps, device, 0, keepdims=False)
        target = (lax.dynamic_slice_in_dim(remote_dst, device * CAP, CAP, 1) + (peer_iota * blocks_dev)[:, None]).reshape(-1)
        used_slots = lax.dynamic_index_in_dim(counts, device, 0, keepdims=False)
        valid_mask = (slot_iota[None, :] < used_slots[:, None]).astype(jnp.float32).reshape(-1)
        world_b, normal_b = pick_points(world_pts[target], normal_pts[target], point_maps)
        terms_a, terms_b = pair_terms(world_pts[source], world_b, normal_b, frag_dirs[source // BF], frag_dirs[target // BF], valid_mask, BF)
        totals = totals.at[source // BF].add(terms_a).at[target // BF].add(terms_b)
        return (totals, None)
    totals, unused = lax.scan(step, jnp.zeros((frag_total, 18), jnp.float32), jnp.arange(devices, dtype=jnp.int32))
    gradient = totals[:, 0:6].T
    hess_products = totals[:, 6:18].T.reshape(2, 6, frag_total)
    return (gradient, hess_products)
```

```python
import jax
import jax.numpy as jnp
import numpy as np
from jax import lax
from jax.experimental import pallas as pl
from jax.experimental.pallas import tpu as pltpu
from jax.sharding import PartitionSpec as P

BF = 32
CAP = 8
N_QTY = 27


def rotations(poses):
    half_angle = poses[0:3] * 0.5
    inverse = 1.0 / jnp.sqrt(
        1.0
        + half_angle[0] * half_angle[0]
        + half_angle[1] * half_angle[1]
        + half_angle[2] * half_angle[2]
    )
    quat_x = half_angle[0] * inverse
    quat_y = half_angle[1] * inverse
    quat_z = half_angle[2] * inverse
    rotation = [
        [
            1.0 - 2.0 * (quat_y * quat_y + quat_z * quat_z),
            2.0 * (quat_x * quat_y - inverse * quat_z),
            2.0 * (quat_x * quat_z + inverse * quat_y),
        ],
        [
            2.0 * (quat_x * quat_y + inverse * quat_z),
            1.0 - 2.0 * (quat_x * quat_x + quat_z * quat_z),
            2.0 * (quat_y * quat_z - inverse * quat_x),
        ],
        [
            2.0 * (quat_x * quat_z - inverse * quat_y),
            2.0 * (quat_y * quat_z + inverse * quat_x),
            1.0 - 2.0 * (quat_x * quat_x + quat_y * quat_y),
        ],
    ]
    return (rotation, poses[3:6])


def to_world_rows(points, normals, poses, per_pose):
    rotation, translation = rotations(poses)

    def spread(values):
        return jnp.repeat(values, per_pose)[:, None]

    world_rows = []
    normal_rows = []
    for i in range(3):
        coeffs = [spread(rotation[i][j]) for j in range(3)]
        world_rows.append(
            coeffs[0] * points[:, 0]
            + coeffs[1] * points[:, 1]
            + coeffs[2] * points[:, 2]
            + spread(translation[i])
        )
        normal_rows.append(
            coeffs[0] * normals[:, 0] + coeffs[1] * normals[:, 1] + coeffs[2] * normals[:, 2]
        )
    return jnp.stack(world_rows + normal_rows, axis=0)


def _lane_of(q):
    lane = 3
    for j in range(5):
        if ((q >> j) & 1) == 0:
            lane += 64 >> j
    return lane


_LANES = np.array([_lane_of(q) for q in range(N_QTY)], np.int32)


def _lane_reduce(vals, lane):
    h = 64
    while len(vals) > 1:
        merged = []
        for i in range(0, len(vals), 2):
            left = vals[i] + pltpu.roll(vals[i], h, 1)
            right = vals[i + 1] + pltpu.roll(vals[i + 1], 128 - h, 1)
            merged.append(jnp.where((lane & h) != 0, left, right))
        vals = merged
        h //= 2
    x = vals[0]
    while h >= 1:
        x = x + pltpu.roll(x, h, 1)
        h //= 2
    return x


def _terms_kernel(xa_ref, tb_ref, map_ref, aux_ref, out_ref):
    groups = out_ref.shape[0] // 8
    lane = lax.broadcasted_iota(jnp.int32, (8, 128), 1)

    def body(g, carry):
        rows = pl.ds(pl.multiple_of(g * 8, 8), 8)
        idx = map_ref[rows, :]
        xa = [xa_ref[c, rows, :] for c in range(3)]
        picked = [
            jnp.take_along_axis(tb_ref[c, rows, :], idx, axis=1, mode="promise_in_bounds")
            for c in range(6)
        ]
        xb = picked[0:3]
        nb = picked[3:6]
        aux = aux_ref[rows, :]

        def col(q):
            return jnp.broadcast_to(aux[:, q : q + 1], (8, 128))

        valid = col(24)
        off = [xa[c] - xb[c] for c in range(3)]
        res = (nb[0] * off[0] + nb[1] * off[1] + nb[2] * off[2]) * valid
        ja = [
            xa[1] * nb[2] - xa[2] * nb[1],
            xa[2] * nb[0] - xa[0] * nb[2],
            xa[0] * nb[1] - xa[1] * nb[0],
            nb[0],
            nb[1],
            nb[2],
        ]
        jb = [
            -(xb[1] * nb[2] - xb[2] * nb[1]),
            -(xb[2] * nb[0] - xb[0] * nb[2]),
            -(xb[0] * nb[1] - xb[1] * nb[0]),
            -nb[0],
            -nb[1],
            -nb[2],
        ]
        weights = [res]
        for v in range(2):
            sa = ja[0] * col(6 * v)
            sb = jb[0] * col(12 + 6 * v)
            for c in range(1, 6):
                sa = sa + ja[c] * col(6 * v + c)
                sb = sb + jb[c] * col(12 + 6 * v + c)
            weights.append((sa + sb) * valid)
        vals = []
        for w in weights:
            vals.extend([w * ja[c] for c in range(6)])
        for w in weights:
            vals.extend([w * jb[c] for c in range(3)])
        zero = jnp.zeros((8, 128), jnp.float32)
        vals.extend([zero] * (32 - len(vals)))
        out_ref[rows, :] = _lane_reduce(vals, lane)
        return carry

    lax.fori_loop(0, groups, body, 0)


def pair_sums(xa, tb, maps, aux, block=256):
    pairs = maps.shape[0]
    block = min(block, pairs)
    return pl.pallas_call(
        _terms_kernel,
        out_shape=jax.ShapeDtypeStruct((pairs, 128), jnp.float32),
        grid=(pairs // block,),
        in_specs=[
            pl.BlockSpec((3, block, 128), lambda i: (0, i, 0)),
            pl.BlockSpec((6, block, 128), lambda i: (0, i, 0)),
            pl.BlockSpec((block, 128), lambda i: (i, 0)),
            pl.BlockSpec((block, 128), lambda i: (i, 0)),
        ],
        out_specs=pl.BlockSpec((block, 128), lambda i: (i, 0)),
    )(xa, tb, maps, aux)


def split_terms(out):
    sel = out[:, _LANES]
    ga = sel[:, 0:6] * (1.0 / 128)
    ha = sel[:, 6:18] * (1.0 / 4096)
    gb = jnp.concatenate([sel[:, 18:21], -sel[:, 3:6]], axis=1) * (1.0 / 128)
    hb0 = jnp.concatenate([sel[:, 21:24], -sel[:, 9:12]], axis=1) * (1.0 / 4096)
    hb1 = jnp.concatenate([sel[:, 24:27], -sel[:, 15:18]], axis=1) * (1.0 / 4096)
    return jnp.concatenate([ga, ha], axis=1), jnp.concatenate([gb, hb0, hb1], axis=1)


def frag_sums(blocks, terms, frag_count):
    onehot = (blocks[:, None] // BF == jnp.arange(frag_count, dtype=jnp.int32)[None, :]).astype(
        jnp.float32
    )
    return jnp.dot(onehot.T, terms, precision=lax.Precision.HIGHEST)


def make_aux(dirs_a, dirs_b, valid):
    pairs = dirs_a.shape[0]
    return jnp.concatenate(
        [dirs_a, dirs_b, valid[:, None], jnp.zeros((pairs, 128 - 25), jnp.float32)], axis=1
    )


def local(
    points,
    normals,
    poses,
    directions,
    local_pairs,
    local_maps,
    remote_src,
    remote_maps,
    remote_dst,
    counts,
):
    axes = ("tile", "band")
    frag_count = poses.shape[1]
    rows6 = to_world_rows(points, normals, poses, BF)
    frag_dirs = directions.reshape(12, frag_count).T
    peers = counts.shape[1]

    source_blocks = remote_src[0]
    valid = (
        (jnp.arange(CAP, dtype=jnp.int32)[None, :] < counts[0][:, None])
        .astype(jnp.float32)
        .reshape(-1)
    )
    xa_send = jnp.transpose(rows6[0:3][:, source_blocks], (1, 0, 2))
    map_send = remote_maps[0].astype(jnp.float32)[:, None, :]
    main = jnp.concatenate([xa_send, map_send], axis=1).reshape(peers, CAP * 4, 128)
    side = jnp.concatenate([frag_dirs[source_blocks // BF], valid[:, None]], axis=1)
    side = side.reshape(peers, CAP * 13)
    side = jnp.concatenate([side, jnp.zeros((peers, 128 - CAP * 13), jnp.float32)], axis=1)
    cargo = jnp.concatenate([main, side[:, None, :]], axis=1)
    arrived = lax.all_to_all(cargo, axes, split_axis=0, concat_axis=0, tiled=True)

    src_l = local_pairs[0]
    tgt_l = local_pairs[1]
    ones = jnp.ones((src_l.shape[0],), jnp.float32)
    out_l = pair_sums(
        rows6[0:3][:, src_l],
        rows6[:, tgt_l],
        local_maps,
        make_aux(frag_dirs[src_l // BF], frag_dirs[tgt_l // BF], ones),
    )
    local_a, local_b = split_terms(out_l)

    target_blocks = remote_dst[0]
    main_in = arrived[:, 0 : CAP * 4].reshape(peers * CAP, 4, 128)
    side_in = arrived[:, CAP * 4, 0 : CAP * 13].reshape(peers * CAP, 13)
    out_r = pair_sums(
        jnp.transpose(main_in[:, 0:3], (1, 0, 2)),
        rows6[:, target_blocks],
        main_in[:, 3].astype(jnp.int32),
        make_aux(side_in[:, 0:12], frag_dirs[target_blocks // BF], side_in[:, 12]),
    )
    remote_a, remote_b = split_terms(out_r)
    returned = lax.all_to_all(
        remote_a.reshape(peers, CAP * 18), axes, split_axis=0, concat_axis=0, tiled=True
    ).reshape(peers * CAP, 18)

    totals = frag_sums(src_l, local_a, frag_count) + frag_sums(tgt_l, local_b, frag_count)
    totals = (
        totals
        + frag_sums(target_blocks, remote_b, frag_count)
        + frag_sums(source_blocks, returned, frag_count)
    )
    gradient = totals[:, 0:6].T
    hess_products = totals[:, 6:18].T.reshape(2, 6, frag_count)
    return (gradient, hess_products)


def solution(mesh):
    placed = (
        P(("tile", "band"), None, None),
        P(("tile", "band"), None, None),
        P(None, ("tile", "band")),
        P(None, None, ("tile", "band")),
        P(None, ("tile", "band")),
        P(("tile", "band"), None),
        P(("tile", "band"), None),
        P(("tile", "band"), None, None),
        P(("tile", "band"), None),
        P(("tile", "band"), None),
    )
    return jax.shard_map(
        local,
        mesh=mesh,
        in_specs=placed,
        out_specs=(P(None, ("tile", "band")), P(None, None, ("tile", "band"))),
        check_vma=False,
    )
```

```python
import jax
import jax.numpy as jnp
from jax import lax
from jax.experimental import pallas as pl
from jax.experimental.pallas import tpu as pltpu
from jax.sharding import PartitionSpec as P

BF = 32
CAP = 8
N_QTY = 27


def rotations(poses):
    half_angle = poses[0:3] * 0.5
    inverse = 1.0 / jnp.sqrt(
        1.0
        + half_angle[0] * half_angle[0]
        + half_angle[1] * half_angle[1]
        + half_angle[2] * half_angle[2]
    )
    quat_x = half_angle[0] * inverse
    quat_y = half_angle[1] * inverse
    quat_z = half_angle[2] * inverse
    rotation = [
        [
            1.0 - 2.0 * (quat_y * quat_y + quat_z * quat_z),
            2.0 * (quat_x * quat_y - inverse * quat_z),
            2.0 * (quat_x * quat_z + inverse * quat_y),
        ],
        [
            2.0 * (quat_x * quat_y + inverse * quat_z),
            1.0 - 2.0 * (quat_x * quat_x + quat_z * quat_z),
            2.0 * (quat_y * quat_z - inverse * quat_x),
        ],
        [
            2.0 * (quat_x * quat_z - inverse * quat_y),
            2.0 * (quat_y * quat_z + inverse * quat_x),
            1.0 - 2.0 * (quat_x * quat_x + quat_y * quat_y),
        ],
    ]
    return (rotation, poses[3:6])


def to_world_rows(points, normals, poses, per_pose):
    rotation, translation = rotations(poses)

    def spread(values):
        return jnp.repeat(values, per_pose)[:, None]

    world_rows = []
    normal_rows = []
    for i in range(3):
        coeffs = [spread(rotation[i][j]) for j in range(3)]
        world_rows.append(
            coeffs[0] * points[:, 0]
            + coeffs[1] * points[:, 1]
            + coeffs[2] * points[:, 2]
            + spread(translation[i])
        )
        normal_rows.append(
            coeffs[0] * normals[:, 0] + coeffs[1] * normals[:, 1] + coeffs[2] * normals[:, 2]
        )
    return jnp.stack(world_rows + normal_rows, axis=0)


def _terms_kernel(xa_ref, tb_ref, map_ref, aux_ref, out_ref, xt_ref, gt_ref):
    chunk = out_ref.shape[1]
    idx = map_ref[...]
    for c in range(3):
        xt_ref[c] = xa_ref[c].T
    for c in range(6):
        picked = jnp.take_along_axis(tb_ref[c], idx, axis=1, mode="promise_in_bounds")
        gt_ref[c] = picked.T

    def col(q):
        return jnp.broadcast_to(aux_ref[q : q + 1, :], (8, chunk))

    def body(s, accs):
        rows = pl.ds(pl.multiple_of(s * 8, 8), 8)
        xa = [xt_ref[c, rows, :] for c in range(3)]
        xb = [gt_ref[c, rows, :] for c in range(3)]
        nb = [gt_ref[3 + c, rows, :] for c in range(3)]
        valid = col(24)
        off = [xa[c] - xb[c] for c in range(3)]
        res = (nb[0] * off[0] + nb[1] * off[1] + nb[2] * off[2]) * valid
        ja = [
            xa[1] * nb[2] - xa[2] * nb[1],
            xa[2] * nb[0] - xa[0] * nb[2],
            xa[0] * nb[1] - xa[1] * nb[0],
            nb[0],
            nb[1],
            nb[2],
        ]
        jb = [
            -(xb[1] * nb[2] - xb[2] * nb[1]),
            -(xb[2] * nb[0] - xb[0] * nb[2]),
            -(xb[0] * nb[1] - xb[1] * nb[0]),
            -nb[0],
            -nb[1],
            -nb[2],
        ]
        weights = [res]
        for v in range(2):
            sa = ja[0] * col(6 * v)
            sb = jb[0] * col(12 + 6 * v)
            for c in range(1, 6):
                sa = sa + ja[c] * col(6 * v + c)
                sb = sb + jb[c] * col(12 + 6 * v + c)
            weights.append((sa + sb) * valid)
        vals = []
        for w in weights:
            vals.extend([w * ja[c] for c in range(6)])
        for w in weights:
            vals.extend([w * jb[c] for c in range(3)])
        return tuple(a + v for a, v in zip(accs, vals))

    zero = jnp.zeros((8, chunk), jnp.float32)
    accs = lax.fori_loop(0, 128 // 8, body, (zero,) * N_QTY)
    for q in range(N_QTY):
        out_ref[q : q + 1, :] = jnp.sum(accs[q], axis=0, keepdims=True)
    out_ref[N_QTY:, :] = jnp.zeros((32 - N_QTY, chunk), jnp.float32)


def pair_sums(xa, tb, maps, aux, chunk=128):
    pairs = maps.shape[0]
    return pl.pallas_call(
        _terms_kernel,
        out_shape=jax.ShapeDtypeStruct((32, pairs), jnp.float32),
        grid=(pairs // chunk,),
        in_specs=[
            pl.BlockSpec((3, chunk, 128), lambda i: (0, i, 0)),
            pl.BlockSpec((6, chunk, 128), lambda i: (0, i, 0)),
            pl.BlockSpec((chunk, 128), lambda i: (i, 0)),
            pl.BlockSpec((32, chunk), lambda i: (0, i)),
        ],
        out_specs=pl.BlockSpec((32, chunk), lambda i: (0, i)),
        scratch_shapes=[
            pltpu.VMEM((3, 128, chunk), jnp.float32),
            pltpu.VMEM((6, 128, chunk), jnp.float32),
        ],
    )(xa, tb, maps, aux)


def split_terms(out):
    sel = out[0:N_QTY].T
    ga = sel[:, 0:6] * (1.0 / 128)
    ha = sel[:, 6:18] * (1.0 / 4096)
    gb = jnp.concatenate([sel[:, 18:21], -sel[:, 3:6]], axis=1) * (1.0 / 128)
    hb0 = jnp.concatenate([sel[:, 21:24], -sel[:, 9:12]], axis=1) * (1.0 / 4096)
    hb1 = jnp.concatenate([sel[:, 24:27], -sel[:, 15:18]], axis=1) * (1.0 / 4096)
    return jnp.concatenate([ga, ha], axis=1), jnp.concatenate([gb, hb0, hb1], axis=1)


def frag_sums(blocks, terms, frag_count):
    onehot = (blocks[:, None] // BF == jnp.arange(frag_count, dtype=jnp.int32)[None, :]).astype(
        jnp.float32
    )
    return jnp.dot(onehot.T, terms, precision=lax.Precision.HIGHEST)


def make_aux(dirs_a, dirs_b, valid):
    pairs = dirs_a.shape[0]
    return jnp.concatenate(
        [dirs_a.T, dirs_b.T, valid[None, :], jnp.zeros((32 - 25, pairs), jnp.float32)], axis=0
    )


def local(
    points,
    normals,
    poses,
    directions,
    local_pairs,
    local_maps,
    remote_src,
    remote_maps,
    remote_dst,
    counts,
):
    axes = ("tile", "band")
    frag_count = poses.shape[1]
    rows6 = to_world_rows(points, normals, poses, BF)
    frag_dirs = directions.reshape(12, frag_count).T
    peers = counts.shape[1]

    source_blocks = remote_src[0]
    valid = (
        (jnp.arange(CAP, dtype=jnp.int32)[None, :] < counts[0][:, None])
        .astype(jnp.float32)
        .reshape(-1)
    )
    xa_send = jnp.transpose(rows6[0:3][:, source_blocks], (1, 0, 2))
    map_send = remote_maps[0].astype(jnp.float32)[:, None, :]
    main = jnp.concatenate([xa_send, map_send], axis=1).reshape(peers, CAP * 4, 128)
    side = jnp.concatenate([frag_dirs[source_blocks // BF], valid[:, None]], axis=1)
    side = side.reshape(peers, CAP * 13)
    side = jnp.concatenate([side, jnp.zeros((peers, 128 - CAP * 13), jnp.float32)], axis=1)
    cargo = jnp.concatenate([main, side[:, None, :]], axis=1)
    arrived = lax.all_to_all(cargo, axes, split_axis=0, concat_axis=0, tiled=True)

    src_l = local_pairs[0]
    tgt_l = local_pairs[1]
    ones = jnp.ones((src_l.shape[0],), jnp.float32)
    out_l = pair_sums(
        rows6[0:3][:, src_l],
        rows6[:, tgt_l],
        local_maps,
        make_aux(frag_dirs[src_l // BF], frag_dirs[tgt_l // BF], ones),
    )
    local_a, local_b = split_terms(out_l)

    target_blocks = remote_dst[0]
    main_in = arrived[:, 0 : CAP * 4].reshape(peers * CAP, 4, 128)
    side_in = arrived[:, CAP * 4, 0 : CAP * 13].reshape(peers * CAP, 13)
    out_r = pair_sums(
        jnp.transpose(main_in[:, 0:3], (1, 0, 2)),
        rows6[:, target_blocks],
        main_in[:, 3].astype(jnp.int32),
        make_aux(side_in[:, 0:12], frag_dirs[target_blocks // BF], side_in[:, 12]),
    )
    remote_a, remote_b = split_terms(out_r)
    returned = lax.all_to_all(
        remote_a.reshape(peers, CAP * 18), axes, split_axis=0, concat_axis=0, tiled=True
    ).reshape(peers * CAP, 18)

    totals = frag_sums(src_l, local_a, frag_count) + frag_sums(tgt_l, local_b, frag_count)
    totals = (
        totals
        + frag_sums(target_blocks, remote_b, frag_count)
        + frag_sums(source_blocks, returned, frag_count)
    )
    gradient = totals[:, 0:6].T
    hess_products = totals[:, 6:18].T.reshape(2, 6, frag_count)
    return (gradient, hess_products)


def solution(mesh):
    placed = (
        P(("tile", "band"), None, None),
        P(("tile", "band"), None, None),
        P(None, ("tile", "band")),
        P(None, None, ("tile", "band")),
        P(None, ("tile", "band")),
        P(("tile", "band"), None),
        P(("tile", "band"), None),
        P(("tile", "band"), None, None),
        P(("tile", "band"), None),
        P(("tile", "band"), None),
    )
    return jax.shard_map(
        local,
        mesh=mesh,
        in_specs=placed,
        out_specs=(P(None, ("tile", "band")), P(None, None, ("tile", "band"))),
        check_vma=False,
    )
```

```python
import functools

import jax
import jax.numpy as jnp
from jax import lax
from jax.experimental import pallas as pl
from jax.experimental.pallas import tpu as pltpu
from jax.sharding import PartitionSpec as P

BF = 32
CAP = 8
N_QTY = 27
MESH = pl.DeviceIdType.MESH


def rotations(poses):
    half_angle = poses[0:3] * 0.5
    inverse = 1.0 / jnp.sqrt(
        1.0
        + half_angle[0] * half_angle[0]
        + half_angle[1] * half_angle[1]
        + half_angle[2] * half_angle[2]
    )
    quat_x = half_angle[0] * inverse
    quat_y = half_angle[1] * inverse
    quat_z = half_angle[2] * inverse
    rotation = [
        [
            1.0 - 2.0 * (quat_y * quat_y + quat_z * quat_z),
            2.0 * (quat_x * quat_y - inverse * quat_z),
            2.0 * (quat_x * quat_z + inverse * quat_y),
        ],
        [
            2.0 * (quat_x * quat_y + inverse * quat_z),
            1.0 - 2.0 * (quat_x * quat_x + quat_z * quat_z),
            2.0 * (quat_y * quat_z - inverse * quat_x),
        ],
        [
            2.0 * (quat_x * quat_z - inverse * quat_y),
            2.0 * (quat_y * quat_z + inverse * quat_x),
            1.0 - 2.0 * (quat_x * quat_x + quat_y * quat_y),
        ],
    ]
    return (rotation, poses[3:6])


def to_world_rows(points, normals, poses, per_pose):
    rotation, translation = rotations(poses)

    def spread(values):
        return jnp.repeat(values, per_pose)[:, None]

    world_rows = []
    normal_rows = []
    for i in range(3):
        coeffs = [spread(rotation[i][j]) for j in range(3)]
        world_rows.append(
            coeffs[0] * points[:, 0]
            + coeffs[1] * points[:, 1]
            + coeffs[2] * points[:, 2]
            + spread(translation[i])
        )
        normal_rows.append(
            coeffs[0] * normals[:, 0] + coeffs[1] * normals[:, 1] + coeffs[2] * normals[:, 2]
        )
    return jnp.stack(world_rows + normal_rows, axis=0)


def _terms_kernel(xa_ref, tb_ref, map_ref, aux_ref, out_ref, xt_ref, gt_ref):
    chunk = out_ref.shape[1]
    idx = map_ref[...]
    for c in range(3):
        xt_ref[c] = xa_ref[c].T
    for c in range(6):
        picked = jnp.take_along_axis(tb_ref[c], idx, axis=1, mode="promise_in_bounds")
        gt_ref[c] = picked.T

    def col(q):
        return jnp.broadcast_to(aux_ref[q : q + 1, :], (8, chunk))

    def body(s, accs):
        rows = pl.ds(pl.multiple_of(s * 8, 8), 8)
        xa = [xt_ref[c, rows, :] for c in range(3)]
        xb = [gt_ref[c, rows, :] for c in range(3)]
        nb = [gt_ref[3 + c, rows, :] for c in range(3)]
        valid = col(24)
        off = [xa[c] - xb[c] for c in range(3)]
        res = (nb[0] * off[0] + nb[1] * off[1] + nb[2] * off[2]) * valid
        ja = [
            xa[1] * nb[2] - xa[2] * nb[1],
            xa[2] * nb[0] - xa[0] * nb[2],
            xa[0] * nb[1] - xa[1] * nb[0],
            nb[0],
            nb[1],
            nb[2],
        ]
        jb = [
            -(xb[1] * nb[2] - xb[2] * nb[1]),
            -(xb[2] * nb[0] - xb[0] * nb[2]),
            -(xb[0] * nb[1] - xb[1] * nb[0]),
            -nb[0],
            -nb[1],
            -nb[2],
        ]
        weights = [res]
        for v in range(2):
            sa = ja[0] * col(6 * v)
            sb = jb[0] * col(12 + 6 * v)
            for c in range(1, 6):
                sa = sa + ja[c] * col(6 * v + c)
                sb = sb + jb[c] * col(12 + 6 * v + c)
            weights.append((sa + sb) * valid)
        vals = []
        for w in weights:
            vals.extend([w * ja[c] for c in range(6)])
        for w in weights:
            vals.extend([w * jb[c] for c in range(3)])
        return tuple(a + v for a, v in zip(accs, vals))

    zero = jnp.zeros((8, chunk), jnp.float32)
    accs = lax.fori_loop(0, 128 // 8, body, (zero,) * N_QTY)
    for q in range(N_QTY):
        out_ref[q : q + 1, :] = jnp.sum(accs[q], axis=0, keepdims=True)
    out_ref[N_QTY:, :] = jnp.zeros((32 - N_QTY, chunk), jnp.float32)


def pair_sums(xa, tb, maps, aux, chunk=128):
    pairs = maps.shape[0]
    return pl.pallas_call(
        _terms_kernel,
        out_shape=jax.ShapeDtypeStruct((32, pairs), jnp.float32),
        grid=(pairs // chunk,),
        in_specs=[
            pl.BlockSpec((3, chunk, 128), lambda i: (0, i, 0)),
            pl.BlockSpec((6, chunk, 128), lambda i: (0, i, 0)),
            pl.BlockSpec((chunk, 128), lambda i: (i, 0)),
            pl.BlockSpec((32, chunk), lambda i: (0, i)),
        ],
        out_specs=pl.BlockSpec((32, chunk), lambda i: (0, i)),
        scratch_shapes=[
            pltpu.VMEM((3, 128, chunk), jnp.float32),
            pltpu.VMEM((6, 128, chunk), jnp.float32),
        ],
    )(xa, tb, maps, aux)


def split_terms(out):
    sel = out[0:N_QTY].T
    ga = sel[:, 0:6] * (1.0 / 128)
    ha = sel[:, 6:18] * (1.0 / 4096)
    gb = jnp.concatenate([sel[:, 18:21], -sel[:, 3:6]], axis=1) * (1.0 / 128)
    hb0 = jnp.concatenate([sel[:, 21:24], -sel[:, 9:12]], axis=1) * (1.0 / 4096)
    hb1 = jnp.concatenate([sel[:, 24:27], -sel[:, 15:18]], axis=1) * (1.0 / 4096)
    return jnp.concatenate([ga, ha], axis=1), jnp.concatenate([gb, hb0, hb1], axis=1)


def _exchange_kernel(n_band, x_ref, out_ref, send_sems, recv_sems, own_sem):
    peers = x_ref.shape[0]
    me = lax.axis_index("tile") * n_band + lax.axis_index("band")

    def peer_of(k):
        p = lax.rem(me + k, peers)
        return p, (p // n_band, p % n_band)

    barrier = pltpu.get_barrier_semaphore()

    def greet(k, carry):
        _, dev = peer_of(k)
        pl.semaphore_signal(barrier, inc=1, device_id=dev, device_id_type=MESH)
        return carry

    lax.fori_loop(1, peers, greet, 0)
    pl.semaphore_wait(barrier, peers - 1)

    own = pltpu.make_async_copy(x_ref.at[me], out_ref.at[me], own_sem)
    own.start()

    def outgoing(k):
        p, dev = peer_of(k)
        return pltpu.make_async_remote_copy(
            src_ref=x_ref.at[p],
            dst_ref=out_ref.at[me],
            send_sem=send_sems.at[p],
            recv_sem=recv_sems.at[me],
            device_id=dev,
            device_id_type=MESH,
        )

    def incoming(k):
        p, dev = peer_of(k)
        return pltpu.make_async_remote_copy(
            src_ref=x_ref.at[p],
            dst_ref=out_ref.at[p],
            send_sem=send_sems.at[p],
            recv_sem=recv_sems.at[p],
            device_id=dev,
            device_id_type=MESH,
        )

    def start(k, carry):
        outgoing(k).start()
        return carry

    lax.fori_loop(1, peers, start, 0)

    def finish(k, carry):
        outgoing(k).wait_send()
        incoming(k).wait_recv()
        return carry

    lax.fori_loop(1, peers, finish, 0)
    own.wait()


def exchange(x, n_band, collective_id):
    peers = x.shape[0]
    return pl.pallas_call(
        functools.partial(_exchange_kernel, n_band),
        out_shape=jax.ShapeDtypeStruct(x.shape, x.dtype),
        in_specs=[pl.BlockSpec(memory_space=pl.ANY)],
        out_specs=pl.BlockSpec(memory_space=pl.ANY),
        scratch_shapes=[
            pltpu.SemaphoreType.DMA((peers,)),
            pltpu.SemaphoreType.DMA((peers,)),
            pltpu.SemaphoreType.DMA(()),
        ],
        compiler_params=pltpu.CompilerParams(collective_id=collective_id, has_side_effects=True),
    )(x)


def frag_sums(blocks, terms, frag_count):
    onehot = (blocks[:, None] // BF == jnp.arange(frag_count, dtype=jnp.int32)[None, :]).astype(
        jnp.float32
    )
    return jnp.dot(onehot.T, terms, precision=lax.Precision.HIGHEST)


def make_aux(dirs_a, dirs_b, valid):
    pairs = dirs_a.shape[0]
    return jnp.concatenate(
        [dirs_a.T, dirs_b.T, valid[None, :], jnp.zeros((32 - 25, pairs), jnp.float32)], axis=0
    )


def local(
    points,
    normals,
    poses,
    directions,
    local_pairs,
    local_maps,
    remote_src,
    remote_maps,
    remote_dst,
    counts,
):
    n_band = lax.axis_size("band")
    frag_count = poses.shape[1]
    rows6 = to_world_rows(points, normals, poses, BF)
    frag_dirs = directions.reshape(12, frag_count).T
    peers = counts.shape[1]

    source_blocks = remote_src[0]
    valid = (
        (jnp.arange(CAP, dtype=jnp.int32)[None, :] < counts[0][:, None])
        .astype(jnp.float32)
        .reshape(-1)
    )
    xa_send = jnp.transpose(rows6[0:3][:, source_blocks], (1, 0, 2))
    map_send = remote_maps[0].astype(jnp.float32)[:, None, :]
    main = jnp.concatenate([xa_send, map_send], axis=1).reshape(peers, CAP * 4, 128)
    side = jnp.concatenate([frag_dirs[source_blocks // BF], valid[:, None]], axis=1)
    side = side.reshape(peers, CAP * 13)
    side = jnp.concatenate([side, jnp.zeros((peers, 128 - CAP * 13), jnp.float32)], axis=1)
    cargo = jnp.concatenate([main, side[:, None, :]], axis=1)
    arrived = exchange(cargo, n_band, 0)

    src_l = local_pairs[0]
    tgt_l = local_pairs[1]
    ones = jnp.ones((src_l.shape[0],), jnp.float32)
    out_l = pair_sums(
        rows6[0:3][:, src_l],
        rows6[:, tgt_l],
        local_maps,
        make_aux(frag_dirs[src_l // BF], frag_dirs[tgt_l // BF], ones),
    )
    local_a, local_b = split_terms(out_l)

    target_blocks = remote_dst[0]
    main_in = arrived[:, 0 : CAP * 4].reshape(peers * CAP, 4, 128)
    side_in = arrived[:, CAP * 4, 0 : CAP * 13].reshape(peers * CAP, 13)
    out_r = pair_sums(
        jnp.transpose(main_in[:, 0:3], (1, 0, 2)),
        rows6[:, target_blocks],
        main_in[:, 3].astype(jnp.int32),
        make_aux(side_in[:, 0:12], frag_dirs[target_blocks // BF], side_in[:, 12]),
    )
    remote_a, remote_b = split_terms(out_r)
    returned = exchange(remote_a.reshape(peers, 1, CAP * 18), n_band, 1).reshape(peers * CAP, 18)

    totals = frag_sums(src_l, local_a, frag_count) + frag_sums(tgt_l, local_b, frag_count)
    totals = (
        totals
        + frag_sums(target_blocks, remote_b, frag_count)
        + frag_sums(source_blocks, returned, frag_count)
    )
    gradient = totals[:, 0:6].T
    hess_products = totals[:, 6:18].T.reshape(2, 6, frag_count)
    return (gradient, hess_products)


def solution(mesh):
    placed = (
        P(("tile", "band"), None, None),
        P(("tile", "band"), None, None),
        P(None, ("tile", "band")),
        P(None, None, ("tile", "band")),
        P(None, ("tile", "band")),
        P(("tile", "band"), None),
        P(("tile", "band"), None),
        P(("tile", "band"), None, None),
        P(("tile", "band"), None),
        P(("tile", "band"), None),
    )
    return jax.shard_map(
        local,
        mesh=mesh,
        in_specs=placed,
        out_specs=(P(None, ("tile", "band")), P(None, None, ("tile", "band"))),
        check_vma=False,
    )
```

```python
import functools

import jax
import jax.numpy as jnp
from jax import lax
from jax.experimental import pallas as pl
from jax.experimental.pallas import tpu as pltpu
from jax.sharding import PartitionSpec as P

BF = 32
CAP = 8
N_QTY = 27


def rotations(poses):
    half_angle = poses[0:3] * 0.5
    inverse = 1.0 / jnp.sqrt(
        1.0
        + half_angle[0] * half_angle[0]
        + half_angle[1] * half_angle[1]
        + half_angle[2] * half_angle[2]
    )
    quat_x = half_angle[0] * inverse
    quat_y = half_angle[1] * inverse
    quat_z = half_angle[2] * inverse
    rotation = [
        [
            1.0 - 2.0 * (quat_y * quat_y + quat_z * quat_z),
            2.0 * (quat_x * quat_y - inverse * quat_z),
            2.0 * (quat_x * quat_z + inverse * quat_y),
        ],
        [
            2.0 * (quat_x * quat_y + inverse * quat_z),
            1.0 - 2.0 * (quat_x * quat_x + quat_z * quat_z),
            2.0 * (quat_y * quat_z - inverse * quat_x),
        ],
        [
            2.0 * (quat_x * quat_z - inverse * quat_y),
            2.0 * (quat_y * quat_z + inverse * quat_x),
            1.0 - 2.0 * (quat_x * quat_x + quat_y * quat_y),
        ],
    ]
    return (rotation, poses[3:6])


def to_world_rows(points, normals, poses, per_pose):
    rotation, translation = rotations(poses)

    def spread(values):
        return jnp.repeat(values, per_pose)[:, None]

    world_rows = []
    normal_rows = []
    for i in range(3):
        coeffs = [spread(rotation[i][j]) for j in range(3)]
        world_rows.append(
            coeffs[0] * points[:, 0]
            + coeffs[1] * points[:, 1]
            + coeffs[2] * points[:, 2]
            + spread(translation[i])
        )
        normal_rows.append(
            coeffs[0] * normals[:, 0] + coeffs[1] * normals[:, 1] + coeffs[2] * normals[:, 2]
        )
    return jnp.stack(world_rows + normal_rows, axis=1)


def _terms_kernel(map_in_a, a_blk, a_row, t_idx, a_ref, w_ref, map_ref, aux_ref, out_ref, xs_ref, ts_ref, ms_ref, xt_ref, gt_ref):
    chunk = out_ref.shape[1]
    base = pl.program_id(0) * chunk

    def fill(j, carry):
        blk = a_blk[base + j]
        row = a_row[base + j]
        tgt = t_idx[base + j]
        for c in range(3):
            xs_ref[c, pl.ds(j, 1), :] = a_ref[blk, pl.ds(row + c, 1), :]
        for c in range(6):
            ts_ref[c, pl.ds(j, 1), :] = w_ref[tgt, pl.ds(c, 1), :]
        if map_in_a:
            ms_ref[pl.ds(j, 1), :] = a_ref[blk, pl.ds(row + 3, 1), :].astype(jnp.int32)
        return carry

    lax.fori_loop(0, chunk, fill, 0)
    idx = ms_ref[...] if map_in_a else map_ref[...]
    for c in range(3):
        xt_ref[c] = xs_ref[c].T
    for c in range(6):
        picked = jnp.take_along_axis(ts_ref[c], idx, axis=1, mode="promise_in_bounds")
        gt_ref[c] = picked.T

    def col(q):
        return jnp.broadcast_to(aux_ref[q : q + 1, :], (8, chunk))

    def body(s, accs):
        rows = pl.ds(pl.multiple_of(s * 8, 8), 8)
        xa = [xt_ref[c, rows, :] for c in range(3)]
        xb = [gt_ref[c, rows, :] for c in range(3)]
        nb = [gt_ref[3 + c, rows, :] for c in range(3)]
        valid = col(24)
        off = [xa[c] - xb[c] for c in range(3)]
        res = (nb[0] * off[0] + nb[1] * off[1] + nb[2] * off[2]) * valid
        ja = [
            xa[1] * nb[2] - xa[2] * nb[1],
            xa[2] * nb[0] - xa[0] * nb[2],
            xa[0] * nb[1] - xa[1] * nb[0],
            nb[0],
            nb[1],
            nb[2],
        ]
        jb = [
            -(xb[1] * nb[2] - xb[2] * nb[1]),
            -(xb[2] * nb[0] - xb[0] * nb[2]),
            -(xb[0] * nb[1] - xb[1] * nb[0]),
            -nb[0],
            -nb[1],
            -nb[2],
        ]
        weights = [res]
        for v in range(2):
            sa = ja[0] * col(6 * v)
            sb = jb[0] * col(12 + 6 * v)
            for c in range(1, 6):
                sa = sa + ja[c] * col(6 * v + c)
                sb = sb + jb[c] * col(12 + 6 * v + c)
            weights.append((sa + sb) * valid)
        vals = []
        for w in weights:
            vals.extend([w * ja[c] for c in range(6)])
        for w in weights:
            vals.extend([w * jb[c] for c in range(3)])
        return tuple(a + v for a, v in zip(accs, vals))

    zero = jnp.zeros((8, chunk), jnp.float32)
    accs = lax.fori_loop(0, 128 // 8, body, (zero,) * N_QTY)
    for q in range(N_QTY):
        out_ref[q : q + 1, :] = jnp.sum(accs[q], axis=0, keepdims=True)
    out_ref[N_QTY:, :] = jnp.zeros((32 - N_QTY, chunk), jnp.float32)


def pair_sums(a_blk, a_row, t_idx, a_src, world, maps, aux, chunk=128):
    pairs = a_blk.shape[0]
    map_in_a = maps is None
    if map_in_a:
        maps = jnp.zeros((8, 128), jnp.int32)
        map_spec = pl.BlockSpec((8, 128), lambda i, *_: (0, 0))
    else:
        map_spec = pl.BlockSpec((chunk, 128), lambda i, *_: (i, 0))
    return pl.pallas_call(
        functools.partial(_terms_kernel, map_in_a),
        out_shape=jax.ShapeDtypeStruct((32, pairs), jnp.float32),
        grid_spec=pltpu.PrefetchScalarGridSpec(
            num_scalar_prefetch=3,
            grid=(pairs // chunk,),
            in_specs=[
                pl.BlockSpec(a_src.shape, lambda i, *_: (0, 0, 0)),
                pl.BlockSpec(world.shape, lambda i, *_: (0, 0, 0)),
                map_spec,
                pl.BlockSpec((32, chunk), lambda i, *_: (0, i)),
            ],
            out_specs=pl.BlockSpec((32, chunk), lambda i, *_: (0, i)),
            scratch_shapes=[
                pltpu.VMEM((3, chunk, 128), jnp.float32),
                pltpu.VMEM((6, chunk, 128), jnp.float32),
                pltpu.VMEM((chunk, 128), jnp.int32),
                pltpu.VMEM((3, 128, chunk), jnp.float32),
                pltpu.VMEM((6, 128, chunk), jnp.float32),
            ],
        ),
    )(a_blk, a_row, t_idx, a_src, world, maps, aux)


def split_terms(out):
    sel = out[0:N_QTY].T
    ga = sel[:, 0:6] * (1.0 / 128)
    ha = sel[:, 6:18] * (1.0 / 4096)
    gb = jnp.concatenate([sel[:, 18:21], -sel[:, 3:6]], axis=1) * (1.0 / 128)
    hb0 = jnp.concatenate([sel[:, 21:24], -sel[:, 9:12]], axis=1) * (1.0 / 4096)
    hb1 = jnp.concatenate([sel[:, 24:27], -sel[:, 15:18]], axis=1) * (1.0 / 4096)
    return jnp.concatenate([ga, ha], axis=1), jnp.concatenate([gb, hb0, hb1], axis=1)


def frag_sums(blocks, terms, frag_count):
    onehot = (blocks[:, None] // BF == jnp.arange(frag_count, dtype=jnp.int32)[None, :]).astype(
        jnp.float32
    )
    return jnp.dot(onehot.T, terms, precision=lax.Precision.HIGHEST)


def make_aux(dirs_a, dirs_b, valid):
    pairs = dirs_a.shape[0]
    return jnp.concatenate(
        [dirs_a.T, dirs_b.T, valid[None, :], jnp.zeros((32 - 25, pairs), jnp.float32)], axis=0
    )


def local(
    points,
    normals,
    poses,
    directions,
    local_pairs,
    local_maps,
    remote_src,
    remote_maps,
    remote_dst,
    counts,
):
    axes = ("tile", "band")
    frag_count = poses.shape[1]
    world = to_world_rows(points, normals, poses, BF)
    frag_dirs = directions.reshape(12, frag_count).T
    peers = counts.shape[1]

    source_blocks = remote_src[0]
    valid = (
        (jnp.arange(CAP, dtype=jnp.int32)[None, :] < counts[0][:, None])
        .astype(jnp.float32)
        .reshape(-1)
    )
    xa_send = world[source_blocks, 0:3]
    map_send = remote_maps[0].astype(jnp.float32)[:, None, :]
    main = jnp.concatenate([xa_send, map_send], axis=1).reshape(peers, CAP * 4, 128)
    side = jnp.concatenate([frag_dirs[source_blocks // BF], valid[:, None]], axis=1)
    side = side.reshape(peers, CAP * 13)
    side = jnp.concatenate([side, jnp.zeros((peers, 128 - CAP * 13), jnp.float32)], axis=1)
    cargo = jnp.concatenate([main, side[:, None, :]], axis=1)
    arrived = lax.all_to_all(cargo, axes, split_axis=0, concat_axis=0, tiled=True)

    src_l = local_pairs[0]
    tgt_l = local_pairs[1]
    ones = jnp.ones((src_l.shape[0],), jnp.float32)
    out_l = pair_sums(
        src_l,
        jnp.zeros_like(src_l),
        tgt_l,
        world,
        world,
        local_maps,
        make_aux(frag_dirs[src_l // BF], frag_dirs[tgt_l // BF], ones),
    )
    local_a, local_b = split_terms(out_l)

    target_blocks = remote_dst[0]
    slots = jnp.arange(peers * CAP, dtype=jnp.int32)
    side_in = arrived[:, CAP * 4, 0 : CAP * 13].reshape(peers * CAP, 13)
    out_r = pair_sums(
        slots // CAP,
        (slots % CAP) * 4,
        target_blocks,
        arrived,
        world,
        None,
        make_aux(side_in[:, 0:12], frag_dirs[target_blocks // BF], side_in[:, 12]),
    )
    remote_a, remote_b = split_terms(out_r)
    returned = lax.all_to_all(
        remote_a.reshape(peers, CAP * 18), axes, split_axis=0, concat_axis=0, tiled=True
    ).reshape(peers * CAP, 18)

    totals = frag_sums(src_l, local_a, frag_count) + frag_sums(tgt_l, local_b, frag_count)
    totals = (
        totals
        + frag_sums(target_blocks, remote_b, frag_count)
        + frag_sums(source_blocks, returned, frag_count)
    )
    gradient = totals[:, 0:6].T
    hess_products = totals[:, 6:18].T.reshape(2, 6, frag_count)
    return (gradient, hess_products)


def solution(mesh):
    placed = (
        P(("tile", "band"), None, None),
        P(("tile", "band"), None, None),
        P(None, ("tile", "band")),
        P(None, None, ("tile", "band")),
        P(None, ("tile", "band")),
        P(("tile", "band"), None),
        P(("tile", "band"), None),
        P(("tile", "band"), None, None),
        P(("tile", "band"), None),
        P(("tile", "band"), None),
    )
    return jax.shard_map(
        local,
        mesh=mesh,
        in_specs=placed,
        out_specs=(P(None, ("tile", "band")), P(None, None, ("tile", "band"))),
        check_vma=False,
    )
```

```python
import functools

import jax
import jax.numpy as jnp
from jax import lax
from jax.experimental import pallas as pl
from jax.experimental.pallas import tpu as pltpu
from jax.sharding import PartitionSpec as P

BF = 32
CAP = 8
N_QTY = 27


def rotations(poses):
    half_angle = poses[0:3] * 0.5
    inverse = 1.0 / jnp.sqrt(
        1.0
        + half_angle[0] * half_angle[0]
        + half_angle[1] * half_angle[1]
        + half_angle[2] * half_angle[2]
    )
    quat_x = half_angle[0] * inverse
    quat_y = half_angle[1] * inverse
    quat_z = half_angle[2] * inverse
    rotation = [
        [
            1.0 - 2.0 * (quat_y * quat_y + quat_z * quat_z),
            2.0 * (quat_x * quat_y - inverse * quat_z),
            2.0 * (quat_x * quat_z + inverse * quat_y),
        ],
        [
            2.0 * (quat_x * quat_y + inverse * quat_z),
            1.0 - 2.0 * (quat_x * quat_x + quat_z * quat_z),
            2.0 * (quat_y * quat_z - inverse * quat_x),
        ],
        [
            2.0 * (quat_x * quat_z - inverse * quat_y),
            2.0 * (quat_y * quat_z + inverse * quat_x),
            1.0 - 2.0 * (quat_x * quat_x + quat_y * quat_y),
        ],
    ]
    return (rotation, poses[3:6])


def to_world_rows(points, normals, poses, per_pose):
    rotation, translation = rotations(poses)

    def spread(values):
        return jnp.repeat(values, per_pose)[:, None]

    world_rows = []
    normal_rows = []
    for i in range(3):
        coeffs = [spread(rotation[i][j]) for j in range(3)]
        world_rows.append(
            coeffs[0] * points[:, 0]
            + coeffs[1] * points[:, 1]
            + coeffs[2] * points[:, 2]
            + spread(translation[i])
        )
        normal_rows.append(
            coeffs[0] * normals[:, 0] + coeffs[1] * normals[:, 1] + coeffs[2] * normals[:, 2]
        )
    return jnp.stack(world_rows + normal_rows, axis=0)


def _terms_kernel(from_cargo, xa_ref, tb_ref, map_ref, aux_ref, out_ref, xt_ref, gt_ref):
    chunk = out_ref.shape[1]
    if from_cargo:
        def cargo_rows(r):
            return xa_ref[:, pl.ds(r, CAP, stride=4), :].reshape(chunk, 128)

        idx = cargo_rows(3).astype(jnp.int32)
        for c in range(3):
            xt_ref[c] = cargo_rows(c).T
    else:
        idx = map_ref[...]
        for c in range(3):
            xt_ref[c] = xa_ref[c].T
    for c in range(6):
        picked = jnp.take_along_axis(tb_ref[c], idx, axis=1, mode="promise_in_bounds")
        gt_ref[c] = picked.T

    def col(q):
        return jnp.broadcast_to(aux_ref[q : q + 1, :], (8, chunk))

    def body(s, accs):
        rows = pl.ds(pl.multiple_of(s * 8, 8), 8)
        xa = [xt_ref[c, rows, :] for c in range(3)]
        xb = [gt_ref[c, rows, :] for c in range(3)]
        nb = [gt_ref[3 + c, rows, :] for c in range(3)]
        valid = col(24)
        off = [xa[c] - xb[c] for c in range(3)]
        res = (nb[0] * off[0] + nb[1] * off[1] + nb[2] * off[2]) * valid
        ja = [
            xa[1] * nb[2] - xa[2] * nb[1],
            xa[2] * nb[0] - xa[0] * nb[2],
            xa[0] * nb[1] - xa[1] * nb[0],
            nb[0],
            nb[1],
            nb[2],
        ]
        jb = [
            -(xb[1] * nb[2] - xb[2] * nb[1]),
            -(xb[2] * nb[0] - xb[0] * nb[2]),
            -(xb[0] * nb[1] - xb[1] * nb[0]),
            -nb[0],
            -nb[1],
            -nb[2],
        ]
        weights = [res]
        for v in range(2):
            sa = ja[0] * col(6 * v)
            sb = jb[0] * col(12 + 6 * v)
            for c in range(1, 6):
                sa = sa + ja[c] * col(6 * v + c)
                sb = sb + jb[c] * col(12 + 6 * v + c)
            weights.append((sa + sb) * valid)
        vals = []
        for w in weights:
            vals.extend([w * ja[c] for c in range(6)])
        for w in weights:
            vals.extend([w * jb[c] for c in range(3)])
        return tuple(a + v for a, v in zip(accs, vals))

    zero = jnp.zeros((8, chunk), jnp.float32)
    accs = lax.fori_loop(0, 128 // 8, body, (zero,) * N_QTY)
    for q in range(N_QTY):
        out_ref[q : q + 1, :] = jnp.sum(accs[q], axis=0, keepdims=True)
    out_ref[N_QTY:, :] = jnp.zeros((32 - N_QTY, chunk), jnp.float32)


def pair_sums(xa, tb, maps, aux, chunk=128):
    pairs = tb.shape[1]
    from_cargo = maps is None
    if from_cargo:
        xa_spec = pl.BlockSpec((chunk // CAP, xa.shape[1], 128), lambda i: (i, 0, 0))
        maps = jnp.zeros((8, 128), jnp.int32)
        map_spec = pl.BlockSpec((8, 128), lambda i: (0, 0))
    else:
        xa_spec = pl.BlockSpec((3, chunk, 128), lambda i: (0, i, 0))
        map_spec = pl.BlockSpec((chunk, 128), lambda i: (i, 0))
    return pl.pallas_call(
        functools.partial(_terms_kernel, from_cargo),
        out_shape=jax.ShapeDtypeStruct((32, pairs), jnp.float32),
        grid=(pairs // chunk,),
        in_specs=[
            xa_spec,
            pl.BlockSpec((6, chunk, 128), lambda i: (0, i, 0)),
            map_spec,
            pl.BlockSpec((32, chunk), lambda i: (0, i)),
        ],
        out_specs=pl.BlockSpec((32, chunk), lambda i: (0, i)),
        scratch_shapes=[
            pltpu.VMEM((3, 128, chunk), jnp.float32),
            pltpu.VMEM((6, 128, chunk), jnp.float32),
        ],
    )(xa, tb, maps, aux)


def split_terms(out):
    sel = out[0:N_QTY].T
    ga = sel[:, 0:6] * (1.0 / 128)
    ha = sel[:, 6:18] * (1.0 / 4096)
    gb = jnp.concatenate([sel[:, 18:21], -sel[:, 3:6]], axis=1) * (1.0 / 128)
    hb0 = jnp.concatenate([sel[:, 21:24], -sel[:, 9:12]], axis=1) * (1.0 / 4096)
    hb1 = jnp.concatenate([sel[:, 24:27], -sel[:, 15:18]], axis=1) * (1.0 / 4096)
    return jnp.concatenate([ga, ha], axis=1), jnp.concatenate([gb, hb0, hb1], axis=1)


def frag_sums(blocks, terms, frag_count):
    onehot = (blocks[:, None] // BF == jnp.arange(frag_count, dtype=jnp.int32)[None, :]).astype(
        jnp.float32
    )
    return jnp.dot(onehot.T, terms, precision=lax.Precision.HIGHEST)


def make_aux(dirs_a, dirs_b, valid):
    pairs = dirs_a.shape[0]
    return jnp.concatenate(
        [dirs_a.T, dirs_b.T, valid[None, :], jnp.zeros((32 - 25, pairs), jnp.float32)], axis=0
    )


def local(
    points,
    normals,
    poses,
    directions,
    local_pairs,
    local_maps,
    remote_src,
    remote_maps,
    remote_dst,
    counts,
):
    axes = ("tile", "band")
    frag_count = poses.shape[1]
    rows6 = to_world_rows(points, normals, poses, BF)
    frag_dirs = directions.reshape(12, frag_count).T
    peers = counts.shape[1]

    source_blocks = remote_src[0]
    valid = (
        (jnp.arange(CAP, dtype=jnp.int32)[None, :] < counts[0][:, None])
        .astype(jnp.float32)
        .reshape(-1)
    )
    pick = (source_blocks[:, None] == jnp.arange(points.shape[0], dtype=jnp.int32)[None, :]).astype(
        jnp.float32
    )
    xa_send = jnp.einsum("sb,cbk->sck", pick, rows6[0:3], precision=lax.Precision.HIGHEST)
    map_send = remote_maps[0].astype(jnp.float32)[:, None, :]
    main = jnp.concatenate([xa_send, map_send], axis=1).reshape(peers, CAP * 4, 128)
    frag_pick = (
        source_blocks[:, None] // BF == jnp.arange(frag_count, dtype=jnp.int32)[None, :]
    ).astype(jnp.float32)
    dirs_send = jnp.dot(frag_pick, frag_dirs, precision=lax.Precision.HIGHEST)
    side = jnp.concatenate([dirs_send, valid[:, None]], axis=1)
    side = side.reshape(peers, CAP * 13)
    side = jnp.concatenate([side, jnp.zeros((peers, 128 - CAP * 13), jnp.float32)], axis=1)
    cargo = jnp.concatenate([main, side[:, None, :]], axis=1)
    arrived = lax.all_to_all(cargo, axes, split_axis=0, concat_axis=0, tiled=True)

    src_l = local_pairs[0]
    tgt_l = local_pairs[1]
    ones = jnp.ones((src_l.shape[0],), jnp.float32)
    out_l = pair_sums(
        rows6[0:3][:, src_l],
        rows6[:, tgt_l],
        local_maps,
        make_aux(frag_dirs[src_l // BF], frag_dirs[tgt_l // BF], ones),
    )
    local_a, local_b = split_terms(out_l)

    target_blocks = remote_dst[0]
    side_in = arrived[:, CAP * 4, 0 : CAP * 13].reshape(peers * CAP, 13)
    out_r = pair_sums(
        arrived,
        rows6[:, target_blocks],
        None,
        make_aux(side_in[:, 0:12], frag_dirs[target_blocks // BF], side_in[:, 12]),
    )
    remote_a, remote_b = split_terms(out_r)
    returned = lax.all_to_all(
        remote_a.reshape(peers, CAP * 18), axes, split_axis=0, concat_axis=0, tiled=True
    ).reshape(peers * CAP, 18)

    totals = frag_sums(src_l, local_a, frag_count) + frag_sums(tgt_l, local_b, frag_count)
    totals = (
        totals
        + frag_sums(target_blocks, remote_b, frag_count)
        + frag_sums(source_blocks, returned, frag_count)
    )
    gradient = totals[:, 0:6].T
    hess_products = totals[:, 6:18].T.reshape(2, 6, frag_count)
    return (gradient, hess_products)


def solution(mesh):
    placed = (
        P(("tile", "band"), None, None),
        P(("tile", "band"), None, None),
        P(None, ("tile", "band")),
        P(None, None, ("tile", "band")),
        P(None, ("tile", "band")),
        P(("tile", "band"), None),
        P(("tile", "band"), None),
        P(("tile", "band"), None, None),
        P(("tile", "band"), None),
        P(("tile", "band"), None),
    )
    return jax.shard_map(
        local,
        mesh=mesh,
        in_specs=placed,
        out_specs=(P(None, ("tile", "band")), P(None, None, ("tile", "band"))),
        check_vma=False,
    )
```

```python
import functools

import jax
import jax.numpy as jnp
from jax import lax
from jax.experimental import pallas as pl
from jax.experimental.pallas import tpu as pltpu
from jax.sharding import PartitionSpec as P

BF = 32
CAP = 8
N_QTY = 27


def rotations(poses):
    half_angle = poses[0:3] * 0.5
    inverse = 1.0 / jnp.sqrt(
        1.0
        + half_angle[0] * half_angle[0]
        + half_angle[1] * half_angle[1]
        + half_angle[2] * half_angle[2]
    )
    quat_x = half_angle[0] * inverse
    quat_y = half_angle[1] * inverse
    quat_z = half_angle[2] * inverse
    rotation = [
        [
            1.0 - 2.0 * (quat_y * quat_y + quat_z * quat_z),
            2.0 * (quat_x * quat_y - inverse * quat_z),
            2.0 * (quat_x * quat_z + inverse * quat_y),
        ],
        [
            2.0 * (quat_x * quat_y + inverse * quat_z),
            1.0 - 2.0 * (quat_x * quat_x + quat_z * quat_z),
            2.0 * (quat_y * quat_z - inverse * quat_x),
        ],
        [
            2.0 * (quat_x * quat_z - inverse * quat_y),
            2.0 * (quat_y * quat_z + inverse * quat_x),
            1.0 - 2.0 * (quat_x * quat_x + quat_y * quat_y),
        ],
    ]
    return (rotation, poses[3:6])


def to_world_rows(points, normals, poses, per_pose):
    rotation, translation = rotations(poses)

    def spread(values):
        return jnp.repeat(values, per_pose)[:, None]

    world_rows = []
    normal_rows = []
    for i in range(3):
        coeffs = [spread(rotation[i][j]) for j in range(3)]
        world_rows.append(
            coeffs[0] * points[:, 0]
            + coeffs[1] * points[:, 1]
            + coeffs[2] * points[:, 2]
            + spread(translation[i])
        )
        normal_rows.append(
            coeffs[0] * normals[:, 0] + coeffs[1] * normals[:, 1] + coeffs[2] * normals[:, 2]
        )
    return jnp.stack(world_rows + normal_rows, axis=0)


def _terms_kernel(from_cargo, xa_ref, tb_ref, map_ref, aux_ref, out_ref, xt_ref, gt_ref):
    chunk = out_ref.shape[1]
    if from_cargo:
        def cargo_rows(r):
            return xa_ref[:, pl.ds(r, CAP, stride=4), :].reshape(chunk, 128)

        idx = cargo_rows(3).astype(jnp.int32)
        for c in range(3):
            xt_ref[c] = cargo_rows(c).T
    else:
        idx = map_ref[...]
        for c in range(3):
            xt_ref[c] = xa_ref[c].T
    for c in range(6):
        picked = jnp.take_along_axis(tb_ref[c], idx, axis=1, mode="promise_in_bounds")
        gt_ref[c] = picked.T

    def col(q):
        return jnp.broadcast_to(aux_ref[q : q + 1, :], (8, chunk))

    def body(s, accs):
        rows = pl.ds(pl.multiple_of(s * 8, 8), 8)
        xa = [xt_ref[c, rows, :] for c in range(3)]
        xb = [gt_ref[c, rows, :] for c in range(3)]
        nb = [gt_ref[3 + c, rows, :] for c in range(3)]
        off = [xa[c] - xb[c] for c in range(3)]
        res = nb[0] * off[0] + nb[1] * off[1] + nb[2] * off[2]
        ja = [
            xa[1] * nb[2] - xa[2] * nb[1],
            xa[2] * nb[0] - xa[0] * nb[2],
            xa[0] * nb[1] - xa[1] * nb[0],
            nb[0],
            nb[1],
            nb[2],
        ]
        kb = [
            xb[1] * nb[2] - xb[2] * nb[1],
            xb[2] * nb[0] - xb[0] * nb[2],
            xb[0] * nb[1] - xb[1] * nb[0],
            nb[0],
            nb[1],
            nb[2],
        ]
        weights = [res]
        for v in range(2):
            sa = ja[0] * col(6 * v)
            sb = kb[0] * col(12 + 6 * v)
            for c in range(1, 6):
                sa = sa + ja[c] * col(6 * v + c)
                sb = sb + kb[c] * col(12 + 6 * v + c)
            weights.append(sa - sb)
        vals = []
        for w in weights:
            vals.extend([w * ja[c] for c in range(6)])
        for w in weights:
            vals.extend([w * kb[c] for c in range(3)])
        return tuple(a + v for a, v in zip(accs, vals))

    zero = jnp.zeros((8, chunk), jnp.float32)
    accs = lax.fori_loop(0, 128 // 8, body, (zero,) * N_QTY, unroll=2)
    valid = aux_ref[24:25, :]
    for q in range(N_QTY):
        out_ref[q : q + 1, :] = jnp.sum(accs[q], axis=0, keepdims=True) * valid
    out_ref[N_QTY:, :] = jnp.zeros((32 - N_QTY, chunk), jnp.float32)


def pair_sums(xa, tb, maps, aux, chunk=128):
    pairs = tb.shape[1]
    from_cargo = maps is None
    if from_cargo:
        xa_spec = pl.BlockSpec((chunk // CAP, xa.shape[1], 128), lambda i: (i, 0, 0))
        maps = jnp.zeros((8, 128), jnp.int32)
        map_spec = pl.BlockSpec((8, 128), lambda i: (0, 0))
    else:
        xa_spec = pl.BlockSpec((3, chunk, 128), lambda i: (0, i, 0))
        map_spec = pl.BlockSpec((chunk, 128), lambda i: (i, 0))
    return pl.pallas_call(
        functools.partial(_terms_kernel, from_cargo),
        out_shape=jax.ShapeDtypeStruct((32, pairs), jnp.float32),
        grid=(pairs // chunk,),
        in_specs=[
            xa_spec,
            pl.BlockSpec((6, chunk, 128), lambda i: (0, i, 0)),
            map_spec,
            pl.BlockSpec((32, chunk), lambda i: (0, i)),
        ],
        out_specs=pl.BlockSpec((32, chunk), lambda i: (0, i)),
        scratch_shapes=[
            pltpu.VMEM((3, 128, chunk), jnp.float32),
            pltpu.VMEM((6, 128, chunk), jnp.float32),
        ],
    )(xa, tb, maps, aux)


def split_terms(out):
    sel = out[0:N_QTY].T
    ga = sel[:, 0:6] * (1.0 / 128)
    ha = sel[:, 6:18] * (1.0 / 4096)
    gb = -jnp.concatenate([sel[:, 18:21], sel[:, 3:6]], axis=1) * (1.0 / 128)
    hb0 = -jnp.concatenate([sel[:, 21:24], sel[:, 9:12]], axis=1) * (1.0 / 4096)
    hb1 = -jnp.concatenate([sel[:, 24:27], sel[:, 15:18]], axis=1) * (1.0 / 4096)
    return jnp.concatenate([ga, ha], axis=1), jnp.concatenate([gb, hb0, hb1], axis=1)


def frag_sums(blocks, terms, frag_count):
    onehot = (blocks[:, None] // BF == jnp.arange(frag_count, dtype=jnp.int32)[None, :]).astype(
        jnp.float32
    )
    return jnp.dot(onehot.T, terms, precision=lax.Precision.HIGHEST)


def make_aux(dirs_a, dirs_b, valid):
    pairs = dirs_a.shape[0]
    return jnp.concatenate(
        [dirs_a.T, dirs_b.T, valid[None, :], jnp.zeros((32 - 25, pairs), jnp.float32)], axis=0
    )


def local(
    points,
    normals,
    poses,
    directions,
    local_pairs,
    local_maps,
    remote_src,
    remote_maps,
    remote_dst,
    counts,
):
    axes = ("tile", "band")
    frag_count = poses.shape[1]
    rows6 = to_world_rows(points, normals, poses, BF)
    frag_dirs = directions.reshape(12, frag_count).T
    peers = counts.shape[1]

    source_blocks = remote_src[0]
    valid = (
        (jnp.arange(CAP, dtype=jnp.int32)[None, :] < counts[0][:, None])
        .astype(jnp.float32)
        .reshape(-1)
    )
    pick = (source_blocks[:, None] == jnp.arange(points.shape[0], dtype=jnp.int32)[None, :]).astype(
        jnp.float32
    )
    xa_send = jnp.einsum("sb,cbk->sck", pick, rows6[0:3], precision=lax.Precision.HIGHEST)
    map_send = remote_maps[0].astype(jnp.float32)[:, None, :]
    main = jnp.concatenate([xa_send, map_send], axis=1).reshape(peers, CAP * 4, 128)
    frag_pick = (
        source_blocks[:, None] // BF == jnp.arange(frag_count, dtype=jnp.int32)[None, :]
    ).astype(jnp.float32)
    dirs_send = jnp.dot(frag_pick, frag_dirs, precision=lax.Precision.HIGHEST)
    side = jnp.concatenate([dirs_send, valid[:, None]], axis=1)
    side = side.reshape(peers, CAP * 13)
    side = jnp.concatenate([side, jnp.zeros((peers, 128 - CAP * 13), jnp.float32)], axis=1)
    cargo = jnp.concatenate([main, side[:, None, :]], axis=1)
    arrived = lax.all_to_all(cargo, axes, split_axis=0, concat_axis=0, tiled=True)

    src_l = local_pairs[0]
    tgt_l = local_pairs[1]
    ones = jnp.ones((src_l.shape[0],), jnp.float32)
    out_l = pair_sums(
        rows6[0:3][:, src_l],
        rows6[:, tgt_l],
        local_maps,
        make_aux(frag_dirs[src_l // BF], frag_dirs[tgt_l // BF], ones),
    )
    local_a, local_b = split_terms(out_l)

    target_blocks = remote_dst[0]
    side_in = arrived[:, CAP * 4, 0 : CAP * 13].reshape(peers * CAP, 13)
    out_r = pair_sums(
        arrived,
        rows6[:, target_blocks],
        None,
        make_aux(side_in[:, 0:12], frag_dirs[target_blocks // BF], side_in[:, 12]),
    )
    remote_a, remote_b = split_terms(out_r)
    returned = lax.all_to_all(
        remote_a.reshape(peers, CAP * 18), axes, split_axis=0, concat_axis=0, tiled=True
    ).reshape(peers * CAP, 18)

    totals = frag_sums(src_l, local_a, frag_count) + frag_sums(tgt_l, local_b, frag_count)
    totals = (
        totals
        + frag_sums(target_blocks, remote_b, frag_count)
        + frag_sums(source_blocks, returned, frag_count)
    )
    gradient = totals[:, 0:6].T
    hess_products = totals[:, 6:18].T.reshape(2, 6, frag_count)
    return (gradient, hess_products)


def solution(mesh):
    placed = (
        P(("tile", "band"), None, None),
        P(("tile", "band"), None, None),
        P(None, ("tile", "band")),
        P(None, None, ("tile", "band")),
        P(None, ("tile", "band")),
        P(("tile", "band"), None),
        P(("tile", "band"), None),
        P(("tile", "band"), None, None),
        P(("tile", "band"), None),
        P(("tile", "band"), None),
    )
    return jax.shard_map(
        local,
        mesh=mesh,
        in_specs=placed,
        out_specs=(P(None, ("tile", "band")), P(None, None, ("tile", "band"))),
        check_vma=False,
    )
```

```python
import functools

import jax
import jax.numpy as jnp
from jax import lax
from jax.experimental import pallas as pl
from jax.experimental.pallas import tpu as pltpu
from jax.sharding import PartitionSpec as P

BF = 32
CAP = 8
N_QTY = 27


def rotations(poses):
    half_angle = poses[0:3] * 0.5
    inverse = 1.0 / jnp.sqrt(
        1.0
        + half_angle[0] * half_angle[0]
        + half_angle[1] * half_angle[1]
        + half_angle[2] * half_angle[2]
    )
    quat_x = half_angle[0] * inverse
    quat_y = half_angle[1] * inverse
    quat_z = half_angle[2] * inverse
    rotation = [
        [
            1.0 - 2.0 * (quat_y * quat_y + quat_z * quat_z),
            2.0 * (quat_x * quat_y - inverse * quat_z),
            2.0 * (quat_x * quat_z + inverse * quat_y),
        ],
        [
            2.0 * (quat_x * quat_y + inverse * quat_z),
            1.0 - 2.0 * (quat_x * quat_x + quat_z * quat_z),
            2.0 * (quat_y * quat_z - inverse * quat_x),
        ],
        [
            2.0 * (quat_x * quat_z - inverse * quat_y),
            2.0 * (quat_y * quat_z + inverse * quat_x),
            1.0 - 2.0 * (quat_x * quat_x + quat_y * quat_y),
        ],
    ]
    return (rotation, poses[3:6])


def to_world_rows(points, normals, poses, per_pose):
    rotation, translation = rotations(poses)

    def spread(values):
        return jnp.repeat(values, per_pose)[:, None]

    world_rows = []
    normal_rows = []
    for i in range(3):
        coeffs = [spread(rotation[i][j]) for j in range(3)]
        world_rows.append(
            coeffs[0] * points[:, 0]
            + coeffs[1] * points[:, 1]
            + coeffs[2] * points[:, 2]
            + spread(translation[i])
        )
        normal_rows.append(
            coeffs[0] * normals[:, 0] + coeffs[1] * normals[:, 1] + coeffs[2] * normals[:, 2]
        )
    return jnp.stack(world_rows + normal_rows, axis=0)


def _terms_kernel(from_cargo, xa_ref, tb_ref, map_ref, aux_ref, out_ref, xt_ref, gt_ref):
    chunk = out_ref.shape[1]
    if from_cargo:
        def cargo_rows(r):
            return xa_ref[pl.ds(r, CAP, stride=4)].reshape(chunk, 128)

        idx = cargo_rows(3).astype(jnp.int32)
        for c in range(3):
            xt_ref[c] = cargo_rows(c).T
    else:
        idx = map_ref[...]
        for c in range(3):
            xt_ref[c] = xa_ref[c].T
    for c in range(6):
        picked = jnp.take_along_axis(tb_ref[c], idx, axis=1, mode="promise_in_bounds")
        gt_ref[c] = picked.T

    def col(q):
        return jnp.broadcast_to(aux_ref[q : q + 1, :], (8, chunk))

    def body(s, accs):
        rows = pl.ds(pl.multiple_of(s * 8, 8), 8)
        xa = [xt_ref[c, rows, :] for c in range(3)]
        xb = [gt_ref[c, rows, :] for c in range(3)]
        nb = [gt_ref[3 + c, rows, :] for c in range(3)]
        off = [xa[c] - xb[c] for c in range(3)]
        res = nb[0] * off[0] + nb[1] * off[1] + nb[2] * off[2]
        ja = [
            xa[1] * nb[2] - xa[2] * nb[1],
            xa[2] * nb[0] - xa[0] * nb[2],
            xa[0] * nb[1] - xa[1] * nb[0],
            nb[0],
            nb[1],
            nb[2],
        ]
        kb = [
            xb[1] * nb[2] - xb[2] * nb[1],
            xb[2] * nb[0] - xb[0] * nb[2],
            xb[0] * nb[1] - xb[1] * nb[0],
            nb[0],
            nb[1],
            nb[2],
        ]
        weights = [res]
        for v in range(2):
            sa = ja[0] * col(6 * v)
            sb = kb[0] * col(12 + 6 * v)
            for c in range(1, 6):
                sa = sa + ja[c] * col(6 * v + c)
                sb = sb + kb[c] * col(12 + 6 * v + c)
            weights.append(sa - sb)
        vals = []
        for w in weights:
            vals.extend([w * ja[c] for c in range(6)])
        for w in weights:
            vals.extend([w * kb[c] for c in range(3)])
        return tuple(a + v for a, v in zip(accs, vals))

    zero = jnp.zeros((8, chunk), jnp.float32)
    accs = lax.fori_loop(0, 128 // 8, body, (zero,) * N_QTY, unroll=2)
    valid = aux_ref[24:25, :]
    for q in range(N_QTY):
        out_ref[q : q + 1, :] = jnp.sum(accs[q], axis=0, keepdims=True) * valid
    out_ref[N_QTY:, :] = jnp.zeros((32 - N_QTY, chunk), jnp.float32)


def pair_sums(xa, tb, maps, aux, chunk=128):
    pairs = tb.shape[1]
    from_cargo = maps is None
    if from_cargo:
        xa_spec = pl.BlockSpec((xa.shape[0], chunk // CAP, 128), lambda i: (0, i, 0))
        maps = aux
        map_spec = pl.BlockSpec((8, 128), lambda i: (0, 0))
    else:
        xa_spec = pl.BlockSpec((3, chunk, 128), lambda i: (0, i, 0))
        map_spec = pl.BlockSpec((chunk, 128), lambda i: (i, 0))
    return pl.pallas_call(
        functools.partial(_terms_kernel, from_cargo),
        out_shape=jax.ShapeDtypeStruct((32, pairs), jnp.float32),
        grid=(pairs // chunk,),
        in_specs=[
            xa_spec,
            pl.BlockSpec((6, chunk, 128), lambda i: (0, i, 0)),
            map_spec,
            pl.BlockSpec((32, chunk), lambda i: (0, i)),
        ],
        out_specs=pl.BlockSpec((32, chunk), lambda i: (0, i)),
        scratch_shapes=[
            pltpu.VMEM((3, 128, chunk), jnp.float32),
            pltpu.VMEM((6, 128, chunk), jnp.float32),
        ],
    )(xa, tb, maps, aux)


def split_terms(out):
    sel = out[0:N_QTY].T
    ga = sel[:, 0:6] * (1.0 / 128)
    ha = sel[:, 6:18] * (1.0 / 4096)
    gb = -jnp.concatenate([sel[:, 18:21], sel[:, 3:6]], axis=1) * (1.0 / 128)
    hb0 = -jnp.concatenate([sel[:, 21:24], sel[:, 9:12]], axis=1) * (1.0 / 4096)
    hb1 = -jnp.concatenate([sel[:, 24:27], sel[:, 15:18]], axis=1) * (1.0 / 4096)
    return jnp.concatenate([ga, ha], axis=1), jnp.concatenate([gb, hb0, hb1], axis=1)


def frag_sums(blocks, terms, frag_count):
    onehot = (blocks[:, None] // BF == jnp.arange(frag_count, dtype=jnp.int32)[None, :]).astype(
        jnp.float32
    )
    return jnp.dot(terms.T, onehot, precision=lax.Precision.HIGHEST)


def make_aux(dirs_a, dirs_b, valid):
    pairs = dirs_a.shape[0]
    return jnp.concatenate(
        [dirs_a.T, dirs_b.T, valid[None, :], jnp.zeros((32 - 25, pairs), jnp.float32)], axis=0
    )


def local(
    points,
    normals,
    poses,
    directions,
    local_pairs,
    local_maps,
    remote_src,
    remote_maps,
    remote_dst,
    counts,
):
    axes = ("tile", "band")
    frag_count = poses.shape[1]
    rows6 = to_world_rows(points, normals, poses, BF)
    frag_dirs = directions.reshape(12, frag_count).T
    peers = counts.shape[1]

    source_blocks = remote_src[0]
    valid = (
        (jnp.arange(CAP, dtype=jnp.int32)[None, :] < counts[0][:, None])
        .astype(jnp.float32)
        .reshape(-1)
    )
    pick = (
        source_blocks.reshape(peers, CAP)[:, :, None]
        == jnp.arange(points.shape[0], dtype=jnp.int32)[None, None, :]
    ).astype(jnp.float32)
    xa_send = jnp.einsum("psb,cbk->scpk", pick, rows6[0:3], precision=lax.Precision.HIGHEST)
    map_send = jnp.transpose(remote_maps[0].reshape(peers, CAP, 128), (1, 0, 2))
    main = jnp.concatenate([xa_send, map_send.astype(jnp.float32)[:, None]], axis=1)
    frag_pick = (
        source_blocks[:, None] // BF == jnp.arange(frag_count, dtype=jnp.int32)[None, :]
    ).astype(jnp.float32)
    dirs_send = jnp.dot(frag_pick, frag_dirs, precision=lax.Precision.HIGHEST)
    side = jnp.concatenate([dirs_send, valid[:, None]], axis=1)
    side = side.reshape(peers, CAP * 13)
    side = jnp.concatenate([side, jnp.zeros((peers, 128 - CAP * 13), jnp.float32)], axis=1)
    cargo = jnp.concatenate([main.reshape(CAP * 4, peers, 128), side[None]], axis=0)
    arrived = lax.all_to_all(cargo, axes, split_axis=1, concat_axis=1, tiled=True)

    src_l = local_pairs[0]
    tgt_l = local_pairs[1]
    ones = jnp.ones((src_l.shape[0],), jnp.float32)
    out_l = pair_sums(
        rows6[0:3][:, src_l],
        rows6[:, tgt_l],
        local_maps,
        make_aux(frag_dirs[src_l // BF], frag_dirs[tgt_l // BF], ones),
    )
    local_a, local_b = split_terms(out_l)

    chunks = peers * CAP // 128

    def to_chunks(x):
        x = x.reshape((chunks, 128 // CAP, CAP) + x.shape[1:])
        return jnp.swapaxes(x, 1, 2).reshape((peers * CAP,) + x.shape[3:])

    def from_chunks(x):
        x = x.reshape((chunks, CAP, 128 // CAP) + x.shape[1:])
        return jnp.swapaxes(x, 1, 2).reshape((peers * CAP,) + x.shape[3:])

    target_blocks = to_chunks(remote_dst[0])
    side_in = to_chunks(arrived[CAP * 4, :, 0 : CAP * 13].reshape(peers * CAP, 13))
    out_r = pair_sums(
        arrived,
        rows6[:, target_blocks],
        None,
        make_aux(side_in[:, 0:12], frag_dirs[target_blocks // BF], side_in[:, 12]),
    )
    remote_a, remote_b = split_terms(out_r)
    returned = lax.all_to_all(
        from_chunks(remote_a).reshape(peers, CAP * 18), axes, split_axis=0, concat_axis=0, tiled=True
    ).reshape(peers * CAP, 18)

    totals = frag_sums(src_l, local_a, frag_count) + frag_sums(tgt_l, local_b, frag_count)
    totals = (
        totals
        + frag_sums(target_blocks, remote_b, frag_count)
        + frag_sums(source_blocks, returned, frag_count)
    )
    gradient = totals[0:6]
    hess_products = totals[6:18].reshape(2, 6, frag_count)
    return (gradient, hess_products)


def solution(mesh):
    placed = (
        P(("tile", "band"), None, None),
        P(("tile", "band"), None, None),
        P(None, ("tile", "band")),
        P(None, None, ("tile", "band")),
        P(None, ("tile", "band")),
        P(("tile", "band"), None),
        P(("tile", "band"), None),
        P(("tile", "band"), None, None),
        P(("tile", "band"), None),
        P(("tile", "band"), None),
    )
    return jax.shard_map(
        local,
        mesh=mesh,
        in_specs=placed,
        out_specs=(P(None, ("tile", "band")), P(None, None, ("tile", "band"))),
        check_vma=False,
    )
```

```python
import functools

import jax
import jax.numpy as jnp
from jax import lax
from jax.experimental import pallas as pl
from jax.experimental.pallas import tpu as pltpu
from jax.sharding import PartitionSpec as P

BF = 32
CAP = 8
N_QTY = 27


def rotations(poses):
    half_angle = poses[0:3] * 0.5
    inverse = 1.0 / jnp.sqrt(
        1.0
        + half_angle[0] * half_angle[0]
        + half_angle[1] * half_angle[1]
        + half_angle[2] * half_angle[2]
    )
    quat_x = half_angle[0] * inverse
    quat_y = half_angle[1] * inverse
    quat_z = half_angle[2] * inverse
    rotation = [
        [
            1.0 - 2.0 * (quat_y * quat_y + quat_z * quat_z),
            2.0 * (quat_x * quat_y - inverse * quat_z),
            2.0 * (quat_x * quat_z + inverse * quat_y),
        ],
        [
            2.0 * (quat_x * quat_y + inverse * quat_z),
            1.0 - 2.0 * (quat_x * quat_x + quat_z * quat_z),
            2.0 * (quat_y * quat_z - inverse * quat_x),
        ],
        [
            2.0 * (quat_x * quat_z - inverse * quat_y),
            2.0 * (quat_y * quat_z + inverse * quat_x),
            1.0 - 2.0 * (quat_x * quat_x + quat_y * quat_y),
        ],
    ]
    return (rotation, poses[3:6])


def to_world_rows(points, normals, poses, per_pose):
    rotation, translation = rotations(poses)

    def spread(values):
        return jnp.repeat(values, per_pose)[:, None]

    world_rows = []
    normal_rows = []
    for i in range(3):
        coeffs = [spread(rotation[i][j]) for j in range(3)]
        world_rows.append(
            coeffs[0] * points[:, 0]
            + coeffs[1] * points[:, 1]
            + coeffs[2] * points[:, 2]
            + spread(translation[i])
        )
        normal_rows.append(
            coeffs[0] * normals[:, 0] + coeffs[1] * normals[:, 1] + coeffs[2] * normals[:, 2]
        )
    return jnp.stack(world_rows + normal_rows, axis=0)


def _terms_kernel(from_cargo, xa_ref, tb_ref, map_ref, aux_ref, out_ref, xt_ref, gt_ref, cs_ref):
    chunk = out_ref.shape[1]
    if from_cargo:
        peers = chunk // CAP
        for r in range(4):
            for s in range(CAP):
                lanes = pl.ds((r * CAP + s) * 128, 128)
                cs_ref[r, pl.ds(s, peers, stride=CAP), :] = xa_ref[:, lanes]
        idx = cs_ref[3].astype(jnp.int32)
        for c in range(3):
            xt_ref[c] = cs_ref[c].T
    else:
        idx = map_ref[...]
        for c in range(3):
            xt_ref[c] = xa_ref[c].T
    for c in range(6):
        picked = jnp.take_along_axis(tb_ref[c], idx, axis=1, mode="promise_in_bounds")
        gt_ref[c] = picked.T

    def col(q):
        return jnp.broadcast_to(aux_ref[q : q + 1, :], (8, chunk))

    def body(s, accs):
        rows = pl.ds(pl.multiple_of(s * 8, 8), 8)
        xa = [xt_ref[c, rows, :] for c in range(3)]
        xb = [gt_ref[c, rows, :] for c in range(3)]
        nb = [gt_ref[3 + c, rows, :] for c in range(3)]
        off = [xa[c] - xb[c] for c in range(3)]
        res = nb[0] * off[0] + nb[1] * off[1] + nb[2] * off[2]
        ja = [
            xa[1] * nb[2] - xa[2] * nb[1],
            xa[2] * nb[0] - xa[0] * nb[2],
            xa[0] * nb[1] - xa[1] * nb[0],
            nb[0],
            nb[1],
            nb[2],
        ]
        kb = [
            xb[1] * nb[2] - xb[2] * nb[1],
            xb[2] * nb[0] - xb[0] * nb[2],
            xb[0] * nb[1] - xb[1] * nb[0],
            nb[0],
            nb[1],
            nb[2],
        ]
        weights = [res]
        for v in range(2):
            sa = ja[0] * col(6 * v)
            sb = kb[0] * col(12 + 6 * v)
            for c in range(1, 6):
                sa = sa + ja[c] * col(6 * v + c)
                sb = sb + kb[c] * col(12 + 6 * v + c)
            weights.append(sa - sb)
        vals = []
        for w in weights:
            vals.extend([w * ja[c] for c in range(6)])
        for w in weights:
            vals.extend([w * kb[c] for c in range(3)])
        return tuple(a + v for a, v in zip(accs, vals))

    zero = jnp.zeros((8, chunk), jnp.float32)
    accs = lax.fori_loop(0, 128 // 8, body, (zero,) * N_QTY, unroll=2)
    valid = aux_ref[24:25, :]
    for q in range(N_QTY):
        out_ref[q : q + 1, :] = jnp.sum(accs[q], axis=0, keepdims=True) * valid
    out_ref[N_QTY:, :] = jnp.zeros((32 - N_QTY, chunk), jnp.float32)


def pair_sums(xa, tb, maps, aux, chunk=128):
    pairs = tb.shape[1]
    from_cargo = maps is None
    if from_cargo:
        xa_spec = pl.BlockSpec((chunk // CAP, xa.shape[1]), lambda i: (i, 0))
        maps = aux
        map_spec = pl.BlockSpec((8, 128), lambda i: (0, 0))
    else:
        xa_spec = pl.BlockSpec((3, chunk, 128), lambda i: (0, i, 0))
        map_spec = pl.BlockSpec((chunk, 128), lambda i: (i, 0))
    return pl.pallas_call(
        functools.partial(_terms_kernel, from_cargo),
        out_shape=jax.ShapeDtypeStruct((32, pairs), jnp.float32),
        grid=(pairs // chunk,),
        in_specs=[
            xa_spec,
            pl.BlockSpec((6, chunk, 128), lambda i: (0, i, 0)),
            map_spec,
            pl.BlockSpec((32, chunk), lambda i: (0, i)),
        ],
        out_specs=pl.BlockSpec((32, chunk), lambda i: (0, i)),
        scratch_shapes=[
            pltpu.VMEM((3, 128, chunk), jnp.float32),
            pltpu.VMEM((6, 128, chunk), jnp.float32),
            pltpu.VMEM((4, chunk, 128), jnp.float32),
        ],
    )(xa, tb, maps, aux)


def _cargo_kernel(src_ref, w_ref, map_ref, side_ref, out_ref, rows_ref):
    chunk = map_ref.shape[0]
    peers = chunk // CAP
    pick = (
        src_ref[...] == lax.broadcasted_iota(jnp.int32, (chunk, w_ref.shape[1]), 1)
    ).astype(jnp.float32)
    for c in range(3):
        rows_ref[...] = jnp.dot(
            pick, w_ref[c], precision=lax.Precision.HIGHEST, preferred_element_type=jnp.float32
        )
        for s in range(CAP):
            lanes = pl.ds((c * CAP + s) * 128, 128)
            out_ref[:, lanes] = rows_ref[pl.ds(s, peers, stride=CAP), :]
    for s in range(CAP):
        lanes = pl.ds((3 * CAP + s) * 128, 128)
        out_ref[:, lanes] = map_ref[pl.ds(s, peers, stride=CAP), :].astype(jnp.float32)
    out_ref[:, pl.ds(4 * CAP * 128, 128)] = side_ref[...]


def build_cargo(source_blocks, world3, maps, side, chunk=128):
    slots = maps.shape[0]
    peers = chunk // CAP
    width = (4 * CAP + 1) * 128
    return pl.pallas_call(
        _cargo_kernel,
        out_shape=jax.ShapeDtypeStruct((slots // CAP, width), jnp.float32),
        grid=(slots // chunk,),
        in_specs=[
            pl.BlockSpec((chunk, 1), lambda i: (i, 0)),
            pl.BlockSpec(world3.shape, lambda i: (0, 0, 0)),
            pl.BlockSpec((chunk, 128), lambda i: (i, 0)),
            pl.BlockSpec((peers, 128), lambda i: (i, 0)),
        ],
        out_specs=pl.BlockSpec((peers, width), lambda i: (i, 0)),
        scratch_shapes=[pltpu.VMEM((chunk, 128), jnp.float32)],
    )(source_blocks[:, None], world3, maps, side)


def split_terms(out):
    sel = out[0:N_QTY].T
    ga = sel[:, 0:6] * (1.0 / 128)
    ha = sel[:, 6:18] * (1.0 / 4096)
    gb = -jnp.concatenate([sel[:, 18:21], sel[:, 3:6]], axis=1) * (1.0 / 128)
    hb0 = -jnp.concatenate([sel[:, 21:24], sel[:, 9:12]], axis=1) * (1.0 / 4096)
    hb1 = -jnp.concatenate([sel[:, 24:27], sel[:, 15:18]], axis=1) * (1.0 / 4096)
    return jnp.concatenate([ga, ha], axis=1), jnp.concatenate([gb, hb0, hb1], axis=1)


def frag_sums(blocks, terms, frag_count):
    onehot = (blocks[:, None] // BF == jnp.arange(frag_count, dtype=jnp.int32)[None, :]).astype(
        jnp.float32
    )
    return jnp.dot(onehot.T, terms, precision=lax.Precision.HIGHEST)


def make_aux(dirs_a, dirs_b, valid):
    pairs = dirs_a.shape[0]
    return jnp.concatenate(
        [dirs_a.T, dirs_b.T, valid[None, :], jnp.zeros((32 - 25, pairs), jnp.float32)], axis=0
    )


def local(
    points,
    normals,
    poses,
    directions,
    local_pairs,
    local_maps,
    remote_src,
    remote_maps,
    remote_dst,
    counts,
):
    axes = ("tile", "band")
    frag_count = poses.shape[1]
    rows6 = to_world_rows(points, normals, poses, BF)
    frag_dirs = directions.reshape(12, frag_count).T
    peers = counts.shape[1]

    source_blocks = remote_src[0]
    valid = (
        (jnp.arange(CAP, dtype=jnp.int32)[None, :] < counts[0][:, None])
        .astype(jnp.float32)
        .reshape(-1)
    )
    frag_pick = (
        source_blocks[:, None] // BF == jnp.arange(frag_count, dtype=jnp.int32)[None, :]
    ).astype(jnp.float32)
    dirs_send = jnp.dot(frag_pick, frag_dirs, precision=lax.Precision.HIGHEST)
    side = jnp.concatenate([dirs_send, valid[:, None]], axis=1)
    side = side.reshape(peers, CAP * 13)
    side = jnp.concatenate([side, jnp.zeros((peers, 128 - CAP * 13), jnp.float32)], axis=1)
    cargo = build_cargo(source_blocks, rows6[0:3], remote_maps[0], side)
    arrived = lax.all_to_all(cargo, axes, split_axis=0, concat_axis=0, tiled=True)

    src_l = local_pairs[0]
    tgt_l = local_pairs[1]
    ones = jnp.ones((src_l.shape[0],), jnp.float32)
    out_l = pair_sums(
        rows6[0:3][:, src_l],
        rows6[:, tgt_l],
        local_maps,
        make_aux(frag_dirs[src_l // BF], frag_dirs[tgt_l // BF], ones),
    )
    local_a, local_b = split_terms(out_l)

    target_blocks = remote_dst[0]
    side_in = arrived[:, CAP * 4 * 128 : CAP * 4 * 128 + CAP * 13].reshape(peers * CAP, 13)
    out_r = pair_sums(
        arrived,
        rows6[:, target_blocks],
        None,
        make_aux(side_in[:, 0:12], frag_dirs[target_blocks // BF], side_in[:, 12]),
    )
    remote_a, remote_b = split_terms(out_r)
    returned = lax.all_to_all(
        remote_a.reshape(peers, CAP * 18), axes, split_axis=0, concat_axis=0, tiled=True
    ).reshape(peers * CAP, 18)

    totals = frag_sums(src_l, local_a, frag_count) + frag_sums(tgt_l, local_b, frag_count)
    totals = (
        totals
        + frag_sums(target_blocks, remote_b, frag_count)
        + frag_sums(source_blocks, returned, frag_count)
    )
    gradient = totals[:, 0:6].T
    hess_products = totals[:, 6:18].T.reshape(2, 6, frag_count)
    return (gradient, hess_products)


def solution(mesh):
    placed = (
        P(("tile", "band"), None, None),
        P(("tile", "band"), None, None),
        P(None, ("tile", "band")),
        P(None, None, ("tile", "band")),
        P(None, ("tile", "band")),
        P(("tile", "band"), None),
        P(("tile", "band"), None),
        P(("tile", "band"), None, None),
        P(("tile", "band"), None),
        P(("tile", "band"), None),
    )
    return jax.shard_map(
        local,
        mesh=mesh,
        in_specs=placed,
        out_specs=(P(None, ("tile", "band")), P(None, None, ("tile", "band"))),
        check_vma=False,
    )
```

```python
import functools

import jax
import jax.numpy as jnp
from jax import lax
from jax.experimental import pallas as pl
from jax.experimental.pallas import tpu as pltpu
from jax.sharding import PartitionSpec as P

BF = 32
CAP = 8
N_QTY = 27


def rotations(poses):
    half_angle = poses[0:3] * 0.5
    inverse = 1.0 / jnp.sqrt(
        1.0
        + half_angle[0] * half_angle[0]
        + half_angle[1] * half_angle[1]
        + half_angle[2] * half_angle[2]
    )
    quat_x = half_angle[0] * inverse
    quat_y = half_angle[1] * inverse
    quat_z = half_angle[2] * inverse
    rotation = [
        [
            1.0 - 2.0 * (quat_y * quat_y + quat_z * quat_z),
            2.0 * (quat_x * quat_y - inverse * quat_z),
            2.0 * (quat_x * quat_z + inverse * quat_y),
        ],
        [
            2.0 * (quat_x * quat_y + inverse * quat_z),
            1.0 - 2.0 * (quat_x * quat_x + quat_z * quat_z),
            2.0 * (quat_y * quat_z - inverse * quat_x),
        ],
        [
            2.0 * (quat_x * quat_z - inverse * quat_y),
            2.0 * (quat_y * quat_z + inverse * quat_x),
            1.0 - 2.0 * (quat_x * quat_x + quat_y * quat_y),
        ],
    ]
    return (rotation, poses[3:6])


def to_world_rows(points, normals, poses, per_pose):
    rotation, translation = rotations(poses)

    def spread(values):
        return jnp.repeat(values, per_pose)[:, None]

    world_rows = []
    normal_rows = []
    for i in range(3):
        coeffs = [spread(rotation[i][j]) for j in range(3)]
        world_rows.append(
            coeffs[0] * points[:, 0]
            + coeffs[1] * points[:, 1]
            + coeffs[2] * points[:, 2]
            + spread(translation[i])
        )
        normal_rows.append(
            coeffs[0] * normals[:, 0] + coeffs[1] * normals[:, 1] + coeffs[2] * normals[:, 2]
        )
    return jnp.stack(world_rows + normal_rows, axis=0)


def _terms_kernel(from_cargo, xa_ref, tb_ref, map_ref, aux_ref, out_ref, xt_ref, gt_ref, cs_ref):
    chunk = out_ref.shape[1]
    if from_cargo:
        peers = chunk // CAP
        for r in range(4):
            for s in range(CAP):
                lanes = pl.ds((r * CAP + s) * 128, 128)
                cs_ref[r, pl.ds(s, peers, stride=CAP), :] = xa_ref[:, 0, lanes]
        idx = cs_ref[3].astype(jnp.int32)
        for c in range(3):
            xt_ref[c] = cs_ref[c].T
    else:
        idx = map_ref[...]
        for c in range(3):
            xt_ref[c] = xa_ref[c].T
    for c in range(6):
        picked = jnp.take_along_axis(tb_ref[c], idx, axis=1, mode="promise_in_bounds")
        gt_ref[c] = picked.T

    def col(q):
        return jnp.broadcast_to(aux_ref[q : q + 1, :], (8, chunk))

    def body(s, accs):
        rows = pl.ds(pl.multiple_of(s * 8, 8), 8)
        xa = [xt_ref[c, rows, :] for c in range(3)]
        xb = [gt_ref[c, rows, :] for c in range(3)]
        nb = [gt_ref[3 + c, rows, :] for c in range(3)]
        off = [xa[c] - xb[c] for c in range(3)]
        res = nb[0] * off[0] + nb[1] * off[1] + nb[2] * off[2]
        ja = [
            xa[1] * nb[2] - xa[2] * nb[1],
            xa[2] * nb[0] - xa[0] * nb[2],
            xa[0] * nb[1] - xa[1] * nb[0],
            nb[0],
            nb[1],
            nb[2],
        ]
        kb = [
            xb[1] * nb[2] - xb[2] * nb[1],
            xb[2] * nb[0] - xb[0] * nb[2],
            xb[0] * nb[1] - xb[1] * nb[0],
            nb[0],
            nb[1],
            nb[2],
        ]
        weights = [res]
        for v in range(2):
            sa = ja[0] * col(6 * v)
            sb = kb[0] * col(12 + 6 * v)
            for c in range(1, 6):
                sa = sa + ja[c] * col(6 * v + c)
                sb = sb + kb[c] * col(12 + 6 * v + c)
            weights.append(sa - sb)
        vals = []
        for w in weights:
            vals.extend([w * ja[c] for c in range(6)])
        for w in weights:
            vals.extend([w * kb[c] for c in range(3)])
        return tuple(a + v for a, v in zip(accs, vals))

    zero = jnp.zeros((8, chunk), jnp.float32)
    accs = lax.fori_loop(0, 128 // 8, body, (zero,) * N_QTY, unroll=2)
    valid = aux_ref[24:25, :]
    for q in range(N_QTY):
        out_ref[q : q + 1, :] = jnp.sum(accs[q], axis=0, keepdims=True) * valid
    out_ref[N_QTY:, :] = jnp.zeros((32 - N_QTY, chunk), jnp.float32)


def pair_sums(xa, tb, maps, aux, chunk=128):
    pairs = tb.shape[1]
    from_cargo = maps is None
    if from_cargo:
        xa_spec = pl.BlockSpec((chunk // CAP, 1, xa.shape[2]), lambda i: (i, 0, 0))
        maps = aux
        map_spec = pl.BlockSpec((8, 128), lambda i: (0, 0))
    else:
        xa_spec = pl.BlockSpec((3, chunk, 128), lambda i: (0, i, 0))
        map_spec = pl.BlockSpec((chunk, 128), lambda i: (i, 0))
    return pl.pallas_call(
        functools.partial(_terms_kernel, from_cargo),
        out_shape=jax.ShapeDtypeStruct((32, pairs), jnp.float32),
        grid=(pairs // chunk,),
        in_specs=[
            xa_spec,
            pl.BlockSpec((6, chunk, 128), lambda i: (0, i, 0)),
            map_spec,
            pl.BlockSpec((32, chunk), lambda i: (0, i)),
        ],
        out_specs=pl.BlockSpec((32, chunk), lambda i: (0, i)),
        scratch_shapes=[
            pltpu.VMEM((3, 128, chunk), jnp.float32),
            pltpu.VMEM((6, 128, chunk), jnp.float32),
            pltpu.VMEM((4, chunk, 128), jnp.float32),
        ],
    )(xa, tb, maps, aux)


def _cargo_kernel(xa_ref, map_ref, side_ref, out_ref):
    peers = side_ref.shape[0]
    for c in range(3):
        for s in range(CAP):
            lanes = pl.ds((c * CAP + s) * 128, 128)
            out_ref[:, 0, lanes] = xa_ref[c, pl.ds(s, peers, stride=CAP), :]
    for s in range(CAP):
        lanes = pl.ds((3 * CAP + s) * 128, 128)
        out_ref[:, 0, lanes] = map_ref[pl.ds(s, peers, stride=CAP), :].astype(jnp.float32)
    out_ref[:, 0, pl.ds(4 * CAP * 128, 128)] = side_ref[...]


def build_cargo(xa3, maps, side, chunk=128):
    slots = maps.shape[0]
    peers = chunk // CAP
    width = (4 * CAP + 1) * 128
    return pl.pallas_call(
        _cargo_kernel,
        out_shape=jax.ShapeDtypeStruct((slots // CAP, 1, width), jnp.float32),
        grid=(slots // chunk,),
        in_specs=[
            pl.BlockSpec((3, chunk, 128), lambda i: (0, i, 0)),
            pl.BlockSpec((chunk, 128), lambda i: (i, 0)),
            pl.BlockSpec((peers, 128), lambda i: (i, 0)),
        ],
        out_specs=pl.BlockSpec((peers, 1, width), lambda i: (i, 0, 0)),
    )(xa3, maps, side)


def split_terms(out):
    sel = out[0:N_QTY].T
    ga = sel[:, 0:6] * (1.0 / 128)
    ha = sel[:, 6:18] * (1.0 / 4096)
    gb = -jnp.concatenate([sel[:, 18:21], sel[:, 3:6]], axis=1) * (1.0 / 128)
    hb0 = -jnp.concatenate([sel[:, 21:24], sel[:, 9:12]], axis=1) * (1.0 / 4096)
    hb1 = -jnp.concatenate([sel[:, 24:27], sel[:, 15:18]], axis=1) * (1.0 / 4096)
    return jnp.concatenate([ga, ha], axis=1), jnp.concatenate([gb, hb0, hb1], axis=1)


def frag_sums(blocks, terms, frag_count):
    onehot = (blocks[:, None] // BF == jnp.arange(frag_count, dtype=jnp.int32)[None, :]).astype(
        jnp.float32
    )
    return jnp.dot(onehot.T, terms, precision=lax.Precision.HIGHEST)


def make_aux(dirs_a, dirs_b, valid):
    pairs = dirs_a.shape[0]
    return jnp.concatenate(
        [dirs_a.T, dirs_b.T, valid[None, :], jnp.zeros((32 - 25, pairs), jnp.float32)], axis=0
    )


def local(
    points,
    normals,
    poses,
    directions,
    local_pairs,
    local_maps,
    remote_src,
    remote_maps,
    remote_dst,
    counts,
):
    axes = ("tile", "band")
    frag_count = poses.shape[1]
    rows6 = to_world_rows(points, normals, poses, BF)
    frag_dirs = directions.reshape(12, frag_count).T
    peers = counts.shape[1]

    source_blocks = remote_src[0]
    valid = (
        (jnp.arange(CAP, dtype=jnp.int32)[None, :] < counts[0][:, None])
        .astype(jnp.float32)
        .reshape(-1)
    )
    frag_pick = (
        source_blocks[:, None] // BF == jnp.arange(frag_count, dtype=jnp.int32)[None, :]
    ).astype(jnp.float32)
    dirs_send = jnp.dot(frag_pick, frag_dirs, precision=lax.Precision.HIGHEST)
    side = jnp.concatenate([dirs_send, valid[:, None]], axis=1)
    side = side.reshape(peers, CAP * 13)
    side = jnp.concatenate([side, jnp.zeros((peers, 128 - CAP * 13), jnp.float32)], axis=1)
    pick = (source_blocks[:, None] == jnp.arange(points.shape[0], dtype=jnp.int32)[None, :]).astype(
        jnp.float32
    )
    xa3 = jnp.einsum("sb,cbk->csk", pick, rows6[0:3], precision=lax.Precision.HIGHEST)
    cargo = build_cargo(xa3, remote_maps[0], side)
    arrived = lax.all_to_all(cargo, axes, split_axis=0, concat_axis=0, tiled=True)

    src_l = local_pairs[0]
    tgt_l = local_pairs[1]
    ones = jnp.ones((src_l.shape[0],), jnp.float32)
    out_l = pair_sums(
        rows6[0:3][:, src_l],
        rows6[:, tgt_l],
        local_maps,
        make_aux(frag_dirs[src_l // BF], frag_dirs[tgt_l // BF], ones),
    )
    local_a, local_b = split_terms(out_l)

    target_blocks = remote_dst[0]
    side_in = arrived[:, 0, CAP * 4 * 128 : CAP * 4 * 128 + CAP * 13].reshape(peers * CAP, 13)
    out_r = pair_sums(
        arrived,
        rows6[:, target_blocks],
        None,
        make_aux(side_in[:, 0:12], frag_dirs[target_blocks // BF], side_in[:, 12]),
    )
    remote_a, remote_b = split_terms(out_r)
    returned = lax.all_to_all(
        remote_a.reshape(peers, CAP * 18), axes, split_axis=0, concat_axis=0, tiled=True
    ).reshape(peers * CAP, 18)

    totals = frag_sums(src_l, local_a, frag_count) + frag_sums(tgt_l, local_b, frag_count)
    totals = (
        totals
        + frag_sums(target_blocks, remote_b, frag_count)
        + frag_sums(source_blocks, returned, frag_count)
    )
    gradient = totals[:, 0:6].T
    hess_products = totals[:, 6:18].T.reshape(2, 6, frag_count)
    return (gradient, hess_products)


def solution(mesh):
    placed = (
        P(("tile", "band"), None, None),
        P(("tile", "band"), None, None),
        P(None, ("tile", "band")),
        P(None, None, ("tile", "band")),
        P(None, ("tile", "band")),
        P(("tile", "band"), None),
        P(("tile", "band"), None),
        P(("tile", "band"), None, None),
        P(("tile", "band"), None),
        P(("tile", "band"), None),
    )
    return jax.shard_map(
        local,
        mesh=mesh,
        in_specs=placed,
        out_specs=(P(None, ("tile", "band")), P(None, None, ("tile", "band"))),
        check_vma=False,
    )
```

```python
import functools

import jax
import jax.numpy as jnp
from jax import lax
from jax.experimental import pallas as pl
from jax.experimental.pallas import tpu as pltpu
from jax.sharding import PartitionSpec as P

BF = 32
CAP = 8
N_QTY = 27


def rotations(poses):
    half_angle = poses[0:3] * 0.5
    inverse = 1.0 / jnp.sqrt(
        1.0
        + half_angle[0] * half_angle[0]
        + half_angle[1] * half_angle[1]
        + half_angle[2] * half_angle[2]
    )
    quat_x = half_angle[0] * inverse
    quat_y = half_angle[1] * inverse
    quat_z = half_angle[2] * inverse
    rotation = [
        [
            1.0 - 2.0 * (quat_y * quat_y + quat_z * quat_z),
            2.0 * (quat_x * quat_y - inverse * quat_z),
            2.0 * (quat_x * quat_z + inverse * quat_y),
        ],
        [
            2.0 * (quat_x * quat_y + inverse * quat_z),
            1.0 - 2.0 * (quat_x * quat_x + quat_z * quat_z),
            2.0 * (quat_y * quat_z - inverse * quat_x),
        ],
        [
            2.0 * (quat_x * quat_z - inverse * quat_y),
            2.0 * (quat_y * quat_z + inverse * quat_x),
            1.0 - 2.0 * (quat_x * quat_x + quat_y * quat_y),
        ],
    ]
    return (rotation, poses[3:6])


def to_world_rows(points, normals, poses, per_pose):
    rotation, translation = rotations(poses)

    def spread(values):
        return jnp.repeat(values, per_pose)[:, None]

    world_rows = []
    normal_rows = []
    for i in range(3):
        coeffs = [spread(rotation[i][j]) for j in range(3)]
        world_rows.append(
            coeffs[0] * points[:, 0]
            + coeffs[1] * points[:, 1]
            + coeffs[2] * points[:, 2]
            + spread(translation[i])
        )
        normal_rows.append(
            coeffs[0] * normals[:, 0] + coeffs[1] * normals[:, 1] + coeffs[2] * normals[:, 2]
        )
    return jnp.stack(world_rows + normal_rows, axis=0)


def _terms_kernel(from_cargo, xa_ref, tb_ref, map_ref, aux_ref, out_ref, xt_ref, gt_ref, cs_ref):
    chunk = out_ref.shape[1]
    if from_cargo:
        peers = chunk // CAP
        height = 4 * CAP + 1
        for p in range(peers):
            for r in range(4):
                cs_ref[r, pl.ds(p * CAP, CAP), :] = xa_ref[pl.ds(p * height + r * CAP, CAP), :]
        idx = cs_ref[3].astype(jnp.int32)
        for c in range(3):
            xt_ref[c] = cs_ref[c].T
    else:
        idx = map_ref[...]
        for c in range(3):
            xt_ref[c] = xa_ref[c].T
    for c in range(6):
        picked = jnp.take_along_axis(tb_ref[c], idx, axis=1, mode="promise_in_bounds")
        gt_ref[c] = picked.T

    def col(q):
        return jnp.broadcast_to(aux_ref[q : q + 1, :], (8, chunk))

    def body(s, accs):
        rows = pl.ds(pl.multiple_of(s * 8, 8), 8)
        xa = [xt_ref[c, rows, :] for c in range(3)]
        xb = [gt_ref[c, rows, :] for c in range(3)]
        nb = [gt_ref[3 + c, rows, :] for c in range(3)]
        off = [xa[c] - xb[c] for c in range(3)]
        res = nb[0] * off[0] + nb[1] * off[1] + nb[2] * off[2]
        ja = [
            xa[1] * nb[2] - xa[2] * nb[1],
            xa[2] * nb[0] - xa[0] * nb[2],
            xa[0] * nb[1] - xa[1] * nb[0],
            nb[0],
            nb[1],
            nb[2],
        ]
        kb = [
            xb[1] * nb[2] - xb[2] * nb[1],
            xb[2] * nb[0] - xb[0] * nb[2],
            xb[0] * nb[1] - xb[1] * nb[0],
            nb[0],
            nb[1],
            nb[2],
        ]
        weights = [res]
        for v in range(2):
            sa = ja[0] * col(6 * v)
            sb = kb[0] * col(12 + 6 * v)
            for c in range(1, 6):
                sa = sa + ja[c] * col(6 * v + c)
                sb = sb + kb[c] * col(12 + 6 * v + c)
            weights.append(sa - sb)
        vals = []
        for w in weights:
            vals.extend([w * ja[c] for c in range(6)])
        for w in weights:
            vals.extend([w * kb[c] for c in range(3)])
        return tuple(a + v for a, v in zip(accs, vals))

    zero = jnp.zeros((8, chunk), jnp.float32)
    accs = lax.fori_loop(0, 128 // 8, body, (zero,) * N_QTY, unroll=2)
    valid = aux_ref[24:25, :]
    for q in range(N_QTY):
        out_ref[q : q + 1, :] = jnp.sum(accs[q], axis=0, keepdims=True) * valid
    out_ref[N_QTY:, :] = jnp.zeros((32 - N_QTY, chunk), jnp.float32)


def pair_sums(xa, tb, maps, aux, chunk=128):
    pairs = tb.shape[1]
    from_cargo = maps is None
    if from_cargo:
        xa = xa.reshape(-1, 128)
        xa_spec = pl.BlockSpec((chunk // CAP * (4 * CAP + 1), 128), lambda i: (i, 0))
        maps = aux
        map_spec = pl.BlockSpec((8, 128), lambda i: (0, 0))
    else:
        xa_spec = pl.BlockSpec((3, chunk, 128), lambda i: (0, i, 0))
        map_spec = pl.BlockSpec((chunk, 128), lambda i: (i, 0))
    return pl.pallas_call(
        functools.partial(_terms_kernel, from_cargo),
        out_shape=jax.ShapeDtypeStruct((32, pairs), jnp.float32),
        grid=(pairs // chunk,),
        in_specs=[
            xa_spec,
            pl.BlockSpec((6, chunk, 128), lambda i: (0, i, 0)),
            map_spec,
            pl.BlockSpec((32, chunk), lambda i: (0, i)),
        ],
        out_specs=pl.BlockSpec((32, chunk), lambda i: (0, i)),
        scratch_shapes=[
            pltpu.VMEM((3, 128, chunk), jnp.float32),
            pltpu.VMEM((6, 128, chunk), jnp.float32),
            pltpu.VMEM((4, chunk, 128), jnp.float32),
        ],
    )(xa, tb, maps, aux)


def _cargo_kernel(xa_ref, map_ref, side_ref, out_ref):
    peers = side_ref.shape[0]
    height = 4 * CAP + 1
    for p in range(peers):
        slots = pl.ds(p * CAP, CAP)
        for c in range(3):
            out_ref[pl.ds(p * height + c * CAP, CAP), :] = xa_ref[c, slots, :]
        out_ref[pl.ds(p * height + 3 * CAP, CAP), :] = map_ref[slots, :].astype(jnp.float32)
        out_ref[pl.ds(p * height + 4 * CAP, 1), :] = side_ref[pl.ds(p, 1), :]


def build_cargo(xa3, maps, side, chunk=128):
    slots = maps.shape[0]
    peers = chunk // CAP
    height = 4 * CAP + 1
    cargo = pl.pallas_call(
        _cargo_kernel,
        out_shape=jax.ShapeDtypeStruct((slots // CAP * height, 128), jnp.float32),
        grid=(slots // chunk,),
        in_specs=[
            pl.BlockSpec((3, chunk, 128), lambda i: (0, i, 0)),
            pl.BlockSpec((chunk, 128), lambda i: (i, 0)),
            pl.BlockSpec((peers, 128), lambda i: (i, 0)),
        ],
        out_specs=pl.BlockSpec((peers * height, 128), lambda i: (i, 0)),
    )(xa3, maps, side)
    return cargo.reshape(slots // CAP, 1, height * 128)


def split_terms(out):
    sel = out[0:N_QTY].T
    ga = sel[:, 0:6] * (1.0 / 128)
    ha = sel[:, 6:18] * (1.0 / 4096)
    gb = -jnp.concatenate([sel[:, 18:21], sel[:, 3:6]], axis=1) * (1.0 / 128)
    hb0 = -jnp.concatenate([sel[:, 21:24], sel[:, 9:12]], axis=1) * (1.0 / 4096)
    hb1 = -jnp.concatenate([sel[:, 24:27], sel[:, 15:18]], axis=1) * (1.0 / 4096)
    return jnp.concatenate([ga, ha], axis=1), jnp.concatenate([gb, hb0, hb1], axis=1)


def pick_rows(blocks, rows):
    onehot = (blocks[:, None] == jnp.arange(rows.shape[1], dtype=jnp.int32)[None, :]).astype(
        jnp.float32
    )
    return jnp.einsum("sb,cbk->csk", onehot, rows, precision=lax.Precision.HIGHEST)


def frag_sums(blocks, terms, frag_count):
    onehot = (blocks[:, None] // BF == jnp.arange(frag_count, dtype=jnp.int32)[None, :]).astype(
        jnp.float32
    )
    return jnp.dot(onehot.T, terms, precision=lax.Precision.HIGHEST)


def make_aux(dirs_a, dirs_b, valid):
    pairs = dirs_a.shape[0]
    return jnp.concatenate(
        [dirs_a.T, dirs_b.T, valid[None, :], jnp.zeros((32 - 25, pairs), jnp.float32)], axis=0
    )


def local(
    points,
    normals,
    poses,
    directions,
    local_pairs,
    local_maps,
    remote_src,
    remote_maps,
    remote_dst,
    counts,
):
    axes = ("tile", "band")
    frag_count = poses.shape[1]
    rows6 = to_world_rows(points, normals, poses, BF)
    frag_dirs = directions.reshape(12, frag_count).T
    peers = counts.shape[1]

    source_blocks = remote_src[0]
    valid = (
        (jnp.arange(CAP, dtype=jnp.int32)[None, :] < counts[0][:, None])
        .astype(jnp.float32)
        .reshape(-1)
    )
    frag_pick = (
        source_blocks[:, None] // BF == jnp.arange(frag_count, dtype=jnp.int32)[None, :]
    ).astype(jnp.float32)
    dirs_send = jnp.dot(frag_pick, frag_dirs, precision=lax.Precision.HIGHEST)
    side = jnp.concatenate([dirs_send, valid[:, None]], axis=1)
    side = side.reshape(peers, CAP * 13)
    side = jnp.concatenate([side, jnp.zeros((peers, 128 - CAP * 13), jnp.float32)], axis=1)
    cargo = build_cargo(pick_rows(source_blocks, rows6[0:3]), remote_maps[0], side)
    arrived = lax.all_to_all(cargo, axes, split_axis=0, concat_axis=0, tiled=True)

    src_l = local_pairs[0]
    tgt_l = local_pairs[1]
    ones = jnp.ones((src_l.shape[0],), jnp.float32)
    out_l = pair_sums(
        pick_rows(src_l, rows6[0:3]),
        pick_rows(tgt_l, rows6),
        local_maps,
        make_aux(frag_dirs[src_l // BF], frag_dirs[tgt_l // BF], ones),
    )
    local_a, local_b = split_terms(out_l)

    target_blocks = remote_dst[0]
    side_in = arrived[:, 0, CAP * 4 * 128 : CAP * 4 * 128 + CAP * 13].reshape(peers * CAP, 13)
    out_r = pair_sums(
        arrived,
        pick_rows(target_blocks, rows6),
        None,
        make_aux(side_in[:, 0:12], frag_dirs[target_blocks // BF], side_in[:, 12]),
    )
    remote_a, remote_b = split_terms(out_r)
    returned = lax.all_to_all(
        remote_a.reshape(peers, CAP * 18), axes, split_axis=0, concat_axis=0, tiled=True
    ).reshape(peers * CAP, 18)

    totals = frag_sums(src_l, local_a, frag_count) + frag_sums(tgt_l, local_b, frag_count)
    totals = (
        totals
        + frag_sums(target_blocks, remote_b, frag_count)
        + frag_sums(source_blocks, returned, frag_count)
    )
    gradient = totals[:, 0:6].T
    hess_products = totals[:, 6:18].T.reshape(2, 6, frag_count)
    return (gradient, hess_products)


def solution(mesh):
    placed = (
        P(("tile", "band"), None, None),
        P(("tile", "band"), None, None),
        P(None, ("tile", "band")),
        P(None, None, ("tile", "band")),
        P(None, ("tile", "band")),
        P(("tile", "band"), None),
        P(("tile", "band"), None),
        P(("tile", "band"), None, None),
        P(("tile", "band"), None),
        P(("tile", "band"), None),
    )
    return jax.shard_map(
        local,
        mesh=mesh,
        in_specs=placed,
        out_specs=(P(None, ("tile", "band")), P(None, None, ("tile", "band"))),
        check_vma=False,
    )
```

```python
import functools

import jax
import jax.numpy as jnp
from jax import lax
from jax.experimental import pallas as pl
from jax.experimental.pallas import tpu as pltpu
from jax.sharding import PartitionSpec as P

BF = 32
CAP = 8
N_QTY = 27


def rotations(poses):
    half_angle = poses[0:3] * 0.5
    inverse = 1.0 / jnp.sqrt(
        1.0
        + half_angle[0] * half_angle[0]
        + half_angle[1] * half_angle[1]
        + half_angle[2] * half_angle[2]
    )
    quat_x = half_angle[0] * inverse
    quat_y = half_angle[1] * inverse
    quat_z = half_angle[2] * inverse
    rotation = [
        [
            1.0 - 2.0 * (quat_y * quat_y + quat_z * quat_z),
            2.0 * (quat_x * quat_y - inverse * quat_z),
            2.0 * (quat_x * quat_z + inverse * quat_y),
        ],
        [
            2.0 * (quat_x * quat_y + inverse * quat_z),
            1.0 - 2.0 * (quat_x * quat_x + quat_z * quat_z),
            2.0 * (quat_y * quat_z - inverse * quat_x),
        ],
        [
            2.0 * (quat_x * quat_z - inverse * quat_y),
            2.0 * (quat_y * quat_z + inverse * quat_x),
            1.0 - 2.0 * (quat_x * quat_x + quat_y * quat_y),
        ],
    ]
    return (rotation, poses[3:6])


def to_world_rows(points, normals, poses, per_pose):
    rotation, translation = rotations(poses)

    def spread(values):
        return jnp.repeat(values, per_pose)[:, None]

    world_rows = []
    normal_rows = []
    for i in range(3):
        coeffs = [spread(rotation[i][j]) for j in range(3)]
        world_rows.append(
            coeffs[0] * points[:, 0]
            + coeffs[1] * points[:, 1]
            + coeffs[2] * points[:, 2]
            + spread(translation[i])
        )
        normal_rows.append(
            coeffs[0] * normals[:, 0] + coeffs[1] * normals[:, 1] + coeffs[2] * normals[:, 2]
        )
    return jnp.stack(world_rows + normal_rows, axis=0)


def _terms_kernel(from_cargo, xa_ref, tb_ref, map_ref, aux_ref, out_ref, xt_ref, gt_ref, cs_ref):
    chunk = out_ref.shape[1]
    if from_cargo:
        peers = chunk // CAP
        height = 4 * CAP + 1
        for p in range(peers):
            for r in range(4):
                cs_ref[r, pl.ds(p * CAP, CAP), :] = xa_ref[pl.ds(p * height + r * CAP, CAP), :]
        idx = cs_ref[3].astype(jnp.int32)
        for c in range(3):
            xt_ref[c] = cs_ref[c].T
    else:
        idx = map_ref[...]
        for c in range(3):
            xt_ref[c] = xa_ref[c].T
    for c in range(6):
        picked = jnp.take_along_axis(tb_ref[c], idx, axis=1, mode="promise_in_bounds")
        gt_ref[c] = picked.T

    def col(q):
        return jnp.broadcast_to(aux_ref[q : q + 1, :], (8, chunk))

    def body(s, accs):
        rows = pl.ds(pl.multiple_of(s * 8, 8), 8)
        xa = [xt_ref[c, rows, :] for c in range(3)]
        xb = [gt_ref[c, rows, :] for c in range(3)]
        nb = [gt_ref[3 + c, rows, :] for c in range(3)]
        off = [xa[c] - xb[c] for c in range(3)]
        res = nb[0] * off[0] + nb[1] * off[1] + nb[2] * off[2]
        ja = [
            xa[1] * nb[2] - xa[2] * nb[1],
            xa[2] * nb[0] - xa[0] * nb[2],
            xa[0] * nb[1] - xa[1] * nb[0],
            nb[0],
            nb[1],
            nb[2],
        ]
        kb = [
            xb[1] * nb[2] - xb[2] * nb[1],
            xb[2] * nb[0] - xb[0] * nb[2],
            xb[0] * nb[1] - xb[1] * nb[0],
            nb[0],
            nb[1],
            nb[2],
        ]
        weights = [res]
        for v in range(2):
            sa = ja[0] * col(6 * v)
            sb = kb[0] * col(12 + 6 * v)
            for c in range(1, 6):
                sa = sa + ja[c] * col(6 * v + c)
                sb = sb + kb[c] * col(12 + 6 * v + c)
            weights.append(sa - sb)
        vals = []
        for w in weights:
            vals.extend([w * ja[c] for c in range(6)])
        for w in weights:
            vals.extend([w * kb[c] for c in range(3)])
        return tuple(a + v for a, v in zip(accs, vals))

    zero = jnp.zeros((8, chunk), jnp.float32)
    accs = lax.fori_loop(0, 128 // 8, body, (zero,) * N_QTY, unroll=2)
    valid = aux_ref[24:25, :]
    for q in range(N_QTY):
        out_ref[q : q + 1, :] = jnp.sum(accs[q], axis=0, keepdims=True) * valid
    out_ref[N_QTY:, :] = jnp.zeros((32 - N_QTY, chunk), jnp.float32)


def pair_sums(xa, tb, maps, aux, chunk=128):
    pairs = tb.shape[1]
    from_cargo = maps is None
    if from_cargo:
        xa = xa.reshape(-1, 128)
        xa_spec = pl.BlockSpec((chunk // CAP * (4 * CAP + 1), 128), lambda i: (i, 0))
        maps = aux
        map_spec = pl.BlockSpec((8, 128), lambda i: (0, 0))
    else:
        xa_spec = pl.BlockSpec((3, chunk, 128), lambda i: (0, i, 0))
        map_spec = pl.BlockSpec((chunk, 128), lambda i: (i, 0))
    return pl.pallas_call(
        functools.partial(_terms_kernel, from_cargo),
        out_shape=jax.ShapeDtypeStruct((32, pairs), jnp.float32),
        grid=(pairs // chunk,),
        in_specs=[
            xa_spec,
            pl.BlockSpec((6, chunk, 128), lambda i: (0, i, 0)),
            map_spec,
            pl.BlockSpec((32, chunk), lambda i: (0, i)),
        ],
        out_specs=pl.BlockSpec((32, chunk), lambda i: (0, i)),
        scratch_shapes=[
            pltpu.VMEM((3, 128, chunk), jnp.float32),
            pltpu.VMEM((6, 128, chunk), jnp.float32),
            pltpu.VMEM((4, chunk, 128), jnp.float32),
        ],
    )(xa, tb, maps, aux)


def _cargo_kernel(xa_ref, map_ref, side_ref, out_ref):
    height = 4 * CAP + 1
    group = 8

    def body(g, carry):
        for q in range(group):
            p = g * group + q
            base = pl.multiple_of(g * (group * height), 8) + q * height
            slots = pl.ds(pl.multiple_of(p * CAP, CAP), CAP)
            for c in range(3):
                out_ref[pl.ds(base + c * CAP, CAP), :] = xa_ref[c, slots, :]
            out_ref[pl.ds(base + 3 * CAP, CAP), :] = map_ref[slots, :].astype(jnp.float32)
            out_ref[pl.ds(base + 4 * CAP, 1), :] = side_ref[pl.ds(p, 1), :]
        return carry

    lax.fori_loop(0, side_ref.shape[0] // group, body, 0)


def build_cargo(xa3, maps, side):
    slots = maps.shape[0]
    height = 4 * CAP + 1
    cargo = pl.pallas_call(
        _cargo_kernel,
        out_shape=jax.ShapeDtypeStruct((slots // CAP * height, 128), jnp.float32),
    )(xa3, maps, side)
    return cargo.reshape(slots // CAP, 1, height * 128)


def split_terms(out):
    sel = out[0:N_QTY].T
    ga = sel[:, 0:6] * (1.0 / 128)
    ha = sel[:, 6:18] * (1.0 / 4096)
    gb = -jnp.concatenate([sel[:, 18:21], sel[:, 3:6]], axis=1) * (1.0 / 128)
    hb0 = -jnp.concatenate([sel[:, 21:24], sel[:, 9:12]], axis=1) * (1.0 / 4096)
    hb1 = -jnp.concatenate([sel[:, 24:27], sel[:, 15:18]], axis=1) * (1.0 / 4096)
    return jnp.concatenate([ga, ha], axis=1), jnp.concatenate([gb, hb0, hb1], axis=1)


def pick_rows(blocks, rows):
    onehot = (blocks[:, None] == jnp.arange(rows.shape[1], dtype=jnp.int32)[None, :]).astype(
        jnp.float32
    )
    return jnp.einsum("sb,cbk->csk", onehot, rows, precision=lax.Precision.HIGHEST)


def frag_sums(blocks, terms, frag_count):
    onehot = (blocks[:, None] // BF == jnp.arange(frag_count, dtype=jnp.int32)[None, :]).astype(
        jnp.float32
    )
    return jnp.dot(onehot.T, terms, precision=lax.Precision.HIGHEST)


def make_aux(dirs_a, dirs_b, valid):
    pairs = dirs_a.shape[0]
    return jnp.concatenate(
        [dirs_a.T, dirs_b.T, valid[None, :], jnp.zeros((32 - 25, pairs), jnp.float32)], axis=0
    )


def local(
    points,
    normals,
    poses,
    directions,
    local_pairs,
    local_maps,
    remote_src,
    remote_maps,
    remote_dst,
    counts,
):
    axes = ("tile", "band")
    frag_count = poses.shape[1]
    rows6 = to_world_rows(points, normals, poses, BF)
    frag_dirs = directions.reshape(12, frag_count).T
    peers = counts.shape[1]

    source_blocks = remote_src[0]
    valid = (
        (jnp.arange(CAP, dtype=jnp.int32)[None, :] < counts[0][:, None])
        .astype(jnp.float32)
        .reshape(-1)
    )
    frag_pick = (
        source_blocks[:, None] // BF == jnp.arange(frag_count, dtype=jnp.int32)[None, :]
    ).astype(jnp.float32)
    dirs_send = jnp.dot(frag_pick, frag_dirs, precision=lax.Precision.HIGHEST)
    side = jnp.concatenate([dirs_send, valid[:, None]], axis=1)
    side = side.reshape(peers, CAP * 13)
    side = jnp.concatenate([side, jnp.zeros((peers, 128 - CAP * 13), jnp.float32)], axis=1)
    cargo = build_cargo(pick_rows(source_blocks, rows6[0:3]), remote_maps[0], side)
    arrived = lax.all_to_all(cargo, axes, split_axis=0, concat_axis=0, tiled=True)

    src_l = local_pairs[0]
    tgt_l = local_pairs[1]
    ones = jnp.ones((src_l.shape[0],), jnp.float32)
    out_l = pair_sums(
        pick_rows(src_l, rows6[0:3]),
        pick_rows(tgt_l, rows6),
        local_maps,
        make_aux(frag_dirs[src_l // BF], frag_dirs[tgt_l // BF], ones),
    )
    local_a, local_b = split_terms(out_l)

    target_blocks = remote_dst[0]
    side_in = arrived[:, 0, CAP * 4 * 128 : CAP * 4 * 128 + CAP * 13].reshape(peers * CAP, 13)
    out_r = pair_sums(
        arrived,
        pick_rows(target_blocks, rows6),
        None,
        make_aux(side_in[:, 0:12], frag_dirs[target_blocks // BF], side_in[:, 12]),
    )
    remote_a, remote_b = split_terms(out_r)
    returned = lax.all_to_all(
        remote_a.reshape(peers, CAP * 18), axes, split_axis=0, concat_axis=0, tiled=True
    ).reshape(peers * CAP, 18)

    totals = frag_sums(src_l, local_a, frag_count) + frag_sums(tgt_l, local_b, frag_count)
    totals = (
        totals
        + frag_sums(target_blocks, remote_b, frag_count)
        + frag_sums(source_blocks, returned, frag_count)
    )
    gradient = totals[:, 0:6].T
    hess_products = totals[:, 6:18].T.reshape(2, 6, frag_count)
    return (gradient, hess_products)


def solution(mesh):
    placed = (
        P(("tile", "band"), None, None),
        P(("tile", "band"), None, None),
        P(None, ("tile", "band")),
        P(None, None, ("tile", "band")),
        P(None, ("tile", "band")),
        P(("tile", "band"), None),
        P(("tile", "band"), None),
        P(("tile", "band"), None, None),
        P(("tile", "band"), None),
        P(("tile", "band"), None),
    )
    return jax.shard_map(
        local,
        mesh=mesh,
        in_specs=placed,
        out_specs=(P(None, ("tile", "band")), P(None, None, ("tile", "band"))),
        check_vma=False,
    )
```

```python
import functools

import jax
import jax.numpy as jnp
from jax import lax
from jax.experimental import pallas as pl
from jax.experimental.pallas import tpu as pltpu
from jax.sharding import PartitionSpec as P

BF = 32
CAP = 8
N_QTY = 27


def rotations(poses):
    half_angle = poses[0:3] * 0.5
    inverse = 1.0 / jnp.sqrt(
        1.0
        + half_angle[0] * half_angle[0]
        + half_angle[1] * half_angle[1]
        + half_angle[2] * half_angle[2]
    )
    quat_x = half_angle[0] * inverse
    quat_y = half_angle[1] * inverse
    quat_z = half_angle[2] * inverse
    rotation = [
        [
            1.0 - 2.0 * (quat_y * quat_y + quat_z * quat_z),
            2.0 * (quat_x * quat_y - inverse * quat_z),
            2.0 * (quat_x * quat_z + inverse * quat_y),
        ],
        [
            2.0 * (quat_x * quat_y + inverse * quat_z),
            1.0 - 2.0 * (quat_x * quat_x + quat_z * quat_z),
            2.0 * (quat_y * quat_z - inverse * quat_x),
        ],
        [
            2.0 * (quat_x * quat_z - inverse * quat_y),
            2.0 * (quat_y * quat_z + inverse * quat_x),
            1.0 - 2.0 * (quat_x * quat_x + quat_y * quat_y),
        ],
    ]
    return (rotation, poses[3:6])


def to_world_rows(points, normals, poses, per_pose):
    rotation, translation = rotations(poses)

    def spread(values):
        return jnp.repeat(values, per_pose)[:, None]

    world_rows = []
    normal_rows = []
    for i in range(3):
        coeffs = [spread(rotation[i][j]) for j in range(3)]
        world_rows.append(
            coeffs[0] * points[:, 0]
            + coeffs[1] * points[:, 1]
            + coeffs[2] * points[:, 2]
            + spread(translation[i])
        )
        normal_rows.append(
            coeffs[0] * normals[:, 0] + coeffs[1] * normals[:, 1] + coeffs[2] * normals[:, 2]
        )
    return jnp.stack(world_rows + normal_rows, axis=0)


def _terms_kernel(from_cargo, xa_ref, tb_ref, map_ref, aux_ref, out_ref, xt_ref, gt_ref, cs_ref):
    chunk = out_ref.shape[1]
    if from_cargo:
        peers = chunk // CAP
        height = 4 * CAP + 1
        for p in range(peers):
            for r in range(4):
                cs_ref[r, pl.ds(p * CAP, CAP), :] = xa_ref[pl.ds(p * height + r * CAP, CAP), :]
        idx = cs_ref[3].astype(jnp.int32)
        for c in range(3):
            xt_ref[c] = cs_ref[c].T
    else:
        idx = map_ref[...]
        for c in range(3):
            xt_ref[c] = xa_ref[c].T
    for c in range(6):
        picked = jnp.take_along_axis(tb_ref[c], idx, axis=1, mode="promise_in_bounds")
        gt_ref[c] = picked.T

    def col(q):
        return jnp.broadcast_to(aux_ref[q : q + 1, :], (8, chunk))

    def body(s, accs):
        rows = pl.ds(pl.multiple_of(s * 8, 8), 8)
        xa = [xt_ref[c, rows, :] for c in range(3)]
        xb = [gt_ref[c, rows, :] for c in range(3)]
        nb = [gt_ref[3 + c, rows, :] for c in range(3)]
        off = [xa[c] - xb[c] for c in range(3)]
        res = nb[0] * off[0] + nb[1] * off[1] + nb[2] * off[2]
        ja = [
            xa[1] * nb[2] - xa[2] * nb[1],
            xa[2] * nb[0] - xa[0] * nb[2],
            xa[0] * nb[1] - xa[1] * nb[0],
            nb[0],
            nb[1],
            nb[2],
        ]
        kb = [
            xb[1] * nb[2] - xb[2] * nb[1],
            xb[2] * nb[0] - xb[0] * nb[2],
            xb[0] * nb[1] - xb[1] * nb[0],
            nb[0],
            nb[1],
            nb[2],
        ]
        weights = [res]
        for v in range(2):
            sa = ja[0] * col(6 * v)
            sb = kb[0] * col(12 + 6 * v)
            for c in range(1, 6):
                sa = sa + ja[c] * col(6 * v + c)
                sb = sb + kb[c] * col(12 + 6 * v + c)
            weights.append(sa - sb)
        vals = []
        for w in weights:
            vals.extend([w * ja[c] for c in range(6)])
        for w in weights:
            vals.extend([w * kb[c] for c in range(3)])
        return tuple(a + v for a, v in zip(accs, vals))

    zero = jnp.zeros((8, chunk), jnp.float32)
    accs = lax.fori_loop(0, 128 // 8, body, (zero,) * N_QTY, unroll=8)
    valid = aux_ref[24:25, :]
    for q in range(N_QTY):
        out_ref[q : q + 1, :] = jnp.sum(accs[q], axis=0, keepdims=True) * valid
    out_ref[N_QTY:, :] = jnp.zeros((32 - N_QTY, chunk), jnp.float32)


def pair_sums(xa, tb, maps, aux, chunk=128):
    pairs = tb.shape[1]
    from_cargo = maps is None
    if from_cargo:
        xa = xa.reshape(-1, 128)
        xa_spec = pl.BlockSpec((chunk // CAP * (4 * CAP + 1), 128), lambda i: (i, 0))
        maps = aux
        map_spec = pl.BlockSpec((8, 128), lambda i: (0, 0))
    else:
        xa_spec = pl.BlockSpec((3, chunk, 128), lambda i: (0, i, 0))
        map_spec = pl.BlockSpec((chunk, 128), lambda i: (i, 0))
    return pl.pallas_call(
        functools.partial(_terms_kernel, from_cargo),
        out_shape=jax.ShapeDtypeStruct((32, pairs), jnp.float32),
        grid=(pairs // chunk,),
        in_specs=[
            xa_spec,
            pl.BlockSpec((6, chunk, 128), lambda i: (0, i, 0)),
            map_spec,
            pl.BlockSpec((32, chunk), lambda i: (0, i)),
        ],
        out_specs=pl.BlockSpec((32, chunk), lambda i: (0, i)),
        scratch_shapes=[
            pltpu.VMEM((3, 128, chunk), jnp.float32),
            pltpu.VMEM((6, 128, chunk), jnp.float32),
            pltpu.VMEM((4, chunk, 128), jnp.float32),
        ],
    )(xa, tb, maps, aux)


def _cargo_kernel(xa_ref, map_ref, side_ref, out_ref):
    height = 4 * CAP + 1
    group = 8

    def body(g, carry):
        for q in range(group):
            p = g * group + q
            base = pl.multiple_of(g * (group * height), 8) + q * height
            slots = pl.ds(pl.multiple_of(p * CAP, CAP), CAP)
            for c in range(3):
                out_ref[pl.ds(base + c * CAP, CAP), :] = xa_ref[c, slots, :]
            out_ref[pl.ds(base + 3 * CAP, CAP), :] = map_ref[slots, :].astype(jnp.float32)
            out_ref[pl.ds(base + 4 * CAP, 1), :] = side_ref[pl.ds(p, 1), :]
        return carry

    lax.fori_loop(0, side_ref.shape[0] // group, body, 0)


def build_cargo(xa3, maps, side):
    slots = maps.shape[0]
    height = 4 * CAP + 1
    cargo = pl.pallas_call(
        _cargo_kernel,
        out_shape=jax.ShapeDtypeStruct((slots // CAP * height, 128), jnp.float32),
    )(xa3, maps, side)
    return cargo.reshape(slots // CAP, 1, height * 128)


def split_terms(out):
    sel = out[0:N_QTY].T
    ga = sel[:, 0:6] * (1.0 / 128)
    ha = sel[:, 6:18] * (1.0 / 4096)
    gb = -jnp.concatenate([sel[:, 18:21], sel[:, 3:6]], axis=1) * (1.0 / 128)
    hb0 = -jnp.concatenate([sel[:, 21:24], sel[:, 9:12]], axis=1) * (1.0 / 4096)
    hb1 = -jnp.concatenate([sel[:, 24:27], sel[:, 15:18]], axis=1) * (1.0 / 4096)
    return jnp.concatenate([ga, ha], axis=1), jnp.concatenate([gb, hb0, hb1], axis=1)


def pick_rows(blocks, rows):
    onehot = (blocks[:, None] == jnp.arange(rows.shape[1], dtype=jnp.int32)[None, :]).astype(
        jnp.float32
    )
    return jnp.einsum("sb,cbk->csk", onehot, rows, precision=lax.Precision.HIGHEST)


def frag_sums(blocks, terms, frag_count):
    onehot = (blocks[:, None] // BF == jnp.arange(frag_count, dtype=jnp.int32)[None, :]).astype(
        jnp.float32
    )
    return jnp.dot(onehot.T, terms, precision=lax.Precision.HIGHEST)


def make_aux(dirs_a, dirs_b, valid):
    pairs = dirs_a.shape[0]
    return jnp.concatenate(
        [dirs_a.T, dirs_b.T, valid[None, :], jnp.zeros((32 - 25, pairs), jnp.float32)], axis=0
    )


def local(
    points,
    normals,
    poses,
    directions,
    local_pairs,
    local_maps,
    remote_src,
    remote_maps,
    remote_dst,
    counts,
):
    axes = ("tile", "band")
    frag_count = poses.shape[1]
    rows6 = to_world_rows(points, normals, poses, BF)
    frag_dirs = directions.reshape(12, frag_count).T
    peers = counts.shape[1]

    source_blocks = remote_src[0]
    valid = (
        (jnp.arange(CAP, dtype=jnp.int32)[None, :] < counts[0][:, None])
        .astype(jnp.float32)
        .reshape(-1)
    )
    frag_pick = (
        source_blocks[:, None] // BF == jnp.arange(frag_count, dtype=jnp.int32)[None, :]
    ).astype(jnp.float32)
    dirs_send = jnp.dot(frag_pick, frag_dirs, precision=lax.Precision.HIGHEST)
    side = jnp.concatenate([dirs_send, valid[:, None]], axis=1)
    side = side.reshape(peers, CAP * 13)
    side = jnp.concatenate([side, jnp.zeros((peers, 128 - CAP * 13), jnp.float32)], axis=1)
    cargo = build_cargo(pick_rows(source_blocks, rows6[0:3]), remote_maps[0], side)
    arrived = lax.all_to_all(cargo, axes, split_axis=0, concat_axis=0, tiled=True)

    src_l = local_pairs[0]
    tgt_l = local_pairs[1]
    ones = jnp.ones((src_l.shape[0],), jnp.float32)
    out_l = pair_sums(
        pick_rows(src_l, rows6[0:3]),
        pick_rows(tgt_l, rows6),
        local_maps,
        make_aux(frag_dirs[src_l // BF], frag_dirs[tgt_l // BF], ones),
    )
    local_a, local_b = split_terms(out_l)

    target_blocks = remote_dst[0]
    side_in = arrived[:, 0, CAP * 4 * 128 : CAP * 4 * 128 + CAP * 13].reshape(peers * CAP, 13)
    out_r = pair_sums(
        arrived,
        pick_rows(target_blocks, rows6),
        None,
        make_aux(side_in[:, 0:12], frag_dirs[target_blocks // BF], side_in[:, 12]),
    )
    remote_a, remote_b = split_terms(out_r)
    returned = lax.all_to_all(
        remote_a.reshape(peers, CAP * 18), axes, split_axis=0, concat_axis=0, tiled=True
    ).reshape(peers * CAP, 18)

    totals = frag_sums(src_l, local_a, frag_count) + frag_sums(tgt_l, local_b, frag_count)
    totals = (
        totals
        + frag_sums(target_blocks, remote_b, frag_count)
        + frag_sums(source_blocks, returned, frag_count)
    )
    gradient = totals[:, 0:6].T
    hess_products = totals[:, 6:18].T.reshape(2, 6, frag_count)
    return (gradient, hess_products)


def solution(mesh):
    placed = (
        P(("tile", "band"), None, None),
        P(("tile", "band"), None, None),
        P(None, ("tile", "band")),
        P(None, None, ("tile", "band")),
        P(None, ("tile", "band")),
        P(("tile", "band"), None),
        P(("tile", "band"), None),
        P(("tile", "band"), None, None),
        P(("tile", "band"), None),
        P(("tile", "band"), None),
    )
    return jax.shard_map(
        local,
        mesh=mesh,
        in_specs=placed,
        out_specs=(P(None, ("tile", "band")), P(None, None, ("tile", "band"))),
        check_vma=False,
    )
```

```python
import functools

import jax
import jax.numpy as jnp
from jax import lax
from jax.experimental import pallas as pl
from jax.experimental.pallas import tpu as pltpu
from jax.sharding import PartitionSpec as P

BF = 32
CAP = 8
N_QTY = 27
MESH = pl.DeviceIdType.MESH


def rotations(poses):
    half_angle = poses[0:3] * 0.5
    inverse = 1.0 / jnp.sqrt(
        1.0
        + half_angle[0] * half_angle[0]
        + half_angle[1] * half_angle[1]
        + half_angle[2] * half_angle[2]
    )
    quat_x = half_angle[0] * inverse
    quat_y = half_angle[1] * inverse
    quat_z = half_angle[2] * inverse
    rotation = [
        [
            1.0 - 2.0 * (quat_y * quat_y + quat_z * quat_z),
            2.0 * (quat_x * quat_y - inverse * quat_z),
            2.0 * (quat_x * quat_z + inverse * quat_y),
        ],
        [
            2.0 * (quat_x * quat_y + inverse * quat_z),
            1.0 - 2.0 * (quat_x * quat_x + quat_z * quat_z),
            2.0 * (quat_y * quat_z - inverse * quat_x),
        ],
        [
            2.0 * (quat_x * quat_z - inverse * quat_y),
            2.0 * (quat_y * quat_z + inverse * quat_x),
            1.0 - 2.0 * (quat_x * quat_x + quat_y * quat_y),
        ],
    ]
    return (rotation, poses[3:6])


def to_world_rows(points, normals, poses, per_pose):
    rotation, translation = rotations(poses)

    def spread(values):
        return jnp.repeat(values, per_pose)[:, None]

    world_rows = []
    normal_rows = []
    for i in range(3):
        coeffs = [spread(rotation[i][j]) for j in range(3)]
        world_rows.append(
            coeffs[0] * points[:, 0]
            + coeffs[1] * points[:, 1]
            + coeffs[2] * points[:, 2]
            + spread(translation[i])
        )
        normal_rows.append(
            coeffs[0] * normals[:, 0] + coeffs[1] * normals[:, 1] + coeffs[2] * normals[:, 2]
        )
    return jnp.stack(world_rows + normal_rows, axis=0)


def _terms_kernel(from_cargo, xa_ref, tb_ref, map_ref, aux_ref, out_ref, xt_ref, gt_ref, cs_ref):
    chunk = out_ref.shape[1]
    if from_cargo:
        peers = chunk // CAP
        height = 4 * CAP + 1
        for p in range(peers):
            for r in range(4):
                cs_ref[r, pl.ds(p * CAP, CAP), :] = xa_ref[pl.ds(p * height + r * CAP, CAP), :]
        idx = cs_ref[3].astype(jnp.int32)
        for c in range(3):
            xt_ref[c] = cs_ref[c].T
    else:
        idx = map_ref[...]
        for c in range(3):
            xt_ref[c] = xa_ref[c].T
    for c in range(6):
        picked = jnp.take_along_axis(tb_ref[c], idx, axis=1, mode="promise_in_bounds")
        gt_ref[c] = picked.T

    def col(q):
        return jnp.broadcast_to(aux_ref[q : q + 1, :], (8, chunk))

    def body(s, accs):
        rows = pl.ds(pl.multiple_of(s * 8, 8), 8)
        xa = [xt_ref[c, rows, :] for c in range(3)]
        xb = [gt_ref[c, rows, :] for c in range(3)]
        nb = [gt_ref[3 + c, rows, :] for c in range(3)]
        off = [xa[c] - xb[c] for c in range(3)]
        res = nb[0] * off[0] + nb[1] * off[1] + nb[2] * off[2]
        ja = [
            xa[1] * nb[2] - xa[2] * nb[1],
            xa[2] * nb[0] - xa[0] * nb[2],
            xa[0] * nb[1] - xa[1] * nb[0],
            nb[0],
            nb[1],
            nb[2],
        ]
        kb = [
            xb[1] * nb[2] - xb[2] * nb[1],
            xb[2] * nb[0] - xb[0] * nb[2],
            xb[0] * nb[1] - xb[1] * nb[0],
            nb[0],
            nb[1],
            nb[2],
        ]
        weights = [res]
        for v in range(2):
            sa = ja[0] * col(6 * v)
            sb = kb[0] * col(12 + 6 * v)
            for c in range(1, 6):
                sa = sa + ja[c] * col(6 * v + c)
                sb = sb + kb[c] * col(12 + 6 * v + c)
            weights.append(sa - sb)
        vals = []
        for w in weights:
            vals.extend([w * ja[c] for c in range(6)])
        for w in weights:
            vals.extend([w * kb[c] for c in range(3)])
        return tuple(a + v for a, v in zip(accs, vals))

    zero = jnp.zeros((8, chunk), jnp.float32)
    accs = lax.fori_loop(0, 128 // 8, body, (zero,) * N_QTY, unroll=8)
    valid = aux_ref[24:25, :]
    for q in range(N_QTY):
        out_ref[q : q + 1, :] = jnp.sum(accs[q], axis=0, keepdims=True) * valid
    out_ref[N_QTY:, :] = jnp.zeros((32 - N_QTY, chunk), jnp.float32)


def pair_sums(xa, tb, maps, aux, chunk=128):
    pairs = tb.shape[1]
    from_cargo = maps is None
    if from_cargo:
        xa = xa.reshape(-1, 128)
        xa_spec = pl.BlockSpec((chunk // CAP * (4 * CAP + 1), 128), lambda i: (i, 0))
        maps = aux
        map_spec = pl.BlockSpec((8, 128), lambda i: (0, 0))
    else:
        xa_spec = pl.BlockSpec((3, chunk, 128), lambda i: (0, i, 0))
        map_spec = pl.BlockSpec((chunk, 128), lambda i: (i, 0))
    return pl.pallas_call(
        functools.partial(_terms_kernel, from_cargo),
        out_shape=jax.ShapeDtypeStruct((32, pairs), jnp.float32),
        grid=(pairs // chunk,),
        in_specs=[
            xa_spec,
            pl.BlockSpec((6, chunk, 128), lambda i: (0, i, 0)),
            map_spec,
            pl.BlockSpec((32, chunk), lambda i: (0, i)),
        ],
        out_specs=pl.BlockSpec((32, chunk), lambda i: (0, i)),
        scratch_shapes=[
            pltpu.VMEM((3, 128, chunk), jnp.float32),
            pltpu.VMEM((6, 128, chunk), jnp.float32),
            pltpu.VMEM((4, chunk, 128), jnp.float32),
        ],
    )(xa, tb, maps, aux)


def _cargo_kernel(xa_ref, map_ref, side_ref, out_ref):
    height = 4 * CAP + 1
    group = 8

    def body(g, carry):
        for q in range(group):
            p = g * group + q
            base = pl.multiple_of(g * (group * height), 8) + q * height
            slots = pl.ds(pl.multiple_of(p * CAP, CAP), CAP)
            for c in range(3):
                out_ref[pl.ds(base + c * CAP, CAP), :] = xa_ref[c, slots, :]
            out_ref[pl.ds(base + 3 * CAP, CAP), :] = map_ref[slots, :].astype(jnp.float32)
            out_ref[pl.ds(base + 4 * CAP, 1), :] = side_ref[pl.ds(p, 1), :]
        return carry

    lax.fori_loop(0, side_ref.shape[0] // group, body, 0)


def build_cargo(xa3, maps, side):
    slots = maps.shape[0]
    height = 4 * CAP + 1
    cargo = pl.pallas_call(
        _cargo_kernel,
        out_shape=jax.ShapeDtypeStruct((slots // CAP * height, 128), jnp.float32),
    )(xa3, maps, side)
    return cargo.reshape(slots // CAP, 1, height * 128)


def split_terms(out):
    sel = out[0:N_QTY].T
    ga = sel[:, 0:6] * (1.0 / 128)
    ha = sel[:, 6:18] * (1.0 / 4096)
    gb = -jnp.concatenate([sel[:, 18:21], sel[:, 3:6]], axis=1) * (1.0 / 128)
    hb0 = -jnp.concatenate([sel[:, 21:24], sel[:, 9:12]], axis=1) * (1.0 / 4096)
    hb1 = -jnp.concatenate([sel[:, 24:27], sel[:, 15:18]], axis=1) * (1.0 / 4096)
    return jnp.concatenate([ga, ha], axis=1), jnp.concatenate([gb, hb0, hb1], axis=1)


def _exchange_kernel(n_band, x_ref, out_ref, send_sems, recv_sems, own_sem):
    peers = x_ref.shape[0]
    me = lax.axis_index("tile") * n_band + lax.axis_index("band")

    def peer_of(k):
        p = lax.rem(me + k, peers)
        return p, (p // n_band, p % n_band)

    barrier = pltpu.get_barrier_semaphore()

    def greet(k, carry):
        _, dev = peer_of(k)
        pl.semaphore_signal(barrier, inc=1, device_id=dev, device_id_type=MESH)
        return carry

    lax.fori_loop(1, peers, greet, 0)
    pl.semaphore_wait(barrier, peers - 1)

    own = pltpu.make_async_copy(x_ref.at[me], out_ref.at[me], own_sem)
    own.start()

    def outgoing(k):
        p, dev = peer_of(k)
        return pltpu.make_async_remote_copy(
            src_ref=x_ref.at[p],
            dst_ref=out_ref.at[me],
            send_sem=send_sems.at[p],
            recv_sem=recv_sems.at[me],
            device_id=dev,
            device_id_type=MESH,
        )

    def incoming(k):
        p, dev = peer_of(k)
        return pltpu.make_async_remote_copy(
            src_ref=x_ref.at[p],
            dst_ref=out_ref.at[p],
            send_sem=send_sems.at[p],
            recv_sem=recv_sems.at[p],
            device_id=dev,
            device_id_type=MESH,
        )

    def start(k, carry):
        outgoing(k).start()
        return carry

    lax.fori_loop(1, peers, start, 0)

    def finish(k, carry):
        outgoing(k).wait_send()
        incoming(k).wait_recv()
        return carry

    lax.fori_loop(1, peers, finish, 0)
    own.wait()


def exchange(x, n_band, collective_id):
    peers = x.shape[0]
    return pl.pallas_call(
        functools.partial(_exchange_kernel, n_band),
        out_shape=jax.ShapeDtypeStruct(x.shape, x.dtype),
        in_specs=[pl.BlockSpec(memory_space=pl.ANY)],
        out_specs=pl.BlockSpec(memory_space=pl.ANY),
        scratch_shapes=[
            pltpu.SemaphoreType.DMA((peers,)),
            pltpu.SemaphoreType.DMA((peers,)),
            pltpu.SemaphoreType.DMA(()),
        ],
        compiler_params=pltpu.CompilerParams(collective_id=collective_id, has_side_effects=True),
    )(x)


def pick_rows(blocks, rows):
    onehot = (blocks[:, None] == jnp.arange(rows.shape[1], dtype=jnp.int32)[None, :]).astype(
        jnp.float32
    )
    return jnp.einsum("sb,cbk->csk", onehot, rows, precision=lax.Precision.HIGHEST)


def frag_sums(blocks, terms, frag_count):
    onehot = (blocks[:, None] // BF == jnp.arange(frag_count, dtype=jnp.int32)[None, :]).astype(
        jnp.float32
    )
    return jnp.dot(onehot.T, terms, precision=lax.Precision.HIGHEST)


def make_aux(dirs_a, dirs_b, valid):
    pairs = dirs_a.shape[0]
    return jnp.concatenate(
        [dirs_a.T, dirs_b.T, valid[None, :], jnp.zeros((32 - 25, pairs), jnp.float32)], axis=0
    )


def local(
    points,
    normals,
    poses,
    directions,
    local_pairs,
    local_maps,
    remote_src,
    remote_maps,
    remote_dst,
    counts,
):
    axes = ("tile", "band")
    n_band = lax.axis_size("band")
    frag_count = poses.shape[1]
    rows6 = to_world_rows(points, normals, poses, BF)
    frag_dirs = directions.reshape(12, frag_count).T
    peers = counts.shape[1]

    source_blocks = remote_src[0]
    valid = (
        (jnp.arange(CAP, dtype=jnp.int32)[None, :] < counts[0][:, None])
        .astype(jnp.float32)
        .reshape(-1)
    )
    frag_pick = (
        source_blocks[:, None] // BF == jnp.arange(frag_count, dtype=jnp.int32)[None, :]
    ).astype(jnp.float32)
    dirs_send = jnp.dot(frag_pick, frag_dirs, precision=lax.Precision.HIGHEST)
    side = jnp.concatenate([dirs_send, valid[:, None]], axis=1)
    side = side.reshape(peers, CAP * 13)
    side = jnp.concatenate([side, jnp.zeros((peers, 128 - CAP * 13), jnp.float32)], axis=1)
    cargo = build_cargo(pick_rows(source_blocks, rows6[0:3]), remote_maps[0], side)
    arrived = lax.all_to_all(cargo, axes, split_axis=0, concat_axis=0, tiled=True)

    src_l = local_pairs[0]
    tgt_l = local_pairs[1]
    ones = jnp.ones((src_l.shape[0],), jnp.float32)
    out_l = pair_sums(
        pick_rows(src_l, rows6[0:3]),
        pick_rows(tgt_l, rows6),
        local_maps,
        make_aux(frag_dirs[src_l // BF], frag_dirs[tgt_l // BF], ones),
    )
    local_a, local_b = split_terms(out_l)

    target_blocks = remote_dst[0]
    side_in = arrived[:, 0, CAP * 4 * 128 : CAP * 4 * 128 + CAP * 13].reshape(peers * CAP, 13)
    out_r = pair_sums(
        arrived,
        pick_rows(target_blocks, rows6),
        None,
        make_aux(side_in[:, 0:12], frag_dirs[target_blocks // BF], side_in[:, 12]),
    )
    remote_a, remote_b = split_terms(out_r)
    returned = exchange(remote_a.reshape(peers, 1, CAP * 18), n_band, 0).reshape(peers * CAP, 18)

    totals = frag_sums(src_l, local_a, frag_count) + frag_sums(tgt_l, local_b, frag_count)
    totals = (
        totals
        + frag_sums(target_blocks, remote_b, frag_count)
        + frag_sums(source_blocks, returned, frag_count)
    )
    gradient = totals[:, 0:6].T
    hess_products = totals[:, 6:18].T.reshape(2, 6, frag_count)
    return (gradient, hess_products)


def solution(mesh):
    placed = (
        P(("tile", "band"), None, None),
        P(("tile", "band"), None, None),
        P(None, ("tile", "band")),
        P(None, None, ("tile", "band")),
        P(None, ("tile", "band")),
        P(("tile", "band"), None),
        P(("tile", "band"), None),
        P(("tile", "band"), None, None),
        P(("tile", "band"), None),
        P(("tile", "band"), None),
    )
    return jax.shard_map(
        local,
        mesh=mesh,
        in_specs=placed,
        out_specs=(P(None, ("tile", "band")), P(None, None, ("tile", "band"))),
        check_vma=False,
    )
```

```python
import functools

import jax
import jax.numpy as jnp
from jax import lax
from jax.experimental import pallas as pl
from jax.experimental.pallas import tpu as pltpu
from jax.sharding import PartitionSpec as P

BF = 32
CAP = 8
N_QTY = 27
MESH = pl.DeviceIdType.MESH


def rotations(poses):
    half_angle = poses[0:3] * 0.5
    inverse = 1.0 / jnp.sqrt(
        1.0
        + half_angle[0] * half_angle[0]
        + half_angle[1] * half_angle[1]
        + half_angle[2] * half_angle[2]
    )
    quat_x = half_angle[0] * inverse
    quat_y = half_angle[1] * inverse
    quat_z = half_angle[2] * inverse
    rotation = [
        [
            1.0 - 2.0 * (quat_y * quat_y + quat_z * quat_z),
            2.0 * (quat_x * quat_y - inverse * quat_z),
            2.0 * (quat_x * quat_z + inverse * quat_y),
        ],
        [
            2.0 * (quat_x * quat_y + inverse * quat_z),
            1.0 - 2.0 * (quat_x * quat_x + quat_z * quat_z),
            2.0 * (quat_y * quat_z - inverse * quat_x),
        ],
        [
            2.0 * (quat_x * quat_z - inverse * quat_y),
            2.0 * (quat_y * quat_z + inverse * quat_x),
            1.0 - 2.0 * (quat_x * quat_x + quat_y * quat_y),
        ],
    ]
    return (rotation, poses[3:6])


def to_world_rows(points, normals, poses, per_pose):
    rotation, translation = rotations(poses)

    def spread(values):
        return jnp.repeat(values, per_pose)[:, None]

    world_rows = []
    normal_rows = []
    for i in range(3):
        coeffs = [spread(rotation[i][j]) for j in range(3)]
        world_rows.append(
            coeffs[0] * points[:, 0]
            + coeffs[1] * points[:, 1]
            + coeffs[2] * points[:, 2]
            + spread(translation[i])
        )
        normal_rows.append(
            coeffs[0] * normals[:, 0] + coeffs[1] * normals[:, 1] + coeffs[2] * normals[:, 2]
        )
    return jnp.stack(world_rows + normal_rows, axis=0)


def _terms_kernel(from_cargo, n_band, xa_ref, tb_ref, map_ref, aux_ref, out_ref, *rest):
    if from_cargo:
        recv_ref, xt_ref, gt_ref, cs_ref, ret_ref, send_sems, recv_sems, own_sem = rest
    else:
        xt_ref, gt_ref, cs_ref = rest
    chunk = out_ref.shape[1]
    if from_cargo:
        peers = chunk // CAP
        height = 4 * CAP + 1
        for p in range(peers):
            for r in range(4):
                cs_ref[r, pl.ds(p * CAP, CAP), :] = xa_ref[pl.ds(p * height + r * CAP, CAP), :]
        idx = cs_ref[3].astype(jnp.int32)
        for c in range(3):
            xt_ref[c] = cs_ref[c].T
    else:
        idx = map_ref[...]
        for c in range(3):
            xt_ref[c] = xa_ref[c].T
    for c in range(6):
        picked = jnp.take_along_axis(tb_ref[c], idx, axis=1, mode="promise_in_bounds")
        gt_ref[c] = picked.T

    def col(q):
        return jnp.broadcast_to(aux_ref[q : q + 1, :], (8, chunk))

    def body(s, accs):
        rows = pl.ds(pl.multiple_of(s * 8, 8), 8)
        xa = [xt_ref[c, rows, :] for c in range(3)]
        xb = [gt_ref[c, rows, :] for c in range(3)]
        nb = [gt_ref[3 + c, rows, :] for c in range(3)]
        off = [xa[c] - xb[c] for c in range(3)]
        res = nb[0] * off[0] + nb[1] * off[1] + nb[2] * off[2]
        ja = [
            xa[1] * nb[2] - xa[2] * nb[1],
            xa[2] * nb[0] - xa[0] * nb[2],
            xa[0] * nb[1] - xa[1] * nb[0],
            nb[0],
            nb[1],
            nb[2],
        ]
        kb = [
            xb[1] * nb[2] - xb[2] * nb[1],
            xb[2] * nb[0] - xb[0] * nb[2],
            xb[0] * nb[1] - xb[1] * nb[0],
            nb[0],
            nb[1],
            nb[2],
        ]
        weights = [res]
        for v in range(2):
            sa = ja[0] * col(6 * v)
            sb = kb[0] * col(12 + 6 * v)
            for c in range(1, 6):
                sa = sa + ja[c] * col(6 * v + c)
                sb = sb + kb[c] * col(12 + 6 * v + c)
            weights.append(sa - sb)
        vals = []
        for w in weights:
            vals.extend([w * ja[c] for c in range(6)])
        for w in weights:
            vals.extend([w * kb[c] for c in range(3)])
        return tuple(a + v for a, v in zip(accs, vals))

    zero = jnp.zeros((8, chunk), jnp.float32)
    accs = lax.fori_loop(0, 128 // 8, body, (zero,) * N_QTY, unroll=8)
    valid = aux_ref[24:25, :]
    for q in range(N_QTY):
        out_ref[q : q + 1, :] = jnp.sum(accs[q], axis=0, keepdims=True) * valid
    out_ref[N_QTY:, :] = jnp.zeros((32 - N_QTY, chunk), jnp.float32)
    if from_cargo:
        _send_back(n_band, out_ref, recv_ref, ret_ref, send_sems, recv_sems, own_sem)


def _send_back(n_band, out_ref, recv_ref, ret_ref, send_sems, recv_sems, own_sem):
    chunk = out_ref.shape[1]
    peers = chunk // CAP
    total = recv_ref.shape[0]
    step = pl.program_id(0)
    last = pl.num_programs(0) - 1
    me = lax.axis_index("tile") * n_band + lax.axis_index("band")
    barrier = pltpu.get_barrier_semaphore()

    def device(p):
        return (p // n_band, p % n_band)

    def copy_to(p):
        return pltpu.make_async_remote_copy(
            src_ref=ret_ref.at[p],
            dst_ref=recv_ref.at[me],
            send_sem=send_sems.at[p],
            recv_sem=recv_sems.at[me],
            device_id=device(p),
            device_id_type=MESH,
        )

    def copy_from(p):
        return pltpu.make_async_remote_copy(
            src_ref=ret_ref.at[p],
            dst_ref=recv_ref.at[p],
            send_sem=send_sems.at[p],
            recv_sem=recv_sems.at[p],
            device_id=device(p),
            device_id_type=MESH,
        )

    own = pltpu.make_async_copy(ret_ref.at[me], recv_ref.at[me], own_sem)

    @pl.when(step == 0)
    def _():
        def greet(k, carry):
            p = lax.rem(me + k, total)
            pl.semaphore_signal(barrier, inc=1, device_id=device(p), device_id_type=MESH)
            return carry

        lax.fori_loop(1, total, greet, 0)

    padded = jnp.concatenate([out_ref[...], jnp.zeros((128 - 32, chunk), jnp.float32)], axis=0)
    ret_ref[pl.ds(pl.multiple_of(step * peers, peers), peers)] = padded.T.reshape(peers, CAP, 128)

    @pl.when(step == 0)
    def _():
        pl.semaphore_wait(barrier, total - 1)

    def start(q, carry):
        p = step * peers + q

        @pl.when(p != me)
        def _():
            copy_to(p).start()

        @pl.when(p == me)
        def _():
            own.start()

        return carry

    lax.fori_loop(0, peers, start, 0)

    @pl.when(step == last)
    def _():
        def finish(k, carry):
            p = lax.rem(me + k, total)
            copy_to(p).wait_send()
            copy_from(p).wait_recv()
            return carry

        lax.fori_loop(1, total, finish, 0)
        own.wait()


def pair_sums(xa, tb, maps, aux, n_band=1, chunk=128):
    pairs = tb.shape[1]
    from_cargo = maps is None
    scratch = [
        pltpu.VMEM((3, 128, chunk), jnp.float32),
        pltpu.VMEM((6, 128, chunk), jnp.float32),
        pltpu.VMEM((4, chunk, 128), jnp.float32),
    ]
    out_shape = jax.ShapeDtypeStruct((32, pairs), jnp.float32)
    out_specs = pl.BlockSpec((32, chunk), lambda i: (0, i))
    params = None
    if from_cargo:
        xa = xa.reshape(-1, 128)
        xa_spec = pl.BlockSpec((chunk // CAP * (4 * CAP + 1), 128), lambda i: (i, 0))
        maps = aux
        map_spec = pl.BlockSpec((8, 128), lambda i: (0, 0))
        peers = pairs // CAP
        out_shape = (out_shape, jax.ShapeDtypeStruct((peers, CAP, 128), jnp.float32))
        out_specs = (out_specs, pl.BlockSpec(memory_space=pl.ANY))
        scratch += [
            pltpu.VMEM((peers, CAP, 128), jnp.float32),
            pltpu.SemaphoreType.DMA((peers,)),
            pltpu.SemaphoreType.DMA((peers,)),
            pltpu.SemaphoreType.DMA(()),
        ]
        params = pltpu.CompilerParams(collective_id=0, has_side_effects=True)
    else:
        xa_spec = pl.BlockSpec((3, chunk, 128), lambda i: (0, i, 0))
        map_spec = pl.BlockSpec((chunk, 128), lambda i: (i, 0))
    return pl.pallas_call(
        functools.partial(_terms_kernel, from_cargo, n_band),
        out_shape=out_shape,
        grid=(pairs // chunk,),
        in_specs=[
            xa_spec,
            pl.BlockSpec((6, chunk, 128), lambda i: (0, i, 0)),
            map_spec,
            pl.BlockSpec((32, chunk), lambda i: (0, i)),
        ],
        out_specs=out_specs,
        scratch_shapes=scratch,
        compiler_params=params,
    )(xa, tb, maps, aux)


def _cargo_kernel(xa_ref, map_ref, side_ref, out_ref):
    height = 4 * CAP + 1
    group = 8

    def body(g, carry):
        for q in range(group):
            p = g * group + q
            base = pl.multiple_of(g * (group * height), 8) + q * height
            slots = pl.ds(pl.multiple_of(p * CAP, CAP), CAP)
            for c in range(3):
                out_ref[pl.ds(base + c * CAP, CAP), :] = xa_ref[c, slots, :]
            out_ref[pl.ds(base + 3 * CAP, CAP), :] = map_ref[slots, :].astype(jnp.float32)
            out_ref[pl.ds(base + 4 * CAP, 1), :] = side_ref[pl.ds(p, 1), :]
        return carry

    lax.fori_loop(0, side_ref.shape[0] // group, body, 0)


def build_cargo(xa3, maps, side):
    slots = maps.shape[0]
    height = 4 * CAP + 1
    cargo = pl.pallas_call(
        _cargo_kernel,
        out_shape=jax.ShapeDtypeStruct((slots // CAP * height, 128), jnp.float32),
    )(xa3, maps, side)
    return cargo.reshape(slots // CAP, 1, height * 128)


def split_terms(out):
    sel = out[0:N_QTY].T
    ga = sel[:, 0:6] * (1.0 / 128)
    ha = sel[:, 6:18] * (1.0 / 4096)
    gb = -jnp.concatenate([sel[:, 18:21], sel[:, 3:6]], axis=1) * (1.0 / 128)
    hb0 = -jnp.concatenate([sel[:, 21:24], sel[:, 9:12]], axis=1) * (1.0 / 4096)
    hb1 = -jnp.concatenate([sel[:, 24:27], sel[:, 15:18]], axis=1) * (1.0 / 4096)
    return jnp.concatenate([ga, ha], axis=1), jnp.concatenate([gb, hb0, hb1], axis=1)


def _exchange_kernel(n_band, x_ref, out_ref, send_sems, recv_sems, own_sem):
    peers = x_ref.shape[0]
    me = lax.axis_index("tile") * n_band + lax.axis_index("band")

    def peer_of(k):
        p = lax.rem(me + k, peers)
        return p, (p // n_band, p % n_band)

    barrier = pltpu.get_barrier_semaphore()

    def greet(k, carry):
        _, dev = peer_of(k)
        pl.semaphore_signal(barrier, inc=1, device_id=dev, device_id_type=MESH)
        return carry

    lax.fori_loop(1, peers, greet, 0)
    pl.semaphore_wait(barrier, peers - 1)

    own = pltpu.make_async_copy(x_ref.at[me], out_ref.at[me], own_sem)
    own.start()

    def outgoing(k):
        p, dev = peer_of(k)
        return pltpu.make_async_remote_copy(
            src_ref=x_ref.at[p],
            dst_ref=out_ref.at[me],
            send_sem=send_sems.at[p],
            recv_sem=recv_sems.at[me],
            device_id=dev,
            device_id_type=MESH,
        )

    def incoming(k):
        p, dev = peer_of(k)
        return pltpu.make_async_remote_copy(
            src_ref=x_ref.at[p],
            dst_ref=out_ref.at[p],
            send_sem=send_sems.at[p],
            recv_sem=recv_sems.at[p],
            device_id=dev,
            device_id_type=MESH,
        )

    def start(k, carry):
        outgoing(k).start()
        return carry

    lax.fori_loop(1, peers, start, 0)

    def finish(k, carry):
        outgoing(k).wait_send()
        incoming(k).wait_recv()
        return carry

    lax.fori_loop(1, peers, finish, 0)
    own.wait()


def exchange(x, n_band, collective_id):
    peers = x.shape[0]
    return pl.pallas_call(
        functools.partial(_exchange_kernel, n_band),
        out_shape=jax.ShapeDtypeStruct(x.shape, x.dtype),
        in_specs=[pl.BlockSpec(memory_space=pl.ANY)],
        out_specs=pl.BlockSpec(memory_space=pl.ANY),
        scratch_shapes=[
            pltpu.SemaphoreType.DMA((peers,)),
            pltpu.SemaphoreType.DMA((peers,)),
            pltpu.SemaphoreType.DMA(()),
        ],
        compiler_params=pltpu.CompilerParams(collective_id=collective_id, has_side_effects=True),
    )(x)


def pick_rows(blocks, rows):
    onehot = (blocks[:, None] == jnp.arange(rows.shape[1], dtype=jnp.int32)[None, :]).astype(
        jnp.float32
    )
    return jnp.einsum("sb,cbk->csk", onehot, rows, precision=lax.Precision.HIGHEST)


def frag_sums(blocks, terms, frag_count):
    onehot = (blocks[:, None] // BF == jnp.arange(frag_count, dtype=jnp.int32)[None, :]).astype(
        jnp.float32
    )
    return jnp.dot(onehot.T, terms, precision=lax.Precision.HIGHEST)


def make_aux(dirs_a, dirs_b, valid):
    pairs = dirs_a.shape[0]
    return jnp.concatenate(
        [dirs_a.T, dirs_b.T, valid[None, :], jnp.zeros((32 - 25, pairs), jnp.float32)], axis=0
    )


def local(
    points,
    normals,
    poses,
    directions,
    local_pairs,
    local_maps,
    remote_src,
    remote_maps,
    remote_dst,
    counts,
):
    axes = ("tile", "band")
    n_band = lax.axis_size("band")
    frag_count = poses.shape[1]
    rows6 = to_world_rows(points, normals, poses, BF)
    frag_dirs = directions.reshape(12, frag_count).T
    peers = counts.shape[1]

    source_blocks = remote_src[0]
    valid = (
        (jnp.arange(CAP, dtype=jnp.int32)[None, :] < counts[0][:, None])
        .astype(jnp.float32)
        .reshape(-1)
    )
    frag_pick = (
        source_blocks[:, None] // BF == jnp.arange(frag_count, dtype=jnp.int32)[None, :]
    ).astype(jnp.float32)
    dirs_send = jnp.dot(frag_pick, frag_dirs, precision=lax.Precision.HIGHEST)
    side = jnp.concatenate([dirs_send, valid[:, None]], axis=1)
    side = side.reshape(peers, CAP * 13)
    side = jnp.concatenate([side, jnp.zeros((peers, 128 - CAP * 13), jnp.float32)], axis=1)
    cargo = build_cargo(pick_rows(source_blocks, rows6[0:3]), remote_maps[0], side)
    arrived = lax.all_to_all(cargo, axes, split_axis=0, concat_axis=0, tiled=True)

    src_l = local_pairs[0]
    tgt_l = local_pairs[1]
    ones = jnp.ones((src_l.shape[0],), jnp.float32)
    out_l = pair_sums(
        pick_rows(src_l, rows6[0:3]),
        pick_rows(tgt_l, rows6),
        local_maps,
        make_aux(frag_dirs[src_l // BF], frag_dirs[tgt_l // BF], ones),
    )
    local_a, local_b = split_terms(out_l)

    target_blocks = remote_dst[0]
    side_in = arrived[:, 0, CAP * 4 * 128 : CAP * 4 * 128 + CAP * 13].reshape(peers * CAP, 13)
    out_r, back = pair_sums(
        arrived,
        pick_rows(target_blocks, rows6),
        None,
        make_aux(side_in[:, 0:12], frag_dirs[target_blocks // BF], side_in[:, 12]),
        n_band,
    )
    unused, remote_b = split_terms(out_r)
    returned, unused = split_terms(back.reshape(peers * CAP, 128)[:, 0:32].T)

    totals = frag_sums(src_l, local_a, frag_count) + frag_sums(tgt_l, local_b, frag_count)
    totals = (
        totals
        + frag_sums(target_blocks, remote_b, frag_count)
        + frag_sums(source_blocks, returned, frag_count)
    )
    gradient = totals[:, 0:6].T
    hess_products = totals[:, 6:18].T.reshape(2, 6, frag_count)
    return (gradient, hess_products)


def solution(mesh):
    placed = (
        P(("tile", "band"), None, None),
        P(("tile", "band"), None, None),
        P(None, ("tile", "band")),
        P(None, None, ("tile", "band")),
        P(None, ("tile", "band")),
        P(("tile", "band"), None),
        P(("tile", "band"), None),
        P(("tile", "band"), None, None),
        P(("tile", "band"), None),
        P(("tile", "band"), None),
    )
    return jax.shard_map(
        local,
        mesh=mesh,
        in_specs=placed,
        out_specs=(P(None, ("tile", "band")), P(None, None, ("tile", "band"))),
        check_vma=False,
    )
```

```python
import functools

import jax
import jax.numpy as jnp
from jax import lax
from jax.experimental import pallas as pl
from jax.experimental.pallas import tpu as pltpu
from jax.sharding import PartitionSpec as P

BF = 32
CAP = 8
N_QTY = 27
MESH = pl.DeviceIdType.MESH


def rotations(poses):
    half_angle = poses[0:3] * 0.5
    inverse = 1.0 / jnp.sqrt(
        1.0
        + half_angle[0] * half_angle[0]
        + half_angle[1] * half_angle[1]
        + half_angle[2] * half_angle[2]
    )
    quat_x = half_angle[0] * inverse
    quat_y = half_angle[1] * inverse
    quat_z = half_angle[2] * inverse
    rotation = [
        [
            1.0 - 2.0 * (quat_y * quat_y + quat_z * quat_z),
            2.0 * (quat_x * quat_y - inverse * quat_z),
            2.0 * (quat_x * quat_z + inverse * quat_y),
        ],
        [
            2.0 * (quat_x * quat_y + inverse * quat_z),
            1.0 - 2.0 * (quat_x * quat_x + quat_z * quat_z),
            2.0 * (quat_y * quat_z - inverse * quat_x),
        ],
        [
            2.0 * (quat_x * quat_z - inverse * quat_y),
            2.0 * (quat_y * quat_z + inverse * quat_x),
            1.0 - 2.0 * (quat_x * quat_x + quat_y * quat_y),
        ],
    ]
    return (rotation, poses[3:6])


def to_world_rows(points, normals, poses, per_pose):
    rotation, translation = rotations(poses)

    def spread(values):
        return jnp.repeat(values, per_pose)[:, None]

    world_rows = []
    normal_rows = []
    for i in range(3):
        coeffs = [spread(rotation[i][j]) for j in range(3)]
        world_rows.append(
            coeffs[0] * points[:, 0]
            + coeffs[1] * points[:, 1]
            + coeffs[2] * points[:, 2]
            + spread(translation[i])
        )
        normal_rows.append(
            coeffs[0] * normals[:, 0] + coeffs[1] * normals[:, 1] + coeffs[2] * normals[:, 2]
        )
    return jnp.stack(world_rows + normal_rows, axis=0)


def _terms_kernel(from_cargo, n_band, xa_ref, tb_ref, map_ref, aux_ref, out_ref, *rest):
    if from_cargo:
        recv_ref, xt_ref, gt_ref, cs_ref, ret_ref, send_sems, recv_sems, own_sem = rest
    else:
        xt_ref, gt_ref, cs_ref = rest
    chunk = out_ref.shape[1]
    if from_cargo:
        peers = chunk // CAP
        height = 4 * CAP + 1
        for p in range(peers):
            for r in range(4):
                cs_ref[r, pl.ds(p * CAP, CAP), :] = xa_ref[pl.ds(p * height + r * CAP, CAP), :]
        idx = cs_ref[3].astype(jnp.int32)
        for c in range(3):
            xt_ref[c] = cs_ref[c].T
    else:
        idx = map_ref[...]
        for c in range(3):
            xt_ref[c] = xa_ref[c].T
    for c in range(6):
        picked = jnp.take_along_axis(tb_ref[c], idx, axis=1, mode="promise_in_bounds")
        gt_ref[c] = picked.T

    def col(q):
        return jnp.broadcast_to(aux_ref[q : q + 1, :], (8, chunk))

    def body(s, accs):
        rows = pl.ds(pl.multiple_of(s * 8, 8), 8)
        xa = [xt_ref[c, rows, :] for c in range(3)]
        xb = [gt_ref[c, rows, :] for c in range(3)]
        nb = [gt_ref[3 + c, rows, :] for c in range(3)]
        off = [xa[c] - xb[c] for c in range(3)]
        res = nb[0] * off[0] + nb[1] * off[1] + nb[2] * off[2]
        ja = [
            xa[1] * nb[2] - xa[2] * nb[1],
            xa[2] * nb[0] - xa[0] * nb[2],
            xa[0] * nb[1] - xa[1] * nb[0],
            nb[0],
            nb[1],
            nb[2],
        ]
        kb = [
            xb[1] * nb[2] - xb[2] * nb[1],
            xb[2] * nb[0] - xb[0] * nb[2],
            xb[0] * nb[1] - xb[1] * nb[0],
            nb[0],
            nb[1],
            nb[2],
        ]
        weights = [res]
        for v in range(2):
            sa = ja[0] * col(6 * v)
            sb = kb[0] * col(12 + 6 * v)
            for c in range(1, 6):
                sa = sa + ja[c] * col(6 * v + c)
                sb = sb + kb[c] * col(12 + 6 * v + c)
            weights.append(sa - sb)
        vals = []
        for w in weights:
            vals.extend([w * ja[c] for c in range(6)])
        for w in weights:
            vals.extend([w * kb[c] for c in range(3)])
        return tuple(a + v for a, v in zip(accs, vals))

    zero = jnp.zeros((8, chunk), jnp.float32)
    accs = lax.fori_loop(0, 128 // 8, body, (zero,) * N_QTY, unroll=8)
    valid = aux_ref[24:25, :]
    for q in range(N_QTY):
        out_ref[q : q + 1, :] = jnp.sum(accs[q], axis=0, keepdims=True) * valid
    out_ref[N_QTY:, :] = jnp.zeros((32 - N_QTY, chunk), jnp.float32)
    if from_cargo:
        _send_back(n_band, out_ref, recv_ref, ret_ref, send_sems, recv_sems, own_sem)


def _first_chunk(n_band, chunks):
    me = lax.axis_index("tile") * n_band + lax.axis_index("band")
    return lax.rem(me, chunks)


def _send_back(n_band, out_ref, recv_ref, ret_ref, send_sems, recv_sems, own_sem):
    chunk = out_ref.shape[1]
    peers = chunk // CAP
    total = recv_ref.shape[0]
    step = pl.program_id(0)
    last = pl.num_programs(0) - 1
    me = lax.axis_index("tile") * n_band + lax.axis_index("band")
    barrier = pltpu.get_barrier_semaphore()

    def device(p):
        return (p // n_band, p % n_band)

    def copy_to(p):
        return pltpu.make_async_remote_copy(
            src_ref=ret_ref.at[p],
            dst_ref=recv_ref.at[me],
            send_sem=send_sems.at[p],
            recv_sem=recv_sems.at[me],
            device_id=device(p),
            device_id_type=MESH,
        )

    def copy_from(p):
        return pltpu.make_async_remote_copy(
            src_ref=ret_ref.at[p],
            dst_ref=recv_ref.at[p],
            send_sem=send_sems.at[p],
            recv_sem=recv_sems.at[p],
            device_id=device(p),
            device_id_type=MESH,
        )

    own = pltpu.make_async_copy(ret_ref.at[me], recv_ref.at[me], own_sem)

    @pl.when(step == 0)
    def _():
        def greet(k, carry):
            p = lax.rem(me + k, total)
            pl.semaphore_signal(barrier, inc=1, device_id=device(p), device_id_type=MESH)
            return carry

        lax.fori_loop(1, total, greet, 0)

    padded = jnp.concatenate([out_ref[...], jnp.zeros((128 - 32, chunk), jnp.float32)], axis=0)
    first = _first_chunk(n_band, pl.num_programs(0))
    part = lax.rem(step + first, pl.num_programs(0))
    ret_ref[pl.ds(pl.multiple_of(part * peers, peers), peers)] = padded.T.reshape(peers, CAP, 128)

    @pl.when(step == 0)
    def _():
        pl.semaphore_wait(barrier, total - 1)

    def start(q, carry):
        p = part * peers + q

        @pl.when(p != me)
        def _():
            copy_to(p).start()

        @pl.when(p == me)
        def _():
            own.start()

        return carry

    lax.fori_loop(0, peers, start, 0)

    @pl.when(step == last)
    def _():
        def finish(k, carry):
            p = lax.rem(me + k, total)
            copy_to(p).wait_send()
            copy_from(p).wait_recv()
            return carry

        lax.fori_loop(1, total, finish, 0)
        own.wait()


def pair_sums(xa, tb, maps, aux, n_band=1, chunk=128):
    pairs = tb.shape[1]
    from_cargo = maps is None
    scratch = [
        pltpu.VMEM((3, 128, chunk), jnp.float32),
        pltpu.VMEM((6, 128, chunk), jnp.float32),
        pltpu.VMEM((4, chunk, 128), jnp.float32),
    ]
    out_shape = jax.ShapeDtypeStruct((32, pairs), jnp.float32)
    out_specs = pl.BlockSpec((32, chunk), lambda i: (0, blk(i)))
    params = None
    chunks = pairs // chunk

    def blk(i):
        if from_cargo:
            return lax.rem(i + _first_chunk(n_band, chunks), chunks)
        return i

    if from_cargo:
        xa = xa.reshape(-1, 128)
        xa_spec = pl.BlockSpec((chunk // CAP * (4 * CAP + 1), 128), lambda i: (blk(i), 0))
        maps = aux
        map_spec = pl.BlockSpec((8, 128), lambda i: (0, 0))
        peers = pairs // CAP
        out_shape = (out_shape, jax.ShapeDtypeStruct((peers, CAP, 128), jnp.float32))
        out_specs = (out_specs, pl.BlockSpec(memory_space=pl.ANY))
        scratch += [
            pltpu.VMEM((peers, CAP, 128), jnp.float32),
            pltpu.SemaphoreType.DMA((peers,)),
            pltpu.SemaphoreType.DMA((peers,)),
            pltpu.SemaphoreType.DMA(()),
        ]
        params = pltpu.CompilerParams(collective_id=0, has_side_effects=True)
    else:
        xa_spec = pl.BlockSpec((3, chunk, 128), lambda i: (0, i, 0))
        map_spec = pl.BlockSpec((chunk, 128), lambda i: (i, 0))
    return pl.pallas_call(
        functools.partial(_terms_kernel, from_cargo, n_band),
        out_shape=out_shape,
        grid=(pairs // chunk,),
        in_specs=[
            xa_spec,
            pl.BlockSpec((6, chunk, 128), lambda i: (0, blk(i), 0)),
            map_spec,
            pl.BlockSpec((32, chunk), lambda i: (0, blk(i))),
        ],
        out_specs=out_specs,
        scratch_shapes=scratch,
        compiler_params=params,
    )(xa, tb, maps, aux)


def _cargo_kernel(xa_ref, map_ref, side_ref, out_ref):
    height = 4 * CAP + 1
    group = 8

    def body(g, carry):
        for q in range(group):
            p = g * group + q
            base = pl.multiple_of(g * (group * height), 8) + q * height
            slots = pl.ds(pl.multiple_of(p * CAP, CAP), CAP)
            for c in range(3):
                out_ref[pl.ds(base + c * CAP, CAP), :] = xa_ref[c, slots, :]
            out_ref[pl.ds(base + 3 * CAP, CAP), :] = map_ref[slots, :].astype(jnp.float32)
            out_ref[pl.ds(base + 4 * CAP, 1), :] = side_ref[pl.ds(p, 1), :]
        return carry

    lax.fori_loop(0, side_ref.shape[0] // group, body, 0)


def build_cargo(xa3, maps, side):
    slots = maps.shape[0]
    height = 4 * CAP + 1
    cargo = pl.pallas_call(
        _cargo_kernel,
        out_shape=jax.ShapeDtypeStruct((slots // CAP * height, 128), jnp.float32),
    )(xa3, maps, side)
    return cargo.reshape(slots // CAP, 1, height * 128)


def split_terms(out):
    sel = out[0:N_QTY].T
    ga = sel[:, 0:6] * (1.0 / 128)
    ha = sel[:, 6:18] * (1.0 / 4096)
    gb = -jnp.concatenate([sel[:, 18:21], sel[:, 3:6]], axis=1) * (1.0 / 128)
    hb0 = -jnp.concatenate([sel[:, 21:24], sel[:, 9:12]], axis=1) * (1.0 / 4096)
    hb1 = -jnp.concatenate([sel[:, 24:27], sel[:, 15:18]], axis=1) * (1.0 / 4096)
    return jnp.concatenate([ga, ha], axis=1), jnp.concatenate([gb, hb0, hb1], axis=1)


def _exchange_kernel(n_band, x_ref, out_ref, send_sems, recv_sems, own_sem):
    peers = x_ref.shape[0]
    me = lax.axis_index("tile") * n_band + lax.axis_index("band")

    def peer_of(k):
        p = lax.rem(me + k, peers)
        return p, (p // n_band, p % n_band)

    barrier = pltpu.get_barrier_semaphore()

    def greet(k, carry):
        _, dev = peer_of(k)
        pl.semaphore_signal(barrier, inc=1, device_id=dev, device_id_type=MESH)
        return carry

    lax.fori_loop(1, peers, greet, 0)
    pl.semaphore_wait(barrier, peers - 1)

    own = pltpu.make_async_copy(x_ref.at[me], out_ref.at[me], own_sem)
    own.start()

    def outgoing(k):
        p, dev = peer_of(k)
        return pltpu.make_async_remote_copy(
            src_ref=x_ref.at[p],
            dst_ref=out_ref.at[me],
            send_sem=send_sems.at[p],
            recv_sem=recv_sems.at[me],
            device_id=dev,
            device_id_type=MESH,
        )

    def incoming(k):
        p, dev = peer_of(k)
        return pltpu.make_async_remote_copy(
            src_ref=x_ref.at[p],
            dst_ref=out_ref.at[p],
            send_sem=send_sems.at[p],
            recv_sem=recv_sems.at[p],
            device_id=dev,
            device_id_type=MESH,
        )

    def start(k, carry):
        outgoing(k).start()
        return carry

    lax.fori_loop(1, peers, start, 0)

    def finish(k, carry):
        outgoing(k).wait_send()
        incoming(k).wait_recv()
        return carry

    lax.fori_loop(1, peers, finish, 0)
    own.wait()


def exchange(x, n_band, collective_id):
    peers = x.shape[0]
    return pl.pallas_call(
        functools.partial(_exchange_kernel, n_band),
        out_shape=jax.ShapeDtypeStruct(x.shape, x.dtype),
        in_specs=[pl.BlockSpec(memory_space=pl.ANY)],
        out_specs=pl.BlockSpec(memory_space=pl.ANY),
        scratch_shapes=[
            pltpu.SemaphoreType.DMA((peers,)),
            pltpu.SemaphoreType.DMA((peers,)),
            pltpu.SemaphoreType.DMA(()),
        ],
        compiler_params=pltpu.CompilerParams(collective_id=collective_id, has_side_effects=True),
    )(x)


def pick_rows(blocks, rows):
    onehot = (blocks[:, None] == jnp.arange(rows.shape[1], dtype=jnp.int32)[None, :]).astype(
        jnp.float32
    )
    return jnp.einsum("sb,cbk->csk", onehot, rows, precision=lax.Precision.HIGHEST)


def frag_sums(blocks, terms, frag_count):
    onehot = (blocks[:, None] // BF == jnp.arange(frag_count, dtype=jnp.int32)[None, :]).astype(
        jnp.float32
    )
    return jnp.dot(onehot.T, terms, precision=lax.Precision.HIGHEST)


def make_aux(dirs_a, dirs_b, valid):
    pairs = dirs_a.shape[0]
    return jnp.concatenate(
        [dirs_a.T, dirs_b.T, valid[None, :], jnp.zeros((32 - 25, pairs), jnp.float32)], axis=0
    )


def local(
    points,
    normals,
    poses,
    directions,
    local_pairs,
    local_maps,
    remote_src,
    remote_maps,
    remote_dst,
    counts,
):
    axes = ("tile", "band")
    n_band = lax.axis_size("band")
    frag_count = poses.shape[1]
    rows6 = to_world_rows(points, normals, poses, BF)
    frag_dirs = directions.reshape(12, frag_count).T
    peers = counts.shape[1]

    source_blocks = remote_src[0]
    valid = (
        (jnp.arange(CAP, dtype=jnp.int32)[None, :] < counts[0][:, None])
        .astype(jnp.float32)
        .reshape(-1)
    )
    frag_pick = (
        source_blocks[:, None] // BF == jnp.arange(frag_count, dtype=jnp.int32)[None, :]
    ).astype(jnp.float32)
    dirs_send = jnp.dot(frag_pick, frag_dirs, precision=lax.Precision.HIGHEST)
    side = jnp.concatenate([dirs_send, valid[:, None]], axis=1)
    side = side.reshape(peers, CAP * 13)
    side = jnp.concatenate([side, jnp.zeros((peers, 128 - CAP * 13), jnp.float32)], axis=1)
    cargo = build_cargo(pick_rows(source_blocks, rows6[0:3]), remote_maps[0], side)
    arrived = lax.all_to_all(cargo, axes, split_axis=0, concat_axis=0, tiled=True)

    src_l = local_pairs[0]
    tgt_l = local_pairs[1]
    ones = jnp.ones((src_l.shape[0],), jnp.float32)
    out_l = pair_sums(
        pick_rows(src_l, rows6[0:3]),
        pick_rows(tgt_l, rows6),
        local_maps,
        make_aux(frag_dirs[src_l // BF], frag_dirs[tgt_l // BF], ones),
    )
    local_a, local_b = split_terms(out_l)

    target_blocks = remote_dst[0]
    side_in = arrived[:, 0, CAP * 4 * 128 : CAP * 4 * 128 + CAP * 13].reshape(peers * CAP, 13)
    out_r, back = pair_sums(
        arrived,
        pick_rows(target_blocks, rows6),
        None,
        make_aux(side_in[:, 0:12], frag_dirs[target_blocks // BF], side_in[:, 12]),
        n_band,
    )
    unused, remote_b = split_terms(out_r)
    returned, unused = split_terms(back.reshape(peers * CAP, 128)[:, 0:32].T)

    totals = frag_sums(src_l, local_a, frag_count) + frag_sums(tgt_l, local_b, frag_count)
    totals = (
        totals
        + frag_sums(target_blocks, remote_b, frag_count)
        + frag_sums(source_blocks, returned, frag_count)
    )
    gradient = totals[:, 0:6].T
    hess_products = totals[:, 6:18].T.reshape(2, 6, frag_count)
    return (gradient, hess_products)


def solution(mesh):
    placed = (
        P(("tile", "band"), None, None),
        P(("tile", "band"), None, None),
        P(None, ("tile", "band")),
        P(None, None, ("tile", "band")),
        P(None, ("tile", "band")),
        P(("tile", "band"), None),
        P(("tile", "band"), None),
        P(("tile", "band"), None, None),
        P(("tile", "band"), None),
        P(("tile", "band"), None),
    )
    return jax.shard_map(
        local,
        mesh=mesh,
        in_specs=placed,
        out_specs=(P(None, ("tile", "band")), P(None, None, ("tile", "band"))),
        check_vma=False,
    )
```

```python
import functools

import jax
import jax.numpy as jnp
from jax import lax
from jax.experimental import pallas as pl
from jax.experimental.pallas import tpu as pltpu
from jax.sharding import PartitionSpec as P

BF = 32
CAP = 8
N_QTY = 27
MESH = pl.DeviceIdType.MESH


def rotations(poses):
    half_angle = poses[0:3] * 0.5
    inverse = 1.0 / jnp.sqrt(
        1.0
        + half_angle[0] * half_angle[0]
        + half_angle[1] * half_angle[1]
        + half_angle[2] * half_angle[2]
    )
    quat_x = half_angle[0] * inverse
    quat_y = half_angle[1] * inverse
    quat_z = half_angle[2] * inverse
    rotation = [
        [
            1.0 - 2.0 * (quat_y * quat_y + quat_z * quat_z),
            2.0 * (quat_x * quat_y - inverse * quat_z),
            2.0 * (quat_x * quat_z + inverse * quat_y),
        ],
        [
            2.0 * (quat_x * quat_y + inverse * quat_z),
            1.0 - 2.0 * (quat_x * quat_x + quat_z * quat_z),
            2.0 * (quat_y * quat_z - inverse * quat_x),
        ],
        [
            2.0 * (quat_x * quat_z - inverse * quat_y),
            2.0 * (quat_y * quat_z + inverse * quat_x),
            1.0 - 2.0 * (quat_x * quat_x + quat_y * quat_y),
        ],
    ]
    return (rotation, poses[3:6])


def to_world_rows(points, normals, poses, per_pose):
    rotation, translation = rotations(poses)

    def spread(values):
        return jnp.repeat(values, per_pose)[:, None]

    world_rows = []
    normal_rows = []
    for i in range(3):
        coeffs = [spread(rotation[i][j]) for j in range(3)]
        world_rows.append(
            coeffs[0] * points[:, 0]
            + coeffs[1] * points[:, 1]
            + coeffs[2] * points[:, 2]
            + spread(translation[i])
        )
        normal_rows.append(
            coeffs[0] * normals[:, 0] + coeffs[1] * normals[:, 1] + coeffs[2] * normals[:, 2]
        )
    return jnp.stack(world_rows + normal_rows, axis=0)


def _terms_kernel(from_cargo, n_band, xa_ref, tb_ref, map_ref, aux_ref, out_ref, *rest):
    if from_cargo:
        recv_ref, xt_ref, gt_ref, cs_ref, ret_ref, send_sems, recv_sems, own_sem = rest
    else:
        xt_ref, gt_ref, cs_ref = rest
    chunk = out_ref.shape[1]
    if from_cargo:
        peers = chunk // CAP
        height = 4 * CAP + 1
        for p in range(peers):
            for r in range(4):
                cs_ref[r, pl.ds(p * CAP, CAP), :] = xa_ref[pl.ds(p * height + r * CAP, CAP), :]
        idx = cs_ref[3].astype(jnp.int32)
        for c in range(3):
            xt_ref[c] = cs_ref[c].T
    else:
        idx = map_ref[...]
        for c in range(3):
            xt_ref[c] = xa_ref[c].T
    for c in range(6):
        picked = jnp.take_along_axis(tb_ref[c], idx, axis=1, mode="promise_in_bounds")
        gt_ref[c] = picked.T

    def col(q):
        return jnp.broadcast_to(aux_ref[q : q + 1, :], (8, chunk))

    def body(s, accs):
        rows = pl.ds(pl.multiple_of(s * 8, 8), 8)
        xa = [xt_ref[c, rows, :] for c in range(3)]
        xb = [gt_ref[c, rows, :] for c in range(3)]
        nb = [gt_ref[3 + c, rows, :] for c in range(3)]
        off = [xa[c] - xb[c] for c in range(3)]
        res = nb[0] * off[0] + nb[1] * off[1] + nb[2] * off[2]
        ja = [
            xa[1] * nb[2] - xa[2] * nb[1],
            xa[2] * nb[0] - xa[0] * nb[2],
            xa[0] * nb[1] - xa[1] * nb[0],
            nb[0],
            nb[1],
            nb[2],
        ]
        kb = [
            xb[1] * nb[2] - xb[2] * nb[1],
            xb[2] * nb[0] - xb[0] * nb[2],
            xb[0] * nb[1] - xb[1] * nb[0],
            nb[0],
            nb[1],
            nb[2],
        ]
        weights = [res]
        for v in range(2):
            sa = ja[0] * col(6 * v)
            sb = kb[0] * col(12 + 6 * v)
            for c in range(1, 6):
                sa = sa + ja[c] * col(6 * v + c)
                sb = sb + kb[c] * col(12 + 6 * v + c)
            weights.append(sa - sb)
        vals = []
        for w in weights:
            vals.extend([w * ja[c] for c in range(6)])
        for w in weights:
            vals.extend([w * kb[c] for c in range(3)])
        return tuple(a + v for a, v in zip(accs, vals))

    zero = jnp.zeros((8, chunk), jnp.float32)
    accs = lax.fori_loop(0, 128 // 8, body, (zero,) * N_QTY, unroll=8)
    valid = aux_ref[24:25, :]
    for q in range(N_QTY):
        out_ref[q : q + 1, :] = jnp.sum(accs[q], axis=0, keepdims=True) * valid
    out_ref[N_QTY:, :] = jnp.zeros((32 - N_QTY, chunk), jnp.float32)
    if from_cargo:
        _send_back(n_band, out_ref, recv_ref, ret_ref, send_sems, recv_sems, own_sem)


def _send_back(n_band, out_ref, recv_ref, ret_ref, send_sems, recv_sems, own_sem):
    chunk = out_ref.shape[1]
    peers = chunk // CAP
    total = recv_ref.shape[0]
    step = pl.program_id(0)
    last = pl.num_programs(0) - 1
    me = lax.axis_index("tile") * n_band + lax.axis_index("band")
    barrier = pltpu.get_barrier_semaphore()

    def device(p):
        return (p // n_band, p % n_band)

    def copy_to(p):
        return pltpu.make_async_remote_copy(
            src_ref=ret_ref.at[p],
            dst_ref=recv_ref.at[me],
            send_sem=send_sems.at[p],
            recv_sem=recv_sems.at[me],
            device_id=device(p),
            device_id_type=MESH,
        )

    def copy_from(p):
        return pltpu.make_async_remote_copy(
            src_ref=ret_ref.at[p],
            dst_ref=recv_ref.at[p],
            send_sem=send_sems.at[p],
            recv_sem=recv_sems.at[p],
            device_id=device(p),
            device_id_type=MESH,
        )

    own = pltpu.make_async_copy(ret_ref.at[me], recv_ref.at[me], own_sem)

    @pl.when(step == 0)
    def _():
        def greet(k, carry):
            p = lax.rem(me + k, total)
            pl.semaphore_signal(barrier, inc=1, device_id=device(p), device_id_type=MESH)
            return carry

        lax.fori_loop(1, total, greet, 0)

    padded = jnp.concatenate([out_ref[...], jnp.zeros((128 - 32, chunk), jnp.float32)], axis=0)
    ret_ref[pl.ds(pl.multiple_of(step * peers, peers), peers)] = padded.T.reshape(peers, CAP, 128)

    hold = jnp.minimum(2, last)

    @pl.when(step == hold)
    def _():
        pl.semaphore_wait(barrier, total - 1)

    def start(q, carry):
        p = q

        @pl.when(p != me)
        def _():
            copy_to(p).start()

        @pl.when(p == me)
        def _():
            own.start()

        return carry

    @pl.when(step == hold)
    def _():
        lax.fori_loop(0, (hold + 1) * peers, start, 0)

    @pl.when(step > hold)
    def _():
        lax.fori_loop(step * peers, (step + 1) * peers, start, 0)

    @pl.when(step == last)
    def _():
        def finish(k, carry):
            p = lax.rem(me + k, total)
            copy_to(p).wait_send()
            copy_from(p).wait_recv()
            return carry

        lax.fori_loop(1, total, finish, 0)
        own.wait()


def pair_sums(xa, tb, maps, aux, n_band=1, chunk=128):
    pairs = tb.shape[1]
    from_cargo = maps is None
    scratch = [
        pltpu.VMEM((3, 128, chunk), jnp.float32),
        pltpu.VMEM((6, 128, chunk), jnp.float32),
        pltpu.VMEM((4, chunk, 128), jnp.float32),
    ]
    out_shape = jax.ShapeDtypeStruct((32, pairs), jnp.float32)
    out_specs = pl.BlockSpec((32, chunk), lambda i: (0, i))
    params = None
    if from_cargo:
        xa = xa.reshape(-1, 128)
        xa_spec = pl.BlockSpec((chunk // CAP * (4 * CAP + 1), 128), lambda i: (i, 0))
        maps = aux
        map_spec = pl.BlockSpec((8, 128), lambda i: (0, 0))
        peers = pairs // CAP
        out_shape = (out_shape, jax.ShapeDtypeStruct((peers, CAP, 128), jnp.float32))
        out_specs = (out_specs, pl.BlockSpec(memory_space=pl.ANY))
        scratch += [
            pltpu.VMEM((peers, CAP, 128), jnp.float32),
            pltpu.SemaphoreType.DMA((peers,)),
            pltpu.SemaphoreType.DMA((peers,)),
            pltpu.SemaphoreType.DMA(()),
        ]
        params = pltpu.CompilerParams(collective_id=0, has_side_effects=True)
    else:
        xa_spec = pl.BlockSpec((3, chunk, 128), lambda i: (0, i, 0))
        map_spec = pl.BlockSpec((chunk, 128), lambda i: (i, 0))
    return pl.pallas_call(
        functools.partial(_terms_kernel, from_cargo, n_band),
        out_shape=out_shape,
        grid=(pairs // chunk,),
        in_specs=[
            xa_spec,
            pl.BlockSpec((6, chunk, 128), lambda i: (0, i, 0)),
            map_spec,
            pl.BlockSpec((32, chunk), lambda i: (0, i)),
        ],
        out_specs=out_specs,
        scratch_shapes=scratch,
        compiler_params=params,
    )(xa, tb, maps, aux)


def _cargo_kernel(xa_ref, map_ref, side_ref, out_ref):
    height = 4 * CAP + 1
    group = 8

    def body(g, carry):
        for q in range(group):
            p = g * group + q
            base = pl.multiple_of(g * (group * height), 8) + q * height
            slots = pl.ds(pl.multiple_of(p * CAP, CAP), CAP)
            for c in range(3):
                out_ref[pl.ds(base + c * CAP, CAP), :] = xa_ref[c, slots, :]
            out_ref[pl.ds(base + 3 * CAP, CAP), :] = map_ref[slots, :].astype(jnp.float32)
            out_ref[pl.ds(base + 4 * CAP, 1), :] = side_ref[pl.ds(p, 1), :]
        return carry

    lax.fori_loop(0, side_ref.shape[0] // group, body, 0)


def build_cargo(xa3, maps, side):
    slots = maps.shape[0]
    height = 4 * CAP + 1
    cargo = pl.pallas_call(
        _cargo_kernel,
        out_shape=jax.ShapeDtypeStruct((slots // CAP * height, 128), jnp.float32),
    )(xa3, maps, side)
    return cargo.reshape(slots // CAP, 1, height * 128)


def split_terms(out):
    sel = out[0:N_QTY].T
    ga = sel[:, 0:6] * (1.0 / 128)
    ha = sel[:, 6:18] * (1.0 / 4096)
    gb = -jnp.concatenate([sel[:, 18:21], sel[:, 3:6]], axis=1) * (1.0 / 128)
    hb0 = -jnp.concatenate([sel[:, 21:24], sel[:, 9:12]], axis=1) * (1.0 / 4096)
    hb1 = -jnp.concatenate([sel[:, 24:27], sel[:, 15:18]], axis=1) * (1.0 / 4096)
    return jnp.concatenate([ga, ha], axis=1), jnp.concatenate([gb, hb0, hb1], axis=1)


def _exchange_kernel(n_band, x_ref, out_ref, send_sems, recv_sems, own_sem):
    peers = x_ref.shape[0]
    me = lax.axis_index("tile") * n_band + lax.axis_index("band")

    def peer_of(k):
        p = lax.rem(me + k, peers)
        return p, (p // n_band, p % n_band)

    barrier = pltpu.get_barrier_semaphore()

    def greet(k, carry):
        _, dev = peer_of(k)
        pl.semaphore_signal(barrier, inc=1, device_id=dev, device_id_type=MESH)
        return carry

    lax.fori_loop(1, peers, greet, 0)
    pl.semaphore_wait(barrier, peers - 1)

    own = pltpu.make_async_copy(x_ref.at[me], out_ref.at[me], own_sem)
    own.start()

    def outgoing(k):
        p, dev = peer_of(k)
        return pltpu.make_async_remote_copy(
            src_ref=x_ref.at[p],
            dst_ref=out_ref.at[me],
            send_sem=send_sems.at[p],
            recv_sem=recv_sems.at[me],
            device_id=dev,
            device_id_type=MESH,
        )

    def incoming(k):
        p, dev = peer_of(k)
        return pltpu.make_async_remote_copy(
            src_ref=x_ref.at[p],
            dst_ref=out_ref.at[p],
            send_sem=send_sems.at[p],
            recv_sem=recv_sems.at[p],
            device_id=dev,
            device_id_type=MESH,
        )

    def start(k, carry):
        outgoing(k).start()
        return carry

    lax.fori_loop(1, peers, start, 0)

    def finish(k, carry):
        outgoing(k).wait_send()
        incoming(k).wait_recv()
        return carry

    lax.fori_loop(1, peers, finish, 0)
    own.wait()


def exchange(x, n_band, collective_id):
    peers = x.shape[0]
    return pl.pallas_call(
        functools.partial(_exchange_kernel, n_band),
        out_shape=jax.ShapeDtypeStruct(x.shape, x.dtype),
        in_specs=[pl.BlockSpec(memory_space=pl.ANY)],
        out_specs=pl.BlockSpec(memory_space=pl.ANY),
        scratch_shapes=[
            pltpu.SemaphoreType.DMA((peers,)),
            pltpu.SemaphoreType.DMA((peers,)),
            pltpu.SemaphoreType.DMA(()),
        ],
        compiler_params=pltpu.CompilerParams(collective_id=collective_id, has_side_effects=True),
    )(x)


def pick_rows(blocks, rows):
    onehot = (blocks[:, None] == jnp.arange(rows.shape[1], dtype=jnp.int32)[None, :]).astype(
        jnp.float32
    )
    return jnp.einsum("sb,cbk->csk", onehot, rows, precision=lax.Precision.HIGHEST)


def frag_sums(blocks, terms, frag_count):
    onehot = (blocks[:, None] // BF == jnp.arange(frag_count, dtype=jnp.int32)[None, :]).astype(
        jnp.float32
    )
    return jnp.dot(onehot.T, terms, precision=lax.Precision.HIGHEST)


def make_aux(dirs_a, dirs_b, valid):
    pairs = dirs_a.shape[0]
    return jnp.concatenate(
        [dirs_a.T, dirs_b.T, valid[None, :], jnp.zeros((32 - 25, pairs), jnp.float32)], axis=0
    )


def local(
    points,
    normals,
    poses,
    directions,
    local_pairs,
    local_maps,
    remote_src,
    remote_maps,
    remote_dst,
    counts,
):
    axes = ("tile", "band")
    n_band = lax.axis_size("band")
    frag_count = poses.shape[1]
    rows6 = to_world_rows(points, normals, poses, BF)
    frag_dirs = directions.reshape(12, frag_count).T
    peers = counts.shape[1]

    source_blocks = remote_src[0]
    valid = (
        (jnp.arange(CAP, dtype=jnp.int32)[None, :] < counts[0][:, None])
        .astype(jnp.float32)
        .reshape(-1)
    )
    frag_pick = (
        source_blocks[:, None] // BF == jnp.arange(frag_count, dtype=jnp.int32)[None, :]
    ).astype(jnp.float32)
    dirs_send = jnp.dot(frag_pick, frag_dirs, precision=lax.Precision.HIGHEST)
    side = jnp.concatenate([dirs_send, valid[:, None]], axis=1)
    side = side.reshape(peers, CAP * 13)
    side = jnp.concatenate([side, jnp.zeros((peers, 128 - CAP * 13), jnp.float32)], axis=1)
    cargo = build_cargo(pick_rows(source_blocks, rows6[0:3]), remote_maps[0], side)
    arrived = lax.all_to_all(cargo, axes, split_axis=0, concat_axis=0, tiled=True)

    src_l = local_pairs[0]
    tgt_l = local_pairs[1]
    ones = jnp.ones((src_l.shape[0],), jnp.float32)
    out_l = pair_sums(
        pick_rows(src_l, rows6[0:3]),
        pick_rows(tgt_l, rows6),
        local_maps,
        make_aux(frag_dirs[src_l // BF], frag_dirs[tgt_l // BF], ones),
    )
    local_a, local_b = split_terms(out_l)

    target_blocks = remote_dst[0]
    side_in = arrived[:, 0, CAP * 4 * 128 : CAP * 4 * 128 + CAP * 13].reshape(peers * CAP, 13)
    out_r, back = pair_sums(
        arrived,
        pick_rows(target_blocks, rows6),
        None,
        make_aux(side_in[:, 0:12], frag_dirs[target_blocks // BF], side_in[:, 12]),
        n_band,
    )
    unused, remote_b = split_terms(out_r)
    returned, unused = split_terms(back.reshape(peers * CAP, 128)[:, 0:32].T)

    totals = frag_sums(src_l, local_a, frag_count) + frag_sums(tgt_l, local_b, frag_count)
    totals = (
        totals
        + frag_sums(target_blocks, remote_b, frag_count)
        + frag_sums(source_blocks, returned, frag_count)
    )
    gradient = totals[:, 0:6].T
    hess_products = totals[:, 6:18].T.reshape(2, 6, frag_count)
    return (gradient, hess_products)


def solution(mesh):
    placed = (
        P(("tile", "band"), None, None),
        P(("tile", "band"), None, None),
        P(None, ("tile", "band")),
        P(None, None, ("tile", "band")),
        P(None, ("tile", "band")),
        P(("tile", "band"), None),
        P(("tile", "band"), None),
        P(("tile", "band"), None, None),
        P(("tile", "band"), None),
        P(("tile", "band"), None),
    )
    return jax.shard_map(
        local,
        mesh=mesh,
        in_specs=placed,
        out_specs=(P(None, ("tile", "band")), P(None, None, ("tile", "band"))),
        check_vma=False,
    )
```

```python
import functools

import jax
import jax.numpy as jnp
from jax import lax
from jax.experimental import pallas as pl
from jax.experimental.pallas import tpu as pltpu
from jax.sharding import PartitionSpec as P

BF = 32
CAP = 8
N_QTY = 27
MESH = pl.DeviceIdType.MESH


def rotations(poses):
    half_angle = poses[0:3] * 0.5
    inverse = 1.0 / jnp.sqrt(
        1.0
        + half_angle[0] * half_angle[0]
        + half_angle[1] * half_angle[1]
        + half_angle[2] * half_angle[2]
    )
    quat_x = half_angle[0] * inverse
    quat_y = half_angle[1] * inverse
    quat_z = half_angle[2] * inverse
    rotation = [
        [
            1.0 - 2.0 * (quat_y * quat_y + quat_z * quat_z),
            2.0 * (quat_x * quat_y - inverse * quat_z),
            2.0 * (quat_x * quat_z + inverse * quat_y),
        ],
        [
            2.0 * (quat_x * quat_y + inverse * quat_z),
            1.0 - 2.0 * (quat_x * quat_x + quat_z * quat_z),
            2.0 * (quat_y * quat_z - inverse * quat_x),
        ],
        [
            2.0 * (quat_x * quat_z - inverse * quat_y),
            2.0 * (quat_y * quat_z + inverse * quat_x),
            1.0 - 2.0 * (quat_x * quat_x + quat_y * quat_y),
        ],
    ]
    return (rotation, poses[3:6])


def to_world_rows(points, normals, poses, per_pose):
    rotation, translation = rotations(poses)

    def spread(values):
        return jnp.repeat(values, per_pose)[:, None]

    world_rows = []
    normal_rows = []
    for i in range(3):
        coeffs = [spread(rotation[i][j]) for j in range(3)]
        world_rows.append(
            coeffs[0] * points[:, 0]
            + coeffs[1] * points[:, 1]
            + coeffs[2] * points[:, 2]
            + spread(translation[i])
        )
        normal_rows.append(
            coeffs[0] * normals[:, 0] + coeffs[1] * normals[:, 1] + coeffs[2] * normals[:, 2]
        )
    return jnp.stack(world_rows + normal_rows, axis=0)


def _terms_kernel(from_cargo, n_band, xa_ref, tb_ref, map_ref, aux_ref, out_ref, *rest):
    if from_cargo:
        recv_ref, xt_ref, gt_ref, cs_ref, ret_ref, send_sems, recv_sems, own_sem = rest
    else:
        xt_ref, gt_ref, cs_ref = rest
    chunk = out_ref.shape[1]
    if from_cargo:
        peers = chunk // CAP
        height = 4 * CAP + 1
        for p in range(peers):
            for r in range(4):
                cs_ref[r, pl.ds(p * CAP, CAP), :] = xa_ref[pl.ds(p * height + r * CAP, CAP), :]
        idx = cs_ref[3].astype(jnp.int32)
        for c in range(3):
            xt_ref[c] = cs_ref[c].T
    else:
        idx = map_ref[...]
        for c in range(3):
            xt_ref[c] = xa_ref[c].T
    for c in range(6):
        picked = jnp.take_along_axis(tb_ref[c], idx, axis=1, mode="promise_in_bounds")
        gt_ref[c] = picked.T

    def col(q):
        return jnp.broadcast_to(aux_ref[q : q + 1, :], (8, chunk))

    def body(s, accs):
        rows = pl.ds(pl.multiple_of(s * 8, 8), 8)
        xa = [xt_ref[c, rows, :] for c in range(3)]
        xb = [gt_ref[c, rows, :] for c in range(3)]
        nb = [gt_ref[3 + c, rows, :] for c in range(3)]
        off = [xa[c] - xb[c] for c in range(3)]
        res = nb[0] * off[0] + nb[1] * off[1] + nb[2] * off[2]
        ja = [
            xa[1] * nb[2] - xa[2] * nb[1],
            xa[2] * nb[0] - xa[0] * nb[2],
            xa[0] * nb[1] - xa[1] * nb[0],
            nb[0],
            nb[1],
            nb[2],
        ]
        kb = [
            xb[1] * nb[2] - xb[2] * nb[1],
            xb[2] * nb[0] - xb[0] * nb[2],
            xb[0] * nb[1] - xb[1] * nb[0],
            nb[0],
            nb[1],
            nb[2],
        ]
        weights = [res]
        for v in range(2):
            sa = ja[0] * col(6 * v)
            sb = kb[0] * col(12 + 6 * v)
            for c in range(1, 6):
                sa = sa + ja[c] * col(6 * v + c)
                sb = sb + kb[c] * col(12 + 6 * v + c)
            weights.append(sa - sb)
        vals = []
        for w in weights:
            vals.extend([w * ja[c] for c in range(6)])
        for w in weights:
            vals.extend([w * kb[c] for c in range(3)])
        return tuple(a + v for a, v in zip(accs, vals))

    zero = jnp.zeros((8, chunk), jnp.float32)
    accs = lax.fori_loop(0, 128 // 8, body, (zero,) * N_QTY, unroll=8)
    valid = aux_ref[24:25, :]
    for q in range(N_QTY):
        out_ref[q : q + 1, :] = jnp.sum(accs[q], axis=0, keepdims=True) * valid
    out_ref[N_QTY:, :] = jnp.zeros((32 - N_QTY, chunk), jnp.float32)
    if from_cargo:
        _send_back(n_band, out_ref, recv_ref, ret_ref, send_sems, recv_sems, own_sem)


def _send_back(n_band, out_ref, recv_ref, ret_ref, send_sems, recv_sems, own_sem):
    chunk = out_ref.shape[1]
    peers = chunk // CAP
    total = recv_ref.shape[0]
    step = pl.program_id(0)
    last = pl.num_programs(0) - 1
    me = lax.axis_index("tile") * n_band + lax.axis_index("band")
    barrier = pltpu.get_barrier_semaphore()

    def device(p):
        return (p // n_band, p % n_band)

    def copy_to(p):
        return pltpu.make_async_remote_copy(
            src_ref=ret_ref.at[p],
            dst_ref=recv_ref.at[me],
            send_sem=send_sems.at[p],
            recv_sem=recv_sems.at[me],
            device_id=device(p),
            device_id_type=MESH,
        )

    def copy_from(p):
        return pltpu.make_async_remote_copy(
            src_ref=ret_ref.at[p],
            dst_ref=recv_ref.at[p],
            send_sem=send_sems.at[p],
            recv_sem=recv_sems.at[p],
            device_id=device(p),
            device_id_type=MESH,
        )

    own = pltpu.make_async_copy(ret_ref.at[me], recv_ref.at[me], own_sem)

    @pl.when(step == 0)
    def _():
        def greet(k, carry):
            p = lax.rem(me + k, total)
            pl.semaphore_signal(barrier, inc=1, device_id=device(p), device_id_type=MESH)
            return carry

        lax.fori_loop(1, total, greet, 0)

    padded = jnp.concatenate([out_ref[...], jnp.zeros((128 - 32, chunk), jnp.float32)], axis=0)
    ret_ref[pl.ds(pl.multiple_of(step * peers, peers), peers)] = padded.T.reshape(peers, CAP, 128)

    hold = jnp.minimum(4, last)

    @pl.when(step == hold)
    def _():
        pl.semaphore_wait(barrier, total - 1)

    def start(q, carry):
        p = q

        @pl.when(p != me)
        def _():
            copy_to(p).start()

        @pl.when(p == me)
        def _():
            own.start()

        return carry

    @pl.when(step == hold)
    def _():
        lax.fori_loop(0, (hold + 1) * peers, start, 0)

    @pl.when(step > hold)
    def _():
        lax.fori_loop(step * peers, (step + 1) * peers, start, 0)

    @pl.when(step == last)
    def _():
        def finish(k, carry):
            p = lax.rem(me + k, total)
            copy_to(p).wait_send()
            copy_from(p).wait_recv()
            return carry

        lax.fori_loop(1, total, finish, 0)
        own.wait()


def pair_sums(xa, tb, maps, aux, n_band=1, chunk=128):
    pairs = tb.shape[1]
    from_cargo = maps is None
    scratch = [
        pltpu.VMEM((3, 128, chunk), jnp.float32),
        pltpu.VMEM((6, 128, chunk), jnp.float32),
        pltpu.VMEM((4, chunk, 128), jnp.float32),
    ]
    out_shape = jax.ShapeDtypeStruct((32, pairs), jnp.float32)
    out_specs = pl.BlockSpec((32, chunk), lambda i: (0, i))
    params = None
    if from_cargo:
        xa = xa.reshape(-1, 128)
        xa_spec = pl.BlockSpec((chunk // CAP * (4 * CAP + 1), 128), lambda i: (i, 0))
        maps = aux
        map_spec = pl.BlockSpec((8, 128), lambda i: (0, 0))
        peers = pairs // CAP
        out_shape = (out_shape, jax.ShapeDtypeStruct((peers, CAP, 128), jnp.float32))
        out_specs = (out_specs, pl.BlockSpec(memory_space=pl.ANY))
        scratch += [
            pltpu.VMEM((peers, CAP, 128), jnp.float32),
            pltpu.SemaphoreType.DMA((peers,)),
            pltpu.SemaphoreType.DMA((peers,)),
            pltpu.SemaphoreType.DMA(()),
        ]
        params = pltpu.CompilerParams(collective_id=0, has_side_effects=True)
    else:
        xa_spec = pl.BlockSpec((3, chunk, 128), lambda i: (0, i, 0))
        map_spec = pl.BlockSpec((chunk, 128), lambda i: (i, 0))
    return pl.pallas_call(
        functools.partial(_terms_kernel, from_cargo, n_band),
        out_shape=out_shape,
        grid=(pairs // chunk,),
        in_specs=[
            xa_spec,
            pl.BlockSpec((6, chunk, 128), lambda i: (0, i, 0)),
            map_spec,
            pl.BlockSpec((32, chunk), lambda i: (0, i)),
        ],
        out_specs=out_specs,
        scratch_shapes=scratch,
        compiler_params=params,
    )(xa, tb, maps, aux)


def _cargo_kernel(xa_ref, map_ref, side_ref, out_ref):
    height = 4 * CAP + 1
    group = 8

    def body(g, carry):
        for q in range(group):
            p = g * group + q
            base = pl.multiple_of(g * (group * height), 8) + q * height
            slots = pl.ds(pl.multiple_of(p * CAP, CAP), CAP)
            for c in range(3):
                out_ref[pl.ds(base + c * CAP, CAP), :] = xa_ref[c, slots, :]
            out_ref[pl.ds(base + 3 * CAP, CAP), :] = map_ref[slots, :].astype(jnp.float32)
            out_ref[pl.ds(base + 4 * CAP, 1), :] = side_ref[pl.ds(p, 1), :]
        return carry

    lax.fori_loop(0, side_ref.shape[0] // group, body, 0)


def build_cargo(xa3, maps, side):
    slots = maps.shape[0]
    height = 4 * CAP + 1
    cargo = pl.pallas_call(
        _cargo_kernel,
        out_shape=jax.ShapeDtypeStruct((slots // CAP * height, 128), jnp.float32),
    )(xa3, maps, side)
    return cargo.reshape(slots // CAP, 1, height * 128)


def split_terms(out):
    sel = out[0:N_QTY].T
    ga = sel[:, 0:6] * (1.0 / 128)
    ha = sel[:, 6:18] * (1.0 / 4096)
    gb = -jnp.concatenate([sel[:, 18:21], sel[:, 3:6]], axis=1) * (1.0 / 128)
    hb0 = -jnp.concatenate([sel[:, 21:24], sel[:, 9:12]], axis=1) * (1.0 / 4096)
    hb1 = -jnp.concatenate([sel[:, 24:27], sel[:, 15:18]], axis=1) * (1.0 / 4096)
    return jnp.concatenate([ga, ha], axis=1), jnp.concatenate([gb, hb0, hb1], axis=1)


def _exchange_kernel(n_band, x_ref, out_ref, send_sems, recv_sems, own_sem):
    peers = x_ref.shape[0]
    me = lax.axis_index("tile") * n_band + lax.axis_index("band")

    def peer_of(k):
        p = lax.rem(me + k, peers)
        return p, (p // n_band, p % n_band)

    barrier = pltpu.get_barrier_semaphore()

    def greet(k, carry):
        _, dev = peer_of(k)
        pl.semaphore_signal(barrier, inc=1, device_id=dev, device_id_type=MESH)
        return carry

    lax.fori_loop(1, peers, greet, 0)
    pl.semaphore_wait(barrier, peers - 1)

    own = pltpu.make_async_copy(x_ref.at[me], out_ref.at[me], own_sem)
    own.start()

    def outgoing(k):
        p, dev = peer_of(k)
        return pltpu.make_async_remote_copy(
            src_ref=x_ref.at[p],
            dst_ref=out_ref.at[me],
            send_sem=send_sems.at[p],
            recv_sem=recv_sems.at[me],
            device_id=dev,
            device_id_type=MESH,
        )

    def incoming(k):
        p, dev = peer_of(k)
        return pltpu.make_async_remote_copy(
            src_ref=x_ref.at[p],
            dst_ref=out_ref.at[p],
            send_sem=send_sems.at[p],
            recv_sem=recv_sems.at[p],
            device_id=dev,
            device_id_type=MESH,
        )

    def start(k, carry):
        outgoing(k).start()
        return carry

    lax.fori_loop(1, peers, start, 0)

    def finish(k, carry):
        outgoing(k).wait_send()
        incoming(k).wait_recv()
        return carry

    lax.fori_loop(1, peers, finish, 0)
    own.wait()


def exchange(x, n_band, collective_id):
    peers = x.shape[0]
    return pl.pallas_call(
        functools.partial(_exchange_kernel, n_band),
        out_shape=jax.ShapeDtypeStruct(x.shape, x.dtype),
        in_specs=[pl.BlockSpec(memory_space=pl.ANY)],
        out_specs=pl.BlockSpec(memory_space=pl.ANY),
        scratch_shapes=[
            pltpu.SemaphoreType.DMA((peers,)),
            pltpu.SemaphoreType.DMA((peers,)),
            pltpu.SemaphoreType.DMA(()),
        ],
        compiler_params=pltpu.CompilerParams(collective_id=collective_id, has_side_effects=True),
    )(x)


def pick_rows(blocks, rows):
    onehot = (blocks[:, None] == jnp.arange(rows.shape[1], dtype=jnp.int32)[None, :]).astype(
        jnp.float32
    )
    return jnp.einsum("sb,cbk->csk", onehot, rows, precision=lax.Precision.HIGHEST)


def frag_sums(blocks, terms, frag_count):
    onehot = (blocks[:, None] // BF == jnp.arange(frag_count, dtype=jnp.int32)[None, :]).astype(
        jnp.float32
    )
    return jnp.dot(onehot.T, terms, precision=lax.Precision.HIGHEST)


def make_aux(dirs_a, dirs_b, valid):
    pairs = dirs_a.shape[0]
    return jnp.concatenate(
        [dirs_a.T, dirs_b.T, valid[None, :], jnp.zeros((32 - 25, pairs), jnp.float32)], axis=0
    )


def local(
    points,
    normals,
    poses,
    directions,
    local_pairs,
    local_maps,
    remote_src,
    remote_maps,
    remote_dst,
    counts,
):
    axes = ("tile", "band")
    n_band = lax.axis_size("band")
    frag_count = poses.shape[1]
    rows6 = to_world_rows(points, normals, poses, BF)
    frag_dirs = directions.reshape(12, frag_count).T
    peers = counts.shape[1]

    source_blocks = remote_src[0]
    valid = (
        (jnp.arange(CAP, dtype=jnp.int32)[None, :] < counts[0][:, None])
        .astype(jnp.float32)
        .reshape(-1)
    )
    frag_pick = (
        source_blocks[:, None] // BF == jnp.arange(frag_count, dtype=jnp.int32)[None, :]
    ).astype(jnp.float32)
    dirs_send = jnp.dot(frag_pick, frag_dirs, precision=lax.Precision.HIGHEST)
    side = jnp.concatenate([dirs_send, valid[:, None]], axis=1)
    side = side.reshape(peers, CAP * 13)
    side = jnp.concatenate([side, jnp.zeros((peers, 128 - CAP * 13), jnp.float32)], axis=1)
    cargo = build_cargo(pick_rows(source_blocks, rows6[0:3]), remote_maps[0], side)
    arrived = lax.all_to_all(cargo, axes, split_axis=0, concat_axis=0, tiled=True)

    src_l = local_pairs[0]
    tgt_l = local_pairs[1]
    ones = jnp.ones((src_l.shape[0],), jnp.float32)
    out_l = pair_sums(
        pick_rows(src_l, rows6[0:3]),
        pick_rows(tgt_l, rows6),
        local_maps,
        make_aux(frag_dirs[src_l // BF], frag_dirs[tgt_l // BF], ones),
    )
    local_a, local_b = split_terms(out_l)

    target_blocks = remote_dst[0]
    side_in = arrived[:, 0, CAP * 4 * 128 : CAP * 4 * 128 + CAP * 13].reshape(peers * CAP, 13)
    out_r, back = pair_sums(
        arrived,
        pick_rows(target_blocks, rows6),
        None,
        make_aux(side_in[:, 0:12], frag_dirs[target_blocks // BF], side_in[:, 12]),
        n_band,
    )
    unused, remote_b = split_terms(out_r)
    returned, unused = split_terms(back.reshape(peers * CAP, 128)[:, 0:32].T)

    totals = frag_sums(src_l, local_a, frag_count) + frag_sums(tgt_l, local_b, frag_count)
    totals = (
        totals
        + frag_sums(target_blocks, remote_b, frag_count)
        + frag_sums(source_blocks, returned, frag_count)
    )
    gradient = totals[:, 0:6].T
    hess_products = totals[:, 6:18].T.reshape(2, 6, frag_count)
    return (gradient, hess_products)


def solution(mesh):
    placed = (
        P(("tile", "band"), None, None),
        P(("tile", "band"), None, None),
        P(None, ("tile", "band")),
        P(None, None, ("tile", "band")),
        P(None, ("tile", "band")),
        P(("tile", "band"), None),
        P(("tile", "band"), None),
        P(("tile", "band"), None, None),
        P(("tile", "band"), None),
        P(("tile", "band"), None),
    )
    return jax.shard_map(
        local,
        mesh=mesh,
        in_specs=placed,
        out_specs=(P(None, ("tile", "band")), P(None, None, ("tile", "band"))),
        check_vma=False,
    )
```

```python
import functools

import jax
import jax.numpy as jnp
from jax import lax
from jax.experimental import pallas as pl
from jax.experimental.pallas import tpu as pltpu
from jax.sharding import PartitionSpec as P

BF = 32
CAP = 8
N_QTY = 27
MESH = pl.DeviceIdType.MESH


def rotations(poses):
    half_angle = poses[0:3] * 0.5
    inverse = 1.0 / jnp.sqrt(
        1.0
        + half_angle[0] * half_angle[0]
        + half_angle[1] * half_angle[1]
        + half_angle[2] * half_angle[2]
    )
    quat_x = half_angle[0] * inverse
    quat_y = half_angle[1] * inverse
    quat_z = half_angle[2] * inverse
    rotation = [
        [
            1.0 - 2.0 * (quat_y * quat_y + quat_z * quat_z),
            2.0 * (quat_x * quat_y - inverse * quat_z),
            2.0 * (quat_x * quat_z + inverse * quat_y),
        ],
        [
            2.0 * (quat_x * quat_y + inverse * quat_z),
            1.0 - 2.0 * (quat_x * quat_x + quat_z * quat_z),
            2.0 * (quat_y * quat_z - inverse * quat_x),
        ],
        [
            2.0 * (quat_x * quat_z - inverse * quat_y),
            2.0 * (quat_y * quat_z + inverse * quat_x),
            1.0 - 2.0 * (quat_x * quat_x + quat_y * quat_y),
        ],
    ]
    return (rotation, poses[3:6])


def to_world_rows(points, normals, poses, per_pose):
    rotation, translation = rotations(poses)

    def spread(values):
        return jnp.repeat(values, per_pose)[:, None]

    world_rows = []
    normal_rows = []
    for i in range(3):
        coeffs = [spread(rotation[i][j]) for j in range(3)]
        world_rows.append(
            coeffs[0] * points[:, 0]
            + coeffs[1] * points[:, 1]
            + coeffs[2] * points[:, 2]
            + spread(translation[i])
        )
        normal_rows.append(
            coeffs[0] * normals[:, 0] + coeffs[1] * normals[:, 1] + coeffs[2] * normals[:, 2]
        )
    return jnp.stack(world_rows + normal_rows, axis=0)


def _terms_kernel(from_cargo, n_band, xa_ref, tb_ref, map_ref, aux_ref, out_ref, *rest):
    if from_cargo:
        recv_ref, xt_ref, gt_ref, cs_ref, ret_ref, send_sems, recv_sems, own_sem = rest
    else:
        xt_ref, gt_ref, cs_ref = rest
    chunk = out_ref.shape[1]
    if from_cargo:
        peers = chunk // CAP
        height = 4 * CAP + 1
        for p in range(peers):
            for r in range(4):
                cs_ref[r, pl.ds(p * CAP, CAP), :] = xa_ref[pl.ds(p * height + r * CAP, CAP), :]
        idx = cs_ref[3].astype(jnp.int32)
        for c in range(3):
            xt_ref[c] = cs_ref[c].T
    else:
        idx = map_ref[...]
        for c in range(3):
            xt_ref[c] = xa_ref[c].T
    for c in range(6):
        picked = jnp.take_along_axis(tb_ref[c], idx, axis=1, mode="promise_in_bounds")
        gt_ref[c] = picked.T

    def col(q):
        return jnp.broadcast_to(aux_ref[q : q + 1, :], (8, chunk))

    def body(s, accs):
        rows = pl.ds(pl.multiple_of(s * 8, 8), 8)
        xa = [xt_ref[c, rows, :] for c in range(3)]
        xb = [gt_ref[c, rows, :] for c in range(3)]
        nb = [gt_ref[3 + c, rows, :] for c in range(3)]
        off = [xa[c] - xb[c] for c in range(3)]
        res = nb[0] * off[0] + nb[1] * off[1] + nb[2] * off[2]
        ja = [
            xa[1] * nb[2] - xa[2] * nb[1],
            xa[2] * nb[0] - xa[0] * nb[2],
            xa[0] * nb[1] - xa[1] * nb[0],
            nb[0],
            nb[1],
            nb[2],
        ]
        kb = [
            xb[1] * nb[2] - xb[2] * nb[1],
            xb[2] * nb[0] - xb[0] * nb[2],
            xb[0] * nb[1] - xb[1] * nb[0],
            nb[0],
            nb[1],
            nb[2],
        ]
        weights = [res]
        for v in range(2):
            sa = ja[0] * col(6 * v)
            sb = kb[0] * col(12 + 6 * v)
            for c in range(1, 6):
                sa = sa + ja[c] * col(6 * v + c)
                sb = sb + kb[c] * col(12 + 6 * v + c)
            weights.append(sa - sb)
        vals = []
        for w in weights:
            vals.extend([w * ja[c] for c in range(6)])
        for w in weights:
            vals.extend([w * kb[c] for c in range(3)])
        return tuple(a + v for a, v in zip(accs, vals))

    zero = jnp.zeros((8, chunk), jnp.float32)
    accs = lax.fori_loop(0, 128 // 8, body, (zero,) * N_QTY, unroll=8)
    valid = aux_ref[24:25, :]
    for q in range(N_QTY):
        out_ref[q : q + 1, :] = jnp.sum(accs[q], axis=0, keepdims=True) * valid
    out_ref[N_QTY:, :] = jnp.zeros((32 - N_QTY, chunk), jnp.float32)
    if from_cargo:
        _send_back(n_band, out_ref, recv_ref, ret_ref, send_sems, recv_sems, own_sem)


def _send_back(n_band, out_ref, recv_ref, ret_ref, send_sems, recv_sems, own_sem):
    chunk = out_ref.shape[1]
    peers = chunk // CAP
    total = recv_ref.shape[0]
    step = pl.program_id(0)
    last = pl.num_programs(0) - 1
    me = lax.axis_index("tile") * n_band + lax.axis_index("band")
    barrier = pltpu.get_barrier_semaphore()

    def device(p):
        return (p // n_band, p % n_band)

    def copy_to(p):
        return pltpu.make_async_remote_copy(
            src_ref=ret_ref.at[p],
            dst_ref=recv_ref.at[me],
            send_sem=send_sems.at[p],
            recv_sem=recv_sems.at[me],
            device_id=device(p),
            device_id_type=MESH,
        )

    def copy_from(p):
        return pltpu.make_async_remote_copy(
            src_ref=ret_ref.at[p],
            dst_ref=recv_ref.at[p],
            send_sem=send_sems.at[p],
            recv_sem=recv_sems.at[p],
            device_id=device(p),
            device_id_type=MESH,
        )

    own = pltpu.make_async_copy(ret_ref.at[me], recv_ref.at[me], own_sem)

    @pl.when(step == 0)
    def _():
        def greet(k, carry):
            p = lax.rem(me + k, total)
            pl.semaphore_signal(barrier, inc=1, device_id=device(p), device_id_type=MESH)
            return carry

        lax.fori_loop(1, total, greet, 0)

    padded = jnp.concatenate([out_ref[...], jnp.zeros((128 - 32, chunk), jnp.float32)], axis=0)
    ret_ref[pl.ds(pl.multiple_of(step * peers, peers), peers)] = padded.T.reshape(peers, CAP, 128)

    hold = jnp.minimum(6, last)

    @pl.when(step == hold)
    def _():
        pl.semaphore_wait(barrier, total - 1)

    def start(q, carry):
        p = q

        @pl.when(p != me)
        def _():
            copy_to(p).start()

        @pl.when(p == me)
        def _():
            own.start()

        return carry

    @pl.when(step == hold)
    def _():
        lax.fori_loop(0, (hold + 1) * peers, start, 0)

    @pl.when(step > hold)
    def _():
        lax.fori_loop(step * peers, (step + 1) * peers, start, 0)

    @pl.when(step == last)
    def _():
        def finish(k, carry):
            p = lax.rem(me + k, total)
            copy_to(p).wait_send()
            copy_from(p).wait_recv()
            return carry

        lax.fori_loop(1, total, finish, 0)
        own.wait()


def pair_sums(xa, tb, maps, aux, n_band=1, chunk=128):
    pairs = tb.shape[1]
    from_cargo = maps is None
    scratch = [
        pltpu.VMEM((3, 128, chunk), jnp.float32),
        pltpu.VMEM((6, 128, chunk), jnp.float32),
        pltpu.VMEM((4, chunk, 128), jnp.float32),
    ]
    out_shape = jax.ShapeDtypeStruct((32, pairs), jnp.float32)
    out_specs = pl.BlockSpec((32, chunk), lambda i: (0, i))
    params = None
    if from_cargo:
        xa = xa.reshape(-1, 128)
        xa_spec = pl.BlockSpec((chunk // CAP * (4 * CAP + 1), 128), lambda i: (i, 0))
        maps = aux
        map_spec = pl.BlockSpec((8, 128), lambda i: (0, 0))
        peers = pairs // CAP
        out_shape = (out_shape, jax.ShapeDtypeStruct((peers, CAP, 128), jnp.float32))
        out_specs = (out_specs, pl.BlockSpec(memory_space=pl.ANY))
        scratch += [
            pltpu.VMEM((peers, CAP, 128), jnp.float32),
            pltpu.SemaphoreType.DMA((peers,)),
            pltpu.SemaphoreType.DMA((peers,)),
            pltpu.SemaphoreType.DMA(()),
        ]
        params = pltpu.CompilerParams(collective_id=0, has_side_effects=True)
    else:
        xa_spec = pl.BlockSpec((3, chunk, 128), lambda i: (0, i, 0))
        map_spec = pl.BlockSpec((chunk, 128), lambda i: (i, 0))
    return pl.pallas_call(
        functools.partial(_terms_kernel, from_cargo, n_band),
        out_shape=out_shape,
        grid=(pairs // chunk,),
        in_specs=[
            xa_spec,
            pl.BlockSpec((6, chunk, 128), lambda i: (0, i, 0)),
            map_spec,
            pl.BlockSpec((32, chunk), lambda i: (0, i)),
        ],
        out_specs=out_specs,
        scratch_shapes=scratch,
        compiler_params=params,
    )(xa, tb, maps, aux)


def _cargo_kernel(xa_ref, map_ref, side_ref, out_ref):
    height = 4 * CAP + 1
    group = 8

    def body(g, carry):
        for q in range(group):
            p = g * group + q
            base = pl.multiple_of(g * (group * height), 8) + q * height
            slots = pl.ds(pl.multiple_of(p * CAP, CAP), CAP)
            for c in range(3):
                out_ref[pl.ds(base + c * CAP, CAP), :] = xa_ref[c, slots, :]
            out_ref[pl.ds(base + 3 * CAP, CAP), :] = map_ref[slots, :].astype(jnp.float32)
            out_ref[pl.ds(base + 4 * CAP, 1), :] = side_ref[pl.ds(p, 1), :]
        return carry

    lax.fori_loop(0, side_ref.shape[0] // group, body, 0)


def build_cargo(xa3, maps, side):
    slots = maps.shape[0]
    height = 4 * CAP + 1
    cargo = pl.pallas_call(
        _cargo_kernel,
        out_shape=jax.ShapeDtypeStruct((slots // CAP * height, 128), jnp.float32),
    )(xa3, maps, side)
    return cargo.reshape(slots // CAP, 1, height * 128)


def split_terms(out):
    sel = out[0:N_QTY].T
    ga = sel[:, 0:6] * (1.0 / 128)
    ha = sel[:, 6:18] * (1.0 / 4096)
    gb = -jnp.concatenate([sel[:, 18:21], sel[:, 3:6]], axis=1) * (1.0 / 128)
    hb0 = -jnp.concatenate([sel[:, 21:24], sel[:, 9:12]], axis=1) * (1.0 / 4096)
    hb1 = -jnp.concatenate([sel[:, 24:27], sel[:, 15:18]], axis=1) * (1.0 / 4096)
    return jnp.concatenate([ga, ha], axis=1), jnp.concatenate([gb, hb0, hb1], axis=1)


def _exchange_kernel(n_band, x_ref, out_ref, send_sems, recv_sems, own_sem):
    peers = x_ref.shape[0]
    me = lax.axis_index("tile") * n_band + lax.axis_index("band")

    def peer_of(k):
        p = lax.rem(me + k, peers)
        return p, (p // n_band, p % n_band)

    barrier = pltpu.get_barrier_semaphore()

    def greet(k, carry):
        _, dev = peer_of(k)
        pl.semaphore_signal(barrier, inc=1, device_id=dev, device_id_type=MESH)
        return carry

    lax.fori_loop(1, peers, greet, 0)
    pl.semaphore_wait(barrier, peers - 1)

    own = pltpu.make_async_copy(x_ref.at[me], out_ref.at[me], own_sem)
    own.start()

    def outgoing(k):
        p, dev = peer_of(k)
        return pltpu.make_async_remote_copy(
            src_ref=x_ref.at[p],
            dst_ref=out_ref.at[me],
            send_sem=send_sems.at[p],
            recv_sem=recv_sems.at[me],
            device_id=dev,
            device_id_type=MESH,
        )

    def incoming(k):
        p, dev = peer_of(k)
        return pltpu.make_async_remote_copy(
            src_ref=x_ref.at[p],
            dst_ref=out_ref.at[p],
            send_sem=send_sems.at[p],
            recv_sem=recv_sems.at[p],
            device_id=dev,
            device_id_type=MESH,
        )

    def start(k, carry):
        outgoing(k).start()
        return carry

    lax.fori_loop(1, peers, start, 0)

    def finish(k, carry):
        outgoing(k).wait_send()
        incoming(k).wait_recv()
        return carry

    lax.fori_loop(1, peers, finish, 0)
    own.wait()


def exchange(x, n_band, collective_id):
    peers = x.shape[0]
    return pl.pallas_call(
        functools.partial(_exchange_kernel, n_band),
        out_shape=jax.ShapeDtypeStruct(x.shape, x.dtype),
        in_specs=[pl.BlockSpec(memory_space=pl.ANY)],
        out_specs=pl.BlockSpec(memory_space=pl.ANY),
        scratch_shapes=[
            pltpu.SemaphoreType.DMA((peers,)),
            pltpu.SemaphoreType.DMA((peers,)),
            pltpu.SemaphoreType.DMA(()),
        ],
        compiler_params=pltpu.CompilerParams(collective_id=collective_id, has_side_effects=True),
    )(x)


def pick_rows(blocks, rows):
    onehot = (blocks[:, None] == jnp.arange(rows.shape[1], dtype=jnp.int32)[None, :]).astype(
        jnp.float32
    )
    return jnp.einsum("sb,cbk->csk", onehot, rows, precision=lax.Precision.HIGHEST)


def frag_sums(blocks, terms, frag_count):
    onehot = (blocks[:, None] // BF == jnp.arange(frag_count, dtype=jnp.int32)[None, :]).astype(
        jnp.float32
    )
    return jnp.dot(onehot.T, terms, precision=lax.Precision.HIGHEST)


def make_aux(dirs_a, dirs_b, valid):
    pairs = dirs_a.shape[0]
    return jnp.concatenate(
        [dirs_a.T, dirs_b.T, valid[None, :], jnp.zeros((32 - 25, pairs), jnp.float32)], axis=0
    )


def local(
    points,
    normals,
    poses,
    directions,
    local_pairs,
    local_maps,
    remote_src,
    remote_maps,
    remote_dst,
    counts,
):
    axes = ("tile", "band")
    n_band = lax.axis_size("band")
    frag_count = poses.shape[1]
    rows6 = to_world_rows(points, normals, poses, BF)
    frag_dirs = directions.reshape(12, frag_count).T
    peers = counts.shape[1]

    source_blocks = remote_src[0]
    valid = (
        (jnp.arange(CAP, dtype=jnp.int32)[None, :] < counts[0][:, None])
        .astype(jnp.float32)
        .reshape(-1)
    )
    frag_pick = (
        source_blocks[:, None] // BF == jnp.arange(frag_count, dtype=jnp.int32)[None, :]
    ).astype(jnp.float32)
    dirs_send = jnp.dot(frag_pick, frag_dirs, precision=lax.Precision.HIGHEST)
    side = jnp.concatenate([dirs_send, valid[:, None]], axis=1)
    side = side.reshape(peers, CAP * 13)
    side = jnp.concatenate([side, jnp.zeros((peers, 128 - CAP * 13), jnp.float32)], axis=1)
    cargo = build_cargo(pick_rows(source_blocks, rows6[0:3]), remote_maps[0], side)
    arrived = lax.all_to_all(cargo, axes, split_axis=0, concat_axis=0, tiled=True)

    src_l = local_pairs[0]
    tgt_l = local_pairs[1]
    ones = jnp.ones((src_l.shape[0],), jnp.float32)
    out_l = pair_sums(
        pick_rows(src_l, rows6[0:3]),
        pick_rows(tgt_l, rows6),
        local_maps,
        make_aux(frag_dirs[src_l // BF], frag_dirs[tgt_l // BF], ones),
    )
    local_a, local_b = split_terms(out_l)

    target_blocks = remote_dst[0]
    side_in = arrived[:, 0, CAP * 4 * 128 : CAP * 4 * 128 + CAP * 13].reshape(peers * CAP, 13)
    out_r, back = pair_sums(
        arrived,
        pick_rows(target_blocks, rows6),
        None,
        make_aux(side_in[:, 0:12], frag_dirs[target_blocks // BF], side_in[:, 12]),
        n_band,
    )
    unused, remote_b = split_terms(out_r)
    returned, unused = split_terms(back.reshape(peers * CAP, 128)[:, 0:32].T)

    totals = frag_sums(src_l, local_a, frag_count) + frag_sums(tgt_l, local_b, frag_count)
    totals = (
        totals
        + frag_sums(target_blocks, remote_b, frag_count)
        + frag_sums(source_blocks, returned, frag_count)
    )
    gradient = totals[:, 0:6].T
    hess_products = totals[:, 6:18].T.reshape(2, 6, frag_count)
    return (gradient, hess_products)


def solution(mesh):
    placed = (
        P(("tile", "band"), None, None),
        P(("tile", "band"), None, None),
        P(None, ("tile", "band")),
        P(None, None, ("tile", "band")),
        P(None, ("tile", "band")),
        P(("tile", "band"), None),
        P(("tile", "band"), None),
        P(("tile", "band"), None, None),
        P(("tile", "band"), None),
        P(("tile", "band"), None),
    )
    return jax.shard_map(
        local,
        mesh=mesh,
        in_specs=placed,
        out_specs=(P(None, ("tile", "band")), P(None, None, ("tile", "band"))),
        check_vma=False,
    )
```

```python
import functools

import jax
import jax.numpy as jnp
from jax import lax
from jax.experimental import pallas as pl
from jax.experimental.pallas import tpu as pltpu
from jax.sharding import PartitionSpec as P

BF = 32
CAP = 8
N_QTY = 27
MESH = pl.DeviceIdType.MESH


def rotations(poses):
    half_angle = poses[0:3] * 0.5
    inverse = 1.0 / jnp.sqrt(
        1.0
        + half_angle[0] * half_angle[0]
        + half_angle[1] * half_angle[1]
        + half_angle[2] * half_angle[2]
    )
    quat_x = half_angle[0] * inverse
    quat_y = half_angle[1] * inverse
    quat_z = half_angle[2] * inverse
    rotation = [
        [
            1.0 - 2.0 * (quat_y * quat_y + quat_z * quat_z),
            2.0 * (quat_x * quat_y - inverse * quat_z),
            2.0 * (quat_x * quat_z + inverse * quat_y),
        ],
        [
            2.0 * (quat_x * quat_y + inverse * quat_z),
            1.0 - 2.0 * (quat_x * quat_x + quat_z * quat_z),
            2.0 * (quat_y * quat_z - inverse * quat_x),
        ],
        [
            2.0 * (quat_x * quat_z - inverse * quat_y),
            2.0 * (quat_y * quat_z + inverse * quat_x),
            1.0 - 2.0 * (quat_x * quat_x + quat_y * quat_y),
        ],
    ]
    return (rotation, poses[3:6])


def to_world_rows(points, normals, poses, per_pose):
    rotation, translation = rotations(poses)

    def spread(values):
        return jnp.repeat(values, per_pose)[:, None]

    world_rows = []
    normal_rows = []
    for i in range(3):
        coeffs = [spread(rotation[i][j]) for j in range(3)]
        world_rows.append(
            coeffs[0] * points[:, 0]
            + coeffs[1] * points[:, 1]
            + coeffs[2] * points[:, 2]
            + spread(translation[i])
        )
        normal_rows.append(
            coeffs[0] * normals[:, 0] + coeffs[1] * normals[:, 1] + coeffs[2] * normals[:, 2]
        )
    return jnp.stack(world_rows + normal_rows, axis=0)


def _terms_kernel(from_cargo, n_band, xa_ref, tb_ref, map_ref, aux_ref, out_ref, *rest):
    if from_cargo:
        recv_ref, xt_ref, gt_ref, cs_ref, ret_ref, send_sems, recv_sems, own_sem = rest
    else:
        xt_ref, gt_ref, cs_ref = rest
    chunk = out_ref.shape[1]
    if from_cargo:
        peers = chunk // CAP
        height = 4 * CAP + 1
        for p in range(peers):
            for r in range(4):
                cs_ref[r, pl.ds(p * CAP, CAP), :] = xa_ref[pl.ds(p * height + r * CAP, CAP), :]
        idx = cs_ref[3].astype(jnp.int32)
        for c in range(3):
            xt_ref[c] = cs_ref[c].T
    else:
        idx = map_ref[...]
        for c in range(3):
            xt_ref[c] = xa_ref[c].T
    for c in range(6):
        picked = jnp.take_along_axis(tb_ref[c], idx, axis=1, mode="promise_in_bounds")
        gt_ref[c] = picked.T

    def col(q):
        return jnp.broadcast_to(aux_ref[q : q + 1, :], (8, chunk))

    def body(s, accs):
        rows = pl.ds(pl.multiple_of(s * 8, 8), 8)
        xa = [xt_ref[c, rows, :] for c in range(3)]
        xb = [gt_ref[c, rows, :] for c in range(3)]
        nb = [gt_ref[3 + c, rows, :] for c in range(3)]
        off = [xa[c] - xb[c] for c in range(3)]
        res = nb[0] * off[0] + nb[1] * off[1] + nb[2] * off[2]
        ja = [
            xa[1] * nb[2] - xa[2] * nb[1],
            xa[2] * nb[0] - xa[0] * nb[2],
            xa[0] * nb[1] - xa[1] * nb[0],
            nb[0],
            nb[1],
            nb[2],
        ]
        kb = [
            xb[1] * nb[2] - xb[2] * nb[1],
            xb[2] * nb[0] - xb[0] * nb[2],
            xb[0] * nb[1] - xb[1] * nb[0],
            nb[0],
            nb[1],
            nb[2],
        ]
        weights = [res]
        for v in range(2):
            sa = ja[0] * col(6 * v)
            sb = kb[0] * col(12 + 6 * v)
            for c in range(1, 6):
                sa = sa + ja[c] * col(6 * v + c)
                sb = sb + kb[c] * col(12 + 6 * v + c)
            weights.append(sa - sb)
        vals = []
        for w in weights:
            vals.extend([w * ja[c] for c in range(6)])
        for w in weights:
            vals.extend([w * kb[c] for c in range(3)])
        return tuple(a + v for a, v in zip(accs, vals))

    zero = jnp.zeros((8, chunk), jnp.float32)
    accs = lax.fori_loop(0, 128 // 8, body, (zero,) * N_QTY, unroll=8)
    valid = aux_ref[24:25, :]
    for q in range(N_QTY):
        out_ref[q : q + 1, :] = jnp.sum(accs[q], axis=0, keepdims=True) * valid
    out_ref[N_QTY:, :] = jnp.zeros((32 - N_QTY, chunk), jnp.float32)
    if from_cargo:
        _send_back(n_band, out_ref, recv_ref, ret_ref, send_sems, recv_sems, own_sem)


def _send_back(n_band, out_ref, recv_ref, ret_ref, send_sems, recv_sems, own_sem):
    chunk = out_ref.shape[1]
    peers = chunk // CAP
    total = recv_ref.shape[0]
    step = pl.program_id(0)
    last = pl.num_programs(0) - 1
    me = lax.axis_index("tile") * n_band + lax.axis_index("band")
    barrier = pltpu.get_barrier_semaphore()

    def device(p):
        return (p // n_band, p % n_band)

    def copy_to(p):
        return pltpu.make_async_remote_copy(
            src_ref=ret_ref.at[p],
            dst_ref=recv_ref.at[me],
            send_sem=send_sems.at[p],
            recv_sem=recv_sems.at[me],
            device_id=device(p),
            device_id_type=MESH,
        )

    def copy_from(p):
        return pltpu.make_async_remote_copy(
            src_ref=ret_ref.at[p],
            dst_ref=recv_ref.at[p],
            send_sem=send_sems.at[p],
            recv_sem=recv_sems.at[p],
            device_id=device(p),
            device_id_type=MESH,
        )

    own = pltpu.make_async_copy(ret_ref.at[me], recv_ref.at[me], own_sem)

    @pl.when(step == 0)
    def _():
        def greet(k, carry):
            p = lax.rem(me + k, total)
            pl.semaphore_signal(barrier, inc=1, device_id=device(p), device_id_type=MESH)
            return carry

        lax.fori_loop(1, total, greet, 0)

    padded = jnp.concatenate([out_ref[...], jnp.zeros((128 - 32, chunk), jnp.float32)], axis=0)
    ret_ref[pl.ds(pl.multiple_of(step * peers, peers), peers)] = padded.T.reshape(peers, CAP, 128)

    hold = jnp.minimum(4, last)

    @pl.when(step == hold)
    def _():
        pl.semaphore_wait(barrier, total - 1)

    def start(q, carry):
        p = q

        @pl.when(p != me)
        def _():
            copy_to(p).start()

        @pl.when(p == me)
        def _():
            own.start()

        return carry

    @pl.when(step == hold)
    def _():
        lax.fori_loop(0, (hold + 1) * peers, start, 0)

    @pl.when(step > hold)
    def _():
        lax.fori_loop(step * peers, (step + 1) * peers, start, 0)

    @pl.when(step == last)
    def _():
        def finish(k, carry):
            p = lax.rem(me + k, total)
            copy_to(p).wait_send()
            copy_from(p).wait_recv()
            return carry

        lax.fori_loop(1, total, finish, 0)
        own.wait()


def pair_sums(xa, tb, maps, aux, n_band=1, chunk=128):
    pairs = tb.shape[1]
    from_cargo = maps is None
    scratch = [
        pltpu.VMEM((3, 128, chunk), jnp.float32),
        pltpu.VMEM((6, 128, chunk), jnp.float32),
        pltpu.VMEM((4, chunk, 128), jnp.float32),
    ]
    out_shape = jax.ShapeDtypeStruct((32, pairs), jnp.float32)
    out_specs = pl.BlockSpec((32, chunk), lambda i: (0, i))
    params = None
    if from_cargo:
        xa = xa.reshape(-1, 128)
        xa_spec = pl.BlockSpec((chunk // CAP * (4 * CAP + 1), 128), lambda i: (i, 0))
        maps = aux
        map_spec = pl.BlockSpec((8, 128), lambda i: (0, 0))
        peers = pairs // CAP
        out_shape = (out_shape, jax.ShapeDtypeStruct((peers, CAP, 128), jnp.float32))
        out_specs = (out_specs, pl.BlockSpec(memory_space=pl.ANY))
        scratch += [
            pltpu.VMEM((peers, CAP, 128), jnp.float32),
            pltpu.SemaphoreType.DMA((peers,)),
            pltpu.SemaphoreType.DMA((peers,)),
            pltpu.SemaphoreType.DMA(()),
        ]
        params = pltpu.CompilerParams(collective_id=0, has_side_effects=True)
    else:
        xa_spec = pl.BlockSpec((3, chunk, 128), lambda i: (0, i, 0))
        map_spec = pl.BlockSpec((chunk, 128), lambda i: (i, 0))
    return pl.pallas_call(
        functools.partial(_terms_kernel, from_cargo, n_band),
        out_shape=out_shape,
        grid=(pairs // chunk,),
        in_specs=[
            xa_spec,
            pl.BlockSpec((6, chunk, 128), lambda i: (0, i, 0)),
            map_spec,
            pl.BlockSpec((32, chunk), lambda i: (0, i)),
        ],
        out_specs=out_specs,
        scratch_shapes=scratch,
        compiler_params=params,
    )(xa, tb, maps, aux)


def _cargo_kernel(xa_ref, map_ref, side_ref, out_ref):
    height = 4 * CAP + 1
    group = 8

    def body(g, carry):
        for q in range(group):
            p = g * group + q
            base = pl.multiple_of(g * (group * height), 8) + q * height
            slots = pl.ds(pl.multiple_of(p * CAP, CAP), CAP)
            for c in range(3):
                out_ref[pl.ds(base + c * CAP, CAP), :] = xa_ref[c, slots, :]
            out_ref[pl.ds(base + 3 * CAP, CAP), :] = map_ref[slots, :].astype(jnp.float32)
            out_ref[pl.ds(base + 4 * CAP, 1), :] = side_ref[pl.ds(p, 1), :]
        return carry

    lax.fori_loop(0, side_ref.shape[0] // group, body, 0)


def build_cargo(xa3, maps, side):
    slots = maps.shape[0]
    height = 4 * CAP + 1
    cargo = pl.pallas_call(
        _cargo_kernel,
        out_shape=jax.ShapeDtypeStruct((slots // CAP * height, 128), jnp.float32),
    )(xa3, maps, side)
    return cargo.reshape(slots // CAP, 1, height * 128)


def split_terms(out):
    sel = out[0:N_QTY].T
    ga = sel[:, 0:6] * (1.0 / 128)
    ha = sel[:, 6:18] * (1.0 / 4096)
    gb = -jnp.concatenate([sel[:, 18:21], sel[:, 3:6]], axis=1) * (1.0 / 128)
    hb0 = -jnp.concatenate([sel[:, 21:24], sel[:, 9:12]], axis=1) * (1.0 / 4096)
    hb1 = -jnp.concatenate([sel[:, 24:27], sel[:, 15:18]], axis=1) * (1.0 / 4096)
    return jnp.concatenate([ga, ha], axis=1), jnp.concatenate([gb, hb0, hb1], axis=1)


def _exchange_kernel(n_band, x_ref, out_ref, send_sems, recv_sems, own_sem):
    peers = x_ref.shape[0]
    me = lax.axis_index("tile") * n_band + lax.axis_index("band")

    def peer_of(k):
        p = lax.rem(me + k, peers)
        return p, (p // n_band, p % n_band)

    barrier = pltpu.get_barrier_semaphore()

    def greet(k, carry):
        _, dev = peer_of(k)
        pl.semaphore_signal(barrier, inc=1, device_id=dev, device_id_type=MESH)
        return carry

    lax.fori_loop(1, peers, greet, 0)
    pl.semaphore_wait(barrier, peers - 1)

    own = pltpu.make_async_copy(x_ref.at[me], out_ref.at[me], own_sem)
    own.start()

    def outgoing(k):
        p, dev = peer_of(k)
        return pltpu.make_async_remote_copy(
            src_ref=x_ref.at[p],
            dst_ref=out_ref.at[me],
            send_sem=send_sems.at[p],
            recv_sem=recv_sems.at[me],
            device_id=dev,
            device_id_type=MESH,
        )

    def incoming(k):
        p, dev = peer_of(k)
        return pltpu.make_async_remote_copy(
            src_ref=x_ref.at[p],
            dst_ref=out_ref.at[p],
            send_sem=send_sems.at[p],
            recv_sem=recv_sems.at[p],
            device_id=dev,
            device_id_type=MESH,
        )

    def start(k, carry):
        outgoing(k).start()
        return carry

    lax.fori_loop(1, peers, start, 0)

    def finish(k, carry):
        outgoing(k).wait_send()
        incoming(k).wait_recv()
        return carry

    lax.fori_loop(1, peers, finish, 0)
    own.wait()


def exchange(x, n_band, collective_id):
    peers = x.shape[0]
    return pl.pallas_call(
        functools.partial(_exchange_kernel, n_band),
        out_shape=jax.ShapeDtypeStruct(x.shape, x.dtype),
        in_specs=[pl.BlockSpec(memory_space=pl.ANY)],
        out_specs=pl.BlockSpec(memory_space=pl.ANY),
        scratch_shapes=[
            pltpu.SemaphoreType.DMA((peers,)),
            pltpu.SemaphoreType.DMA((peers,)),
            pltpu.SemaphoreType.DMA(()),
        ],
        compiler_params=pltpu.CompilerParams(collective_id=collective_id, has_side_effects=True),
    )(x)


def pick_rows(blocks, rows):
    onehot = (blocks[:, None] == jnp.arange(rows.shape[1], dtype=jnp.int32)[None, :]).astype(
        jnp.float32
    )
    return jnp.einsum("sb,cbk->csk", onehot, rows, precision=lax.Precision.HIGHEST)


def frag_sums(blocks, terms, frag_count):
    onehot = (blocks[:, None] // BF == jnp.arange(frag_count, dtype=jnp.int32)[None, :]).astype(
        jnp.float32
    )
    return jnp.dot(onehot.T, terms, precision=lax.Precision.HIGHEST)


def make_aux(dirs_a, dirs_b, valid):
    pairs = dirs_a.shape[0]
    return jnp.concatenate(
        [dirs_a.T, dirs_b.T, valid[None, :], jnp.zeros((32 - 25, pairs), jnp.float32)], axis=0
    )


def local(
    points,
    normals,
    poses,
    directions,
    local_pairs,
    local_maps,
    remote_src,
    remote_maps,
    remote_dst,
    counts,
):
    axes = ("tile", "band")
    n_band = lax.axis_size("band")
    frag_count = poses.shape[1]
    rows6 = to_world_rows(points, normals, poses, BF)
    frag_dirs = directions.reshape(12, frag_count).T
    peers = counts.shape[1]

    source_blocks = remote_src[0]
    valid = (
        (jnp.arange(CAP, dtype=jnp.int32)[None, :] < counts[0][:, None])
        .astype(jnp.float32)
        .reshape(-1)
    )
    frag_pick = (
        source_blocks[:, None] // BF == jnp.arange(frag_count, dtype=jnp.int32)[None, :]
    ).astype(jnp.float32)
    dirs_send = jnp.dot(frag_pick, frag_dirs, precision=lax.Precision.HIGHEST)
    side = jnp.concatenate([dirs_send, valid[:, None]], axis=1)
    side = side.reshape(peers, CAP * 13)
    side = jnp.concatenate([side, jnp.zeros((peers, 128 - CAP * 13), jnp.float32)], axis=1)
    cargo = build_cargo(pick_rows(source_blocks, rows6[0:3]), remote_maps[0], side)
    arrived = lax.all_to_all(cargo, axes, split_axis=0, concat_axis=0, tiled=True)

    src_l = local_pairs[0]
    tgt_l = local_pairs[1]
    ones = jnp.ones((src_l.shape[0],), jnp.float32)
    out_l = pair_sums(
        pick_rows(src_l, rows6[0:3]),
        pick_rows(tgt_l, rows6),
        local_maps,
        make_aux(frag_dirs[src_l // BF], frag_dirs[tgt_l // BF], ones),
    )
    local_a, local_b = split_terms(out_l)

    target_blocks = remote_dst[0]
    side_in = arrived[:, 0, CAP * 4 * 128 : CAP * 4 * 128 + CAP * 13].reshape(peers * CAP, 13)
    out_r, back = pair_sums(
        arrived,
        pick_rows(target_blocks, rows6),
        None,
        make_aux(side_in[:, 0:12], frag_dirs[target_blocks // BF], side_in[:, 12]),
        n_band,
    )
    unused, remote_b = split_terms(out_r)
    back_sums = frag_sums(source_blocks, back.reshape(peers * CAP, 128), frag_count)
    returned = jnp.concatenate([back_sums[:, 0:6] * (1.0 / 128), back_sums[:, 6:18] * (1.0 / 4096)], axis=1)

    totals = frag_sums(src_l, local_a, frag_count) + frag_sums(tgt_l, local_b, frag_count)
    totals = (
        totals
        + frag_sums(target_blocks, remote_b, frag_count)
        + returned
    )
    gradient = totals[:, 0:6].T
    hess_products = totals[:, 6:18].T.reshape(2, 6, frag_count)
    return (gradient, hess_products)


def solution(mesh):
    placed = (
        P(("tile", "band"), None, None),
        P(("tile", "band"), None, None),
        P(None, ("tile", "band")),
        P(None, None, ("tile", "band")),
        P(None, ("tile", "band")),
        P(("tile", "band"), None),
        P(("tile", "band"), None),
        P(("tile", "band"), None, None),
        P(("tile", "band"), None),
        P(("tile", "band"), None),
    )
    return jax.shard_map(
        local,
        mesh=mesh,
        in_specs=placed,
        out_specs=(P(None, ("tile", "band")), P(None, None, ("tile", "band"))),
        check_vma=False,
    )
```

```python
import functools

import jax
import jax.numpy as jnp
from jax import lax
from jax.experimental import pallas as pl
from jax.experimental.pallas import tpu as pltpu
from jax.sharding import PartitionSpec as P

BF = 32
CAP = 8
N_QTY = 27
MESH = pl.DeviceIdType.MESH


def rotations(poses):
    half_angle = poses[0:3] * 0.5
    inverse = 1.0 / jnp.sqrt(
        1.0
        + half_angle[0] * half_angle[0]
        + half_angle[1] * half_angle[1]
        + half_angle[2] * half_angle[2]
    )
    quat_x = half_angle[0] * inverse
    quat_y = half_angle[1] * inverse
    quat_z = half_angle[2] * inverse
    rotation = [
        [
            1.0 - 2.0 * (quat_y * quat_y + quat_z * quat_z),
            2.0 * (quat_x * quat_y - inverse * quat_z),
            2.0 * (quat_x * quat_z + inverse * quat_y),
        ],
        [
            2.0 * (quat_x * quat_y + inverse * quat_z),
            1.0 - 2.0 * (quat_x * quat_x + quat_z * quat_z),
            2.0 * (quat_y * quat_z - inverse * quat_x),
        ],
        [
            2.0 * (quat_x * quat_z - inverse * quat_y),
            2.0 * (quat_y * quat_z + inverse * quat_x),
            1.0 - 2.0 * (quat_x * quat_x + quat_y * quat_y),
        ],
    ]
    return (rotation, poses[3:6])


def to_world_rows(points, normals, poses, per_pose):
    rotation, translation = rotations(poses)

    def spread(values):
        return jnp.repeat(values, per_pose)[:, None]

    world_rows = []
    normal_rows = []
    for i in range(3):
        coeffs = [spread(rotation[i][j]) for j in range(3)]
        world_rows.append(
            coeffs[0] * points[:, 0]
            + coeffs[1] * points[:, 1]
            + coeffs[2] * points[:, 2]
            + spread(translation[i])
        )
        normal_rows.append(
            coeffs[0] * normals[:, 0] + coeffs[1] * normals[:, 1] + coeffs[2] * normals[:, 2]
        )
    return jnp.stack(world_rows + normal_rows, axis=0)


def _terms_kernel(from_cargo, n_band, xa_ref, tb_ref, map_ref, aux_ref, out_ref, *rest):
    if from_cargo:
        recv_ref, xt_ref, gt_ref, cs_ref, ret_ref, send_sems, recv_sems, own_sem = rest
    else:
        xt_ref, gt_ref, cs_ref = rest
    chunk = out_ref.shape[1]
    if from_cargo:
        peers = chunk // CAP
        height = 4 * CAP + 1
        for p in range(peers):
            for r in range(4):
                cs_ref[r, pl.ds(p * CAP, CAP), :] = xa_ref[pl.ds(p * height + r * CAP, CAP), :]
        idx = cs_ref[3].astype(jnp.int32)
        for c in range(3):
            xt_ref[c] = cs_ref[c].T
    else:
        idx = map_ref[...]
        for c in range(3):
            xt_ref[c] = xa_ref[c].T
    for c in range(6):
        picked = jnp.take_along_axis(tb_ref[c], idx, axis=1, mode="promise_in_bounds")
        gt_ref[c] = picked.T

    def col(q):
        return jnp.broadcast_to(aux_ref[q : q + 1, :], (8, chunk))

    def body(s, accs):
        rows = pl.ds(pl.multiple_of(s * 8, 8), 8)
        xa = [xt_ref[c, rows, :] for c in range(3)]
        xb = [gt_ref[c, rows, :] for c in range(3)]
        nb = [gt_ref[3 + c, rows, :] for c in range(3)]
        off = [xa[c] - xb[c] for c in range(3)]
        res = nb[0] * off[0] + nb[1] * off[1] + nb[2] * off[2]
        ja = [
            xa[1] * nb[2] - xa[2] * nb[1],
            xa[2] * nb[0] - xa[0] * nb[2],
            xa[0] * nb[1] - xa[1] * nb[0],
            nb[0],
            nb[1],
            nb[2],
        ]
        kb = [
            xb[1] * nb[2] - xb[2] * nb[1],
            xb[2] * nb[0] - xb[0] * nb[2],
            xb[0] * nb[1] - xb[1] * nb[0],
            nb[0],
            nb[1],
            nb[2],
        ]
        weights = [res]
        for v in range(2):
            sa = ja[0] * col(6 * v)
            sb = kb[0] * col(12 + 6 * v)
            for c in range(1, 6):
                sa = sa + ja[c] * col(6 * v + c)
                sb = sb + kb[c] * col(12 + 6 * v + c)
            weights.append(sa - sb)
        vals = []
        for w in weights:
            vals.extend([w * ja[c] for c in range(6)])
        for w in weights:
            vals.extend([w * kb[c] for c in range(3)])
        return tuple(a + v for a, v in zip(accs, vals))

    zero = jnp.zeros((8, chunk), jnp.float32)
    accs = lax.fori_loop(0, 128 // 8, body, (zero,) * N_QTY, unroll=8)
    valid = aux_ref[24:25, :]
    for q in range(N_QTY):
        out_ref[q : q + 1, :] = jnp.sum(accs[q], axis=0, keepdims=True) * valid
    out_ref[N_QTY:, :] = jnp.zeros((32 - N_QTY, chunk), jnp.float32)
    if from_cargo:
        _send_back(n_band, out_ref, recv_ref, ret_ref, send_sems, recv_sems, own_sem)


def _send_back(n_band, out_ref, recv_ref, ret_ref, send_sems, recv_sems, own_sem):
    chunk = out_ref.shape[1]
    peers = chunk // CAP
    total = recv_ref.shape[0]
    step = pl.program_id(0)
    last = pl.num_programs(0) - 1
    me = lax.axis_index("tile") * n_band + lax.axis_index("band")

    def device(p):
        return (p // n_band, p % n_band)

    def copy_to(p):
        return pltpu.make_async_remote_copy(
            src_ref=ret_ref.at[p],
            dst_ref=recv_ref.at[me],
            send_sem=send_sems.at[p],
            recv_sem=recv_sems.at[me],
            device_id=device(p),
            device_id_type=MESH,
        )

    def copy_from(p):
        return pltpu.make_async_remote_copy(
            src_ref=ret_ref.at[p],
            dst_ref=recv_ref.at[p],
            send_sem=send_sems.at[p],
            recv_sem=recv_sems.at[p],
            device_id=device(p),
            device_id_type=MESH,
        )

    own = pltpu.make_async_copy(ret_ref.at[me], recv_ref.at[me], own_sem)

    padded = jnp.concatenate([out_ref[...], jnp.zeros((128 - 32, chunk), jnp.float32)], axis=0)
    ret_ref[pl.ds(pl.multiple_of(step * peers, peers), peers)] = padded.T.reshape(peers, CAP, 128)

    hold = jnp.minimum(4, last)

    def start(q, carry):
        p = q

        @pl.when(p != me)
        def _():
            copy_to(p).start()

        @pl.when(p == me)
        def _():
            own.start()

        return carry

    @pl.when(step == hold)
    def _():
        lax.fori_loop(0, (hold + 1) * peers, start, 0)

    @pl.when(step > hold)
    def _():
        lax.fori_loop(step * peers, (step + 1) * peers, start, 0)

    @pl.when(step == last)
    def _():
        def finish(k, carry):
            p = lax.rem(me + k, total)
            copy_to(p).wait_send()
            copy_from(p).wait_recv()
            return carry

        lax.fori_loop(1, total, finish, 0)
        own.wait()


def pair_sums(xa, tb, maps, aux, n_band=1, chunk=128):
    pairs = tb.shape[1]
    from_cargo = maps is None
    scratch = [
        pltpu.VMEM((3, 128, chunk), jnp.float32),
        pltpu.VMEM((6, 128, chunk), jnp.float32),
        pltpu.VMEM((4, chunk, 128), jnp.float32),
    ]
    out_shape = jax.ShapeDtypeStruct((32, pairs), jnp.float32)
    out_specs = pl.BlockSpec((32, chunk), lambda i: (0, i))
    params = None
    if from_cargo:
        xa = xa.reshape(-1, 128)
        xa_spec = pl.BlockSpec((chunk // CAP * (4 * CAP + 1), 128), lambda i: (i, 0))
        maps = aux
        map_spec = pl.BlockSpec((8, 128), lambda i: (0, 0))
        peers = pairs // CAP
        out_shape = (out_shape, jax.ShapeDtypeStruct((peers, CAP, 128), jnp.float32))
        out_specs = (out_specs, pl.BlockSpec(memory_space=pl.ANY))
        scratch += [
            pltpu.VMEM((peers, CAP, 128), jnp.float32),
            pltpu.SemaphoreType.DMA((peers,)),
            pltpu.SemaphoreType.DMA((peers,)),
            pltpu.SemaphoreType.DMA(()),
        ]
        params = pltpu.CompilerParams(has_side_effects=True)
    else:
        xa_spec = pl.BlockSpec((3, chunk, 128), lambda i: (0, i, 0))
        map_spec = pl.BlockSpec((chunk, 128), lambda i: (i, 0))
    return pl.pallas_call(
        functools.partial(_terms_kernel, from_cargo, n_band),
        out_shape=out_shape,
        grid=(pairs // chunk,),
        in_specs=[
            xa_spec,
            pl.BlockSpec((6, chunk, 128), lambda i: (0, i, 0)),
            map_spec,
            pl.BlockSpec((32, chunk), lambda i: (0, i)),
        ],
        out_specs=out_specs,
        scratch_shapes=scratch,
        compiler_params=params,
    )(xa, tb, maps, aux)


def _cargo_kernel(xa_ref, map_ref, side_ref, out_ref):
    height = 4 * CAP + 1
    group = 8

    def body(g, carry):
        for q in range(group):
            p = g * group + q
            base = pl.multiple_of(g * (group * height), 8) + q * height
            slots = pl.ds(pl.multiple_of(p * CAP, CAP), CAP)
            for c in range(3):
                out_ref[pl.ds(base + c * CAP, CAP), :] = xa_ref[c, slots, :]
            out_ref[pl.ds(base + 3 * CAP, CAP), :] = map_ref[slots, :].astype(jnp.float32)
            out_ref[pl.ds(base + 4 * CAP, 1), :] = side_ref[pl.ds(p, 1), :]
        return carry

    lax.fori_loop(0, side_ref.shape[0] // group, body, 0)


def build_cargo(xa3, maps, side):
    slots = maps.shape[0]
    height = 4 * CAP + 1
    cargo = pl.pallas_call(
        _cargo_kernel,
        out_shape=jax.ShapeDtypeStruct((slots // CAP * height, 128), jnp.float32),
    )(xa3, maps, side)
    return cargo.reshape(slots // CAP, 1, height * 128)


def split_terms(out):
    sel = out[0:N_QTY].T
    ga = sel[:, 0:6] * (1.0 / 128)
    ha = sel[:, 6:18] * (1.0 / 4096)
    gb = -jnp.concatenate([sel[:, 18:21], sel[:, 3:6]], axis=1) * (1.0 / 128)
    hb0 = -jnp.concatenate([sel[:, 21:24], sel[:, 9:12]], axis=1) * (1.0 / 4096)
    hb1 = -jnp.concatenate([sel[:, 24:27], sel[:, 15:18]], axis=1) * (1.0 / 4096)
    return jnp.concatenate([ga, ha], axis=1), jnp.concatenate([gb, hb0, hb1], axis=1)


def _exchange_kernel(n_band, x_ref, out_ref, send_sems, recv_sems, own_sem):
    peers = x_ref.shape[0]
    me = lax.axis_index("tile") * n_band + lax.axis_index("band")

    def peer_of(k):
        p = lax.rem(me + k, peers)
        return p, (p // n_band, p % n_band)


    def greet(k, carry):
        _, dev = peer_of(k)
        pl.semaphore_signal(barrier, inc=1, device_id=dev, device_id_type=MESH)
        return carry

    lax.fori_loop(1, peers, greet, 0)
    pl.semaphore_wait(barrier, peers - 1)

    own = pltpu.make_async_copy(x_ref.at[me], out_ref.at[me], own_sem)
    own.start()

    def outgoing(k):
        p, dev = peer_of(k)
        return pltpu.make_async_remote_copy(
            src_ref=x_ref.at[p],
            dst_ref=out_ref.at[me],
            send_sem=send_sems.at[p],
            recv_sem=recv_sems.at[me],
            device_id=dev,
            device_id_type=MESH,
        )

    def incoming(k):
        p, dev = peer_of(k)
        return pltpu.make_async_remote_copy(
            src_ref=x_ref.at[p],
            dst_ref=out_ref.at[p],
            send_sem=send_sems.at[p],
            recv_sem=recv_sems.at[p],
            device_id=dev,
            device_id_type=MESH,
        )

    def start(k, carry):
        outgoing(k).start()
        return carry

    lax.fori_loop(1, peers, start, 0)

    def finish(k, carry):
        outgoing(k).wait_send()
        incoming(k).wait_recv()
        return carry

    lax.fori_loop(1, peers, finish, 0)
    own.wait()


def exchange(x, n_band, collective_id):
    peers = x.shape[0]
    return pl.pallas_call(
        functools.partial(_exchange_kernel, n_band),
        out_shape=jax.ShapeDtypeStruct(x.shape, x.dtype),
        in_specs=[pl.BlockSpec(memory_space=pl.ANY)],
        out_specs=pl.BlockSpec(memory_space=pl.ANY),
        scratch_shapes=[
            pltpu.SemaphoreType.DMA((peers,)),
            pltpu.SemaphoreType.DMA((peers,)),
            pltpu.SemaphoreType.DMA(()),
        ],
        compiler_params=pltpu.CompilerParams(collective_id=collective_id, has_side_effects=True),
    )(x)


def pick_rows(blocks, rows):
    onehot = (blocks[:, None] == jnp.arange(rows.shape[1], dtype=jnp.int32)[None, :]).astype(
        jnp.float32
    )
    return jnp.einsum("sb,cbk->csk", onehot, rows, precision=lax.Precision.HIGHEST)


def frag_sums(blocks, terms, frag_count):
    onehot = (blocks[:, None] // BF == jnp.arange(frag_count, dtype=jnp.int32)[None, :]).astype(
        jnp.float32
    )
    return jnp.dot(onehot.T, terms, precision=lax.Precision.HIGHEST)


def make_aux(dirs_a, dirs_b, valid):
    pairs = dirs_a.shape[0]
    return jnp.concatenate(
        [dirs_a.T, dirs_b.T, valid[None, :], jnp.zeros((32 - 25, pairs), jnp.float32)], axis=0
    )


def local(
    points,
    normals,
    poses,
    directions,
    local_pairs,
    local_maps,
    remote_src,
    remote_maps,
    remote_dst,
    counts,
):
    axes = ("tile", "band")
    n_band = lax.axis_size("band")
    frag_count = poses.shape[1]
    rows6 = to_world_rows(points, normals, poses, BF)
    frag_dirs = directions.reshape(12, frag_count).T
    peers = counts.shape[1]

    source_blocks = remote_src[0]
    valid = (
        (jnp.arange(CAP, dtype=jnp.int32)[None, :] < counts[0][:, None])
        .astype(jnp.float32)
        .reshape(-1)
    )
    frag_pick = (
        source_blocks[:, None] // BF == jnp.arange(frag_count, dtype=jnp.int32)[None, :]
    ).astype(jnp.float32)
    dirs_send = jnp.dot(frag_pick, frag_dirs, precision=lax.Precision.HIGHEST)
    side = jnp.concatenate([dirs_send, valid[:, None]], axis=1)
    side = side.reshape(peers, CAP * 13)
    side = jnp.concatenate([side, jnp.zeros((peers, 128 - CAP * 13), jnp.float32)], axis=1)
    cargo = build_cargo(pick_rows(source_blocks, rows6[0:3]), remote_maps[0], side)
    arrived = lax.all_to_all(cargo, axes, split_axis=0, concat_axis=0, tiled=True)

    src_l = local_pairs[0]
    tgt_l = local_pairs[1]
    ones = jnp.ones((src_l.shape[0],), jnp.float32)
    out_l = pair_sums(
        pick_rows(src_l, rows6[0:3]),
        pick_rows(tgt_l, rows6),
        local_maps,
        make_aux(frag_dirs[src_l // BF], frag_dirs[tgt_l // BF], ones),
    )
    local_a, local_b = split_terms(out_l)

    target_blocks = remote_dst[0]
    side_in = arrived[:, 0, CAP * 4 * 128 : CAP * 4 * 128 + CAP * 13].reshape(peers * CAP, 13)
    out_r, back = pair_sums(
        arrived,
        pick_rows(target_blocks, rows6),
        None,
        make_aux(side_in[:, 0:12], frag_dirs[target_blocks // BF], side_in[:, 12]),
        n_band,
    )
    unused, remote_b = split_terms(out_r)
    returned, unused = split_terms(back.reshape(peers * CAP, 128)[:, 0:32].T)

    totals = frag_sums(src_l, local_a, frag_count) + frag_sums(tgt_l, local_b, frag_count)
    totals = (
        totals
        + frag_sums(target_blocks, remote_b, frag_count)
        + frag_sums(source_blocks, returned, frag_count)
    )
    gradient = totals[:, 0:6].T
    hess_products = totals[:, 6:18].T.reshape(2, 6, frag_count)
    return (gradient, hess_products)


def solution(mesh):
    placed = (
        P(("tile", "band"), None, None),
        P(("tile", "band"), None, None),
        P(None, ("tile", "band")),
        P(None, None, ("tile", "band")),
        P(None, ("tile", "band")),
        P(("tile", "band"), None),
        P(("tile", "band"), None),
        P(("tile", "band"), None, None),
        P(("tile", "band"), None),
        P(("tile", "band"), None),
    )
    return jax.shard_map(
        local,
        mesh=mesh,
        in_specs=placed,
        out_specs=(P(None, ("tile", "band")), P(None, None, ("tile", "band"))),
        check_vma=False,
    )
```

```python
import functools

import jax
import jax.numpy as jnp
from jax import lax
from jax.experimental import pallas as pl
from jax.experimental.pallas import tpu as pltpu
from jax.sharding import PartitionSpec as P

BF = 32
CAP = 8
N_QTY = 27
MESH = pl.DeviceIdType.MESH


def rotations(poses):
    half_angle = poses[0:3] * 0.5
    inverse = 1.0 / jnp.sqrt(
        1.0
        + half_angle[0] * half_angle[0]
        + half_angle[1] * half_angle[1]
        + half_angle[2] * half_angle[2]
    )
    quat_x = half_angle[0] * inverse
    quat_y = half_angle[1] * inverse
    quat_z = half_angle[2] * inverse
    rotation = [
        [
            1.0 - 2.0 * (quat_y * quat_y + quat_z * quat_z),
            2.0 * (quat_x * quat_y - inverse * quat_z),
            2.0 * (quat_x * quat_z + inverse * quat_y),
        ],
        [
            2.0 * (quat_x * quat_y + inverse * quat_z),
            1.0 - 2.0 * (quat_x * quat_x + quat_z * quat_z),
            2.0 * (quat_y * quat_z - inverse * quat_x),
        ],
        [
            2.0 * (quat_x * quat_z - inverse * quat_y),
            2.0 * (quat_y * quat_z + inverse * quat_x),
            1.0 - 2.0 * (quat_x * quat_x + quat_y * quat_y),
        ],
    ]
    return (rotation, poses[3:6])


def to_world_rows(points, normals, poses, per_pose):
    rotation, translation = rotations(poses)

    def spread(values):
        return jnp.repeat(values, per_pose)[:, None]

    world_rows = []
    normal_rows = []
    for i in range(3):
        coeffs = [spread(rotation[i][j]) for j in range(3)]
        world_rows.append(
            coeffs[0] * points[:, 0]
            + coeffs[1] * points[:, 1]
            + coeffs[2] * points[:, 2]
            + spread(translation[i])
        )
        normal_rows.append(
            coeffs[0] * normals[:, 0] + coeffs[1] * normals[:, 1] + coeffs[2] * normals[:, 2]
        )
    return jnp.stack(world_rows + normal_rows, axis=0)


def _terms_kernel(from_cargo, n_band, xa_ref, tb_ref, map_ref, aux_ref, out_ref, *rest):
    if from_cargo:
        recv_ref, xt_ref, gt_ref, cs_ref, ret_ref, send_sems, recv_sems, own_sem = rest
    else:
        xt_ref, gt_ref, cs_ref = rest
    chunk = out_ref.shape[1]
    if from_cargo:
        peers = chunk // CAP
        height = 4 * CAP + 1
        for p in range(peers):
            for r in range(4):
                cs_ref[r, pl.ds(p * CAP, CAP), :] = xa_ref[pl.ds(p * height + r * CAP, CAP), :]
        idx = cs_ref[3].astype(jnp.int32)
        for c in range(3):
            xt_ref[c] = cs_ref[c].T
    else:
        idx = map_ref[...]
        for c in range(3):
            xt_ref[c] = xa_ref[c].T
    for c in range(6):
        picked = jnp.take_along_axis(tb_ref[c], idx, axis=1, mode="promise_in_bounds")
        gt_ref[c] = picked.T

    def col(q):
        return jnp.broadcast_to(aux_ref[q : q + 1, :], (8, chunk))

    def body(s, accs):
        rows = pl.ds(pl.multiple_of(s * 8, 8), 8)
        xa = [xt_ref[c, rows, :] for c in range(3)]
        xb = [gt_ref[c, rows, :] for c in range(3)]
        nb = [gt_ref[3 + c, rows, :] for c in range(3)]
        off = [xa[c] - xb[c] for c in range(3)]
        res = nb[0] * off[0] + nb[1] * off[1] + nb[2] * off[2]
        ja = [
            xa[1] * nb[2] - xa[2] * nb[1],
            xa[2] * nb[0] - xa[0] * nb[2],
            xa[0] * nb[1] - xa[1] * nb[0],
            nb[0],
            nb[1],
            nb[2],
        ]
        kb = [
            xb[1] * nb[2] - xb[2] * nb[1],
            xb[2] * nb[0] - xb[0] * nb[2],
            xb[0] * nb[1] - xb[1] * nb[0],
            nb[0],
            nb[1],
            nb[2],
        ]
        weights = [res]
        for v in range(2):
            sa = ja[0] * col(6 * v)
            sb = kb[0] * col(12 + 6 * v)
            for c in range(1, 6):
                sa = sa + ja[c] * col(6 * v + c)
                sb = sb + kb[c] * col(12 + 6 * v + c)
            weights.append(sa - sb)
        vals = []
        for w in weights:
            vals.extend([w * ja[c] for c in range(6)])
        for w in weights:
            vals.extend([w * kb[c] for c in range(3)])
        return tuple(a + v for a, v in zip(accs, vals))

    zero = jnp.zeros((8, chunk), jnp.float32)
    accs = lax.fori_loop(0, 128 // 8, body, (zero,) * N_QTY, unroll=8)
    valid = aux_ref[24:25, :]
    for q in range(N_QTY):
        out_ref[q : q + 1, :] = jnp.sum(accs[q], axis=0, keepdims=True) * valid
    out_ref[N_QTY:, :] = jnp.zeros((32 - N_QTY, chunk), jnp.float32)
    if from_cargo:
        _send_back(n_band, out_ref, recv_ref, ret_ref, send_sems, recv_sems, own_sem)


def _send_back(n_band, out_ref, recv_ref, ret_ref, send_sems, recv_sems, own_sem):
    chunk = out_ref.shape[1]
    peers = chunk // CAP
    total = recv_ref.shape[0]
    step = pl.program_id(0)
    last = pl.num_programs(0) - 1
    me = lax.axis_index("tile") * n_band + lax.axis_index("band")
    barrier = pltpu.get_barrier_semaphore()

    def device(p):
        return (p // n_band, p % n_band)

    def copy_to(p):
        return pltpu.make_async_remote_copy(
            src_ref=ret_ref.at[p],
            dst_ref=recv_ref.at[me],
            send_sem=send_sems.at[p],
            recv_sem=recv_sems.at[me],
            device_id=device(p),
            device_id_type=MESH,
        )

    def copy_from(p):
        return pltpu.make_async_remote_copy(
            src_ref=ret_ref.at[p],
            dst_ref=recv_ref.at[p],
            send_sem=send_sems.at[p],
            recv_sem=recv_sems.at[p],
            device_id=device(p),
            device_id_type=MESH,
        )

    own = pltpu.make_async_copy(ret_ref.at[me], recv_ref.at[me], own_sem)

    @pl.when(step == 0)
    def _():
        def greet(k, carry):
            p = lax.rem(me + k, total)
            pl.semaphore_signal(barrier, inc=1, device_id=device(p), device_id_type=MESH)
            return carry

        lax.fori_loop(1, total, greet, 0)

    padded = jnp.concatenate([out_ref[...], jnp.zeros((128 - 32, chunk), jnp.float32)], axis=0)
    ret_ref[pl.ds(pl.multiple_of(step * peers, peers), peers)] = padded.T.reshape(peers, CAP, 128)

    hold = jnp.minimum(4, last)

    @pl.when(step == hold)
    def _():
        pl.semaphore_wait(barrier, total - 1)

    def start(q, carry):
        p = q

        @pl.when(p != me)
        def _():
            copy_to(p).start()

        @pl.when(p == me)
        def _():
            own.start()

        return carry

    @pl.when(step == hold)
    def _():
        lax.fori_loop(0, (hold + 1) * peers, start, 0)

    @pl.when(step > hold)
    def _():
        lax.fori_loop(step * peers, (step + 1) * peers, start, 0)

    @pl.when(step == last)
    def _():
        def finish(k, carry):
            p = lax.rem(me + k, total)
            copy_to(p).wait_send()
            copy_from(p).wait_recv()
            return carry

        lax.fori_loop(1, total, finish, 0)
        own.wait()


def pair_sums(xa, tb, maps, aux, n_band=1, chunk=128):
    pairs = tb.shape[1]
    from_cargo = maps is None
    scratch = [
        pltpu.VMEM((3, 128, chunk), jnp.float32),
        pltpu.VMEM((6, 128, chunk), jnp.float32),
        pltpu.VMEM((4, chunk, 128), jnp.float32),
    ]
    out_shape = jax.ShapeDtypeStruct((32, pairs), jnp.float32)
    out_specs = pl.BlockSpec((32, chunk), lambda i: (0, i))
    params = None
    if from_cargo:
        xa = xa.reshape(-1, 128)
        xa_spec = pl.BlockSpec((chunk // CAP * (4 * CAP + 1), 128), lambda i: (i, 0))
        maps = aux
        map_spec = pl.BlockSpec((8, 128), lambda i: (0, 0))
        peers = pairs // CAP
        out_shape = (out_shape, jax.ShapeDtypeStruct((peers, CAP, 128), jnp.float32))
        out_specs = (out_specs, pl.BlockSpec(memory_space=pl.ANY))
        scratch += [
            pltpu.VMEM((peers, CAP, 128), jnp.float32),
            pltpu.SemaphoreType.DMA((peers,)),
            pltpu.SemaphoreType.DMA((peers,)),
            pltpu.SemaphoreType.DMA(()),
        ]
        params = pltpu.CompilerParams(collective_id=0, has_side_effects=True)
    else:
        xa_spec = pl.BlockSpec((3, chunk, 128), lambda i: (0, i, 0))
        map_spec = pl.BlockSpec((chunk, 128), lambda i: (i, 0))
    return pl.pallas_call(
        functools.partial(_terms_kernel, from_cargo, n_band),
        out_shape=out_shape,
        grid=(pairs // chunk,),
        in_specs=[
            xa_spec,
            pl.BlockSpec((6, chunk, 128), lambda i: (0, i, 0)),
            map_spec,
            pl.BlockSpec((32, chunk), lambda i: (0, i)),
        ],
        out_specs=out_specs,
        scratch_shapes=scratch,
        compiler_params=params,
    )(xa, tb, maps, aux)


def _cargo_kernel(xa_ref, map_ref, side_ref, out_ref):
    height = 4 * CAP + 1
    group = 8

    def body(g, carry):
        for q in range(group):
            p = g * group + q
            base = pl.multiple_of(g * (group * height), 8) + q * height
            slots = pl.ds(pl.multiple_of(p * CAP, CAP), CAP)
            for c in range(3):
                out_ref[pl.ds(base + c * CAP, CAP), :] = xa_ref[c, slots, :]
            out_ref[pl.ds(base + 3 * CAP, CAP), :] = map_ref[slots, :].astype(jnp.float32)
            out_ref[pl.ds(base + 4 * CAP, 1), :] = side_ref[pl.ds(p, 1), :]
        return carry

    lax.fori_loop(0, side_ref.shape[0] // group, body, 0)


def build_cargo(xa3, maps, side):
    slots = maps.shape[0]
    height = 4 * CAP + 1
    chunk = slots // 4
    peers = chunk // CAP
    cargo = pl.pallas_call(
        _cargo_kernel,
        out_shape=jax.ShapeDtypeStruct((slots // CAP * height, 128), jnp.float32),
        grid=(slots // chunk,),
        in_specs=[
            pl.BlockSpec((3, chunk, 128), lambda i: (0, i, 0)),
            pl.BlockSpec((chunk, 128), lambda i: (i, 0)),
            pl.BlockSpec((peers, 128), lambda i: (i, 0)),
        ],
        out_specs=pl.BlockSpec((peers * height, 128), lambda i: (i, 0)),
    )(xa3, maps, side)
    return cargo.reshape(slots // CAP, 1, height * 128)


def split_terms(out):
    sel = out[0:N_QTY].T
    ga = sel[:, 0:6] * (1.0 / 128)
    ha = sel[:, 6:18] * (1.0 / 4096)
    gb = -jnp.concatenate([sel[:, 18:21], sel[:, 3:6]], axis=1) * (1.0 / 128)
    hb0 = -jnp.concatenate([sel[:, 21:24], sel[:, 9:12]], axis=1) * (1.0 / 4096)
    hb1 = -jnp.concatenate([sel[:, 24:27], sel[:, 15:18]], axis=1) * (1.0 / 4096)
    return jnp.concatenate([ga, ha], axis=1), jnp.concatenate([gb, hb0, hb1], axis=1)


def _exchange_kernel(n_band, x_ref, out_ref, send_sems, recv_sems, own_sem):
    peers = x_ref.shape[0]
    me = lax.axis_index("tile") * n_band + lax.axis_index("band")

    def peer_of(k):
        p = lax.rem(me + k, peers)
        return p, (p // n_band, p % n_band)

    barrier = pltpu.get_barrier_semaphore()

    def greet(k, carry):
        _, dev = peer_of(k)
        pl.semaphore_signal(barrier, inc=1, device_id=dev, device_id_type=MESH)
        return carry

    lax.fori_loop(1, peers, greet, 0)
    pl.semaphore_wait(barrier, peers - 1)

    own = pltpu.make_async_copy(x_ref.at[me], out_ref.at[me], own_sem)
    own.start()

    def outgoing(k):
        p, dev = peer_of(k)
        return pltpu.make_async_remote_copy(
            src_ref=x_ref.at[p],
            dst_ref=out_ref.at[me],
            send_sem=send_sems.at[p],
            recv_sem=recv_sems.at[me],
            device_id=dev,
            device_id_type=MESH,
        )

    def incoming(k):
        p, dev = peer_of(k)
        return pltpu.make_async_remote_copy(
            src_ref=x_ref.at[p],
            dst_ref=out_ref.at[p],
            send_sem=send_sems.at[p],
            recv_sem=recv_sems.at[p],
            device_id=dev,
            device_id_type=MESH,
        )

    def start(k, carry):
        outgoing(k).start()
        return carry

    lax.fori_loop(1, peers, start, 0)

    def finish(k, carry):
        outgoing(k).wait_send()
        incoming(k).wait_recv()
        return carry

    lax.fori_loop(1, peers, finish, 0)
    own.wait()


def exchange(x, n_band, collective_id):
    peers = x.shape[0]
    return pl.pallas_call(
        functools.partial(_exchange_kernel, n_band),
        out_shape=jax.ShapeDtypeStruct(x.shape, x.dtype),
        in_specs=[pl.BlockSpec(memory_space=pl.ANY)],
        out_specs=pl.BlockSpec(memory_space=pl.ANY),
        scratch_shapes=[
            pltpu.SemaphoreType.DMA((peers,)),
            pltpu.SemaphoreType.DMA((peers,)),
            pltpu.SemaphoreType.DMA(()),
        ],
        compiler_params=pltpu.CompilerParams(collective_id=collective_id, has_side_effects=True),
    )(x)


def pick_rows(blocks, rows):
    onehot = (blocks[:, None] == jnp.arange(rows.shape[1], dtype=jnp.int32)[None, :]).astype(
        jnp.float32
    )
    return jnp.einsum("sb,cbk->csk", onehot, rows, precision=lax.Precision.HIGHEST)


def frag_sums(blocks, terms, frag_count):
    onehot = (blocks[:, None] // BF == jnp.arange(frag_count, dtype=jnp.int32)[None, :]).astype(
        jnp.float32
    )
    return jnp.dot(onehot.T, terms, precision=lax.Precision.HIGHEST)


def make_aux(dirs_a, dirs_b, valid):
    pairs = dirs_a.shape[0]
    return jnp.concatenate(
        [dirs_a.T, dirs_b.T, valid[None, :], jnp.zeros((32 - 25, pairs), jnp.float32)], axis=0
    )


def local(
    points,
    normals,
    poses,
    directions,
    local_pairs,
    local_maps,
    remote_src,
    remote_maps,
    remote_dst,
    counts,
):
    axes = ("tile", "band")
    n_band = lax.axis_size("band")
    frag_count = poses.shape[1]
    rows6 = to_world_rows(points, normals, poses, BF)
    frag_dirs = directions.reshape(12, frag_count).T
    peers = counts.shape[1]

    source_blocks = remote_src[0]
    valid = (
        (jnp.arange(CAP, dtype=jnp.int32)[None, :] < counts[0][:, None])
        .astype(jnp.float32)
        .reshape(-1)
    )
    frag_pick = (
        source_blocks[:, None] // BF == jnp.arange(frag_count, dtype=jnp.int32)[None, :]
    ).astype(jnp.float32)
    dirs_send = jnp.dot(frag_pick, frag_dirs, precision=lax.Precision.HIGHEST)
    side = jnp.concatenate([dirs_send, valid[:, None]], axis=1)
    side = side.reshape(peers, CAP * 13)
    side = jnp.concatenate([side, jnp.zeros((peers, 128 - CAP * 13), jnp.float32)], axis=1)
    cargo = build_cargo(pick_rows(source_blocks, rows6[0:3]), remote_maps[0], side)
    arrived = lax.all_to_all(cargo, axes, split_axis=0, concat_axis=0, tiled=True)

    src_l = local_pairs[0]
    tgt_l = local_pairs[1]
    ones = jnp.ones((src_l.shape[0],), jnp.float32)
    out_l = pair_sums(
        pick_rows(src_l, rows6[0:3]),
        pick_rows(tgt_l, rows6),
        local_maps,
        make_aux(frag_dirs[src_l // BF], frag_dirs[tgt_l // BF], ones),
    )
    local_a, local_b = split_terms(out_l)

    target_blocks = remote_dst[0]
    side_in = arrived[:, 0, CAP * 4 * 128 : CAP * 4 * 128 + CAP * 13].reshape(peers * CAP, 13)
    out_r, back = pair_sums(
        arrived,
        pick_rows(target_blocks, rows6),
        None,
        make_aux(side_in[:, 0:12], frag_dirs[target_blocks // BF], side_in[:, 12]),
        n_band,
    )
    unused, remote_b = split_terms(out_r)
    returned, unused = split_terms(back.reshape(peers * CAP, 128)[:, 0:32].T)

    totals = frag_sums(src_l, local_a, frag_count) + frag_sums(tgt_l, local_b, frag_count)
    totals = (
        totals
        + frag_sums(target_blocks, remote_b, frag_count)
        + frag_sums(source_blocks, returned, frag_count)
    )
    gradient = totals[:, 0:6].T
    hess_products = totals[:, 6:18].T.reshape(2, 6, frag_count)
    return (gradient, hess_products)


def solution(mesh):
    placed = (
        P(("tile", "band"), None, None),
        P(("tile", "band"), None, None),
        P(None, ("tile", "band")),
        P(None, None, ("tile", "band")),
        P(None, ("tile", "band")),
        P(("tile", "band"), None),
        P(("tile", "band"), None),
        P(("tile", "band"), None, None),
        P(("tile", "band"), None),
        P(("tile", "band"), None),
    )
    return jax.shard_map(
        local,
        mesh=mesh,
        in_specs=placed,
        out_specs=(P(None, ("tile", "band")), P(None, None, ("tile", "band"))),
        check_vma=False,
    )
```

```python
import functools

import jax
import jax.numpy as jnp
from jax import lax
from jax.experimental import pallas as pl
from jax.experimental.pallas import tpu as pltpu
from jax.sharding import PartitionSpec as P

BF = 32
CAP = 8
N_QTY = 27
MESH = pl.DeviceIdType.MESH


def rotations(poses):
    half_angle = poses[0:3] * 0.5
    inverse = 1.0 / jnp.sqrt(
        1.0
        + half_angle[0] * half_angle[0]
        + half_angle[1] * half_angle[1]
        + half_angle[2] * half_angle[2]
    )
    quat_x = half_angle[0] * inverse
    quat_y = half_angle[1] * inverse
    quat_z = half_angle[2] * inverse
    rotation = [
        [
            1.0 - 2.0 * (quat_y * quat_y + quat_z * quat_z),
            2.0 * (quat_x * quat_y - inverse * quat_z),
            2.0 * (quat_x * quat_z + inverse * quat_y),
        ],
        [
            2.0 * (quat_x * quat_y + inverse * quat_z),
            1.0 - 2.0 * (quat_x * quat_x + quat_z * quat_z),
            2.0 * (quat_y * quat_z - inverse * quat_x),
        ],
        [
            2.0 * (quat_x * quat_z - inverse * quat_y),
            2.0 * (quat_y * quat_z + inverse * quat_x),
            1.0 - 2.0 * (quat_x * quat_x + quat_y * quat_y),
        ],
    ]
    return (rotation, poses[3:6])


def to_world_rows(points, normals, poses, per_pose):
    rotation, translation = rotations(poses)

    def spread(values):
        return jnp.repeat(values, per_pose)[:, None]

    world_rows = []
    normal_rows = []
    for i in range(3):
        coeffs = [spread(rotation[i][j]) for j in range(3)]
        world_rows.append(
            coeffs[0] * points[:, 0]
            + coeffs[1] * points[:, 1]
            + coeffs[2] * points[:, 2]
            + spread(translation[i])
        )
        normal_rows.append(
            coeffs[0] * normals[:, 0] + coeffs[1] * normals[:, 1] + coeffs[2] * normals[:, 2]
        )
    return jnp.stack(world_rows + normal_rows, axis=0)


def _terms_kernel(from_cargo, n_band, xa_ref, tb_ref, map_ref, aux_ref, out_ref, *rest):
    if from_cargo:
        recv_ref, xt_ref, gt_ref, cs_ref, ret_ref, send_sems, recv_sems, own_sem = rest
        _greet(n_band, recv_ref.shape[0])
    else:
        xt_ref, gt_ref, cs_ref = rest
    chunk = out_ref.shape[1]
    if from_cargo:
        peers = chunk // CAP
        height = 4 * CAP + 1
        for p in range(peers):
            for r in range(4):
                cs_ref[r, pl.ds(p * CAP, CAP), :] = xa_ref[pl.ds(p * height + r * CAP, CAP), :]
        idx = cs_ref[3].astype(jnp.int32)
        for c in range(3):
            xt_ref[c] = cs_ref[c].T
    else:
        idx = map_ref[...]
        for c in range(3):
            xt_ref[c] = xa_ref[c].T
    for c in range(6):
        picked = jnp.take_along_axis(tb_ref[c], idx, axis=1, mode="promise_in_bounds")
        gt_ref[c] = picked.T

    def col(q):
        return jnp.broadcast_to(aux_ref[q : q + 1, :], (8, chunk))

    def body(s, accs):
        rows = pl.ds(pl.multiple_of(s * 8, 8), 8)
        xa = [xt_ref[c, rows, :] for c in range(3)]
        xb = [gt_ref[c, rows, :] for c in range(3)]
        nb = [gt_ref[3 + c, rows, :] for c in range(3)]
        off = [xa[c] - xb[c] for c in range(3)]
        res = nb[0] * off[0] + nb[1] * off[1] + nb[2] * off[2]
        ja = [
            xa[1] * nb[2] - xa[2] * nb[1],
            xa[2] * nb[0] - xa[0] * nb[2],
            xa[0] * nb[1] - xa[1] * nb[0],
            nb[0],
            nb[1],
            nb[2],
        ]
        kb = [
            xb[1] * nb[2] - xb[2] * nb[1],
            xb[2] * nb[0] - xb[0] * nb[2],
            xb[0] * nb[1] - xb[1] * nb[0],
            nb[0],
            nb[1],
            nb[2],
        ]
        weights = [res]
        for v in range(2):
            sa = ja[0] * col(6 * v)
            sb = kb[0] * col(12 + 6 * v)
            for c in range(1, 6):
                sa = sa + ja[c] * col(6 * v + c)
                sb = sb + kb[c] * col(12 + 6 * v + c)
            weights.append(sa - sb)
        vals = []
        for w in weights:
            vals.extend([w * ja[c] for c in range(6)])
        for w in weights:
            vals.extend([w * kb[c] for c in range(3)])
        return tuple(a + v for a, v in zip(accs, vals))

    zero = jnp.zeros((8, chunk), jnp.float32)
    accs = lax.fori_loop(0, 128 // 8, body, (zero,) * N_QTY, unroll=8)
    valid = aux_ref[24:25, :]
    for q in range(N_QTY):
        out_ref[q : q + 1, :] = jnp.sum(accs[q], axis=0, keepdims=True) * valid
    out_ref[N_QTY:, :] = jnp.zeros((32 - N_QTY, chunk), jnp.float32)
    if from_cargo:
        _send_back(n_band, out_ref, recv_ref, ret_ref, send_sems, recv_sems, own_sem)


def _greet(n_band, total):
    me = lax.axis_index("tile") * n_band + lax.axis_index("band")
    barrier = pltpu.get_barrier_semaphore()

    @pl.when(pl.program_id(0) == 0)
    def _():
        def greet(k, carry):
            p = lax.rem(me + k, total)
            pl.semaphore_signal(
                barrier, inc=1, device_id=(p // n_band, p % n_band), device_id_type=MESH
            )
            return carry

        lax.fori_loop(1, total, greet, 0)


def _send_back(n_band, out_ref, recv_ref, ret_ref, send_sems, recv_sems, own_sem):
    chunk = out_ref.shape[1]
    peers = chunk // CAP
    total = recv_ref.shape[0]
    step = pl.program_id(0)
    last = pl.num_programs(0) - 1
    me = lax.axis_index("tile") * n_band + lax.axis_index("band")
    barrier = pltpu.get_barrier_semaphore()

    def device(p):
        return (p // n_band, p % n_band)

    def copy_to(p):
        return pltpu.make_async_remote_copy(
            src_ref=ret_ref.at[p],
            dst_ref=recv_ref.at[me],
            send_sem=send_sems.at[p],
            recv_sem=recv_sems.at[me],
            device_id=device(p),
            device_id_type=MESH,
        )

    def copy_from(p):
        return pltpu.make_async_remote_copy(
            src_ref=ret_ref.at[p],
            dst_ref=recv_ref.at[p],
            send_sem=send_sems.at[p],
            recv_sem=recv_sems.at[p],
            device_id=device(p),
            device_id_type=MESH,
        )

    own = pltpu.make_async_copy(ret_ref.at[me], recv_ref.at[me], own_sem)

    padded = jnp.concatenate([out_ref[...], jnp.zeros((128 - 32, chunk), jnp.float32)], axis=0)
    ret_ref[pl.ds(pl.multiple_of(step * peers, peers), peers)] = padded.T.reshape(peers, CAP, 128)

    hold = jnp.minimum(4, last)

    @pl.when(step == hold)
    def _():
        pl.semaphore_wait(barrier, total - 1)

    def start(q, carry):
        p = q

        @pl.when(p != me)
        def _():
            copy_to(p).start()

        @pl.when(p == me)
        def _():
            own.start()

        return carry

    @pl.when(step == hold)
    def _():
        lax.fori_loop(0, (hold + 1) * peers, start, 0)

    @pl.when(step > hold)
    def _():
        lax.fori_loop(step * peers, (step + 1) * peers, start, 0)

    @pl.when(step == last)
    def _():
        def finish(k, carry):
            p = lax.rem(me + k, total)
            copy_to(p).wait_send()
            copy_from(p).wait_recv()
            return carry

        lax.fori_loop(1, total, finish, 0)
        own.wait()


def pair_sums(xa, tb, maps, aux, n_band=1, chunk=128):
    pairs = tb.shape[1]
    from_cargo = maps is None
    scratch = [
        pltpu.VMEM((3, 128, chunk), jnp.float32),
        pltpu.VMEM((6, 128, chunk), jnp.float32),
        pltpu.VMEM((4, chunk, 128), jnp.float32),
    ]
    out_shape = jax.ShapeDtypeStruct((32, pairs), jnp.float32)
    out_specs = pl.BlockSpec((32, chunk), lambda i: (0, i))
    params = None
    if from_cargo:
        xa = xa.reshape(-1, 128)
        xa_spec = pl.BlockSpec((chunk // CAP * (4 * CAP + 1), 128), lambda i: (i, 0))
        maps = aux
        map_spec = pl.BlockSpec((8, 128), lambda i: (0, 0))
        peers = pairs // CAP
        out_shape = (out_shape, jax.ShapeDtypeStruct((peers, CAP, 128), jnp.float32))
        out_specs = (out_specs, pl.BlockSpec(memory_space=pl.ANY))
        scratch += [
            pltpu.VMEM((peers, CAP, 128), jnp.float32),
            pltpu.SemaphoreType.DMA((peers,)),
            pltpu.SemaphoreType.DMA((peers,)),
            pltpu.SemaphoreType.DMA(()),
        ]
        params = pltpu.CompilerParams(collective_id=0, has_side_effects=True)
    else:
        xa_spec = pl.BlockSpec((3, chunk, 128), lambda i: (0, i, 0))
        map_spec = pl.BlockSpec((chunk, 128), lambda i: (i, 0))
    return pl.pallas_call(
        functools.partial(_terms_kernel, from_cargo, n_band),
        out_shape=out_shape,
        grid=(pairs // chunk,),
        in_specs=[
            xa_spec,
            pl.BlockSpec((6, chunk, 128), lambda i: (0, i, 0)),
            map_spec,
            pl.BlockSpec((32, chunk), lambda i: (0, i)),
        ],
        out_specs=out_specs,
        scratch_shapes=scratch,
        compiler_params=params,
    )(xa, tb, maps, aux)


def _cargo_kernel(xa_ref, map_ref, side_ref, out_ref):
    height = 4 * CAP + 1
    group = 8

    def body(g, carry):
        for q in range(group):
            p = g * group + q
            base = pl.multiple_of(g * (group * height), 8) + q * height
            slots = pl.ds(pl.multiple_of(p * CAP, CAP), CAP)
            for c in range(3):
                out_ref[pl.ds(base + c * CAP, CAP), :] = xa_ref[c, slots, :]
            out_ref[pl.ds(base + 3 * CAP, CAP), :] = map_ref[slots, :].astype(jnp.float32)
            out_ref[pl.ds(base + 4 * CAP, 1), :] = side_ref[pl.ds(p, 1), :]
        return carry

    lax.fori_loop(0, side_ref.shape[0] // group, body, 0)


def build_cargo(xa3, maps, side):
    slots = maps.shape[0]
    height = 4 * CAP + 1
    cargo = pl.pallas_call(
        _cargo_kernel,
        out_shape=jax.ShapeDtypeStruct((slots // CAP * height, 128), jnp.float32),
    )(xa3, maps, side)
    return cargo.reshape(slots // CAP, 1, height * 128)


def split_terms(out):
    sel = out[0:N_QTY].T
    ga = sel[:, 0:6] * (1.0 / 128)
    ha = sel[:, 6:18] * (1.0 / 4096)
    gb = -jnp.concatenate([sel[:, 18:21], sel[:, 3:6]], axis=1) * (1.0 / 128)
    hb0 = -jnp.concatenate([sel[:, 21:24], sel[:, 9:12]], axis=1) * (1.0 / 4096)
    hb1 = -jnp.concatenate([sel[:, 24:27], sel[:, 15:18]], axis=1) * (1.0 / 4096)
    return jnp.concatenate([ga, ha], axis=1), jnp.concatenate([gb, hb0, hb1], axis=1)


def _exchange_kernel(n_band, x_ref, out_ref, send_sems, recv_sems, own_sem):
    peers = x_ref.shape[0]
    me = lax.axis_index("tile") * n_band + lax.axis_index("band")

    def peer_of(k):
        p = lax.rem(me + k, peers)
        return p, (p // n_band, p % n_band)

    barrier = pltpu.get_barrier_semaphore()

    def greet(k, carry):
        _, dev = peer_of(k)
        pl.semaphore_signal(barrier, inc=1, device_id=dev, device_id_type=MESH)
        return carry

    lax.fori_loop(1, peers, greet, 0)
    pl.semaphore_wait(barrier, peers - 1)

    own = pltpu.make_async_copy(x_ref.at[me], out_ref.at[me], own_sem)
    own.start()

    def outgoing(k):
        p, dev = peer_of(k)
        return pltpu.make_async_remote_copy(
            src_ref=x_ref.at[p],
            dst_ref=out_ref.at[me],
            send_sem=send_sems.at[p],
            recv_sem=recv_sems.at[me],
            device_id=dev,
            device_id_type=MESH,
        )

    def incoming(k):
        p, dev = peer_of(k)
        return pltpu.make_async_remote_copy(
            src_ref=x_ref.at[p],
            dst_ref=out_ref.at[p],
            send_sem=send_sems.at[p],
            recv_sem=recv_sems.at[p],
            device_id=dev,
            device_id_type=MESH,
        )

    def start(k, carry):
        outgoing(k).start()
        return carry

    lax.fori_loop(1, peers, start, 0)

    def finish(k, carry):
        outgoing(k).wait_send()
        incoming(k).wait_recv()
        return carry

    lax.fori_loop(1, peers, finish, 0)
    own.wait()


def exchange(x, n_band, collective_id):
    peers = x.shape[0]
    return pl.pallas_call(
        functools.partial(_exchange_kernel, n_band),
        out_shape=jax.ShapeDtypeStruct(x.shape, x.dtype),
        in_specs=[pl.BlockSpec(memory_space=pl.ANY)],
        out_specs=pl.BlockSpec(memory_space=pl.ANY),
        scratch_shapes=[
            pltpu.SemaphoreType.DMA((peers,)),
            pltpu.SemaphoreType.DMA((peers,)),
            pltpu.SemaphoreType.DMA(()),
        ],
        compiler_params=pltpu.CompilerParams(collective_id=collective_id, has_side_effects=True),
    )(x)


def pick_rows(blocks, rows):
    onehot = (blocks[:, None] == jnp.arange(rows.shape[1], dtype=jnp.int32)[None, :]).astype(
        jnp.float32
    )
    return jnp.einsum("sb,cbk->csk", onehot, rows, precision=lax.Precision.HIGHEST)


def frag_sums(blocks, terms, frag_count):
    onehot = (blocks[:, None] // BF == jnp.arange(frag_count, dtype=jnp.int32)[None, :]).astype(
        jnp.float32
    )
    return jnp.dot(onehot.T, terms, precision=lax.Precision.HIGHEST)


def make_aux(dirs_a, dirs_b, valid):
    pairs = dirs_a.shape[0]
    return jnp.concatenate(
        [dirs_a.T, dirs_b.T, valid[None, :], jnp.zeros((32 - 25, pairs), jnp.float32)], axis=0
    )


def local(
    points,
    normals,
    poses,
    directions,
    local_pairs,
    local_maps,
    remote_src,
    remote_maps,
    remote_dst,
    counts,
):
    axes = ("tile", "band")
    n_band = lax.axis_size("band")
    frag_count = poses.shape[1]
    rows6 = to_world_rows(points, normals, poses, BF)
    frag_dirs = directions.reshape(12, frag_count).T
    peers = counts.shape[1]

    source_blocks = remote_src[0]
    valid = (
        (jnp.arange(CAP, dtype=jnp.int32)[None, :] < counts[0][:, None])
        .astype(jnp.float32)
        .reshape(-1)
    )
    frag_pick = (
        source_blocks[:, None] // BF == jnp.arange(frag_count, dtype=jnp.int32)[None, :]
    ).astype(jnp.float32)
    dirs_send = jnp.dot(frag_pick, frag_dirs, precision=lax.Precision.HIGHEST)
    side = jnp.concatenate([dirs_send, valid[:, None]], axis=1)
    side = side.reshape(peers, CAP * 13)
    side = jnp.concatenate([side, jnp.zeros((peers, 128 - CAP * 13), jnp.float32)], axis=1)
    cargo = build_cargo(pick_rows(source_blocks, rows6[0:3]), remote_maps[0], side)
    arrived = lax.all_to_all(cargo, axes, split_axis=0, concat_axis=0, tiled=True)

    src_l = local_pairs[0]
    tgt_l = local_pairs[1]
    ones = jnp.ones((src_l.shape[0],), jnp.float32)
    out_l = pair_sums(
        pick_rows(src_l, rows6[0:3]),
        pick_rows(tgt_l, rows6),
        local_maps,
        make_aux(frag_dirs[src_l // BF], frag_dirs[tgt_l // BF], ones),
    )
    local_a, local_b = split_terms(out_l)

    target_blocks = remote_dst[0]
    side_in = arrived[:, 0, CAP * 4 * 128 : CAP * 4 * 128 + CAP * 13].reshape(peers * CAP, 13)
    out_r, back = pair_sums(
        arrived,
        pick_rows(target_blocks, rows6),
        None,
        make_aux(side_in[:, 0:12], frag_dirs[target_blocks // BF], side_in[:, 12]),
        n_band,
    )
    unused, remote_b = split_terms(out_r)
    returned, unused = split_terms(back.reshape(peers * CAP, 128)[:, 0:32].T)

    totals = frag_sums(src_l, local_a, frag_count) + frag_sums(tgt_l, local_b, frag_count)
    totals = (
        totals
        + frag_sums(target_blocks, remote_b, frag_count)
        + frag_sums(source_blocks, returned, frag_count)
    )
    gradient = totals[:, 0:6].T
    hess_products = totals[:, 6:18].T.reshape(2, 6, frag_count)
    return (gradient, hess_products)


def solution(mesh):
    placed = (
        P(("tile", "band"), None, None),
        P(("tile", "band"), None, None),
        P(None, ("tile", "band")),
        P(None, None, ("tile", "band")),
        P(None, ("tile", "band")),
        P(("tile", "band"), None),
        P(("tile", "band"), None),
        P(("tile", "band"), None, None),
        P(("tile", "band"), None),
        P(("tile", "band"), None),
    )
    return jax.shard_map(
        local,
        mesh=mesh,
        in_specs=placed,
        out_specs=(P(None, ("tile", "band")), P(None, None, ("tile", "band"))),
        check_vma=False,
    )
```

```python
import functools

import jax
import jax.numpy as jnp
from jax import lax
from jax.experimental import pallas as pl
from jax.experimental.pallas import tpu as pltpu
from jax.sharding import PartitionSpec as P

BF = 32
CAP = 8
N_QTY = 27
MESH = pl.DeviceIdType.MESH


def rotations(poses):
    half_angle = poses[0:3] * 0.5
    inverse = 1.0 / jnp.sqrt(
        1.0
        + half_angle[0] * half_angle[0]
        + half_angle[1] * half_angle[1]
        + half_angle[2] * half_angle[2]
    )
    quat_x = half_angle[0] * inverse
    quat_y = half_angle[1] * inverse
    quat_z = half_angle[2] * inverse
    rotation = [
        [
            1.0 - 2.0 * (quat_y * quat_y + quat_z * quat_z),
            2.0 * (quat_x * quat_y - inverse * quat_z),
            2.0 * (quat_x * quat_z + inverse * quat_y),
        ],
        [
            2.0 * (quat_x * quat_y + inverse * quat_z),
            1.0 - 2.0 * (quat_x * quat_x + quat_z * quat_z),
            2.0 * (quat_y * quat_z - inverse * quat_x),
        ],
        [
            2.0 * (quat_x * quat_z - inverse * quat_y),
            2.0 * (quat_y * quat_z + inverse * quat_x),
            1.0 - 2.0 * (quat_x * quat_x + quat_y * quat_y),
        ],
    ]
    return (rotation, poses[3:6])


def to_world_rows(points, normals, poses, per_pose):
    rotation, translation = rotations(poses)

    def spread(values):
        return jnp.repeat(values, per_pose)[:, None]

    world_rows = []
    normal_rows = []
    for i in range(3):
        coeffs = [spread(rotation[i][j]) for j in range(3)]
        world_rows.append(
            coeffs[0] * points[:, 0]
            + coeffs[1] * points[:, 1]
            + coeffs[2] * points[:, 2]
            + spread(translation[i])
        )
        normal_rows.append(
            coeffs[0] * normals[:, 0] + coeffs[1] * normals[:, 1] + coeffs[2] * normals[:, 2]
        )
    return jnp.stack(world_rows + normal_rows, axis=0)


def _terms_kernel(from_cargo, n_band, xa_ref, tb_ref, map_ref, aux_ref, out_ref, *rest):
    if from_cargo:
        recv_ref, xt_ref, gt_ref, cs_ref, ret_ref, send_sems, recv_sems, own_sem = rest
        _greet(n_band, recv_ref.shape[0])
    else:
        xt_ref, gt_ref, cs_ref = rest
    chunk = out_ref.shape[1]
    if from_cargo:
        peers = chunk // CAP
        height = 4 * CAP + 1
        for p in range(peers):
            for r in range(4):
                cs_ref[r, pl.ds(p * CAP, CAP), :] = xa_ref[pl.ds(p * height + r * CAP, CAP), :]
        idx = cs_ref[3].astype(jnp.int32)
        for c in range(3):
            xt_ref[c] = cs_ref[c].T
    else:
        idx = map_ref[...]
        for c in range(3):
            xt_ref[c] = xa_ref[c].T
    for c in range(6):
        picked = jnp.take_along_axis(tb_ref[c], idx, axis=1, mode="promise_in_bounds")
        gt_ref[c] = picked.T

    def col(q):
        return jnp.broadcast_to(aux_ref[q : q + 1, :], (8, chunk))

    def body(s, accs):
        rows = pl.ds(pl.multiple_of(s * 8, 8), 8)
        xa = [xt_ref[c, rows, :] for c in range(3)]
        xb = [gt_ref[c, rows, :] for c in range(3)]
        nb = [gt_ref[3 + c, rows, :] for c in range(3)]
        off = [xa[c] - xb[c] for c in range(3)]
        res = nb[0] * off[0] + nb[1] * off[1] + nb[2] * off[2]
        ja = [
            xa[1] * nb[2] - xa[2] * nb[1],
            xa[2] * nb[0] - xa[0] * nb[2],
            xa[0] * nb[1] - xa[1] * nb[0],
            nb[0],
            nb[1],
            nb[2],
        ]
        kb = [
            xb[1] * nb[2] - xb[2] * nb[1],
            xb[2] * nb[0] - xb[0] * nb[2],
            xb[0] * nb[1] - xb[1] * nb[0],
            nb[0],
            nb[1],
            nb[2],
        ]
        weights = [res]
        for v in range(2):
            sa = ja[0] * col(6 * v)
            sb = kb[0] * col(12 + 6 * v)
            for c in range(1, 6):
                sa = sa + ja[c] * col(6 * v + c)
                sb = sb + kb[c] * col(12 + 6 * v + c)
            weights.append(sa - sb)
        vals = []
        for w in weights:
            vals.extend([w * ja[c] for c in range(6)])
        for w in weights:
            vals.extend([w * kb[c] for c in range(3)])
        return tuple(a + v for a, v in zip(accs, vals))

    zero = jnp.zeros((8, chunk), jnp.float32)
    accs = lax.fori_loop(0, 128 // 8, body, (zero,) * N_QTY, unroll=8)
    valid = aux_ref[24:25, :]
    for q in range(N_QTY):
        out_ref[q : q + 1, :] = jnp.sum(accs[q], axis=0, keepdims=True) * valid
    out_ref[N_QTY:, :] = jnp.zeros((32 - N_QTY, chunk), jnp.float32)
    if from_cargo:
        _send_back(n_band, out_ref, recv_ref, ret_ref, send_sems, recv_sems, own_sem)


def _greet(n_band, total):
    me = lax.axis_index("tile") * n_band + lax.axis_index("band")
    barrier = pltpu.get_barrier_semaphore()

    @pl.when(pl.program_id(0) == 0)
    def _():
        def greet(k, carry):
            p = lax.rem(me + k, total)
            pl.semaphore_signal(
                barrier, inc=1, device_id=(p // n_band, p % n_band), device_id_type=MESH
            )
            return carry

        lax.fori_loop(1, total, greet, 0)


def _send_back(n_band, out_ref, recv_ref, ret_ref, send_sems, recv_sems, own_sem):
    chunk = out_ref.shape[1]
    peers = chunk // CAP
    total = recv_ref.shape[0]
    step = pl.program_id(0)
    last = pl.num_programs(0) - 1
    me = lax.axis_index("tile") * n_band + lax.axis_index("band")
    barrier = pltpu.get_barrier_semaphore()

    def device(p):
        return (p // n_band, p % n_band)

    def copy_to(p):
        return pltpu.make_async_remote_copy(
            src_ref=ret_ref.at[p],
            dst_ref=recv_ref.at[me],
            send_sem=send_sems.at[p],
            recv_sem=recv_sems.at[me],
            device_id=device(p),
            device_id_type=MESH,
        )

    def copy_from(p):
        return pltpu.make_async_remote_copy(
            src_ref=ret_ref.at[p],
            dst_ref=recv_ref.at[p],
            send_sem=send_sems.at[p],
            recv_sem=recv_sems.at[p],
            device_id=device(p),
            device_id_type=MESH,
        )

    own = pltpu.make_async_copy(ret_ref.at[me], recv_ref.at[me], own_sem)

    padded = jnp.concatenate([out_ref[...], jnp.zeros((128 - 32, chunk), jnp.float32)], axis=0)
    ret_ref[pl.ds(pl.multiple_of(step * peers, peers), peers)] = padded.T.reshape(peers, CAP, 128)

    hold = jnp.minimum(3, last)

    @pl.when(step == hold)
    def _():
        pl.semaphore_wait(barrier, total - 1)

    def start(q, carry):
        p = q

        @pl.when(p != me)
        def _():
            copy_to(p).start()

        @pl.when(p == me)
        def _():
            own.start()

        return carry

    @pl.when(step == hold)
    def _():
        lax.fori_loop(0, (hold + 1) * peers, start, 0)

    @pl.when(step > hold)
    def _():
        lax.fori_loop(step * peers, (step + 1) * peers, start, 0)

    @pl.when(step == last)
    def _():
        def finish(k, carry):
            p = lax.rem(me + k, total)
            copy_to(p).wait_send()
            copy_from(p).wait_recv()
            return carry

        lax.fori_loop(1, total, finish, 0)
        own.wait()


def pair_sums(xa, tb, maps, aux, n_band=1, chunk=128):
    pairs = tb.shape[1]
    from_cargo = maps is None
    scratch = [
        pltpu.VMEM((3, 128, chunk), jnp.float32),
        pltpu.VMEM((6, 128, chunk), jnp.float32),
        pltpu.VMEM((4, chunk, 128), jnp.float32),
    ]
    out_shape = jax.ShapeDtypeStruct((32, pairs), jnp.float32)
    out_specs = pl.BlockSpec((32, chunk), lambda i: (0, i))
    params = None
    if from_cargo:
        xa = xa.reshape(-1, 128)
        xa_spec = pl.BlockSpec((chunk // CAP * (4 * CAP + 1), 128), lambda i: (i, 0))
        maps = aux
        map_spec = pl.BlockSpec((8, 128), lambda i: (0, 0))
        peers = pairs // CAP
        out_shape = (out_shape, jax.ShapeDtypeStruct((peers, CAP, 128), jnp.float32))
        out_specs = (out_specs, pl.BlockSpec(memory_space=pl.ANY))
        scratch += [
            pltpu.VMEM((peers, CAP, 128), jnp.float32),
            pltpu.SemaphoreType.DMA((peers,)),
            pltpu.SemaphoreType.DMA((peers,)),
            pltpu.SemaphoreType.DMA(()),
        ]
        params = pltpu.CompilerParams(collective_id=0, has_side_effects=True)
    else:
        xa_spec = pl.BlockSpec((3, chunk, 128), lambda i: (0, i, 0))
        map_spec = pl.BlockSpec((chunk, 128), lambda i: (i, 0))
    return pl.pallas_call(
        functools.partial(_terms_kernel, from_cargo, n_band),
        out_shape=out_shape,
        grid=(pairs // chunk,),
        in_specs=[
            xa_spec,
            pl.BlockSpec((6, chunk, 128), lambda i: (0, i, 0)),
            map_spec,
            pl.BlockSpec((32, chunk), lambda i: (0, i)),
        ],
        out_specs=out_specs,
        scratch_shapes=scratch,
        compiler_params=params,
    )(xa, tb, maps, aux)


def _cargo_kernel(xa_ref, map_ref, side_ref, out_ref):
    height = 4 * CAP + 1
    group = 8

    def body(g, carry):
        for q in range(group):
            p = g * group + q
            base = pl.multiple_of(g * (group * height), 8) + q * height
            slots = pl.ds(pl.multiple_of(p * CAP, CAP), CAP)
            for c in range(3):
                out_ref[pl.ds(base + c * CAP, CAP), :] = xa_ref[c, slots, :]
            out_ref[pl.ds(base + 3 * CAP, CAP), :] = map_ref[slots, :].astype(jnp.float32)
            out_ref[pl.ds(base + 4 * CAP, 1), :] = side_ref[pl.ds(p, 1), :]
        return carry

    lax.fori_loop(0, side_ref.shape[0] // group, body, 0)


def build_cargo(xa3, maps, side):
    slots = maps.shape[0]
    height = 4 * CAP + 1
    cargo = pl.pallas_call(
        _cargo_kernel,
        out_shape=jax.ShapeDtypeStruct((slots // CAP * height, 128), jnp.float32),
    )(xa3, maps, side)
    return cargo.reshape(slots // CAP, 1, height * 128)


def split_terms(out):
    sel = out[0:N_QTY].T
    ga = sel[:, 0:6] * (1.0 / 128)
    ha = sel[:, 6:18] * (1.0 / 4096)
    gb = -jnp.concatenate([sel[:, 18:21], sel[:, 3:6]], axis=1) * (1.0 / 128)
    hb0 = -jnp.concatenate([sel[:, 21:24], sel[:, 9:12]], axis=1) * (1.0 / 4096)
    hb1 = -jnp.concatenate([sel[:, 24:27], sel[:, 15:18]], axis=1) * (1.0 / 4096)
    return jnp.concatenate([ga, ha], axis=1), jnp.concatenate([gb, hb0, hb1], axis=1)


def _exchange_kernel(n_band, x_ref, out_ref, send_sems, recv_sems, own_sem):
    peers = x_ref.shape[0]
    me = lax.axis_index("tile") * n_band + lax.axis_index("band")

    def peer_of(k):
        p = lax.rem(me + k, peers)
        return p, (p // n_band, p % n_band)

    barrier = pltpu.get_barrier_semaphore()

    def greet(k, carry):
        _, dev = peer_of(k)
        pl.semaphore_signal(barrier, inc=1, device_id=dev, device_id_type=MESH)
        return carry

    lax.fori_loop(1, peers, greet, 0)
    pl.semaphore_wait(barrier, peers - 1)

    own = pltpu.make_async_copy(x_ref.at[me], out_ref.at[me], own_sem)
    own.start()

    def outgoing(k):
        p, dev = peer_of(k)
        return pltpu.make_async_remote_copy(
            src_ref=x_ref.at[p],
            dst_ref=out_ref.at[me],
            send_sem=send_sems.at[p],
            recv_sem=recv_sems.at[me],
            device_id=dev,
            device_id_type=MESH,
        )

    def incoming(k):
        p, dev = peer_of(k)
        return pltpu.make_async_remote_copy(
            src_ref=x_ref.at[p],
            dst_ref=out_ref.at[p],
            send_sem=send_sems.at[p],
            recv_sem=recv_sems.at[p],
            device_id=dev,
            device_id_type=MESH,
        )

    def start(k, carry):
        outgoing(k).start()
        return carry

    lax.fori_loop(1, peers, start, 0)

    def finish(k, carry):
        outgoing(k).wait_send()
        incoming(k).wait_recv()
        return carry

    lax.fori_loop(1, peers, finish, 0)
    own.wait()


def exchange(x, n_band, collective_id):
    peers = x.shape[0]
    return pl.pallas_call(
        functools.partial(_exchange_kernel, n_band),
        out_shape=jax.ShapeDtypeStruct(x.shape, x.dtype),
        in_specs=[pl.BlockSpec(memory_space=pl.ANY)],
        out_specs=pl.BlockSpec(memory_space=pl.ANY),
        scratch_shapes=[
            pltpu.SemaphoreType.DMA((peers,)),
            pltpu.SemaphoreType.DMA((peers,)),
            pltpu.SemaphoreType.DMA(()),
        ],
        compiler_params=pltpu.CompilerParams(collective_id=collective_id, has_side_effects=True),
    )(x)


def pick_rows(blocks, rows):
    onehot = (blocks[:, None] == jnp.arange(rows.shape[1], dtype=jnp.int32)[None, :]).astype(
        jnp.float32
    )
    return jnp.einsum("sb,cbk->csk", onehot, rows, precision=lax.Precision.HIGHEST)


def frag_sums(blocks, terms, frag_count):
    onehot = (blocks[:, None] // BF == jnp.arange(frag_count, dtype=jnp.int32)[None, :]).astype(
        jnp.float32
    )
    return jnp.dot(onehot.T, terms, precision=lax.Precision.HIGHEST)


def make_aux(dirs_a, dirs_b, valid):
    pairs = dirs_a.shape[0]
    return jnp.concatenate(
        [dirs_a.T, dirs_b.T, valid[None, :], jnp.zeros((32 - 25, pairs), jnp.float32)], axis=0
    )


def local(
    points,
    normals,
    poses,
    directions,
    local_pairs,
    local_maps,
    remote_src,
    remote_maps,
    remote_dst,
    counts,
):
    axes = ("tile", "band")
    n_band = lax.axis_size("band")
    frag_count = poses.shape[1]
    rows6 = to_world_rows(points, normals, poses, BF)
    frag_dirs = directions.reshape(12, frag_count).T
    peers = counts.shape[1]

    source_blocks = remote_src[0]
    valid = (
        (jnp.arange(CAP, dtype=jnp.int32)[None, :] < counts[0][:, None])
        .astype(jnp.float32)
        .reshape(-1)
    )
    frag_pick = (
        source_blocks[:, None] // BF == jnp.arange(frag_count, dtype=jnp.int32)[None, :]
    ).astype(jnp.float32)
    dirs_send = jnp.dot(frag_pick, frag_dirs, precision=lax.Precision.HIGHEST)
    side = jnp.concatenate([dirs_send, valid[:, None]], axis=1)
    side = side.reshape(peers, CAP * 13)
    side = jnp.concatenate([side, jnp.zeros((peers, 128 - CAP * 13), jnp.float32)], axis=1)
    cargo = build_cargo(pick_rows(source_blocks, rows6[0:3]), remote_maps[0], side)
    arrived = lax.all_to_all(cargo, axes, split_axis=0, concat_axis=0, tiled=True)

    src_l = local_pairs[0]
    tgt_l = local_pairs[1]
    ones = jnp.ones((src_l.shape[0],), jnp.float32)
    out_l = pair_sums(
        pick_rows(src_l, rows6[0:3]),
        pick_rows(tgt_l, rows6),
        local_maps,
        make_aux(frag_dirs[src_l // BF], frag_dirs[tgt_l // BF], ones),
    )
    local_a, local_b = split_terms(out_l)

    target_blocks = remote_dst[0]
    side_in = arrived[:, 0, CAP * 4 * 128 : CAP * 4 * 128 + CAP * 13].reshape(peers * CAP, 13)
    out_r, back = pair_sums(
        arrived,
        pick_rows(target_blocks, rows6),
        None,
        make_aux(side_in[:, 0:12], frag_dirs[target_blocks // BF], side_in[:, 12]),
        n_band,
    )
    unused, remote_b = split_terms(out_r)
    returned, unused = split_terms(back.reshape(peers * CAP, 128)[:, 0:32].T)

    totals = frag_sums(src_l, local_a, frag_count) + frag_sums(tgt_l, local_b, frag_count)
    totals = (
        totals
        + frag_sums(target_blocks, remote_b, frag_count)
        + frag_sums(source_blocks, returned, frag_count)
    )
    gradient = totals[:, 0:6].T
    hess_products = totals[:, 6:18].T.reshape(2, 6, frag_count)
    return (gradient, hess_products)


def solution(mesh):
    placed = (
        P(("tile", "band"), None, None),
        P(("tile", "band"), None, None),
        P(None, ("tile", "band")),
        P(None, None, ("tile", "band")),
        P(None, ("tile", "band")),
        P(("tile", "band"), None),
        P(("tile", "band"), None),
        P(("tile", "band"), None, None),
        P(("tile", "band"), None),
        P(("tile", "band"), None),
    )
    return jax.shard_map(
        local,
        mesh=mesh,
        in_specs=placed,
        out_specs=(P(None, ("tile", "band")), P(None, None, ("tile", "band"))),
        check_vma=False,
    )
```

```python
import functools

import jax
import jax.numpy as jnp
from jax import lax
from jax.experimental import pallas as pl
from jax.experimental.pallas import tpu as pltpu
from jax.sharding import PartitionSpec as P

BF = 32
CAP = 8
N_QTY = 27
MESH = pl.DeviceIdType.MESH


def rotations(poses):
    half_angle = poses[0:3] * 0.5
    inverse = 1.0 / jnp.sqrt(
        1.0
        + half_angle[0] * half_angle[0]
        + half_angle[1] * half_angle[1]
        + half_angle[2] * half_angle[2]
    )
    quat_x = half_angle[0] * inverse
    quat_y = half_angle[1] * inverse
    quat_z = half_angle[2] * inverse
    rotation = [
        [
            1.0 - 2.0 * (quat_y * quat_y + quat_z * quat_z),
            2.0 * (quat_x * quat_y - inverse * quat_z),
            2.0 * (quat_x * quat_z + inverse * quat_y),
        ],
        [
            2.0 * (quat_x * quat_y + inverse * quat_z),
            1.0 - 2.0 * (quat_x * quat_x + quat_z * quat_z),
            2.0 * (quat_y * quat_z - inverse * quat_x),
        ],
        [
            2.0 * (quat_x * quat_z - inverse * quat_y),
            2.0 * (quat_y * quat_z + inverse * quat_x),
            1.0 - 2.0 * (quat_x * quat_x + quat_y * quat_y),
        ],
    ]
    return (rotation, poses[3:6])


def to_world_rows(points, normals, poses, per_pose):
    rotation, translation = rotations(poses)

    def spread(values):
        return jnp.repeat(values, per_pose)[:, None]

    world_rows = []
    normal_rows = []
    for i in range(3):
        coeffs = [spread(rotation[i][j]) for j in range(3)]
        world_rows.append(
            coeffs[0] * points[:, 0]
            + coeffs[1] * points[:, 1]
            + coeffs[2] * points[:, 2]
            + spread(translation[i])
        )
        normal_rows.append(
            coeffs[0] * normals[:, 0] + coeffs[1] * normals[:, 1] + coeffs[2] * normals[:, 2]
        )
    return jnp.stack(world_rows + normal_rows, axis=0)


def _terms_kernel(from_cargo, n_band, xa_ref, tb_ref, map_ref, aux_ref, out_ref, *rest):
    if from_cargo:
        recv_ref, xt_ref, gt_ref, cs_ref, ret_ref, send_sems, recv_sems, own_sem = rest
        _greet(n_band, recv_ref.shape[0])
    else:
        xt_ref, gt_ref, cs_ref = rest
    chunk = out_ref.shape[1]
    if from_cargo:
        peers = chunk // CAP
        height = 4 * CAP + 1
        for p in range(peers):
            for r in range(4):
                cs_ref[r, pl.ds(p * CAP, CAP), :] = xa_ref[pl.ds(p * height + r * CAP, CAP), :]
        idx = cs_ref[3].astype(jnp.int32)
        for c in range(3):
            xt_ref[c] = cs_ref[c].T
    else:
        idx = map_ref[...]
        for c in range(3):
            xt_ref[c] = xa_ref[c].T
    for c in range(6):
        picked = jnp.take_along_axis(tb_ref[c], idx, axis=1, mode="promise_in_bounds")
        gt_ref[c] = picked.T

    def col(q):
        return jnp.broadcast_to(aux_ref[q : q + 1, :], (8, chunk))

    def body(s, accs):
        rows = pl.ds(pl.multiple_of(s * 8, 8), 8)
        xa = [xt_ref[c, rows, :] for c in range(3)]
        xb = [gt_ref[c, rows, :] for c in range(3)]
        nb = [gt_ref[3 + c, rows, :] for c in range(3)]
        off = [xa[c] - xb[c] for c in range(3)]
        res = nb[0] * off[0] + nb[1] * off[1] + nb[2] * off[2]
        ja = [
            xa[1] * nb[2] - xa[2] * nb[1],
            xa[2] * nb[0] - xa[0] * nb[2],
            xa[0] * nb[1] - xa[1] * nb[0],
            nb[0],
            nb[1],
            nb[2],
        ]
        kb = [
            xb[1] * nb[2] - xb[2] * nb[1],
            xb[2] * nb[0] - xb[0] * nb[2],
            xb[0] * nb[1] - xb[1] * nb[0],
            nb[0],
            nb[1],
            nb[2],
        ]
        weights = [res]
        for v in range(2):
            sa = ja[0] * col(6 * v)
            sb = kb[0] * col(12 + 6 * v)
            for c in range(1, 6):
                sa = sa + ja[c] * col(6 * v + c)
                sb = sb + kb[c] * col(12 + 6 * v + c)
            weights.append(sa - sb)
        vals = []
        for w in weights:
            vals.extend([w * ja[c] for c in range(6)])
        for w in weights:
            vals.extend([w * kb[c] for c in range(3)])
        return tuple(a + v for a, v in zip(accs, vals))

    zero = jnp.zeros((8, chunk), jnp.float32)
    accs = lax.fori_loop(0, 128 // 8, body, (zero,) * N_QTY, unroll=8)
    valid = aux_ref[24:25, :]
    for q in range(N_QTY):
        out_ref[q : q + 1, :] = jnp.sum(accs[q], axis=0, keepdims=True) * valid
    out_ref[N_QTY:, :] = jnp.zeros((32 - N_QTY, chunk), jnp.float32)
    if from_cargo:
        _send_back(n_band, out_ref, recv_ref, ret_ref, send_sems, recv_sems, own_sem)


def _greet(n_band, total):
    me = lax.axis_index("tile") * n_band + lax.axis_index("band")
    barrier = pltpu.get_barrier_semaphore()

    @pl.when(pl.program_id(0) == 0)
    def _():
        def greet(k, carry):
            p = lax.rem(me + k, total)
            pl.semaphore_signal(
                barrier, inc=1, device_id=(p // n_band, p % n_band), device_id_type=MESH
            )
            return carry

        lax.fori_loop(1, total, greet, 0)


def _send_back(n_band, out_ref, recv_ref, ret_ref, send_sems, recv_sems, own_sem):
    chunk = out_ref.shape[1]
    peers = chunk // CAP
    total = recv_ref.shape[0]
    step = pl.program_id(0)
    last = pl.num_programs(0) - 1
    me = lax.axis_index("tile") * n_band + lax.axis_index("band")
    barrier = pltpu.get_barrier_semaphore()

    def device(p):
        return (p // n_band, p % n_band)

    def copy_to(p):
        return pltpu.make_async_remote_copy(
            src_ref=ret_ref.at[p],
            dst_ref=recv_ref.at[me],
            send_sem=send_sems.at[p],
            recv_sem=recv_sems.at[me],
            device_id=device(p),
            device_id_type=MESH,
        )

    def copy_from(p):
        return pltpu.make_async_remote_copy(
            src_ref=ret_ref.at[p],
            dst_ref=recv_ref.at[p],
            send_sem=send_sems.at[p],
            recv_sem=recv_sems.at[p],
            device_id=device(p),
            device_id_type=MESH,
        )

    own = pltpu.make_async_copy(ret_ref.at[me], recv_ref.at[me], own_sem)

    padded = jnp.concatenate([out_ref[...], jnp.zeros((128 - 32, chunk), jnp.float32)], axis=0)
    ret_ref[pl.ds(pl.multiple_of(step * peers, peers), peers)] = padded.T.reshape(peers, CAP, 128)

    hold = jnp.minimum(2, last)

    @pl.when(step == hold)
    def _():
        pl.semaphore_wait(barrier, total - 1)

    def start(q, carry):
        p = q

        @pl.when(p != me)
        def _():
            copy_to(p).start()

        @pl.when(p == me)
        def _():
            own.start()

        return carry

    @pl.when(step == hold)
    def _():
        lax.fori_loop(0, (hold + 1) * peers, start, 0)

    @pl.when(step > hold)
    def _():
        lax.fori_loop(step * peers, (step + 1) * peers, start, 0)

    @pl.when(step == last)
    def _():
        def finish(k, carry):
            p = lax.rem(me + k, total)
            copy_to(p).wait_send()
            copy_from(p).wait_recv()
            return carry

        lax.fori_loop(1, total, finish, 0)
        own.wait()


def pair_sums(xa, tb, maps, aux, n_band=1, chunk=128):
    pairs = tb.shape[1]
    from_cargo = maps is None
    scratch = [
        pltpu.VMEM((3, 128, chunk), jnp.float32),
        pltpu.VMEM((6, 128, chunk), jnp.float32),
        pltpu.VMEM((4, chunk, 128), jnp.float32),
    ]
    out_shape = jax.ShapeDtypeStruct((32, pairs), jnp.float32)
    out_specs = pl.BlockSpec((32, chunk), lambda i: (0, i))
    params = None
    if from_cargo:
        xa = xa.reshape(-1, 128)
        xa_spec = pl.BlockSpec((chunk // CAP * (4 * CAP + 1), 128), lambda i: (i, 0))
        maps = aux
        map_spec = pl.BlockSpec((8, 128), lambda i: (0, 0))
        peers = pairs // CAP
        out_shape = (out_shape, jax.ShapeDtypeStruct((peers, CAP, 128), jnp.float32))
        out_specs = (out_specs, pl.BlockSpec(memory_space=pl.ANY))
        scratch += [
            pltpu.VMEM((peers, CAP, 128), jnp.float32),
            pltpu.SemaphoreType.DMA((peers,)),
            pltpu.SemaphoreType.DMA((peers,)),
            pltpu.SemaphoreType.DMA(()),
        ]
        params = pltpu.CompilerParams(collective_id=0, has_side_effects=True)
    else:
        xa_spec = pl.BlockSpec((3, chunk, 128), lambda i: (0, i, 0))
        map_spec = pl.BlockSpec((chunk, 128), lambda i: (i, 0))
    return pl.pallas_call(
        functools.partial(_terms_kernel, from_cargo, n_band),
        out_shape=out_shape,
        grid=(pairs // chunk,),
        in_specs=[
            xa_spec,
            pl.BlockSpec((6, chunk, 128), lambda i: (0, i, 0)),
            map_spec,
            pl.BlockSpec((32, chunk), lambda i: (0, i)),
        ],
        out_specs=out_specs,
        scratch_shapes=scratch,
        compiler_params=params,
    )(xa, tb, maps, aux)


def _cargo_kernel(xa_ref, map_ref, side_ref, out_ref):
    height = 4 * CAP + 1
    group = 8

    def body(g, carry):
        for q in range(group):
            p = g * group + q
            base = pl.multiple_of(g * (group * height), 8) + q * height
            slots = pl.ds(pl.multiple_of(p * CAP, CAP), CAP)
            for c in range(3):
                out_ref[pl.ds(base + c * CAP, CAP), :] = xa_ref[c, slots, :]
            out_ref[pl.ds(base + 3 * CAP, CAP), :] = map_ref[slots, :].astype(jnp.float32)
            out_ref[pl.ds(base + 4 * CAP, 1), :] = side_ref[pl.ds(p, 1), :]
        return carry

    lax.fori_loop(0, side_ref.shape[0] // group, body, 0)


def build_cargo(xa3, maps, side):
    slots = maps.shape[0]
    height = 4 * CAP + 1
    cargo = pl.pallas_call(
        _cargo_kernel,
        out_shape=jax.ShapeDtypeStruct((slots // CAP * height, 128), jnp.float32),
    )(xa3, maps, side)
    return cargo.reshape(slots // CAP, 1, height * 128)


def split_terms(out):
    sel = out[0:N_QTY].T
    ga = sel[:, 0:6] * (1.0 / 128)
    ha = sel[:, 6:18] * (1.0 / 4096)
    gb = -jnp.concatenate([sel[:, 18:21], sel[:, 3:6]], axis=1) * (1.0 / 128)
    hb0 = -jnp.concatenate([sel[:, 21:24], sel[:, 9:12]], axis=1) * (1.0 / 4096)
    hb1 = -jnp.concatenate([sel[:, 24:27], sel[:, 15:18]], axis=1) * (1.0 / 4096)
    return jnp.concatenate([ga, ha], axis=1), jnp.concatenate([gb, hb0, hb1], axis=1)


def _exchange_kernel(n_band, x_ref, out_ref, send_sems, recv_sems, own_sem):
    peers = x_ref.shape[0]
    me = lax.axis_index("tile") * n_band + lax.axis_index("band")

    def peer_of(k):
        p = lax.rem(me + k, peers)
        return p, (p // n_band, p % n_band)

    barrier = pltpu.get_barrier_semaphore()

    def greet(k, carry):
        _, dev = peer_of(k)
        pl.semaphore_signal(barrier, inc=1, device_id=dev, device_id_type=MESH)
        return carry

    lax.fori_loop(1, peers, greet, 0)
    pl.semaphore_wait(barrier, peers - 1)

    own = pltpu.make_async_copy(x_ref.at[me], out_ref.at[me], own_sem)
    own.start()

    def outgoing(k):
        p, dev = peer_of(k)
        return pltpu.make_async_remote_copy(
            src_ref=x_ref.at[p],
            dst_ref=out_ref.at[me],
            send_sem=send_sems.at[p],
            recv_sem=recv_sems.at[me],
            device_id=dev,
            device_id_type=MESH,
        )

    def incoming(k):
        p, dev = peer_of(k)
        return pltpu.make_async_remote_copy(
            src_ref=x_ref.at[p],
            dst_ref=out_ref.at[p],
            send_sem=send_sems.at[p],
            recv_sem=recv_sems.at[p],
            device_id=dev,
            device_id_type=MESH,
        )

    def start(k, carry):
        outgoing(k).start()
        return carry

    lax.fori_loop(1, peers, start, 0)

    def finish(k, carry):
        outgoing(k).wait_send()
        incoming(k).wait_recv()
        return carry

    lax.fori_loop(1, peers, finish, 0)
    own.wait()


def exchange(x, n_band, collective_id):
    peers = x.shape[0]
    return pl.pallas_call(
        functools.partial(_exchange_kernel, n_band),
        out_shape=jax.ShapeDtypeStruct(x.shape, x.dtype),
        in_specs=[pl.BlockSpec(memory_space=pl.ANY)],
        out_specs=pl.BlockSpec(memory_space=pl.ANY),
        scratch_shapes=[
            pltpu.SemaphoreType.DMA((peers,)),
            pltpu.SemaphoreType.DMA((peers,)),
            pltpu.SemaphoreType.DMA(()),
        ],
        compiler_params=pltpu.CompilerParams(collective_id=collective_id, has_side_effects=True),
    )(x)


def pick_rows(blocks, rows):
    onehot = (blocks[:, None] == jnp.arange(rows.shape[1], dtype=jnp.int32)[None, :]).astype(
        jnp.float32
    )
    return jnp.einsum("sb,cbk->csk", onehot, rows, precision=lax.Precision.HIGHEST)


def frag_sums(blocks, terms, frag_count):
    onehot = (blocks[:, None] // BF == jnp.arange(frag_count, dtype=jnp.int32)[None, :]).astype(
        jnp.float32
    )
    return jnp.dot(onehot.T, terms, precision=lax.Precision.HIGHEST)


def make_aux(dirs_a, dirs_b, valid):
    pairs = dirs_a.shape[0]
    return jnp.concatenate(
        [dirs_a.T, dirs_b.T, valid[None, :], jnp.zeros((32 - 25, pairs), jnp.float32)], axis=0
    )


def local(
    points,
    normals,
    poses,
    directions,
    local_pairs,
    local_maps,
    remote_src,
    remote_maps,
    remote_dst,
    counts,
):
    axes = ("tile", "band")
    n_band = lax.axis_size("band")
    frag_count = poses.shape[1]
    rows6 = to_world_rows(points, normals, poses, BF)
    frag_dirs = directions.reshape(12, frag_count).T
    peers = counts.shape[1]

    source_blocks = remote_src[0]
    valid = (
        (jnp.arange(CAP, dtype=jnp.int32)[None, :] < counts[0][:, None])
        .astype(jnp.float32)
        .reshape(-1)
    )
    frag_pick = (
        source_blocks[:, None] // BF == jnp.arange(frag_count, dtype=jnp.int32)[None, :]
    ).astype(jnp.float32)
    dirs_send = jnp.dot(frag_pick, frag_dirs, precision=lax.Precision.HIGHEST)
    side = jnp.concatenate([dirs_send, valid[:, None]], axis=1)
    side = side.reshape(peers, CAP * 13)
    side = jnp.concatenate([side, jnp.zeros((peers, 128 - CAP * 13), jnp.float32)], axis=1)
    cargo = build_cargo(pick_rows(source_blocks, rows6[0:3]), remote_maps[0], side)
    arrived = lax.all_to_all(cargo, axes, split_axis=0, concat_axis=0, tiled=True)

    src_l = local_pairs[0]
    tgt_l = local_pairs[1]
    ones = jnp.ones((src_l.shape[0],), jnp.float32)
    out_l = pair_sums(
        pick_rows(src_l, rows6[0:3]),
        pick_rows(tgt_l, rows6),
        local_maps,
        make_aux(frag_dirs[src_l // BF], frag_dirs[tgt_l // BF], ones),
    )
    local_a, local_b = split_terms(out_l)

    target_blocks = remote_dst[0]
    side_in = arrived[:, 0, CAP * 4 * 128 : CAP * 4 * 128 + CAP * 13].reshape(peers * CAP, 13)
    out_r, back = pair_sums(
        arrived,
        pick_rows(target_blocks, rows6),
        None,
        make_aux(side_in[:, 0:12], frag_dirs[target_blocks // BF], side_in[:, 12]),
        n_band,
    )
    unused, remote_b = split_terms(out_r)
    returned, unused = split_terms(back.reshape(peers * CAP, 128)[:, 0:32].T)

    totals = frag_sums(src_l, local_a, frag_count) + frag_sums(tgt_l, local_b, frag_count)
    totals = (
        totals
        + frag_sums(target_blocks, remote_b, frag_count)
        + frag_sums(source_blocks, returned, frag_count)
    )
    gradient = totals[:, 0:6].T
    hess_products = totals[:, 6:18].T.reshape(2, 6, frag_count)
    return (gradient, hess_products)


def solution(mesh):
    placed = (
        P(("tile", "band"), None, None),
        P(("tile", "band"), None, None),
        P(None, ("tile", "band")),
        P(None, None, ("tile", "band")),
        P(None, ("tile", "band")),
        P(("tile", "band"), None),
        P(("tile", "band"), None),
        P(("tile", "band"), None, None),
        P(("tile", "band"), None),
        P(("tile", "band"), None),
    )
    return jax.shard_map(
        local,
        mesh=mesh,
        in_specs=placed,
        out_specs=(P(None, ("tile", "band")), P(None, None, ("tile", "band"))),
        check_vma=False,
    )
```

```python
import functools

import jax
import jax.numpy as jnp
from jax import lax
from jax.experimental import pallas as pl
from jax.experimental.pallas import tpu as pltpu
from jax.sharding import PartitionSpec as P

BF = 32
CAP = 8
N_QTY = 27
MESH = pl.DeviceIdType.MESH


def rotations(poses):
    half_angle = poses[0:3] * 0.5
    inverse = 1.0 / jnp.sqrt(
        1.0
        + half_angle[0] * half_angle[0]
        + half_angle[1] * half_angle[1]
        + half_angle[2] * half_angle[2]
    )
    quat_x = half_angle[0] * inverse
    quat_y = half_angle[1] * inverse
    quat_z = half_angle[2] * inverse
    rotation = [
        [
            1.0 - 2.0 * (quat_y * quat_y + quat_z * quat_z),
            2.0 * (quat_x * quat_y - inverse * quat_z),
            2.0 * (quat_x * quat_z + inverse * quat_y),
        ],
        [
            2.0 * (quat_x * quat_y + inverse * quat_z),
            1.0 - 2.0 * (quat_x * quat_x + quat_z * quat_z),
            2.0 * (quat_y * quat_z - inverse * quat_x),
        ],
        [
            2.0 * (quat_x * quat_z - inverse * quat_y),
            2.0 * (quat_y * quat_z + inverse * quat_x),
            1.0 - 2.0 * (quat_x * quat_x + quat_y * quat_y),
        ],
    ]
    return (rotation, poses[3:6])


def to_world_rows(points, normals, poses, per_pose):
    rotation, translation = rotations(poses)

    def spread(values):
        return jnp.repeat(values, per_pose)[:, None]

    world_rows = []
    normal_rows = []
    for i in range(3):
        coeffs = [spread(rotation[i][j]) for j in range(3)]
        world_rows.append(
            coeffs[0] * points[:, 0]
            + coeffs[1] * points[:, 1]
            + coeffs[2] * points[:, 2]
            + spread(translation[i])
        )
        normal_rows.append(
            coeffs[0] * normals[:, 0] + coeffs[1] * normals[:, 1] + coeffs[2] * normals[:, 2]
        )
    return jnp.stack(world_rows + normal_rows, axis=0)


def _terms_kernel(from_cargo, n_band, xa_ref, tb_ref, map_ref, aux_ref, out_ref, *rest):
    if from_cargo:
        recv_ref, xt_ref, gt_ref, cs_ref, ret_ref, send_sems, recv_sems, own_sem = rest
        _greet(n_band, recv_ref.shape[0])
    else:
        xt_ref, gt_ref, cs_ref = rest
    chunk = out_ref.shape[1]
    if from_cargo:
        peers = chunk // CAP
        height = 4 * CAP + 1
        for p in range(peers):
            for r in range(4):
                cs_ref[r, pl.ds(p * CAP, CAP), :] = xa_ref[pl.ds(p * height + r * CAP, CAP), :]
        idx = cs_ref[3].astype(jnp.int32)
        for c in range(3):
            xt_ref[c] = cs_ref[c].T
    else:
        idx = map_ref[...]
        for c in range(3):
            xt_ref[c] = xa_ref[c].T
    for c in range(6):
        picked = jnp.take_along_axis(tb_ref[c], idx, axis=1, mode="promise_in_bounds")
        gt_ref[c] = picked.T

    def col(q):
        return jnp.broadcast_to(aux_ref[q : q + 1, :], (8, chunk))

    def body(s, accs):
        rows = pl.ds(pl.multiple_of(s * 8, 8), 8)
        xa = [xt_ref[c, rows, :] for c in range(3)]
        xb = [gt_ref[c, rows, :] for c in range(3)]
        nb = [gt_ref[3 + c, rows, :] for c in range(3)]
        off = [xa[c] - xb[c] for c in range(3)]
        res = nb[0] * off[0] + nb[1] * off[1] + nb[2] * off[2]
        ja = [
            xa[1] * nb[2] - xa[2] * nb[1],
            xa[2] * nb[0] - xa[0] * nb[2],
            xa[0] * nb[1] - xa[1] * nb[0],
            nb[0],
            nb[1],
            nb[2],
        ]
        kb = [
            xb[1] * nb[2] - xb[2] * nb[1],
            xb[2] * nb[0] - xb[0] * nb[2],
            xb[0] * nb[1] - xb[1] * nb[0],
            nb[0],
            nb[1],
            nb[2],
        ]
        weights = [res]
        for v in range(2):
            sa = ja[0] * col(6 * v)
            sb = kb[0] * col(12 + 6 * v)
            for c in range(1, 6):
                sa = sa + ja[c] * col(6 * v + c)
                sb = sb + kb[c] * col(12 + 6 * v + c)
            weights.append(sa - sb)
        vals = []
        for w in weights:
            vals.extend([w * ja[c] for c in range(6)])
        for w in weights:
            vals.extend([w * kb[c] for c in range(3)])
        return tuple(a + v for a, v in zip(accs, vals))

    zero = jnp.zeros((8, chunk), jnp.float32)
    accs = lax.fori_loop(0, 128 // 8, body, (zero,) * N_QTY, unroll=True)
    valid = aux_ref[24:25, :]
    for q in range(N_QTY):
        out_ref[q : q + 1, :] = jnp.sum(accs[q], axis=0, keepdims=True) * valid
    out_ref[N_QTY:, :] = jnp.zeros((32 - N_QTY, chunk), jnp.float32)
    if from_cargo:
        _send_back(n_band, out_ref, recv_ref, ret_ref, send_sems, recv_sems, own_sem)


def _greet(n_band, total):
    me = lax.axis_index("tile") * n_band + lax.axis_index("band")
    barrier = pltpu.get_barrier_semaphore()

    @pl.when(pl.program_id(0) == 0)
    def _():
        def greet(k, carry):
            p = lax.rem(me + k, total)
            pl.semaphore_signal(
                barrier, inc=1, device_id=(p // n_band, p % n_band), device_id_type=MESH
            )
            return carry

        lax.fori_loop(1, total, greet, 0)


def _send_back(n_band, out_ref, recv_ref, ret_ref, send_sems, recv_sems, own_sem):
    chunk = out_ref.shape[1]
    peers = chunk // CAP
    total = recv_ref.shape[0]
    step = pl.program_id(0)
    last = pl.num_programs(0) - 1
    me = lax.axis_index("tile") * n_band + lax.axis_index("band")
    barrier = pltpu.get_barrier_semaphore()

    def device(p):
        return (p // n_band, p % n_band)

    def copy_to(p):
        return pltpu.make_async_remote_copy(
            src_ref=ret_ref.at[p],
            dst_ref=recv_ref.at[me],
            send_sem=send_sems.at[p],
            recv_sem=recv_sems.at[me],
            device_id=device(p),
            device_id_type=MESH,
        )

    def copy_from(p):
        return pltpu.make_async_remote_copy(
            src_ref=ret_ref.at[p],
            dst_ref=recv_ref.at[p],
            send_sem=send_sems.at[p],
            recv_sem=recv_sems.at[p],
            device_id=device(p),
            device_id_type=MESH,
        )

    own = pltpu.make_async_copy(ret_ref.at[me], recv_ref.at[me], own_sem)

    padded = jnp.concatenate([out_ref[...], jnp.zeros((128 - 32, chunk), jnp.float32)], axis=0)
    ret_ref[pl.ds(pl.multiple_of(step * peers, peers), peers)] = padded.T.reshape(peers, CAP, 128)

    hold = jnp.minimum(3, last)

    @pl.when(step == hold)
    def _():
        pl.semaphore_wait(barrier, total - 1)

    def start(q, carry):
        p = q

        @pl.when(p != me)
        def _():
            copy_to(p).start()

        @pl.when(p == me)
        def _():
            own.start()

        return carry

    @pl.when(step == hold)
    def _():
        lax.fori_loop(0, (hold + 1) * peers, start, 0)

    @pl.when(step > hold)
    def _():
        lax.fori_loop(step * peers, (step + 1) * peers, start, 0)

    @pl.when(step == last)
    def _():
        def finish(k, carry):
            p = lax.rem(me + k, total)
            copy_to(p).wait_send()
            copy_from(p).wait_recv()
            return carry

        lax.fori_loop(1, total, finish, 0)
        own.wait()


def pair_sums(xa, tb, maps, aux, n_band=1, chunk=128):
    pairs = tb.shape[1]
    from_cargo = maps is None
    scratch = [
        pltpu.VMEM((3, 128, chunk), jnp.float32),
        pltpu.VMEM((6, 128, chunk), jnp.float32),
        pltpu.VMEM((4, chunk, 128), jnp.float32),
    ]
    out_shape = jax.ShapeDtypeStruct((32, pairs), jnp.float32)
    out_specs = pl.BlockSpec((32, chunk), lambda i: (0, i))
    params = None
    if from_cargo:
        xa = xa.reshape(-1, 128)
        xa_spec = pl.BlockSpec((chunk // CAP * (4 * CAP + 1), 128), lambda i: (i, 0))
        maps = aux
        map_spec = pl.BlockSpec((8, 128), lambda i: (0, 0))
        peers = pairs // CAP
        out_shape = (out_shape, jax.ShapeDtypeStruct((peers, CAP, 128), jnp.float32))
        out_specs = (out_specs, pl.BlockSpec(memory_space=pl.ANY))
        scratch += [
            pltpu.VMEM((peers, CAP, 128), jnp.float32),
            pltpu.SemaphoreType.DMA((peers,)),
            pltpu.SemaphoreType.DMA((peers,)),
            pltpu.SemaphoreType.DMA(()),
        ]
        params = pltpu.CompilerParams(collective_id=0, has_side_effects=True)
    else:
        xa_spec = pl.BlockSpec((3, chunk, 128), lambda i: (0, i, 0))
        map_spec = pl.BlockSpec((chunk, 128), lambda i: (i, 0))
    return pl.pallas_call(
        functools.partial(_terms_kernel, from_cargo, n_band),
        out_shape=out_shape,
        grid=(pairs // chunk,),
        in_specs=[
            xa_spec,
            pl.BlockSpec((6, chunk, 128), lambda i: (0, i, 0)),
            map_spec,
            pl.BlockSpec((32, chunk), lambda i: (0, i)),
        ],
        out_specs=out_specs,
        scratch_shapes=scratch,
        compiler_params=params,
    )(xa, tb, maps, aux)


def _cargo_kernel(xa_ref, map_ref, side_ref, out_ref):
    height = 4 * CAP + 1
    group = 8

    def body(g, carry):
        for q in range(group):
            p = g * group + q
            base = pl.multiple_of(g * (group * height), 8) + q * height
            slots = pl.ds(pl.multiple_of(p * CAP, CAP), CAP)
            for c in range(3):
                out_ref[pl.ds(base + c * CAP, CAP), :] = xa_ref[c, slots, :]
            out_ref[pl.ds(base + 3 * CAP, CAP), :] = map_ref[slots, :].astype(jnp.float32)
            out_ref[pl.ds(base + 4 * CAP, 1), :] = side_ref[pl.ds(p, 1), :]
        return carry

    lax.fori_loop(0, side_ref.shape[0] // group, body, 0)


def build_cargo(xa3, maps, side):
    slots = maps.shape[0]
    height = 4 * CAP + 1
    cargo = pl.pallas_call(
        _cargo_kernel,
        out_shape=jax.ShapeDtypeStruct((slots // CAP * height, 128), jnp.float32),
    )(xa3, maps, side)
    return cargo.reshape(slots // CAP, 1, height * 128)


def split_terms(out):
    sel = out[0:N_QTY].T
    ga = sel[:, 0:6] * (1.0 / 128)
    ha = sel[:, 6:18] * (1.0 / 4096)
    gb = -jnp.concatenate([sel[:, 18:21], sel[:, 3:6]], axis=1) * (1.0 / 128)
    hb0 = -jnp.concatenate([sel[:, 21:24], sel[:, 9:12]], axis=1) * (1.0 / 4096)
    hb1 = -jnp.concatenate([sel[:, 24:27], sel[:, 15:18]], axis=1) * (1.0 / 4096)
    return jnp.concatenate([ga, ha], axis=1), jnp.concatenate([gb, hb0, hb1], axis=1)


def _exchange_kernel(n_band, x_ref, out_ref, send_sems, recv_sems, own_sem):
    peers = x_ref.shape[0]
    me = lax.axis_index("tile") * n_band + lax.axis_index("band")

    def peer_of(k):
        p = lax.rem(me + k, peers)
        return p, (p // n_band, p % n_band)

    barrier = pltpu.get_barrier_semaphore()

    def greet(k, carry):
        _, dev = peer_of(k)
        pl.semaphore_signal(barrier, inc=1, device_id=dev, device_id_type=MESH)
        return carry

    lax.fori_loop(1, peers, greet, 0)
    pl.semaphore_wait(barrier, peers - 1)

    own = pltpu.make_async_copy(x_ref.at[me], out_ref.at[me], own_sem)
    own.start()

    def outgoing(k):
        p, dev = peer_of(k)
        return pltpu.make_async_remote_copy(
            src_ref=x_ref.at[p],
            dst_ref=out_ref.at[me],
            send_sem=send_sems.at[p],
            recv_sem=recv_sems.at[me],
            device_id=dev,
            device_id_type=MESH,
        )

    def incoming(k):
        p, dev = peer_of(k)
        return pltpu.make_async_remote_copy(
            src_ref=x_ref.at[p],
            dst_ref=out_ref.at[p],
            send_sem=send_sems.at[p],
            recv_sem=recv_sems.at[p],
            device_id=dev,
            device_id_type=MESH,
        )

    def start(k, carry):
        outgoing(k).start()
        return carry

    lax.fori_loop(1, peers, start, 0)

    def finish(k, carry):
        outgoing(k).wait_send()
        incoming(k).wait_recv()
        return carry

    lax.fori_loop(1, peers, finish, 0)
    own.wait()


def exchange(x, n_band, collective_id):
    peers = x.shape[0]
    return pl.pallas_call(
        functools.partial(_exchange_kernel, n_band),
        out_shape=jax.ShapeDtypeStruct(x.shape, x.dtype),
        in_specs=[pl.BlockSpec(memory_space=pl.ANY)],
        out_specs=pl.BlockSpec(memory_space=pl.ANY),
        scratch_shapes=[
            pltpu.SemaphoreType.DMA((peers,)),
            pltpu.SemaphoreType.DMA((peers,)),
            pltpu.SemaphoreType.DMA(()),
        ],
        compiler_params=pltpu.CompilerParams(collective_id=collective_id, has_side_effects=True),
    )(x)


def pick_rows(blocks, rows):
    onehot = (blocks[:, None] == jnp.arange(rows.shape[1], dtype=jnp.int32)[None, :]).astype(
        jnp.float32
    )
    return jnp.einsum("sb,cbk->csk", onehot, rows, precision=lax.Precision.HIGHEST)


def frag_sums(blocks, terms, frag_count):
    onehot = (blocks[:, None] // BF == jnp.arange(frag_count, dtype=jnp.int32)[None, :]).astype(
        jnp.float32
    )
    return jnp.dot(onehot.T, terms, precision=lax.Precision.HIGHEST)


def make_aux(dirs_a, dirs_b, valid):
    pairs = dirs_a.shape[0]
    return jnp.concatenate(
        [dirs_a.T, dirs_b.T, valid[None, :], jnp.zeros((32 - 25, pairs), jnp.float32)], axis=0
    )


def local(
    points,
    normals,
    poses,
    directions,
    local_pairs,
    local_maps,
    remote_src,
    remote_maps,
    remote_dst,
    counts,
):
    axes = ("tile", "band")
    n_band = lax.axis_size("band")
    frag_count = poses.shape[1]
    rows6 = to_world_rows(points, normals, poses, BF)
    frag_dirs = directions.reshape(12, frag_count).T
    peers = counts.shape[1]

    source_blocks = remote_src[0]
    valid = (
        (jnp.arange(CAP, dtype=jnp.int32)[None, :] < counts[0][:, None])
        .astype(jnp.float32)
        .reshape(-1)
    )
    frag_pick = (
        source_blocks[:, None] // BF == jnp.arange(frag_count, dtype=jnp.int32)[None, :]
    ).astype(jnp.float32)
    dirs_send = jnp.dot(frag_pick, frag_dirs, precision=lax.Precision.HIGHEST)
    side = jnp.concatenate([dirs_send, valid[:, None]], axis=1)
    side = side.reshape(peers, CAP * 13)
    side = jnp.concatenate([side, jnp.zeros((peers, 128 - CAP * 13), jnp.float32)], axis=1)
    cargo = build_cargo(pick_rows(source_blocks, rows6[0:3]), remote_maps[0], side)
    arrived = lax.all_to_all(cargo, axes, split_axis=0, concat_axis=0, tiled=True)

    src_l = local_pairs[0]
    tgt_l = local_pairs[1]
    ones = jnp.ones((src_l.shape[0],), jnp.float32)
    out_l = pair_sums(
        pick_rows(src_l, rows6[0:3]),
        pick_rows(tgt_l, rows6),
        local_maps,
        make_aux(frag_dirs[src_l // BF], frag_dirs[tgt_l // BF], ones),
    )
    local_a, local_b = split_terms(out_l)

    target_blocks = remote_dst[0]
    side_in = arrived[:, 0, CAP * 4 * 128 : CAP * 4 * 128 + CAP * 13].reshape(peers * CAP, 13)
    out_r, back = pair_sums(
        arrived,
        pick_rows(target_blocks, rows6),
        None,
        make_aux(side_in[:, 0:12], frag_dirs[target_blocks // BF], side_in[:, 12]),
        n_band,
    )
    unused, remote_b = split_terms(out_r)
    returned, unused = split_terms(back.reshape(peers * CAP, 128)[:, 0:32].T)

    totals = frag_sums(src_l, local_a, frag_count) + frag_sums(tgt_l, local_b, frag_count)
    totals = (
        totals
        + frag_sums(target_blocks, remote_b, frag_count)
        + frag_sums(source_blocks, returned, frag_count)
    )
    gradient = totals[:, 0:6].T
    hess_products = totals[:, 6:18].T.reshape(2, 6, frag_count)
    return (gradient, hess_products)


def solution(mesh):
    placed = (
        P(("tile", "band"), None, None),
        P(("tile", "band"), None, None),
        P(None, ("tile", "band")),
        P(None, None, ("tile", "band")),
        P(None, ("tile", "band")),
        P(("tile", "band"), None),
        P(("tile", "band"), None),
        P(("tile", "band"), None, None),
        P(("tile", "band"), None),
        P(("tile", "band"), None),
    )
    return jax.shard_map(
        local,
        mesh=mesh,
        in_specs=placed,
        out_specs=(P(None, ("tile", "band")), P(None, None, ("tile", "band"))),
        check_vma=False,
    )
```

```python
import functools

import jax
import jax.numpy as jnp
from jax import lax
from jax.experimental import pallas as pl
from jax.experimental.pallas import tpu as pltpu
from jax.sharding import PartitionSpec as P

BF = 32
CAP = 8
N_QTY = 27
MESH = pl.DeviceIdType.MESH


def rotations(poses):
    half_angle = poses[0:3] * 0.5
    inverse = 1.0 / jnp.sqrt(
        1.0
        + half_angle[0] * half_angle[0]
        + half_angle[1] * half_angle[1]
        + half_angle[2] * half_angle[2]
    )
    quat_x = half_angle[0] * inverse
    quat_y = half_angle[1] * inverse
    quat_z = half_angle[2] * inverse
    rotation = [
        [
            1.0 - 2.0 * (quat_y * quat_y + quat_z * quat_z),
            2.0 * (quat_x * quat_y - inverse * quat_z),
            2.0 * (quat_x * quat_z + inverse * quat_y),
        ],
        [
            2.0 * (quat_x * quat_y + inverse * quat_z),
            1.0 - 2.0 * (quat_x * quat_x + quat_z * quat_z),
            2.0 * (quat_y * quat_z - inverse * quat_x),
        ],
        [
            2.0 * (quat_x * quat_z - inverse * quat_y),
            2.0 * (quat_y * quat_z + inverse * quat_x),
            1.0 - 2.0 * (quat_x * quat_x + quat_y * quat_y),
        ],
    ]
    return (rotation, poses[3:6])


def to_world_rows(points, normals, poses, per_pose):
    rotation, translation = rotations(poses)

    def spread(values):
        return jnp.repeat(values, per_pose)[:, None]

    world_rows = []
    normal_rows = []
    for i in range(3):
        coeffs = [spread(rotation[i][j]) for j in range(3)]
        world_rows.append(
            coeffs[0] * points[:, 0]
            + coeffs[1] * points[:, 1]
            + coeffs[2] * points[:, 2]
            + spread(translation[i])
        )
        normal_rows.append(
            coeffs[0] * normals[:, 0] + coeffs[1] * normals[:, 1] + coeffs[2] * normals[:, 2]
        )
    return jnp.stack(world_rows + normal_rows, axis=0)


def _terms_kernel(from_cargo, n_band, xa_ref, tb_ref, map_ref, aux_ref, out_ref, *rest):
    if from_cargo:
        recv_ref, xt_ref, gt_ref, cs_ref, ret_ref, send_sems, recv_sems, own_sem = rest
        _greet(n_band, recv_ref.shape[0])
    else:
        xt_ref, gt_ref, cs_ref = rest
    chunk = out_ref.shape[1]
    if from_cargo:
        peers = chunk // CAP
        height = 4 * CAP + 1
        for p in range(peers):
            for r in range(4):
                cs_ref[r, pl.ds(p * CAP, CAP), :] = xa_ref[pl.ds(p * height + r * CAP, CAP), :]
        idx = cs_ref[3].astype(jnp.int32)
        for c in range(3):
            xt_ref[c] = cs_ref[c].T
    else:
        idx = map_ref[...]
        for c in range(3):
            xt_ref[c] = xa_ref[c].T
    for c in range(6):
        picked = jnp.take_along_axis(tb_ref[c], idx, axis=1, mode="promise_in_bounds")
        gt_ref[c] = picked.T

    def col(q):
        return jnp.broadcast_to(aux_ref[q : q + 1, :], (8, chunk))

    def body(s, accs):
        rows = pl.ds(pl.multiple_of(s * 8, 8), 8)
        xa = [xt_ref[c, rows, :] for c in range(3)]
        xb = [gt_ref[c, rows, :] for c in range(3)]
        nb = [gt_ref[3 + c, rows, :] for c in range(3)]
        off = [xa[c] - xb[c] for c in range(3)]
        res = nb[0] * off[0] + nb[1] * off[1] + nb[2] * off[2]
        ja = [
            xa[1] * nb[2] - xa[2] * nb[1],
            xa[2] * nb[0] - xa[0] * nb[2],
            xa[0] * nb[1] - xa[1] * nb[0],
            nb[0],
            nb[1],
            nb[2],
        ]
        kb = [
            xb[1] * nb[2] - xb[2] * nb[1],
            xb[2] * nb[0] - xb[0] * nb[2],
            xb[0] * nb[1] - xb[1] * nb[0],
            nb[0],
            nb[1],
            nb[2],
        ]
        weights = [res]
        for v in range(2):
            sa = ja[0] * col(6 * v)
            sb = kb[0] * col(12 + 6 * v)
            for c in range(1, 6):
                sa = sa + ja[c] * col(6 * v + c)
                sb = sb + kb[c] * col(12 + 6 * v + c)
            weights.append(sa - sb)
        vals = []
        for w in weights:
            vals.extend([w * ja[c] for c in range(6)])
        for w in weights:
            vals.extend([w * kb[c] for c in range(3)])
        return tuple(a + v for a, v in zip(accs, vals))

    zero = jnp.zeros((8, chunk), jnp.float32)
    accs = lax.fori_loop(0, 128 // 8, body, (zero,) * N_QTY, unroll=True)
    valid = aux_ref[24:25, :]
    for q in range(N_QTY):
        out_ref[q : q + 1, :] = jnp.sum(accs[q], axis=0, keepdims=True) * valid
    out_ref[N_QTY:, :] = jnp.zeros((32 - N_QTY, chunk), jnp.float32)
    if from_cargo:
        _send_back(n_band, out_ref, recv_ref, ret_ref, send_sems, recv_sems, own_sem)


def _greet(n_band, total):
    me = lax.axis_index("tile") * n_band + lax.axis_index("band")
    barrier = pltpu.get_barrier_semaphore()

    @pl.when(pl.program_id(0) == 0)
    def _():
        def greet(k, carry):
            p = lax.rem(me + k, total)
            pl.semaphore_signal(
                barrier, inc=1, device_id=(p // n_band, p % n_band), device_id_type=MESH
            )
            return carry

        lax.fori_loop(1, total, greet, 0)


def _send_back(n_band, out_ref, recv_ref, ret_ref, send_sems, recv_sems, own_sem):
    chunk = out_ref.shape[1]
    peers = chunk // CAP
    total = recv_ref.shape[0]
    step = pl.program_id(0)
    last = pl.num_programs(0) - 1
    me = lax.axis_index("tile") * n_band + lax.axis_index("band")
    barrier = pltpu.get_barrier_semaphore()

    def device(p):
        return (p // n_band, p % n_band)

    def copy_to(p):
        return pltpu.make_async_remote_copy(
            src_ref=ret_ref.at[p],
            dst_ref=recv_ref.at[me],
            send_sem=send_sems.at[p],
            recv_sem=recv_sems.at[me],
            device_id=device(p),
            device_id_type=MESH,
        )

    def copy_from(p):
        return pltpu.make_async_remote_copy(
            src_ref=ret_ref.at[p],
            dst_ref=recv_ref.at[p],
            send_sem=send_sems.at[p],
            recv_sem=recv_sems.at[p],
            device_id=device(p),
            device_id_type=MESH,
        )

    own = pltpu.make_async_copy(ret_ref.at[me], recv_ref.at[me], own_sem)

    padded = jnp.concatenate([out_ref[...], jnp.zeros((128 - 32, chunk), jnp.float32)], axis=0)
    ret_ref[pl.ds(pl.multiple_of(step * peers, peers), peers)] = padded.T.reshape(peers, CAP, 128)

    hold = jnp.minimum(4, last)

    @pl.when(step == hold)
    def _():
        pl.semaphore_wait(barrier, total - 1)

    def start(q, carry):
        p = q

        @pl.when(p != me)
        def _():
            copy_to(p).start()

        @pl.when(p == me)
        def _():
            own.start()

        return carry

    @pl.when(step == hold)
    def _():
        lax.fori_loop(0, (hold + 1) * peers, start, 0)

    @pl.when(step > hold)
    def _():
        lax.fori_loop(step * peers, (step + 1) * peers, start, 0)

    @pl.when(step == last)
    def _():
        def finish(k, carry):
            p = lax.rem(me + k, total)
            copy_to(p).wait_send()
            copy_from(p).wait_recv()
            return carry

        lax.fori_loop(1, total, finish, 0)
        own.wait()


def pair_sums(xa, tb, maps, aux, n_band=1, chunk=128):
    pairs = tb.shape[1]
    from_cargo = maps is None
    scratch = [
        pltpu.VMEM((3, 128, chunk), jnp.float32),
        pltpu.VMEM((6, 128, chunk), jnp.float32),
        pltpu.VMEM((4, chunk, 128), jnp.float32),
    ]
    out_shape = jax.ShapeDtypeStruct((32, pairs), jnp.float32)
    out_specs = pl.BlockSpec((32, chunk), lambda i: (0, i))
    params = None
    if from_cargo:
        xa = xa.reshape(-1, 128)
        xa_spec = pl.BlockSpec((chunk // CAP * (4 * CAP + 1), 128), lambda i: (i, 0))
        maps = aux
        map_spec = pl.BlockSpec((8, 128), lambda i: (0, 0))
        peers = pairs // CAP
        out_shape = (out_shape, jax.ShapeDtypeStruct((peers, CAP, 128), jnp.float32))
        out_specs = (out_specs, pl.BlockSpec(memory_space=pl.ANY))
        scratch += [
            pltpu.VMEM((peers, CAP, 128), jnp.float32),
            pltpu.SemaphoreType.DMA((peers,)),
            pltpu.SemaphoreType.DMA((peers,)),
            pltpu.SemaphoreType.DMA(()),
        ]
        params = pltpu.CompilerParams(collective_id=0, has_side_effects=True)
    else:
        xa_spec = pl.BlockSpec((3, chunk, 128), lambda i: (0, i, 0))
        map_spec = pl.BlockSpec((chunk, 128), lambda i: (i, 0))
    return pl.pallas_call(
        functools.partial(_terms_kernel, from_cargo, n_band),
        out_shape=out_shape,
        grid=(pairs // chunk,),
        in_specs=[
            xa_spec,
            pl.BlockSpec((6, chunk, 128), lambda i: (0, i, 0)),
            map_spec,
            pl.BlockSpec((32, chunk), lambda i: (0, i)),
        ],
        out_specs=out_specs,
        scratch_shapes=scratch,
        compiler_params=params,
    )(xa, tb, maps, aux)


def _cargo_kernel(xa_ref, map_ref, side_ref, out_ref):
    height = 4 * CAP + 1
    group = 8

    def body(g, carry):
        for q in range(group):
            p = g * group + q
            base = pl.multiple_of(g * (group * height), 8) + q * height
            slots = pl.ds(pl.multiple_of(p * CAP, CAP), CAP)
            for c in range(3):
                out_ref[pl.ds(base + c * CAP, CAP), :] = xa_ref[c, slots, :]
            out_ref[pl.ds(base + 3 * CAP, CAP), :] = map_ref[slots, :].astype(jnp.float32)
            out_ref[pl.ds(base + 4 * CAP, 1), :] = side_ref[pl.ds(p, 1), :]
        return carry

    lax.fori_loop(0, side_ref.shape[0] // group, body, 0)


def build_cargo(xa3, maps, side):
    slots = maps.shape[0]
    height = 4 * CAP + 1
    cargo = pl.pallas_call(
        _cargo_kernel,
        out_shape=jax.ShapeDtypeStruct((slots // CAP * height, 128), jnp.float32),
    )(xa3, maps, side)
    return cargo.reshape(slots // CAP, 1, height * 128)


def split_terms(out):
    sel = out[0:N_QTY].T
    ga = sel[:, 0:6] * (1.0 / 128)
    ha = sel[:, 6:18] * (1.0 / 4096)
    gb = -jnp.concatenate([sel[:, 18:21], sel[:, 3:6]], axis=1) * (1.0 / 128)
    hb0 = -jnp.concatenate([sel[:, 21:24], sel[:, 9:12]], axis=1) * (1.0 / 4096)
    hb1 = -jnp.concatenate([sel[:, 24:27], sel[:, 15:18]], axis=1) * (1.0 / 4096)
    return jnp.concatenate([ga, ha], axis=1), jnp.concatenate([gb, hb0, hb1], axis=1)


def _exchange_kernel(n_band, x_ref, out_ref, send_sems, recv_sems, own_sem):
    peers = x_ref.shape[0]
    me = lax.axis_index("tile") * n_band + lax.axis_index("band")

    def peer_of(k):
        p = lax.rem(me + k, peers)
        return p, (p // n_band, p % n_band)

    barrier = pltpu.get_barrier_semaphore()

    def greet(k, carry):
        _, dev = peer_of(k)
        pl.semaphore_signal(barrier, inc=1, device_id=dev, device_id_type=MESH)
        return carry

    lax.fori_loop(1, peers, greet, 0)
    pl.semaphore_wait(barrier, peers - 1)

    own = pltpu.make_async_copy(x_ref.at[me], out_ref.at[me], own_sem)
    own.start()

    def outgoing(k):
        p, dev = peer_of(k)
        return pltpu.make_async_remote_copy(
            src_ref=x_ref.at[p],
            dst_ref=out_ref.at[me],
            send_sem=send_sems.at[p],
            recv_sem=recv_sems.at[me],
            device_id=dev,
            device_id_type=MESH,
        )

    def incoming(k):
        p, dev = peer_of(k)
        return pltpu.make_async_remote_copy(
            src_ref=x_ref.at[p],
            dst_ref=out_ref.at[p],
            send_sem=send_sems.at[p],
            recv_sem=recv_sems.at[p],
            device_id=dev,
            device_id_type=MESH,
        )

    def start(k, carry):
        outgoing(k).start()
        return carry

    lax.fori_loop(1, peers, start, 0)

    def finish(k, carry):
        outgoing(k).wait_send()
        incoming(k).wait_recv()
        return carry

    lax.fori_loop(1, peers, finish, 0)
    own.wait()


def exchange(x, n_band, collective_id):
    peers = x.shape[0]
    return pl.pallas_call(
        functools.partial(_exchange_kernel, n_band),
        out_shape=jax.ShapeDtypeStruct(x.shape, x.dtype),
        in_specs=[pl.BlockSpec(memory_space=pl.ANY)],
        out_specs=pl.BlockSpec(memory_space=pl.ANY),
        scratch_shapes=[
            pltpu.SemaphoreType.DMA((peers,)),
            pltpu.SemaphoreType.DMA((peers,)),
            pltpu.SemaphoreType.DMA(()),
        ],
        compiler_params=pltpu.CompilerParams(collective_id=collective_id, has_side_effects=True),
    )(x)


def pick_rows(blocks, rows):
    onehot = (blocks[:, None] == jnp.arange(rows.shape[1], dtype=jnp.int32)[None, :]).astype(
        jnp.float32
    )
    return jnp.einsum("sb,cbk->csk", onehot, rows, precision=lax.Precision.HIGHEST)


def frag_sums(blocks, terms, frag_count):
    onehot = (blocks[:, None] // BF == jnp.arange(frag_count, dtype=jnp.int32)[None, :]).astype(
        jnp.float32
    )
    return jnp.dot(onehot.T, terms, precision=lax.Precision.HIGHEST)


def make_aux(dirs_a, dirs_b, valid):
    pairs = dirs_a.shape[0]
    return jnp.concatenate(
        [dirs_a.T, dirs_b.T, valid[None, :], jnp.zeros((32 - 25, pairs), jnp.float32)], axis=0
    )


def local(
    points,
    normals,
    poses,
    directions,
    local_pairs,
    local_maps,
    remote_src,
    remote_maps,
    remote_dst,
    counts,
):
    axes = ("tile", "band")
    n_band = lax.axis_size("band")
    frag_count = poses.shape[1]
    rows6 = to_world_rows(points, normals, poses, BF)
    frag_dirs = directions.reshape(12, frag_count).T
    peers = counts.shape[1]

    source_blocks = remote_src[0]
    valid = (
        (jnp.arange(CAP, dtype=jnp.int32)[None, :] < counts[0][:, None])
        .astype(jnp.float32)
        .reshape(-1)
    )
    frag_pick = (
        source_blocks[:, None] // BF == jnp.arange(frag_count, dtype=jnp.int32)[None, :]
    ).astype(jnp.float32)
    dirs_send = jnp.dot(frag_pick, frag_dirs, precision=lax.Precision.HIGHEST)
    side = jnp.concatenate([dirs_send, valid[:, None]], axis=1)
    side = side.reshape(peers, CAP * 13)
    side = jnp.concatenate([side, jnp.zeros((peers, 128 - CAP * 13), jnp.float32)], axis=1)
    cargo = build_cargo(pick_rows(source_blocks, rows6[0:3]), remote_maps[0], side)
    arrived = lax.all_to_all(cargo, axes, split_axis=0, concat_axis=0, tiled=True)

    src_l = local_pairs[0]
    tgt_l = local_pairs[1]
    ones = jnp.ones((src_l.shape[0],), jnp.float32)
    out_l = pair_sums(
        pick_rows(src_l, rows6[0:3]),
        pick_rows(tgt_l, rows6),
        local_maps,
        make_aux(frag_dirs[src_l // BF], frag_dirs[tgt_l // BF], ones),
    )
    local_a, local_b = split_terms(out_l)

    target_blocks = remote_dst[0]
    side_in = arrived[:, 0, CAP * 4 * 128 : CAP * 4 * 128 + CAP * 13].reshape(peers * CAP, 13)
    out_r, back = pair_sums(
        arrived,
        pick_rows(target_blocks, rows6),
        None,
        make_aux(side_in[:, 0:12], frag_dirs[target_blocks // BF], side_in[:, 12]),
        n_band,
    )
    unused, remote_b = split_terms(out_r)
    returned, unused = split_terms(back.reshape(peers * CAP, 128)[:, 0:32].T)

    totals = frag_sums(src_l, local_a, frag_count) + frag_sums(tgt_l, local_b, frag_count)
    totals = (
        totals
        + frag_sums(target_blocks, remote_b, frag_count)
        + frag_sums(source_blocks, returned, frag_count)
    )
    gradient = totals[:, 0:6].T
    hess_products = totals[:, 6:18].T.reshape(2, 6, frag_count)
    return (gradient, hess_products)


def solution(mesh):
    placed = (
        P(("tile", "band"), None, None),
        P(("tile", "band"), None, None),
        P(None, ("tile", "band")),
        P(None, None, ("tile", "band")),
        P(None, ("tile", "band")),
        P(("tile", "band"), None),
        P(("tile", "band"), None),
        P(("tile", "band"), None, None),
        P(("tile", "band"), None),
        P(("tile", "band"), None),
    )
    return jax.shard_map(
        local,
        mesh=mesh,
        in_specs=placed,
        out_specs=(P(None, ("tile", "band")), P(None, None, ("tile", "band"))),
        check_vma=False,
    )
```
